32 devices in a mesh: batch: 4 (over y, x), seq: 4 (over z), seqb: 2 (over core).
Axes of the slice: x: 2, y: 2, z: 4, core: 2. Of those that a mesh axis runs over, the one named last changes fastest.
Arguments:
- tokens: bfloat16 [16, 1024, 768], P(('batch', 'seq'), 'seqb'), may hold values from -6 to 6
- lengths: int32 [16], P(('batch', 'seq')), may hold values from 65 to 1024, as said below
- owner: int32 [16, 2], P(('batch', 'seq')), may hold values from 0 to 1, each once within a row
- w_query: bfloat16 [768, 768], replicated, may hold values from -0.21875 to 0.21875
- w_key: bfloat16 [768, 768], replicated, may hold values from -0.21875 to 0.21875
- w_value: bfloat16 [768, 768], replicated, may hold values from -0.21875 to 0.21875
- w_out: bfloat16 [768, 768], replicated, may hold values from -6 to 6
- w_gate: bfloat16 [768, 2048], replicated, may hold values from -0.21875 to 0.21875
- w_up: bfloat16 [768, 2048], replicated, may hold values from -0.21875 to 0.21875
- w_down: bfloat16 [2048, 768], replicated, may hold values from -0.125 to 0.125
- gain_attn: float32 [768], replicated, may hold values from 0.25 to 1.75
- gain_mlp: float32 [768], replicated, may hold values from 0.25 to 1.75
- cotangent: bfloat16 [16, 1024, 768], P(('batch', 'seq'), 'seqb'), may hold values from -6 to 6
Outputs:
- layer_out: bfloat16 [16, 1024, 768], P(('batch', 'seq'), 'seqb')
- input_grad: bfloat16 [16, 1024, 768], P(('batch', 'seq'), 'seqb')
- grad_query: float32 [768, 768], P(('seq', 'seqb'))
- grad_key: float32 [768, 768], P(('seq', 'seqb'))
- grad_value: float32 [768, 768], P(('seq', 'seqb'))
- grad_out: float32 [768, 768], P(('seq', 'seqb'))
- grad_gate: float32 [768, 2048], P(('seq', 'seqb'))
- grad_up: float32 [768, 2048], P(('seq', 'seqb'))
- grad_down: float32 [2048, 768], P(('seq', 'seqb'))
- grad_gain_attn: float32 [768], P(('seq', 'seqb'))
- grad_gain_mlp: float32 [768], P(('seq', 'seqb'))
The draws below stay inside these ranges and needn't reach their ends.
Inputs may be any that keep to these rules, and one draw needn't show every extreme that they name: `lengths`: valid tokens of each sequence; in every draw some sequence has all 1024. Each row is a permutation; stored rows b * 512 to b * 512 + 511 of a sequence hold positions owner[b] * 512 onward.
All inputs are finite; a program needn't handle non-finite values.
Results may differ from the reference program's by a relative error of at most 0.022.
Values may be sent and summed in bfloat16 or wider, within the bound.
No kernel may reach another device: no remote copies, remote signals or barrier semaphores. Data moves between devices by JAX's collectives and lax.ppermute only.
A program may use at most 192 MiB of HBM per device.

```python
import math
import jax
import jax.numpy as jnp
from jax import lax

D = 768
HEADS = 12
HEAD_DIM = 64
FF = 2048
SEQLEN = 1024
SHARDS = 2
ROWS = 512
SEQS = 16


def draw_lengths(key, part):
    level_key, cut_key, pick_key = jax.random.split(key, 3)
    level = jax.random.randint(level_key, (SEQS,), 0, 4).astype(jnp.int32)
    span = jnp.right_shift(jnp.full((SEQS,), SEQLEN, jnp.int32), level)
    cut = jax.random.randint(cut_key, (SEQS,), 0, 1 << 20) % (span // 2)
    longest = jax.random.randint(pick_key, (), 0, SEQS)
    drawn = span - cut
    return jnp.where(jnp.arange(SEQS) == longest, SEQLEN, drawn).astype(jnp.int32)


def shard_levels(stream_key, shape, pieces, low, largest):
    factor_of = 1.0
    for position, shards_of in pieces:
        heights = jax.random.uniform(jax.random.fold_in(jax.random.fold_in(stream_key, 6), position), (shards_of,), jnp.float32, low / len(pieces), largest / len(pieces))
        factor_of = factor_of * jnp.repeat(jnp.exp(heights), shape[position] // shards_of).reshape((-1,) + (1,) * (len(shape) - 1 - position))
    return factor_of


def bell_draw(key, dims, scale, bound, pieces=(), kind=jnp.bfloat16):
    array = scale * jax.random.normal(key, dims, jnp.float32)
    if pieces:
        array = array * shard_levels(key, dims, pieces, -0.22, 0.18)
    return jnp.clip(array, -bound, bound).astype(kind)


def setup_inputs(seed: int = 0) -> dict:
    key_list = jax.random.split(jax.random.key(seed), 14)
    tokens = bell_draw(key_list[0], (SEQS, SEQLEN, D), 1.0, 6.0, ((0, 16), (1, 2)))
    lengths = draw_lengths(jax.random.fold_in(key_list[13], 71), 0)
    owner = jax.vmap(lambda own: jax.random.permutation(own, SHARDS))(jax.random.split(key_list[2], SEQS)).reshape((SEQS, SHARDS)).astype(jnp.int32)
    w_query = bell_draw(key_list[3], (D, D), D ** -0.5, 0.21875)
    w_key = bell_draw(key_list[4], (D, D), D ** -0.5, 0.21875)
    w_value = bell_draw(key_list[5], (D, D), D ** -0.5, 0.21875)
    w_out = bell_draw(key_list[6], (D, D), 1 ** -0.5, 6.0)
    w_gate = bell_draw(key_list[7], (D, FF), D ** -0.5, 0.21875)
    w_up = bell_draw(key_list[8], (D, FF), D ** -0.5, 0.21875)
    w_down = bell_draw(key_list[9], (FF, D), FF ** -0.5, 0.125)
    gain_attn = jnp.clip(1.0 + 0.15 * jax.random.normal(key_list[10], (D,), jnp.float32), 0.25, 1.75)
    gain_mlp = jnp.clip(1.0 + 0.15 * jax.random.normal(key_list[11], (D,), jnp.float32), 0.25, 1.75)
    cotangent = bell_draw(key_list[12], (SEQS, SEQLEN, D), 1.0, 6.0, ((0, 16), (1, 2)))
    return {"tokens": tokens, "lengths": lengths, "owner": owner, "w_query": w_query, "w_key": w_key, "w_value": w_value, "w_out": w_out, "w_gate": w_gate, "w_up": w_up, "w_down": w_down, "gain_attn": gain_attn, "gain_mlp": gain_mlp, "cotangent": cotangent}


@jax.custom_vjp
def low(v):
    return lax.optimization_barrier(v.astype(jnp.bfloat16)).astype(jnp.float32)

@jax.custom_vjp
def low_back(v):
    return v

def low_keep(v):
    return (low(v), None)

def low_pass(kept, grad):
    return (grad,)

def back_keep(v):
    return (v, None)

def back_low(kept, grad):
    return (low(grad),)
low.defvjp(low_keep, low_pass)
low_back.defvjp(back_keep, back_low)
epsilon = 1e-05
rope_base = 10000.0
masked_score = -1e+30
highest = lax.Precision.HIGHEST

def rms_scale(rows, gain):
    return rows * lax.rsqrt(lax.optimization_barrier(jnp.mean(rows * rows, axis=-1, keepdims=True)) + epsilon) * gain

def rotation_tables(positions):
    half = HEAD_DIM // 2
    freq = rope_base ** (-(2.0 * jnp.arange(half, dtype=jnp.float32)) / HEAD_DIM)
    angles = positions.astype(jnp.float32)[:, None] * freq[None, :]
    return (jnp.cos(angles), jnp.sin(angles))

def rotate(rows, cosine, sine):
    shaped = rows.reshape(rows.shape[0], HEADS, HEAD_DIM)
    half = HEAD_DIM // 2
    first = shaped[..., :half]
    second = shaped[..., half:]
    cos_part = cosine[:, None, :]
    sin_part = sine[:, None, :]
    return jnp.concatenate([first * cos_part - second * sin_part, second * cos_part + first * sin_part], axis=-1)

def layer_forward(inputs, w_query, w_key, w_value, w_out, w_gate, w_up, w_down, gain_attn, gain_mlp, positions, live, cosine, sine):
    total_rows = inputs.shape[0]
    rows = jnp.where(live[:, None], inputs, 0.0)
    normed = low(rms_scale(rows, gain_attn))
    query_pre = low_back(jnp.dot(normed, w_query, precision=highest))
    key_pre = low_back(jnp.dot(normed, w_key, precision=highest))
    values = low(low_back(jnp.dot(normed, w_value, precision=highest))).reshape(total_rows, HEADS, HEAD_DIM)
    queries = low(rotate(query_pre, cosine, sine))
    keys = low(rotate(key_pre, cosine, sine))
    block_rows = math.gcd(total_rows, 512)
    scale = HEAD_DIM ** (-0.5)

    def attend(block):
        query_block, query_pos = block
        scores = low_back(jnp.einsum('qhd,khd->hqk', query_block, keys, precision=highest) * scale)
        allowed = (positions[None, :] <= query_pos[:, None]) & live[None, :]
        scores = jnp.where(allowed[None], scores, masked_score)
        shifted = scores - lax.optimization_barrier(jnp.max(scores, axis=-1, keepdims=True))
        expo = jnp.exp(shifted)
        weights = expo / lax.optimization_barrier(jnp.sum(expo, axis=-1, keepdims=True))
        return jnp.einsum('hqk,khd->qhd', low(weights), values, precision=highest)
    blocks = total_rows // block_rows
    mixed = lax.map(jax.checkpoint(attend), (queries.reshape(blocks, block_rows, HEADS, HEAD_DIM), positions.reshape(blocks, block_rows)))
    attn = low(low_back(mixed.reshape(total_rows, D)))
    middle = rows + low_back(jnp.dot(attn, w_out, precision=highest))
    normed_mlp = low(rms_scale(middle, gain_mlp))
    gate = low_back(jnp.dot(normed_mlp, w_gate, precision=highest))
    up_proj = low_back(jnp.dot(normed_mlp, w_up, precision=highest))
    hidden = low(jax.nn.silu(gate) * up_proj)
    out = middle + jnp.dot(hidden, w_down, precision=highest)
    return jnp.where(live[:, None], out, 0.0)

def reference(tokens, lengths, owner, w_query, w_key, w_value, w_out, w_gate, w_up, w_down, gain_attn, gain_mlp, cotangent):
    params = (w_query.astype(jnp.float32), w_key.astype(jnp.float32), w_value.astype(jnp.float32), w_out.astype(jnp.float32), w_gate.astype(jnp.float32), w_up.astype(jnp.float32), w_down.astype(jnp.float32), gain_attn.astype(jnp.float32), gain_mlp.astype(jnp.float32))
    row_ids = jnp.arange(SEQLEN, dtype=jnp.int32)

    def one_sequence(sums, slot):
        inputs, upstream, length, order = slot
        positions = (order[row_ids // ROWS] * ROWS + row_ids % ROWS).astype(jnp.int32)
        live = positions < length
        cosine, sine = rotation_tables(positions)

        def forward(rows, p_query, p_key, p_value, p_out, p_gate, p_up, p_down, p_gain_attn, p_gain_mlp):
            return layer_forward(rows, p_query, p_key, p_value, p_out, p_gate, p_up, p_down, p_gain_attn, p_gain_mlp, positions, live, cosine, sine)
        out, pull = jax.vjp(forward, inputs.astype(jnp.float32), *params)
        grads = pull(upstream.astype(jnp.float32))
        sums = tuple((total + grad for total, grad in zip(sums, grads[1:])))
        return (sums, (out.astype(jnp.bfloat16), grads[0].astype(jnp.bfloat16)))
    start_sums = tuple((jnp.zeros(p.shape, jnp.float32) for p in params))
    sums, (outputs, input_grads) = lax.scan(one_sequence, start_sums, (tokens, cotangent, lengths, owner))
    return (outputs, input_grads, sums[0], sums[1], sums[2], sums[3], sums[4], sums[5], sums[6], sums[7], sums[8])
```

```python
import functools
import math

import jax
import jax.numpy as jnp
import numpy as np
from jax import lax
from jax.experimental import pallas as pl
from jax.experimental.pallas import tpu as pltpu
from jax.sharding import PartitionSpec as P

HEADS = 12
HEAD_DIM = 64


epsilon = 1e-05
rope_base = 10000.0
masked_score = -1e30


def rms_forward(rows, gain):
    factor = lax.rsqrt(jnp.mean(rows * rows, axis=-1, keepdims=True) + epsilon)
    return (rows * factor * gain, factor)


def rms_backward(rows, factor, gain, upstream):
    scaled = upstream * gain
    return factor * scaled - rows * (factor * factor * factor) * jnp.mean(
        rows * scaled, axis=-1, keepdims=True
    )


def rotation_tables(positions):
    half = HEAD_DIM // 2
    freq = rope_base ** (-(2.0 * jnp.arange(half, dtype=jnp.float32)) / HEAD_DIM)
    angles = positions.astype(jnp.float32)[..., None] * freq
    return (jnp.cos(angles), jnp.sin(angles))


def split_heads(rows):
    return rows.reshape(rows.shape[0], rows.shape[1], HEADS, HEAD_DIM)


def rotate(rows, cosine, sine, inverse):
    shaped = split_heads(rows)
    half = HEAD_DIM // 2
    first = shaped[..., :half]
    second = shaped[..., half:]
    cos_part = cosine[:, :, None, :]
    sin_part = sine[:, :, None, :]
    if inverse:
        turned = jnp.concatenate(
            [first * cos_part + second * sin_part, second * cos_part - first * sin_part], axis=-1
        )
    else:
        turned = jnp.concatenate(
            [first * cos_part - second * sin_part, second * cos_part + first * sin_part], axis=-1
        )
    return turned.reshape(rows.shape)


def range_positions(owner, count, span):
    offsets = jnp.arange(span, dtype=jnp.int32)
    return (owner[:, :, None] * span + offsets[None, None, :]).reshape(owner.shape[0], count)


def fold_keys(parts, combine, initial):
    return combine(
        initial,
        (
            lax.all_gather(parts[0], "seqb", axis=1, tiled=True),
            lax.all_gather(parts[1], "seqb", axis=1, tiled=True),
        ),
        jnp.int32(0),
    )


def general_step(
    tokens,
    lengths,
    owner,
    w_query,
    w_key,
    w_value,
    w_out,
    w_gate,
    w_up,
    w_down,
    gain_attn,
    gain_mlp,
    cotangent,
):
    seqs, span, width = tokens.shape
    scale = HEAD_DIM ** (-0.5)
    place = lax.axis_index("seqb")
    own_block = lax.dynamic_slice_in_dim(owner, place, 1, 1)
    local_pos = own_block * span + jnp.arange(span, dtype=jnp.int32)[None, :]
    local_live = local_pos < lengths[:, None]
    live_rows = local_live[:, :, None]
    inputs = jnp.where(live_rows, tokens.astype(jnp.float32), 0.0)
    normed, factor_attn = rms_forward(inputs, gain_attn)
    normed_low = normed.astype(jnp.bfloat16)
    cosine, sine = rotation_tables(local_pos)
    query_pre = jnp.einsum("scd,de->sce", normed_low, w_query, preferred_element_type=jnp.float32)
    key_pre = jnp.einsum("scd,de->sce", normed_low, w_key, preferred_element_type=jnp.float32)
    value_low = jnp.einsum(
        "scd,de->sce", normed_low, w_value, preferred_element_type=jnp.float32
    ).astype(jnp.bfloat16)
    query_rot = rotate(query_pre, cosine, sine, False).astype(jnp.bfloat16)
    key_rot = rotate(key_pre, cosine, sine, False).astype(jnp.bfloat16)
    query_heads = split_heads(query_rot)
    key_heads = split_heads(key_rot)
    value_heads = split_heads(value_low)

    def attend(state, piece, start):
        keys, values = piece
        count = keys.shape[1]
        key_pos = range_positions(owner, count, span)
        key_live = key_pos < lengths[:, None]
        stride = math.gcd(count, 512)

        def attend_one_block(index, inner):
            offset = index * stride
            key_block = split_heads(lax.dynamic_slice_in_dim(keys, offset, stride, 1))
            value_block = split_heads(lax.dynamic_slice_in_dim(values, offset, stride, 1))
            pos_block = lax.dynamic_slice_in_dim(key_pos, offset, stride, 1)
            live_block = lax.dynamic_slice_in_dim(key_live, offset, stride, 1)
            allowed = (
                (pos_block[:, None, :] <= local_pos[:, :, None])
                & live_block[:, None, :]
                & local_live[:, :, None]
            )

            def attend_update(carried):
                peak, total, summed = carried
                scores = (
                    jnp.einsum(
                        "sqhd,skhd->shqk",
                        query_heads,
                        key_block,
                        preferred_element_type=jnp.float32,
                    )
                    * scale
                )
                mask = allowed[:, None, :, :]
                new_peak = jnp.maximum(
                    peak, jnp.max(jnp.where(mask, scores, masked_score), axis=-1)
                )
                weights = jnp.where(mask, jnp.exp(scores - new_peak[..., None]), 0.0)
                factor = jnp.exp(peak - new_peak)
                total = total * factor + jnp.sum(weights, axis=-1)
                term = jnp.einsum(
                    "shqk,skhd->sqhd",
                    weights.astype(jnp.bfloat16),
                    value_block,
                    preferred_element_type=jnp.float32,
                )
                summed = (
                    split_heads(summed) * jnp.transpose(factor, (0, 2, 1))[..., None] + term
                ).reshape(summed.shape)
                return (new_peak, total, summed)

            return lax.cond(jnp.any(allowed), attend_update, lambda carried: carried, inner)

        return lax.fori_loop(0, count // stride, attend_one_block, state)

    start_state = (
        jnp.full((seqs, HEADS, span), masked_score, jnp.float32),
        jnp.zeros((seqs, HEADS, span), jnp.float32),
        jnp.zeros((seqs, span, width), jnp.float32),
    )
    peak, total, summed = fold_keys((key_rot, value_low), attend, start_state)
    safe_total = jnp.where(local_live[:, None, :], total, 1.0)
    attn = split_heads(summed) / jnp.transpose(safe_total, (0, 2, 1))[..., None]
    attn = jnp.where(local_live[:, :, None, None], attn, 0.0).reshape(seqs, span, width)
    log_total = jnp.where(local_live[:, None, :], peak + jnp.log(safe_total), 0.0)
    attn_low = attn.astype(jnp.bfloat16)
    middle = inputs + jnp.einsum("scd,de->sce", attn_low, w_out, preferred_element_type=jnp.float32)
    normed_mlp, factor_mlp = rms_forward(middle, gain_mlp)
    normed_mlp_low = normed_mlp.astype(jnp.bfloat16)
    gate = jnp.einsum("scd,df->scf", normed_mlp_low, w_gate, preferred_element_type=jnp.float32)
    up_proj = jnp.einsum("scd,df->scf", normed_mlp_low, w_up, preferred_element_type=jnp.float32)
    hidden = (jax.nn.silu(gate) * up_proj).astype(jnp.bfloat16)
    out = middle + jnp.einsum("scf,fd->scd", hidden, w_down, preferred_element_type=jnp.float32)
    layer_out = jnp.where(live_rows, out, 0.0).astype(jnp.bfloat16)
    upstream = jnp.where(live_rows, cotangent, jnp.zeros_like(cotangent))
    grad_down = jnp.einsum("scf,scd->fd", hidden, upstream, preferred_element_type=jnp.float32)
    d_hidden = jnp.einsum("scd,fd->scf", upstream, w_down, preferred_element_type=jnp.float32)
    sigmoid_gate = jax.nn.sigmoid(gate)
    d_gate = (d_hidden * up_proj * sigmoid_gate * (1.0 + gate * (1.0 - sigmoid_gate))).astype(
        jnp.bfloat16
    )
    d_up = (d_hidden * gate * sigmoid_gate).astype(jnp.bfloat16)
    grad_gate = jnp.einsum(
        "scd,scf->df", normed_mlp_low, d_gate, preferred_element_type=jnp.float32
    )
    grad_up = jnp.einsum("scd,scf->df", normed_mlp_low, d_up, preferred_element_type=jnp.float32)
    d_normed_mlp = jnp.einsum(
        "scf,df->scd", d_gate, w_gate, preferred_element_type=jnp.float32
    ) + jnp.einsum("scf,df->scd", d_up, w_up, preferred_element_type=jnp.float32)
    grad_gain_mlp = jnp.sum(d_normed_mlp * (middle * factor_mlp), axis=(0, 1))
    d_middle = upstream.astype(jnp.float32) + rms_backward(
        middle, factor_mlp, gain_mlp, d_normed_mlp
    )
    d_branch = d_middle.astype(jnp.bfloat16)
    grad_out = jnp.einsum("scd,sce->de", attn_low, d_branch, preferred_element_type=jnp.float32)
    d_attn = jnp.einsum("sce,de->scd", d_branch, w_out, preferred_element_type=jnp.float32).astype(
        jnp.bfloat16
    )
    first_done = (grad_out, grad_gate, grad_up, grad_down, grad_gain_mlp)
    delta = jnp.sum(split_heads(d_attn.astype(jnp.float32) * attn), axis=-1)
    delta_heads = jnp.transpose(delta, (0, 2, 1))
    grad_heads = split_heads(d_attn)

    def query_grads(state, piece, start):
        keys, values = piece
        count = keys.shape[1]
        key_pos = range_positions(owner, count, span)
        key_live = key_pos < lengths[:, None]
        stride = math.gcd(count, 512)

        def query_one_block(index, inner):
            offset = index * stride
            key_block = split_heads(lax.dynamic_slice_in_dim(keys, offset, stride, 1))
            value_block = split_heads(lax.dynamic_slice_in_dim(values, offset, stride, 1))
            pos_block = lax.dynamic_slice_in_dim(key_pos, offset, stride, 1)
            live_block = lax.dynamic_slice_in_dim(key_live, offset, stride, 1)
            allowed = (
                (pos_block[:, None, :] <= local_pos[:, :, None])
                & live_block[:, None, :]
                & local_live[:, :, None]
            )

            def query_update(carried):
                scores = (
                    jnp.einsum(
                        "sqhd,skhd->shqk",
                        query_heads,
                        key_block,
                        preferred_element_type=jnp.float32,
                    )
                    * scale
                )
                probs = jnp.where(
                    allowed[:, None, :, :], jnp.exp(scores - log_total[..., None]), 0.0
                )
                d_probs = jnp.einsum(
                    "sqhd,skhd->shqk", grad_heads, value_block, preferred_element_type=jnp.float32
                )
                d_scores = (probs * (d_probs - delta_heads[..., None])).astype(jnp.bfloat16)
                term = (
                    jnp.einsum(
                        "shqk,skhd->sqhd", d_scores, key_block, preferred_element_type=jnp.float32
                    )
                    * scale
                )
                return carried + term.reshape(carried.shape)

            return lax.cond(jnp.any(allowed), query_update, lambda carried: carried, inner)

        return lax.fori_loop(0, count // stride, query_one_block, state)

    zero_query = jnp.zeros((seqs, span, width), jnp.float32)
    d_query = fold_keys((key_rot, value_low), query_grads, zero_query)
    lse_all, delta_all = (
        lax.all_gather(jnp.transpose(log_total, (0, 2, 1)), "seqb", axis=1, tiled=True),
        lax.all_gather(delta, "seqb", axis=1, tiled=True),
    )
    zero_rows = jnp.zeros((seqs, span, width), jnp.float32)
    queries = lax.all_gather(query_rot, "seqb", axis=1, tiled=True)
    d_rows = lax.all_gather(d_attn, "seqb", axis=1, tiled=True)
    count = queries.shape[1]
    row_pos = range_positions(owner, count, span)
    row_live = row_pos < lengths[:, None]
    stride = math.gcd(count, 512)

    def key_one_block(index, inner):
        offset = index * stride
        query_block = split_heads(lax.dynamic_slice_in_dim(queries, offset, stride, 1))
        grad_block = split_heads(lax.dynamic_slice_in_dim(d_rows, offset, stride, 1))
        pos_block = lax.dynamic_slice_in_dim(row_pos, offset, stride, 1)
        live_block = lax.dynamic_slice_in_dim(row_live, offset, stride, 1)
        lse_block = jnp.transpose(lax.dynamic_slice_in_dim(lse_all, offset, stride, 1), (0, 2, 1))
        delta_block = jnp.transpose(
            lax.dynamic_slice_in_dim(delta_all, offset, stride, 1), (0, 2, 1)
        )
        allowed = (
            (local_pos[:, None, :] <= pos_block[:, :, None])
            & local_live[:, None, :]
            & live_block[:, :, None]
        )

        def key_update(carried):
            d_key, d_value = carried
            scores = (
                jnp.einsum(
                    "sqhd,skhd->shqk", query_block, key_heads, preferred_element_type=jnp.float32
                )
                * scale
            )
            probs = jnp.where(allowed[:, None, :, :], jnp.exp(scores - lse_block[..., None]), 0.0)
            value_term = jnp.einsum(
                "shqk,sqhd->skhd",
                probs.astype(jnp.bfloat16),
                grad_block,
                preferred_element_type=jnp.float32,
            )
            d_probs = jnp.einsum(
                "sqhd,skhd->shqk", grad_block, value_heads, preferred_element_type=jnp.float32
            )
            d_scores = (probs * (d_probs - delta_block[..., None])).astype(jnp.bfloat16)
            key_term = (
                jnp.einsum(
                    "shqk,sqhd->skhd", d_scores, query_block, preferred_element_type=jnp.float32
                )
                * scale
            )
            return (
                d_key + key_term.reshape(d_key.shape),
                d_value + value_term.reshape(d_value.shape),
            )

        return lax.cond(jnp.any(allowed), key_update, lambda carried: carried, inner)

    d_key, d_value = lax.fori_loop(0, count // stride, key_one_block, (zero_rows, zero_rows))
    d_query_pre = rotate(d_query, cosine, sine, True).astype(jnp.bfloat16)
    d_key_pre = rotate(d_key, cosine, sine, True).astype(jnp.bfloat16)
    d_value_low = d_value.astype(jnp.bfloat16)
    grad_query = jnp.einsum(
        "scd,sce->de", normed_low, d_query_pre, preferred_element_type=jnp.float32
    )
    grad_key = jnp.einsum("scd,sce->de", normed_low, d_key_pre, preferred_element_type=jnp.float32)
    grad_value = jnp.einsum(
        "scd,sce->de", normed_low, d_value_low, preferred_element_type=jnp.float32
    )
    d_normed = jnp.einsum("sce,de->scd", d_query_pre, w_query, preferred_element_type=jnp.float32)
    d_normed = d_normed + jnp.einsum(
        "sce,de->scd", d_key_pre, w_key, preferred_element_type=jnp.float32
    )
    d_normed = d_normed + jnp.einsum(
        "sce,de->scd", d_value_low, w_value, preferred_element_type=jnp.float32
    )
    grad_gain_attn = jnp.sum(d_normed * (inputs * factor_attn), axis=(0, 1))
    d_inputs = d_middle + rms_backward(inputs, factor_attn, gain_attn, d_normed)
    input_grad = jnp.where(live_rows, d_inputs, 0.0).astype(jnp.bfloat16)
    summed_parts = (
        lax.psum_scatter(grad_query, ("seq", "seqb"), scatter_dimension=0, tiled=True),
        lax.psum_scatter(grad_key, ("seq", "seqb"), scatter_dimension=0, tiled=True),
        lax.psum_scatter(grad_value, ("seq", "seqb"), scatter_dimension=0, tiled=True),
        lax.psum_scatter(grad_gain_attn, ("seq", "seqb"), scatter_dimension=0, tiled=True),
        lax.psum_scatter(first_done[0], ("seq", "seqb"), scatter_dimension=0, tiled=True),
        lax.psum_scatter(first_done[1], ("seq", "seqb"), scatter_dimension=0, tiled=True),
        lax.psum_scatter(first_done[2], ("seq", "seqb"), scatter_dimension=0, tiled=True),
        lax.psum_scatter(first_done[3], ("seq", "seqb"), scatter_dimension=0, tiled=True),
        lax.psum_scatter(first_done[4], ("seq", "seqb"), scatter_dimension=0, tiled=True),
    )
    all_done = (
        lax.psum(summed_parts[0].astype(jnp.bfloat16), "batch").astype(jnp.float32),
        lax.psum(summed_parts[1].astype(jnp.bfloat16), "batch").astype(jnp.float32),
        lax.psum(summed_parts[2].astype(jnp.bfloat16), "batch").astype(jnp.float32),
        lax.psum(summed_parts[3].astype(jnp.bfloat16), "batch").astype(jnp.float32),
        lax.psum(summed_parts[4].astype(jnp.bfloat16), "batch").astype(jnp.float32),
        lax.psum(summed_parts[5].astype(jnp.bfloat16), "batch").astype(jnp.float32),
        lax.psum(summed_parts[6].astype(jnp.bfloat16), "batch").astype(jnp.float32),
        lax.psum(summed_parts[7].astype(jnp.bfloat16), "batch").astype(jnp.float32),
        lax.psum(summed_parts[8].astype(jnp.bfloat16), "batch").astype(jnp.float32),
    )
    second_done = (all_done[0], all_done[1], all_done[2], all_done[3])
    first_done = (all_done[4], all_done[5], all_done[6], all_done[7], all_done[8])
    return (
        layer_out,
        input_grad,
        second_done[0],
        second_done[1],
        second_done[2],
        first_done[0],
        first_done[1],
        first_done[2],
        first_done[3],
        second_done[3],
        first_done[4],
    )


AXES = ("batch", "seq", "seqb")
BF = jnp.bfloat16
F32 = jnp.float32
MIB = 1 << 20


def fast_layout(mesh):
    return mesh.shape["batch"] == 4 and mesh.shape["seq"] == 4 and mesh.shape["seqb"] == 2


def exchange(rows, kind):
    pairs = []
    for b in range(4):
        for s in range(4):
            for c in range(2):
                first = 1 if c == 0 else 2
                target = {
                    "core": (b, s, 1 - c),
                    "first": (b ^ first, s, c),
                    "second": (b ^ (3 - first), s, c),
                    "near": (b, s ^ 1, c),
                    "far": (b, s ^ 2, c),
                }[kind]
                pairs.append((b * 8 + s * 2 + c, target[0] * 8 + target[1] * 2 + target[2]))
    return lax.ppermute(rows, AXES, pairs)


def dot(a, b):
    return lax.dot_general(a, b, (((1,), (0,)), ((), ())), preferred_element_type=F32)


def dot_nt(a, b):
    return lax.dot_general(a, b, (((1,), (1,)), ((), ())), preferred_element_type=F32)


def position_tables(count):
    half = HEAD_DIM // 2
    freq = rope_base ** (-(2.0 * np.arange(half)) / HEAD_DIM)
    angles = np.arange(count)[:, None] * freq[None, :]
    cosine, sine = np.cos(angles), np.sin(angles)
    return (
        np.concatenate([cosine, cosine, cosine, cosine], 1).astype(np.float32),
        np.concatenate([-sine, sine, -sine, sine], 1).astype(np.float32),
    )


def swap_halves(u):
    lane = lax.broadcasted_iota(jnp.int32, u.shape, 1) % HEAD_DIM
    return jnp.where(lane < HEAD_DIM // 2, pltpu.roll(u, 96, 1), pltpu.roll(u, 32, 1))


def turn(rows, cosine, sine):
    parts = []
    for g in range(rows.shape[1] // 128):
        u = rows[:, g * 128 : (g + 1) * 128]
        parts.append(u * cosine + swap_halves(u) * sine)
    return parts[0] if len(parts) == 1 else jnp.concatenate(parts, axis=1)


def live_mask(sc, row0, count):
    span_pos = sc[1] * SPAN + row0 + lax.broadcasted_iota(jnp.int32, (count, 1), 0)
    return span_pos < sc[2]


SPAN = 512
SEQ = 1024
WIDTH = 768
GROUP = 384
HID = 2048


def hbm():
    return pl.BlockSpec(memory_space=pl.ANY)


def whole(shape):
    return pl.BlockSpec(shape, lambda i, sc: (0,) * len(shape))


def call(body, name, sc, args, in_specs, out_shapes, out_specs, scratch, vmem, cost):
    flops, moved, trans = cost
    return pl.pallas_call(
        body,
        name=name,
        out_shape=out_shapes,
        grid_spec=pltpu.PrefetchScalarGridSpec(
            num_scalar_prefetch=1,
            grid=(1,),
            in_specs=in_specs,
            out_specs=out_specs,
            scratch_shapes=scratch,
        ),
        compiler_params=pltpu.CompilerParams(vmem_limit_bytes=vmem * MIB),
        cost_estimate=pl.CostEstimate(
            flops=int(flops), bytes_accessed=int(moved), transcendentals=int(trans)
        ),
    )(sc, *args)


def sds(shape, dtype=BF):
    return jax.ShapeDtypeStruct(shape, dtype)


def qkv_body(sc, x_ref, gain_ref, cos_ref, sin_ref, wq, wk, wv, *rest, flip):
    if flip:
        o_ref, n_ref, ws, sem = rest
    else:
        o_ref, ws, sem = rest
    col = (1 - sc[0]) if flip else sc[0]
    col = pl.multiple_of(col * GROUP, 128)
    copies = [
        pltpu.make_async_copy(w.at[:, pl.ds(col, GROUP)], ws.at[t], sem.at[t])
        for t, w in enumerate((wq, wk, wv))
    ]
    for cp in copies:
        cp.start()
    normed = []
    for r in range(0, SPAN, 256):
        x = jnp.where(live_mask(sc, r, 256), x_ref[0, r : r + 256, :].astype(F32), 0.0)
        factor = lax.rsqrt(jnp.mean(x * x, axis=-1, keepdims=True) + epsilon)
        n1 = (x * factor * gain_ref[...]).astype(BF)
        if flip:
            n_ref[r : r + 256, :] = n1
        normed.append(n1)
    for t in range(3):
        copies[t].wait()
        for i, r in enumerate(range(0, SPAN, 256)):
            y = dot(normed[i], ws[t])
            if t < 2:
                y = turn(y, cos_ref[r : r + 256, :], sin_ref[r : r + 256, :])
            if t == 0:
                y = y * (HEAD_DIM**-0.5)
            o_ref[t, r : r + 256, :] = y.astype(BF)


def qkv_call(sc, tokens, gain, cosine, sine, wq, wk, wv, flip):
    out_shapes = [sds((3, SPAN, GROUP))]
    out_specs = [whole((3, SPAN, GROUP))]
    if flip:
        out_shapes.append(sds((SPAN, WIDTH)))
        out_specs.append(whole((SPAN, WIDTH)))
    table = pl.BlockSpec((SPAN, 128), lambda i, sc: (sc[1], 0))
    return call(
        functools.partial(qkv_body, flip=flip),
        "qkv_other" if flip else "qkv_own",
        sc,
        (tokens, gain, cosine, sine, wq, wk, wv),
        [whole((1, SPAN, WIDTH)), whole((1, WIDTH)), table, table, hbm(), hbm(), hbm()],
        out_shapes,
        out_specs,
        [pltpu.VMEM((3, WIDTH, GROUP), BF), pltpu.SemaphoreType.DMA((3,))],
        24,
        (3 * 2 * SPAN * WIDTH * GROUP, 5e6, 1e3),
    )


def gather_rows(sc, own, other, places, sem):
    copies = []
    for t, place in enumerate(places):
        for k, src in enumerate((own, other)):
            pos = sc[1] if k == 0 else 1 - sc[1]
            row = pl.multiple_of(pos * SPAN, SPAN)
            source = src.at[t] if len(src.shape) == 3 else src
            copies.append(
                pltpu.make_async_copy(source, place.at[pl.ds(row, SPAN), :], sem.at[2 * t + k])
            )
    for cp in copies:
        cp.start()
    return copies


def attend_body(sc, own, other, ot_ref, lse_ref, mine, theirs, qs, ks, vs, at, sem):
    copies = gather_rows(sc, own, other, (qs, ks, vs), sem)
    for cp in copies:
        cp.wait()
    lane = lax.broadcasted_iota(jnp.int32, (256, 128), 1)
    key_id = lax.broadcasted_iota(jnp.int32, (256, 256), 0)
    row_id = lax.broadcasted_iota(jnp.int32, (256, 256), 1)
    keep = key_id <= row_id

    def pair(hp, carry):
        cols = pl.ds(pl.multiple_of(hp * 128, 128), 128)
        vt = jnp.transpose(vs[:, cols].astype(F32)).astype(BF)
        for h in range(2):
            for i in range(4):
                n = 256 * (i + 1)
                qm = jnp.where(lane // HEAD_DIM == h, qs[256 * i : n, cols], jnp.zeros((), BF))
                st = dot_nt(ks[0:n, cols], qm)
                diag = jnp.where(keep, st[n - 256 :, :], masked_score)
                st = diag if i == 0 else jnp.concatenate([st[: n - 256, :], diag], axis=0)
                peak = jnp.max(st, axis=0, keepdims=True)
                p = jnp.exp(st - peak)
                total = jnp.sum(p, axis=0, keepdims=True)
                o = dot(vt[h * 64 : h * 64 + 64, :n], p.astype(BF))
                o = o * (1.0 / total)
                row = pl.multiple_of(hp * 128 + h * 64, 64)
                ot_ref[pl.ds(row, 64), 256 * i : n] = o
                lse_ref[pl.ds(hp * 2 + h, 1), 256 * i : n] = peak + jnp.log(total)
        a = jnp.transpose(ot_ref[pl.ds(pl.multiple_of(hp * 128, 128), 128), :]).astype(BF)
        at[:, cols] = a
        return carry

    lax.fori_loop(0, 3, pair, 0)
    row = pl.multiple_of(sc[1] * SPAN, SPAN)
    row_other = pl.multiple_of((1 - sc[1]) * SPAN, SPAN)
    out_other = pltpu.make_async_copy(at.at[pl.ds(row_other, SPAN), :], theirs, sem.at[0])
    out_own = pltpu.make_async_copy(at.at[pl.ds(row, SPAN), :], mine, sem.at[1])
    out_other.start()
    out_own.start()
    out_other.wait()
    out_own.wait()


def attend_call(sc, own, other):
    return call(
        attend_body,
        "attend",
        sc,
        (own, other),
        [hbm(), hbm()],
        [sds((GROUP, SEQ), F32), sds((8, SEQ), F32), sds((SPAN, GROUP)), sds((SPAN, GROUP))],
        [whole((GROUP, SEQ)), whole((8, SEQ)), hbm(), hbm()],
        [pltpu.VMEM((SEQ, GROUP), BF)] * 4 + [pltpu.SemaphoreType.DMA((6,))],
        32,
        (6 * 4 * SEQ * SEQ * 64, 6e6, 4e6),
    )


def place_of(s, half):
    return half * 4 + (s % 2) * 2 + s // 2


def store_pieces(keep_ref, send_ref, offset, tile, rows, result, cols):
    for s in range(4):
        for xb in range(2):
            start = s * 2 * rows + xb * rows
            for k, ref in enumerate((keep_ref, send_ref)):
                lo = start + k * 8 * rows
                ref[place_of(s, xb), offset + tile * rows : offset + (tile + 1) * rows, :] = result[
                    lo : lo + rows, cols
                ].astype(BF)


def mlp_body(sc, *refs, half):
    if half == 0:
        (x_ref, dy_ref, ak_ref, ar_ref, gain_ref, wo, wg, wu, wd) = refs[:9]
        (keep_ref, send_ref, m_ref, acc_ref, dn_ref) = refs[9:14]
        scratch = refs[14:]
        m_in = m_ref
    else:
        (dy_ref, ak_ref, ar_ref, gain_ref, wo, wg, wu, wd, m_in, acc_in, dn_in) = refs[:11]
        (keep_ref, send_ref, lay_ref, dak_ref, das_ref, dm_ref) = refs[11:17]
        scratch = refs[17:]
    (wo_s, wg_s, wu_s, wd_s, dy_s, n_s, nt_s, np_s, h_s, dg_s, du_s, ht_s) = scratch[:12]
    if half == 0:
        (sem,) = scratch[12:]
    else:
        (acc_ref, dn_ref, at_s, sem) = scratch[12:]
    c = sc[0]
    first = pltpu.make_async_copy(wo, wo_s, sem.at[24])
    if half == 0:
        first.start()
    copies = []
    for j in range(8):
        src = 256 * j + 128 * half
        copies.append(
            (
                pltpu.make_async_copy(
                    wg.at[:, src : src + 128], wg_s.at[:, 128 * j : 128 * j + 128], sem.at[3 * j]
                ),
                pltpu.make_async_copy(
                    wu.at[:, src : src + 128],
                    wu_s.at[:, 128 * j : 128 * j + 128],
                    sem.at[3 * j + 1],
                ),
                pltpu.make_async_copy(
                    wd.at[src : src + 128, :],
                    wd_s.at[128 * j : 128 * j + 128, :],
                    sem.at[3 * j + 2],
                ),
            )
        )
        for cp in copies[-1]:
            cp.start()
    if half == 1:
        first.start()
    own_cols = pl.multiple_of(c * GROUP, 128)
    other_cols = pl.multiple_of((1 - c) * GROUP, 128)
    for r in range(0, SPAN, 256):
        live = live_mask(sc, r, 256)
        dy_s[r : r + 256, :] = jnp.where(live, dy_ref[0, r : r + 256, :], jnp.zeros((), BF))
    if half == 0:
        first.wait()
    for r in range(0, SPAN, 256):
        if half == 0:
            live = live_mask(sc, r, 256)
            m = jnp.where(live, x_ref[0, r : r + 256, :].astype(F32), 0.0)
            m = m + dot(ak_ref[r : r + 256, :], wo_s[pl.ds(own_cols, GROUP), :])
            m = m + dot(ar_ref[r : r + 256, :], wo_s[pl.ds(other_cols, GROUP), :])
            m_ref[r : r + 256, :] = m
        else:
            m = m_in[r : r + 256, :]
        factor = lax.rsqrt(jnp.mean(m * m, axis=-1, keepdims=True) + epsilon)
        n2 = m * factor * gain_ref[...]
        n_s[r : r + 256, :] = n2.astype(BF)
        nt_s[:, r : r + 256] = jnp.transpose(n2).astype(BF)
    for s in range(4):
        mine = pl.multiple_of((2 * s + c) * 96, 32)
        theirs = pl.multiple_of((2 * s + 1 - c) * 96, 32)
        np_s[s * 96 : s * 96 + 96, :] = nt_s[pl.ds(mine, 96), :]
        np_s[384 + s * 96 : 384 + s * 96 + 96, :] = nt_s[pl.ds(theirs, 96), :]
    for t in range(2):
        for j in range(4 * t, 4 * t + 4):
            for cp in copies[j]:
                cp.wait()
        fc = slice(512 * t, 512 * t + 512)
        for r in range(0, SPAN, 256):
            rr = slice(r, r + 256)
            g = dot(n_s[rr, :], wg_s[:, fc])
            u = dot(n_s[rr, :], wu_s[:, fc])
            dh = dot_nt(dy_s[rr, :], wd_s[fc, :])
            sg = jax.nn.sigmoid(g)
            gs = g * sg
            h = gs * u
            h_s[rr, :] = h.astype(BF)
            ht_s[:, rr] = jnp.transpose(h).astype(BF)
            du = (dh * gs).astype(BF)
            dg = (dh * u * (sg + gs * (1.0 - sg))).astype(BF)
            dg_s[rr, :] = dg
            du_s[rr, :] = du
            acc = dot(h_s[rr, :], wd_s[fc, :])
            dn = dot_nt(dg, wg_s[:, fc]) + dot_nt(du, wu_s[:, fc])
            if t == 0 and half == 0:
                acc_ref[rr, :] = acc
                dn_ref[rr, :] = dn
            elif t == 0:
                acc_ref[rr, :] = acc_in[rr, :] + acc
                dn_ref[rr, :] = dn_in[rr, :] + dn
            else:
                acc_ref[rr, :] += acc
                dn_ref[rr, :] += dn
        for base, src in ((0, dg_s), (192, du_s)):
            for ct in range(2):
                res = dot(np_s[...], src[:, 256 * ct : 256 * ct + 256])
                store_pieces(keep_ref, send_ref, base, 2 * t + ct, 48, res, slice(0, 256))
        mine = [ht_s[pl.ds(pl.multiple_of((2 * q + c) * 128, 128), 128), :] for q in range(2)]
        theirs = [ht_s[pl.ds(pl.multiple_of((2 * q + 1 - c) * 128, 128), 128), :] for q in range(2)]
        lhs = jnp.concatenate(mine + theirs, axis=0)
        for n in range(3):
            res = dot(lhs, dy_s[:, 256 * n : 256 * n + 256])
            for q in range(2):
                for xb in range(2):
                    for k, ref in enumerate((keep_ref, send_ref)):
                        lo = k * 256 + q * 128 + xb * 64
                        ref[place_of(2 * t + q, xb), 384 + n * 64 : 448 + n * 64, :] = res[
                            lo : lo + 64, :
                        ].astype(BF)
    if half == 0:
        return
    first.wait()
    gain = gain_ref[...]
    for r in range(0, SPAN, 256):
        rr = slice(r, r + 256)
        live = live_mask(sc, r, 256)
        m = m_in[rr, :]
        factor = lax.rsqrt(jnp.mean(m * m, axis=-1, keepdims=True) + epsilon)
        lay_ref[0, rr, :] = jnp.where(live, m + acc_ref[rr, :], 0.0).astype(BF)
        scaled = dn_ref[rr, :] * gain
        dm = dy_s[rr, :].astype(F32) + (
            factor * scaled
            - m * (factor * factor * factor) * jnp.mean(m * scaled, axis=-1, keepdims=True)
        )
        dm_ref[rr, :] = dm
        db = dm.astype(BF)
        n_s[rr, :] = db
        das_ref[rr, :] = dot_nt(db, wo_s[pl.ds(other_cols, GROUP), :]).astype(BF)
        dak_ref[rr, :] = dot_nt(db, wo_s[pl.ds(own_cols, GROUP), :]).astype(BF)
    at_s[pl.ds(own_cols, GROUP), :] = jnp.transpose(ak_ref[...].astype(F32)).astype(BF)
    at_s[pl.ds(other_cols, GROUP), :] = jnp.transpose(ar_ref[...].astype(F32)).astype(BF)
    for s in range(4):
        mine = pl.multiple_of((2 * s + c) * 96, 32)
        theirs = pl.multiple_of((2 * s + 1 - c) * 96, 32)
        np_s[s * 96 : s * 96 + 96, :] = at_s[pl.ds(mine, 96), :]
        np_s[384 + s * 96 : 384 + s * 96 + 96, :] = at_s[pl.ds(theirs, 96), :]
    for n in range(3):
        res = dot(np_s[...], n_s[:, 256 * n : 256 * n + 256])
        store_pieces(keep_ref, send_ref, 576, n, 48, res, slice(0, 256))


def mlp_call(sc, half, rows, args):
    pieces = 576 if half == 0 else 720
    full = [whole((1, SPAN, WIDTH))]
    acts = [whole((SPAN, GROUP))] * 2 + [whole((1, WIDTH))] + [hbm()] * 4
    sums = [whole((SPAN, WIDTH))]
    packed = [whole((8, pieces, 256))] * 2
    packed_shape = [sds((8, pieces, 256))] * 2
    if half == 0:
        in_specs = full * 2 + acts
        out_shapes = packed_shape + [sds((SPAN, WIDTH), F32)] * 3
        out_specs = packed + sums * 3
    else:
        in_specs = full + acts + sums * 3
        out_shapes = packed_shape + [
            sds((1, SPAN, WIDTH)),
            sds((SPAN, GROUP)),
            sds((SPAN, GROUP)),
            sds((SPAN, WIDTH), F32),
        ]
        out_specs = packed + full + [whole((SPAN, GROUP))] * 2 + sums
    scratch = [
        pltpu.VMEM((WIDTH, WIDTH), BF),
        pltpu.VMEM((WIDTH, HID // 2), BF),
        pltpu.VMEM((WIDTH, HID // 2), BF),
        pltpu.VMEM((HID // 2, WIDTH), BF),
        pltpu.VMEM((SPAN, WIDTH), BF),
        pltpu.VMEM((SPAN, WIDTH), BF),
        pltpu.VMEM((WIDTH, SPAN), BF),
        pltpu.VMEM((WIDTH, SPAN), BF),
        pltpu.VMEM((SPAN, 512), BF),
        pltpu.VMEM((SPAN, 512), BF),
        pltpu.VMEM((SPAN, 512), BF),
        pltpu.VMEM((512, SPAN), BF),
    ]
    if half == 1:
        scratch += [
            pltpu.VMEM((SPAN, WIDTH), F32),
            pltpu.VMEM((SPAN, WIDTH), F32),
            pltpu.VMEM((WIDTH, SPAN), BF),
        ]
    scratch.append(pltpu.SemaphoreType.DMA((25,)))
    return call(
        functools.partial(mlp_body, half=half),
        "mlp_first" if half == 0 else "mlp_second",
        sc,
        args,
        in_specs,
        out_shapes,
        out_specs,
        scratch,
        52,
        (9 * 2 * SPAN * WIDTH * 1024, 16e6, 2e6),
    )


def attend_back_body(
    sc,
    own,
    other,
    ot_ref,
    lse_ref,
    dak,
    dar,
    nk,
    nr,
    cos_ref,
    sin_ref,
    send_ref,
    keep_ref,
    mine,
    theirs,
    qs,
    ks,
    vs,
    das,
    ns,
    nt,
    ds_all,
    dqt,
    dkv,
    res_s,
    sem,
):
    copies = gather_rows(sc, own, other, (qs, ks, vs), sem)
    copies += gather_rows(sc, dak, dar, (das,), sem.at[pl.ds(6, 2)])
    late = gather_rows(sc, nk, nr, (ns,), sem.at[pl.ds(8, 2)])
    for cp in copies:
        cp.wait()
    lane = lax.broadcasted_iota(jnp.int32, (SEQ, 128), 1)
    key_id = lax.broadcasted_iota(jnp.int32, (256, 256), 0)
    row_id = lax.broadcasted_iota(jnp.int32, (256, 256), 1)
    keep = key_id <= row_id

    def pair(hp, carry):
        cols = pl.ds(pl.multiple_of(hp * 128, 128), 128)
        kt = jnp.transpose(ks[:, cols].astype(F32)).astype(BF)
        dat = jnp.transpose(das[:, cols].astype(F32))
        for h in range(2):
            qm = jnp.where(lane // HEAD_DIM == h, qs[:, cols], jnp.zeros((), BF))
            dam = jnp.where(lane // HEAD_DIM == h, das[:, cols], jnp.zeros((), BF))
            row = pl.multiple_of(hp * 128 + h * 64, 64)
            delta = jnp.sum(
                dat[h * 64 : h * 64 + 64, :] * ot_ref[pl.ds(row, 64), :], axis=0, keepdims=True
            )
            lse = lse_ref[pl.ds(hp * 2 + h, 1), :]
            for j in range(4):
                lo = 256 * j
                st = dot_nt(ks[lo : lo + 256, cols], qm[lo:, :])
                p = jnp.exp(st - lse[:, lo:])
                diag = jnp.where(keep, p[:, :256], 0.0)
                p = diag if j == 3 else jnp.concatenate([diag, p[:, 256:]], axis=1)
                dp = dot_nt(vs[lo : lo + 256, cols], dam[lo:, :])
                ds = (p * (dp - delta[:, lo:])).astype(BF)
                dv = dot(p.astype(BF), dam[lo:, :])
                dk = dot(ds, qm[lo:, :])
                dq = dot(kt[h * 64 : h * 64 + 64, lo : lo + 256], ds)
                if h == 0:
                    dkv[0, lo : lo + 256, :] = dk
                    dkv[1, lo : lo + 256, :] = dv
                else:
                    dkv[0, lo : lo + 256, :] += dk
                    dkv[1, lo : lo + 256, :] += dv
                if j == 0:
                    dqt[h * 64 : h * 64 + 64, :] = dq
                else:
                    dqt[h * 64 : h * 64 + 64, lo:] += dq
        dq = jnp.transpose(dqt[...]) * (HEAD_DIM**-0.5)
        back = -sin_ref[...]
        ds_all[0, :, cols] = turn(dq, cos_ref[...], back).astype(BF)
        ds_all[1, :, cols] = turn(dkv[0], cos_ref[...], back).astype(BF)
        ds_all[2, :, cols] = dkv[1].astype(BF)
        return carry

    lax.fori_loop(0, 3, pair, 0)
    row = pl.multiple_of(sc[1] * SPAN, SPAN)
    row_other = pl.multiple_of((1 - sc[1]) * SPAN, SPAN)
    outs = [
        pltpu.make_async_copy(ds_all.at[:, pl.ds(row_other, SPAN), :], theirs, sem.at[0]),
        pltpu.make_async_copy(ds_all.at[:, pl.ds(row, SPAN), :], mine, sem.at[1]),
    ]
    for cp in outs:
        cp.start()
    for cp in late:
        cp.wait()
    nt[...] = jnp.transpose(ns[...].astype(F32)).astype(BF)
    for t in range(3):
        res_s[...] = dot(nt[...], ds_all[t])
        for s in range(4):
            place = (s % 2) * 2 + s // 2
            for cc in range(2):
                base = (s * 2 + cc) * 96
                to = t * 96 + cc * 48
                lo = pl.multiple_of(base + (1 - sc[3]) * 48, 16)
                send_ref[place, to : to + 48, :] = res_s[pl.ds(lo, 48), :].astype(BF)
                lo = pl.multiple_of(base + sc[3] * 48, 16)
                keep_ref[place, to : to + 48, :] = res_s[pl.ds(lo, 48), :].astype(BF)
    for cp in outs:
        cp.wait()


def attend_back_call(sc, own, other, ot, lse, dak, dar, nk, nr, cosine, sine):
    return call(
        attend_back_body,
        "attend_back",
        sc,
        (own, other, ot, lse, dak, dar, nk, nr, cosine, sine),
        [hbm(), hbm(), whole((GROUP, SEQ)), whole((8, SEQ))]
        + [hbm()] * 4
        + [whole((SEQ, 128))] * 2,
        [sds((4, 288, GROUP))] * 2 + [sds((3, SPAN, GROUP))] * 2,
        [whole((4, 288, GROUP))] * 2 + [hbm()] * 2,
        [pltpu.VMEM((SEQ, GROUP), BF)] * 4
        + [
            pltpu.VMEM((SEQ, WIDTH), BF),
            pltpu.VMEM((WIDTH, SEQ), BF),
            pltpu.VMEM((3, SEQ, GROUP), BF),
            pltpu.VMEM((128, SEQ), F32),
            pltpu.VMEM((2, SEQ, 128), F32),
            pltpu.VMEM((WIDTH, GROUP), F32),
            pltpu.SemaphoreType.DMA((10,)),
        ],
        48,
        (6 * 10 * SEQ * SEQ * 64, 12e6, 4e6),
    )


def input_grad_body(sc, x_ref, gain_ref, dm_ref, dk, dr, wq, wk, wv, o_ref, dk_s, dr_s, ws, sem):
    copies = []
    for t, w in enumerate((wq, wk, wv)):
        copies.append(pltpu.make_async_copy(w, ws.at[t], sem.at[t]))
    copies.append(pltpu.make_async_copy(dk, dk_s, sem.at[3]))
    copies.append(pltpu.make_async_copy(dr, dr_s, sem.at[4]))
    for cp in copies:
        cp.start()
    for cp in copies:
        cp.wait()
    own_cols = pl.multiple_of(sc[0] * GROUP, 128)
    other_cols = pl.multiple_of((1 - sc[0]) * GROUP, 128)
    gain = gain_ref[...]
    for r in range(0, SPAN, 256):
        rr = slice(r, r + 256)
        dn = dot_nt(dk_s[0, rr, :], ws[0, :, pl.ds(own_cols, GROUP)])
        dn = dn + dot_nt(dr_s[0, rr, :], ws[0, :, pl.ds(other_cols, GROUP)])
        for t in (1, 2):
            dn = dn + dot_nt(dk_s[t, rr, :], ws[t, :, pl.ds(own_cols, GROUP)])
            dn = dn + dot_nt(dr_s[t, rr, :], ws[t, :, pl.ds(other_cols, GROUP)])
        live = live_mask(sc, r, 256)
        x = jnp.where(live, x_ref[0, rr, :].astype(F32), 0.0)
        factor = lax.rsqrt(jnp.mean(x * x, axis=-1, keepdims=True) + epsilon)
        scaled = dn * gain
        dx = dm_ref[rr, :] + (
            factor * scaled
            - x * (factor * factor * factor) * jnp.mean(x * scaled, axis=-1, keepdims=True)
        )
        o_ref[0, rr, :] = jnp.where(live, dx, 0.0).astype(BF)


def input_grad_call(sc, tokens, gain, dm, dk, dr, wq, wk, wv):
    return call(
        input_grad_body,
        "input_grad",
        sc,
        (tokens, gain, dm, dk, dr, wq, wk, wv),
        [whole((1, SPAN, WIDTH)), whole((1, WIDTH)), whole((SPAN, WIDTH))] + [hbm()] * 5,
        sds((1, SPAN, WIDTH)),
        whole((1, SPAN, WIDTH)),
        [
            pltpu.VMEM((3, SPAN, GROUP), BF),
            pltpu.VMEM((3, SPAN, GROUP), BF),
            pltpu.VMEM((3, WIDTH, WIDTH), BF),
            pltpu.SemaphoreType.DMA((5,)),
        ],
        32,
        (3 * 2 * SPAN * WIDTH * WIDTH, 10e6, 1e3),
    )


def add_pieces(sc, count, picks, arrays, name):
    rows, cols = arrays[0].shape[1:]

    def body(sc_ref, *refs):
        total = refs[0][...].astype(F32)
        for ref in refs[1:-1]:
            total = total + ref[...].astype(F32)
        refs[-1][...] = total.astype(BF)

    def spec(pick):
        return pl.BlockSpec((1, rows, cols), lambda j, sc_ref: (pick(sc_ref, j), 0, 0))

    size = count * rows * cols
    return pl.pallas_call(
        body,
        name=name,
        out_shape=sds((count, rows, cols)),
        grid_spec=pltpu.PrefetchScalarGridSpec(
            num_scalar_prefetch=1,
            grid=(count,),
            in_specs=[spec(pick) for pick in picks],
            out_specs=pl.BlockSpec((1, rows, cols), lambda j, sc_ref: (j, 0, 0)),
        ),
        compiler_params=pltpu.CompilerParams(vmem_limit_bytes=16 * MIB),
        cost_estimate=pl.CostEstimate(
            flops=size * len(arrays), bytes_accessed=2 * size * (len(arrays) + 1), transcendentals=0
        ),
    )(sc, *arrays)


def reduce_rest(sc, parts, picks8, got, name):
    near = exchange(
        add_pieces(
            sc,
            2,
            [lambda t, j, p=p: p(t, (1 - t[4]) * 2 + j) for p in picks8]
            + [lambda t, j: (1 - t[4]) * 2 + j],
            parts + [got],
            name + "_b",
        ),
        "near",
    )
    far = exchange(
        add_pieces(
            sc,
            1,
            [lambda t, j, p=p: p(t, t[4] * 2 + 1 - t[5]) for p in picks8]
            + [lambda t, j: t[4] * 2 + 1 - t[5], lambda t, j: 1 - t[5]],
            parts + [got, near],
            name + "_c",
        ),
        "far",
    )
    piece = add_pieces(
        sc,
        1,
        [lambda t, j, p=p: p(t, t[4] * 2 + t[5]) for p in picks8]
        + [lambda t, j: t[4] * 2 + t[5], lambda t, j: t[5], lambda t, j: 0],
        parts + [got, near, far],
        name + "_d",
    )
    zero = lambda t, j: 0
    total = add_pieces(sc, 1, [zero, zero], [piece, exchange(piece, "second")], name + "_e")
    return total, exchange(total, "first")


def reduce_group(sc, keep, send, name):
    got = exchange(send, "core")
    other = lambda t, j: (1 - t[3]) * 4 + j
    mine = lambda t, j: t[3] * 4 + j
    first = exchange(add_pieces(sc, 4, [other, other], [keep, got], name + "_a"), "first")
    return reduce_rest(sc, [keep, got], [mine, mine], first, name)


def mlp_result_body(
    sc, t0, r0, t1, r1, wg_ref, wu_ref, gain_ref, gate_ref, up_ref, down_ref, out_ref, gg_ref
):
    for half, (own, peer) in enumerate(((t0, r0), (t1, r1))):
        for k, src in enumerate((own, peer)):
            xb = sc[3] if k == 0 else 1 - sc[3]
            rows = pl.ds(pl.multiple_of(xb * 48, 16), 48)
            for tile in range(4):
                for base, ref in ((0, gate_ref), (192, up_ref)):
                    lo = base + tile * 48
                    block = src[0, lo : lo + 48, :].astype(F32)
                    for q in range(2):
                        col = 256 * (2 * tile + q) + 128 * half
                        ref[rows, col : col + 128] = block[:, 128 * q : 128 * q + 128]
            down_rows = pl.ds(pl.multiple_of(128 * half + xb * 64, 64), 64)
            for n in range(3):
                cols = slice(256 * n, 256 * n + 256)
                lo = 384 + n * 64
                down_ref[down_rows, cols] = src[0, lo : lo + 64, :].astype(F32)
                if half == 1:
                    lo = 576 + n * 48
                    out_ref[rows, cols] = src[0, lo : lo + 48, :].astype(F32)
    gate = jnp.sum(wg_ref[...].astype(F32) * gate_ref[...], axis=-1, keepdims=True)
    up = jnp.sum(wu_ref[...].astype(F32) * up_ref[...], axis=-1, keepdims=True)
    gg_ref[...] = (gate + up) / gain_ref[...]


def row_block(rows, cols):
    return pl.BlockSpec((rows, cols), lambda i, sc: (sc[6], 0))


def mlp_result_call(sc, t0, r0, t1, r1, wg, wu, gain):
    return call(
        mlp_result_body,
        "mlp_result",
        sc,
        (t0, r0, t1, r1, wg, wu, gain),
        [whole((1, 576, 256))] * 2
        + [whole((1, 720, 256))] * 2
        + [row_block(96, HID)] * 2
        + [row_block(96, 1)],
        [
            sds((96, HID), F32),
            sds((96, HID), F32),
            sds((256, WIDTH), F32),
            sds((96, WIDTH), F32),
            sds((96, 1), F32),
        ],
        [
            whole((96, HID)),
            whole((96, HID)),
            whole((256, WIDTH)),
            whole((96, WIDTH)),
            whole((96, 1)),
        ],
        [],
        24,
        (1e6, 6e6, 0),
    )


def trade_body(sc, own, peer, send_ref):
    for k, src in enumerate((own, peer)):
        xb = sc[3] if k == 0 else 1 - sc[3]
        for t in range(3):
            lo = pl.multiple_of(t * 96 + (1 - sc[0]) * 48, 16)
            send_ref[xb, t * 48 : t * 48 + 48, :] = src[0, pl.ds(lo, 48), :]


def qkv_result_body(sc, own, peer, got, wq_ref, wk_ref, wv_ref, gain_ref, q_ref, k_ref, v_ref, gg):
    own_cols = pl.ds(pl.multiple_of(sc[0] * GROUP, 128), GROUP)
    other_cols = pl.ds(pl.multiple_of((1 - sc[0]) * GROUP, 128), GROUP)
    total = jnp.zeros((96, 1), F32)
    for t, (ref, w_ref) in enumerate(((q_ref, wq_ref), (k_ref, wk_ref), (v_ref, wv_ref))):
        for k, src in enumerate((own, peer)):
            xb = sc[3] if k == 0 else 1 - sc[3]
            rows = pl.ds(pl.multiple_of(xb * 48, 16), 48)
            lo = pl.multiple_of(t * 96 + sc[0] * 48, 16)
            ref[rows, own_cols] = src[0, pl.ds(lo, 48), :].astype(F32)
        for xb in range(2):
            ref[xb * 48 : xb * 48 + 48, other_cols] = got[xb, t * 48 : t * 48 + 48, :].astype(F32)
        total = total + jnp.sum(w_ref[...].astype(F32) * ref[...], axis=-1, keepdims=True)
    gg[...] = total / gain_ref[...]


def qkv_result_call(sc, own, peer, wq, wk, wv, gain):
    send = call(
        trade_body,
        "trade",
        sc,
        (own, peer),
        [whole((1, 288, GROUP))] * 2,
        sds((2, 144, GROUP)),
        whole((2, 144, GROUP)),
        [],
        8,
        (1e3, 1e6, 0),
    )
    return call(
        qkv_result_body,
        "qkv_result",
        sc,
        (own, peer, exchange(send, "core"), wq, wk, wv, gain),
        [whole((1, 288, GROUP))] * 2
        + [whole((2, 144, GROUP))]
        + [row_block(96, WIDTH)] * 3
        + [row_block(96, 1)],
        [sds((96, WIDTH), F32)] * 3 + [sds((96, 1), F32)],
        [whole((96, WIDTH))] * 3 + [whole((96, 1))],
        [],
        16,
        (1e6, 3e6, 0),
    )


def fast_step(
    tokens,
    lengths,
    owner,
    w_query,
    w_key,
    w_value,
    w_out,
    w_gate,
    w_up,
    w_down,
    gain_attn,
    gain_mlp,
    cotangent,
):
    batch, seq, core = (lax.axis_index(name) for name in AXES)
    own_pos = jnp.where(core == 0, owner[0, 0], owner[0, 1])
    first_bit = jnp.where(core == 0, batch % 2, batch // 2)
    sc = jnp.stack(
        [core, own_pos, lengths[0], first_bit, seq % 2, seq // 2, seq * 2 + core, core]
    ).astype(jnp.int32)
    tables = position_tables(SEQ)
    cosine, sine = jnp.asarray(tables[0]), jnp.asarray(tables[1])
    gain_row = gain_attn.reshape(1, WIDTH)
    gain_mlp_row = gain_mlp.reshape(1, WIDTH)
    weights = (w_query, w_key, w_value)
    qkv_send, normed = qkv_call(sc, tokens, gain_row, cosine, sine, *weights, True)
    qkv_other = exchange(qkv_send, "core")
    (qkv_own,) = qkv_call(sc, tokens, gain_row, cosine, sine, *weights, False)
    normed_other = exchange(normed, "core")
    attn_t, lse, attn_own, attn_send = attend_call(sc, qkv_own, qkv_other)
    attn_other = exchange(attn_send, "core")
    common = (attn_own, attn_other, gain_mlp_row, w_out, w_gate, w_up, w_down)
    keep0, send0, middle, acc, dn = mlp_call(sc, 0, 576, (tokens, cotangent) + common)
    t0, r0 = reduce_group(sc, keep0, send0, "g0")
    keep1, send1, layer_out, da_own, da_send, d_middle = mlp_call(
        sc, 1, 720, (cotangent,) + common + (middle, acc, dn)
    )
    da_other = exchange(da_send, "core")
    t1, r1 = reduce_group(sc, keep1, send1, "g1")
    send2, keep2, d_own, d_send = attend_back_call(
        sc, qkv_own, qkv_other, attn_t, lse, da_own, da_other, normed, normed_other, cosine, sine
    )
    got2 = exchange(send2, "first")
    d_other = exchange(d_send, "core")
    t2, r2 = reduce_rest(sc, [keep2], [lambda t, j: j], got2, "g2")
    input_grad = input_grad_call(sc, tokens, gain_row, d_middle, d_own, d_other, *weights)
    gate, up, down, out, gain_m = mlp_result_call(
        sc, t0, r0, t1, r1, w_gate, w_up, gain_mlp.reshape(WIDTH, 1)
    )
    query, key, value, gain_a = qkv_result_call(sc, t2, r2, *weights, gain_attn.reshape(WIDTH, 1))
    return (
        layer_out,
        input_grad,
        query,
        key,
        value,
        out,
        gate,
        up,
        down,
        gain_a.reshape(96),
        gain_m.reshape(96),
    )


def solution(mesh):
    in_specs = (
        P(("batch", "seq"), "seqb", None),
        P(("batch", "seq")),
        P(("batch", "seq"), None),
        P(),
        P(),
        P(),
        P(),
        P(),
        P(),
        P(),
        P(),
        P(),
        P(("batch", "seq"), "seqb", None),
    )
    out_specs = (
        P(("batch", "seq"), "seqb", None),
        P(("batch", "seq"), "seqb", None),
        P(("seq", "seqb"), None),
        P(("seq", "seqb"), None),
        P(("seq", "seqb"), None),
        P(("seq", "seqb"), None),
        P(("seq", "seqb"), None),
        P(("seq", "seqb"), None),
        P(("seq", "seqb"), None),
        P(("seq", "seqb")),
        P(("seq", "seqb")),
    )
    step = fast_step if fast_layout(mesh) else general_step
    return jax.shard_map(step, mesh=mesh, in_specs=in_specs, out_specs=out_specs, check_vma=False)
```

```python
import functools
import math

import jax
import jax.numpy as jnp
import numpy as np
from jax import lax
from jax.experimental import pallas as pl
from jax.experimental.pallas import tpu as pltpu
from jax.sharding import PartitionSpec as P

HEADS = 12
HEAD_DIM = 64


epsilon = 1e-05
rope_base = 10000.0
masked_score = -1e30


def rms_forward(rows, gain):
    factor = lax.rsqrt(jnp.mean(rows * rows, axis=-1, keepdims=True) + epsilon)
    return (rows * factor * gain, factor)


def rms_backward(rows, factor, gain, upstream):
    scaled = upstream * gain
    return factor * scaled - rows * (factor * factor * factor) * jnp.mean(
        rows * scaled, axis=-1, keepdims=True
    )


def rotation_tables(positions):
    half = HEAD_DIM // 2
    freq = rope_base ** (-(2.0 * jnp.arange(half, dtype=jnp.float32)) / HEAD_DIM)
    angles = positions.astype(jnp.float32)[..., None] * freq
    return (jnp.cos(angles), jnp.sin(angles))


def split_heads(rows):
    return rows.reshape(rows.shape[0], rows.shape[1], HEADS, HEAD_DIM)


def rotate(rows, cosine, sine, inverse):
    shaped = split_heads(rows)
    half = HEAD_DIM // 2
    first = shaped[..., :half]
    second = shaped[..., half:]
    cos_part = cosine[:, :, None, :]
    sin_part = sine[:, :, None, :]
    if inverse:
        turned = jnp.concatenate(
            [first * cos_part + second * sin_part, second * cos_part - first * sin_part], axis=-1
        )
    else:
        turned = jnp.concatenate(
            [first * cos_part - second * sin_part, second * cos_part + first * sin_part], axis=-1
        )
    return turned.reshape(rows.shape)


def range_positions(owner, count, span):
    offsets = jnp.arange(span, dtype=jnp.int32)
    return (owner[:, :, None] * span + offsets[None, None, :]).reshape(owner.shape[0], count)


def fold_keys(parts, combine, initial):
    return combine(
        initial,
        (
            lax.all_gather(parts[0], "seqb", axis=1, tiled=True),
            lax.all_gather(parts[1], "seqb", axis=1, tiled=True),
        ),
        jnp.int32(0),
    )


def general_step(
    tokens,
    lengths,
    owner,
    w_query,
    w_key,
    w_value,
    w_out,
    w_gate,
    w_up,
    w_down,
    gain_attn,
    gain_mlp,
    cotangent,
):
    seqs, span, width = tokens.shape
    scale = HEAD_DIM ** (-0.5)
    place = lax.axis_index("seqb")
    own_block = lax.dynamic_slice_in_dim(owner, place, 1, 1)
    local_pos = own_block * span + jnp.arange(span, dtype=jnp.int32)[None, :]
    local_live = local_pos < lengths[:, None]
    live_rows = local_live[:, :, None]
    inputs = jnp.where(live_rows, tokens.astype(jnp.float32), 0.0)
    normed, factor_attn = rms_forward(inputs, gain_attn)
    normed_low = normed.astype(jnp.bfloat16)
    cosine, sine = rotation_tables(local_pos)
    query_pre = jnp.einsum("scd,de->sce", normed_low, w_query, preferred_element_type=jnp.float32)
    key_pre = jnp.einsum("scd,de->sce", normed_low, w_key, preferred_element_type=jnp.float32)
    value_low = jnp.einsum(
        "scd,de->sce", normed_low, w_value, preferred_element_type=jnp.float32
    ).astype(jnp.bfloat16)
    query_rot = rotate(query_pre, cosine, sine, False).astype(jnp.bfloat16)
    key_rot = rotate(key_pre, cosine, sine, False).astype(jnp.bfloat16)
    query_heads = split_heads(query_rot)
    key_heads = split_heads(key_rot)
    value_heads = split_heads(value_low)

    def attend(state, piece, start):
        keys, values = piece
        count = keys.shape[1]
        key_pos = range_positions(owner, count, span)
        key_live = key_pos < lengths[:, None]
        stride = math.gcd(count, 512)

        def attend_one_block(index, inner):
            offset = index * stride
            key_block = split_heads(lax.dynamic_slice_in_dim(keys, offset, stride, 1))
            value_block = split_heads(lax.dynamic_slice_in_dim(values, offset, stride, 1))
            pos_block = lax.dynamic_slice_in_dim(key_pos, offset, stride, 1)
            live_block = lax.dynamic_slice_in_dim(key_live, offset, stride, 1)
            allowed = (
                (pos_block[:, None, :] <= local_pos[:, :, None])
                & live_block[:, None, :]
                & local_live[:, :, None]
            )

            def attend_update(carried):
                peak, total, summed = carried
                scores = (
                    jnp.einsum(
                        "sqhd,skhd->shqk",
                        query_heads,
                        key_block,
                        preferred_element_type=jnp.float32,
                    )
                    * scale
                )
                mask = allowed[:, None, :, :]
                new_peak = jnp.maximum(
                    peak, jnp.max(jnp.where(mask, scores, masked_score), axis=-1)
                )
                weights = jnp.where(mask, jnp.exp(scores - new_peak[..., None]), 0.0)
                factor = jnp.exp(peak - new_peak)
                total = total * factor + jnp.sum(weights, axis=-1)
                term = jnp.einsum(
                    "shqk,skhd->sqhd",
                    weights.astype(jnp.bfloat16),
                    value_block,
                    preferred_element_type=jnp.float32,
                )
                summed = (
                    split_heads(summed) * jnp.transpose(factor, (0, 2, 1))[..., None] + term
                ).reshape(summed.shape)
                return (new_peak, total, summed)

            return lax.cond(jnp.any(allowed), attend_update, lambda carried: carried, inner)

        return lax.fori_loop(0, count // stride, attend_one_block, state)

    start_state = (
        jnp.full((seqs, HEADS, span), masked_score, jnp.float32),
        jnp.zeros((seqs, HEADS, span), jnp.float32),
        jnp.zeros((seqs, span, width), jnp.float32),
    )
    peak, total, summed = fold_keys((key_rot, value_low), attend, start_state)
    safe_total = jnp.where(local_live[:, None, :], total, 1.0)
    attn = split_heads(summed) / jnp.transpose(safe_total, (0, 2, 1))[..., None]
    attn = jnp.where(local_live[:, :, None, None], attn, 0.0).reshape(seqs, span, width)
    log_total = jnp.where(local_live[:, None, :], peak + jnp.log(safe_total), 0.0)
    attn_low = attn.astype(jnp.bfloat16)
    middle = inputs + jnp.einsum("scd,de->sce", attn_low, w_out, preferred_element_type=jnp.float32)
    normed_mlp, factor_mlp = rms_forward(middle, gain_mlp)
    normed_mlp_low = normed_mlp.astype(jnp.bfloat16)
    gate = jnp.einsum("scd,df->scf", normed_mlp_low, w_gate, preferred_element_type=jnp.float32)
    up_proj = jnp.einsum("scd,df->scf", normed_mlp_low, w_up, preferred_element_type=jnp.float32)
    hidden = (jax.nn.silu(gate) * up_proj).astype(jnp.bfloat16)
    out = middle + jnp.einsum("scf,fd->scd", hidden, w_down, preferred_element_type=jnp.float32)
    layer_out = jnp.where(live_rows, out, 0.0).astype(jnp.bfloat16)
    upstream = jnp.where(live_rows, cotangent, jnp.zeros_like(cotangent))
    grad_down = jnp.einsum("scf,scd->fd", hidden, upstream, preferred_element_type=jnp.float32)
    d_hidden = jnp.einsum("scd,fd->scf", upstream, w_down, preferred_element_type=jnp.float32)
    sigmoid_gate = jax.nn.sigmoid(gate)
    d_gate = (d_hidden * up_proj * sigmoid_gate * (1.0 + gate * (1.0 - sigmoid_gate))).astype(
        jnp.bfloat16
    )
    d_up = (d_hidden * gate * sigmoid_gate).astype(jnp.bfloat16)
    grad_gate = jnp.einsum(
        "scd,scf->df", normed_mlp_low, d_gate, preferred_element_type=jnp.float32
    )
    grad_up = jnp.einsum("scd,scf->df", normed_mlp_low, d_up, preferred_element_type=jnp.float32)
    d_normed_mlp = jnp.einsum(
        "scf,df->scd", d_gate, w_gate, preferred_element_type=jnp.float32
    ) + jnp.einsum("scf,df->scd", d_up, w_up, preferred_element_type=jnp.float32)
    grad_gain_mlp = jnp.sum(d_normed_mlp * (middle * factor_mlp), axis=(0, 1))
    d_middle = upstream.astype(jnp.float32) + rms_backward(
        middle, factor_mlp, gain_mlp, d_normed_mlp
    )
    d_branch = d_middle.astype(jnp.bfloat16)
    grad_out = jnp.einsum("scd,sce->de", attn_low, d_branch, preferred_element_type=jnp.float32)
    d_attn = jnp.einsum("sce,de->scd", d_branch, w_out, preferred_element_type=jnp.float32).astype(
        jnp.bfloat16
    )
    first_done = (grad_out, grad_gate, grad_up, grad_down, grad_gain_mlp)
    delta = jnp.sum(split_heads(d_attn.astype(jnp.float32) * attn), axis=-1)
    delta_heads = jnp.transpose(delta, (0, 2, 1))
    grad_heads = split_heads(d_attn)

    def query_grads(state, piece, start):
        keys, values = piece
        count = keys.shape[1]
        key_pos = range_positions(owner, count, span)
        key_live = key_pos < lengths[:, None]
        stride = math.gcd(count, 512)

        def query_one_block(index, inner):
            offset = index * stride
            key_block = split_heads(lax.dynamic_slice_in_dim(keys, offset, stride, 1))
            value_block = split_heads(lax.dynamic_slice_in_dim(values, offset, stride, 1))
            pos_block = lax.dynamic_slice_in_dim(key_pos, offset, stride, 1)
            live_block = lax.dynamic_slice_in_dim(key_live, offset, stride, 1)
            allowed = (
                (pos_block[:, None, :] <= local_pos[:, :, None])
                & live_block[:, None, :]
                & local_live[:, :, None]
            )

            def query_update(carried):
                scores = (
                    jnp.einsum(
                        "sqhd,skhd->shqk",
                        query_heads,
                        key_block,
                        preferred_element_type=jnp.float32,
                    )
                    * scale
                )
                probs = jnp.where(
                    allowed[:, None, :, :], jnp.exp(scores - log_total[..., None]), 0.0
                )
                d_probs = jnp.einsum(
                    "sqhd,skhd->shqk", grad_heads, value_block, preferred_element_type=jnp.float32
                )
                d_scores = (probs * (d_probs - delta_heads[..., None])).astype(jnp.bfloat16)
                term = (
                    jnp.einsum(
                        "shqk,skhd->sqhd", d_scores, key_block, preferred_element_type=jnp.float32
                    )
                    * scale
                )
                return carried + term.reshape(carried.shape)

            return lax.cond(jnp.any(allowed), query_update, lambda carried: carried, inner)

        return lax.fori_loop(0, count // stride, query_one_block, state)

    zero_query = jnp.zeros((seqs, span, width), jnp.float32)
    d_query = fold_keys((key_rot, value_low), query_grads, zero_query)
    lse_all, delta_all = (
        lax.all_gather(jnp.transpose(log_total, (0, 2, 1)), "seqb", axis=1, tiled=True),
        lax.all_gather(delta, "seqb", axis=1, tiled=True),
    )
    zero_rows = jnp.zeros((seqs, span, width), jnp.float32)
    queries = lax.all_gather(query_rot, "seqb", axis=1, tiled=True)
    d_rows = lax.all_gather(d_attn, "seqb", axis=1, tiled=True)
    count = queries.shape[1]
    row_pos = range_positions(owner, count, span)
    row_live = row_pos < lengths[:, None]
    stride = math.gcd(count, 512)

    def key_one_block(index, inner):
        offset = index * stride
        query_block = split_heads(lax.dynamic_slice_in_dim(queries, offset, stride, 1))
        grad_block = split_heads(lax.dynamic_slice_in_dim(d_rows, offset, stride, 1))
        pos_block = lax.dynamic_slice_in_dim(row_pos, offset, stride, 1)
        live_block = lax.dynamic_slice_in_dim(row_live, offset, stride, 1)
        lse_block = jnp.transpose(lax.dynamic_slice_in_dim(lse_all, offset, stride, 1), (0, 2, 1))
        delta_block = jnp.transpose(
            lax.dynamic_slice_in_dim(delta_all, offset, stride, 1), (0, 2, 1)
        )
        allowed = (
            (local_pos[:, None, :] <= pos_block[:, :, None])
            & local_live[:, None, :]
            & live_block[:, :, None]
        )

        def key_update(carried):
            d_key, d_value = carried
            scores = (
                jnp.einsum(
                    "sqhd,skhd->shqk", query_block, key_heads, preferred_element_type=jnp.float32
                )
                * scale
            )
            probs = jnp.where(allowed[:, None, :, :], jnp.exp(scores - lse_block[..., None]), 0.0)
            value_term = jnp.einsum(
                "shqk,sqhd->skhd",
                probs.astype(jnp.bfloat16),
                grad_block,
                preferred_element_type=jnp.float32,
            )
            d_probs = jnp.einsum(
                "sqhd,skhd->shqk", grad_block, value_heads, preferred_element_type=jnp.float32
            )
            d_scores = (probs * (d_probs - delta_block[..., None])).astype(jnp.bfloat16)
            key_term = (
                jnp.einsum(
                    "shqk,sqhd->skhd", d_scores, query_block, preferred_element_type=jnp.float32
                )
                * scale
            )
            return (
                d_key + key_term.reshape(d_key.shape),
                d_value + value_term.reshape(d_value.shape),
            )

        return lax.cond(jnp.any(allowed), key_update, lambda carried: carried, inner)

    d_key, d_value = lax.fori_loop(0, count // stride, key_one_block, (zero_rows, zero_rows))
    d_query_pre = rotate(d_query, cosine, sine, True).astype(jnp.bfloat16)
    d_key_pre = rotate(d_key, cosine, sine, True).astype(jnp.bfloat16)
    d_value_low = d_value.astype(jnp.bfloat16)
    grad_query = jnp.einsum(
        "scd,sce->de", normed_low, d_query_pre, preferred_element_type=jnp.float32
    )
    grad_key = jnp.einsum("scd,sce->de", normed_low, d_key_pre, preferred_element_type=jnp.float32)
    grad_value = jnp.einsum(
        "scd,sce->de", normed_low, d_value_low, preferred_element_type=jnp.float32
    )
    d_normed = jnp.einsum("sce,de->scd", d_query_pre, w_query, preferred_element_type=jnp.float32)
    d_normed = d_normed + jnp.einsum(
        "sce,de->scd", d_key_pre, w_key, preferred_element_type=jnp.float32
    )
    d_normed = d_normed + jnp.einsum(
        "sce,de->scd", d_value_low, w_value, preferred_element_type=jnp.float32
    )
    grad_gain_attn = jnp.sum(d_normed * (inputs * factor_attn), axis=(0, 1))
    d_inputs = d_middle + rms_backward(inputs, factor_attn, gain_attn, d_normed)
    input_grad = jnp.where(live_rows, d_inputs, 0.0).astype(jnp.bfloat16)
    summed_parts = (
        lax.psum_scatter(grad_query, ("seq", "seqb"), scatter_dimension=0, tiled=True),
        lax.psum_scatter(grad_key, ("seq", "seqb"), scatter_dimension=0, tiled=True),
        lax.psum_scatter(grad_value, ("seq", "seqb"), scatter_dimension=0, tiled=True),
        lax.psum_scatter(grad_gain_attn, ("seq", "seqb"), scatter_dimension=0, tiled=True),
        lax.psum_scatter(first_done[0], ("seq", "seqb"), scatter_dimension=0, tiled=True),
        lax.psum_scatter(first_done[1], ("seq", "seqb"), scatter_dimension=0, tiled=True),
        lax.psum_scatter(first_done[2], ("seq", "seqb"), scatter_dimension=0, tiled=True),
        lax.psum_scatter(first_done[3], ("seq", "seqb"), scatter_dimension=0, tiled=True),
        lax.psum_scatter(first_done[4], ("seq", "seqb"), scatter_dimension=0, tiled=True),
    )
    all_done = (
        lax.psum(summed_parts[0].astype(jnp.bfloat16), "batch").astype(jnp.float32),
        lax.psum(summed_parts[1].astype(jnp.bfloat16), "batch").astype(jnp.float32),
        lax.psum(summed_parts[2].astype(jnp.bfloat16), "batch").astype(jnp.float32),
        lax.psum(summed_parts[3].astype(jnp.bfloat16), "batch").astype(jnp.float32),
        lax.psum(summed_parts[4].astype(jnp.bfloat16), "batch").astype(jnp.float32),
        lax.psum(summed_parts[5].astype(jnp.bfloat16), "batch").astype(jnp.float32),
        lax.psum(summed_parts[6].astype(jnp.bfloat16), "batch").astype(jnp.float32),
        lax.psum(summed_parts[7].astype(jnp.bfloat16), "batch").astype(jnp.float32),
        lax.psum(summed_parts[8].astype(jnp.bfloat16), "batch").astype(jnp.float32),
    )
    second_done = (all_done[0], all_done[1], all_done[2], all_done[3])
    first_done = (all_done[4], all_done[5], all_done[6], all_done[7], all_done[8])
    return (
        layer_out,
        input_grad,
        second_done[0],
        second_done[1],
        second_done[2],
        first_done[0],
        first_done[1],
        first_done[2],
        first_done[3],
        second_done[3],
        first_done[4],
    )


AXES = ("batch", "seq", "seqb")
BF = jnp.bfloat16
F32 = jnp.float32
MIB = 1 << 20
COST = 1e9
KERNEL_US = {
    "qkv_other": 4,
    "qkv_own": 4,
    "attend": 13,
    "proj": 3,
    "ffn_first": 8,
    "ffn_second": 8,
    "ffn_out": 9,
    "middle": 1.4,
    "attend_back": 6,
    "square": 5.5,
    "input_grad": 6.5,
    "ffn_result": 2,
    "square_result": 2,
}


def fast_layout(mesh):
    return mesh.shape["batch"] == 4 and mesh.shape["seq"] == 4 and mesh.shape["seqb"] == 2


def exchange(rows, kind):
    pairs = []
    for b in range(4):
        for s in range(4):
            for c in range(2):
                first = 1 if c == 0 else 2
                target = {
                    "core": (b, s, 1 - c),
                    "first": (b ^ first, s, c),
                    "second": (b ^ (3 - first), s, c),
                    "near": (b, s ^ 1, c),
                    "far": (b, s ^ 2, c),
                    "across": (b ^ 3, s, c),
                }[kind]
                pairs.append((b * 8 + s * 2 + c, target[0] * 8 + target[1] * 2 + target[2]))
    return lax.ppermute(rows, AXES, pairs)


def dot(a, b):
    return lax.dot_general(a, b, (((1,), (0,)), ((), ())), preferred_element_type=F32)


def dot_nt(a, b):
    return lax.dot_general(a, b, (((1,), (1,)), ((), ())), preferred_element_type=F32)


def position_tables(count):
    half = HEAD_DIM // 2
    freq = rope_base ** (-(2.0 * np.arange(half)) / HEAD_DIM)
    angles = np.arange(count)[:, None] * freq[None, :]
    cosine, sine = np.cos(angles), np.sin(angles)
    return (
        np.concatenate([cosine, cosine, cosine, cosine], 1).astype(np.float32),
        np.concatenate([-sine, sine, -sine, sine], 1).astype(np.float32),
    )


def swap_halves(u):
    lane = lax.broadcasted_iota(jnp.int32, u.shape, 1) % HEAD_DIM
    return jnp.where(lane < HEAD_DIM // 2, pltpu.roll(u, 96, 1), pltpu.roll(u, 32, 1))


def turn(rows, cosine, sine):
    parts = []
    for g in range(rows.shape[1] // 128):
        u = rows[:, g * 128 : (g + 1) * 128]
        parts.append(u * cosine + swap_halves(u) * sine)
    return parts[0] if len(parts) == 1 else jnp.concatenate(parts, axis=1)


def live_mask(sc, row0, count):
    span_pos = sc[1] * SPAN + row0 + lax.broadcasted_iota(jnp.int32, (count, 1), 0)
    return span_pos < sc[2]


SPAN = 512
SEQ = 1024
WIDTH = 768
GROUP = 384
HID = 2048


def hbm():
    return pl.BlockSpec(memory_space=pl.ANY)


def far_hbm():
    return pl.BlockSpec(memory_space=pltpu.HBM)


def after(sc, *deps):
    return lax.optimization_barrier((sc,) + deps)[0]


def dot_tn(a, b):
    return lax.dot_general(a, b, (((0,), (0,)), ((), ())), preferred_element_type=F32)


def whole(shape):
    return pl.BlockSpec(shape, lambda i, sc: (0,) * len(shape))


def call(body, name, sc, args, in_specs, out_shapes, out_specs, scratch, vmem, cost):
    flops, moved, trans = cost
    args = [
        pltpu.with_memory_space_constraint(a, pltpu.HBM) if spec.memory_space is pltpu.HBM else a
        for a, spec in zip(args, in_specs)
    ]
    return pl.pallas_call(
        body,
        name=name,
        out_shape=out_shapes,
        grid_spec=pltpu.PrefetchScalarGridSpec(
            num_scalar_prefetch=1,
            grid=(1,),
            in_specs=in_specs,
            out_specs=out_specs,
            scratch_shapes=scratch,
        ),
        compiler_params=pltpu.CompilerParams(vmem_limit_bytes=vmem * MIB),
        cost_estimate=pl.CostEstimate(
            flops=int(COST * KERNEL_US[name]), bytes_accessed=1000, transcendentals=0
        ),
    )(sc, *args)


def sds(shape, dtype=BF):
    return jax.ShapeDtypeStruct(shape, dtype)


def qkv_body(sc, x_hbm, cos_hbm, sin_hbm, gain_ref, wq, wk, wv, *rest, flip):
    if flip:
        o_ref, n_ref, xs, cs, ss, ws, sem = rest
    else:
        o_ref, xs, cs, ss, ws, sem = rest
    col = (1 - sc[0]) if flip else sc[0]
    col = pl.multiple_of(col * GROUP, 128)
    row = pl.multiple_of(sc[1] * SPAN, SPAN)
    x_copy = pltpu.make_async_copy(x_hbm.at[0], xs, sem.at[3])
    x_copy.start()
    copies = [
        pltpu.make_async_copy(w.at[:, pl.ds(col, GROUP)], ws.at[t], sem.at[t])
        for t, w in enumerate((wq, wk, wv))
    ]
    tables = [
        pltpu.make_async_copy(cos_hbm.at[pl.ds(row, SPAN), :], cs, sem.at[4]),
        pltpu.make_async_copy(sin_hbm.at[pl.ds(row, SPAN), :], ss, sem.at[5]),
    ]
    for cp in [copies[0]] + tables + copies[1:]:
        cp.start()
    x_copy.wait()
    normed = []
    for r in range(0, SPAN, 256):
        x = jnp.where(live_mask(sc, r, 256), xs[r : r + 256, :].astype(F32), 0.0)
        factor = lax.rsqrt(jnp.mean(x * x, axis=-1, keepdims=True) + epsilon)
        n1 = (x * factor * gain_ref[...]).astype(BF)
        if flip:
            n_ref[r : r + 256, :] = n1
        normed.append(n1)
    copies[0].wait()
    for cp in tables:
        cp.wait()
    for t in range(3):
        if t:
            copies[t].wait()
        for i, r in enumerate(range(0, SPAN, 256)):
            y = dot(normed[i], ws[t])
            if t < 2:
                y = turn(y, cs[r : r + 256, :], ss[r : r + 256, :])
            if t == 0:
                y = y * (HEAD_DIM**-0.5)
            o_ref[t, r : r + 256, :] = y.astype(BF)


def qkv_call(sc, tokens, gain, cosine, sine, wq, wk, wv, flip):
    out_shapes = [sds((3, SPAN, GROUP))]
    out_specs = [whole((3, SPAN, GROUP))]
    if flip:
        out_shapes.append(sds((SPAN, WIDTH)))
        out_specs.append(whole((SPAN, WIDTH)))
    return call(
        functools.partial(qkv_body, flip=flip),
        "qkv_other" if flip else "qkv_own",
        sc,
        (tokens, cosine, sine, gain, wq, wk, wv),
        [far_hbm(), far_hbm(), far_hbm(), whole((1, WIDTH)), far_hbm(), far_hbm(), far_hbm()],
        out_shapes,
        out_specs,
        [
            pltpu.VMEM((SPAN, WIDTH), BF),
            pltpu.VMEM((SPAN, 128), F32),
            pltpu.VMEM((SPAN, 128), F32),
            pltpu.VMEM((3, WIDTH, GROUP), BF),
            pltpu.SemaphoreType.DMA((6,)),
        ],
        9,
        (3 * 2 * SPAN * WIDTH * GROUP, 5e6, 1e3),
    )


def gather_rows(sc, own, other, places, sem):
    copies = []
    for t, place in enumerate(places):
        for k, src in enumerate((own, other)):
            pos = sc[1] if k == 0 else 1 - sc[1]
            row = pl.multiple_of(pos * SPAN, SPAN)
            source = src.at[t] if len(src.shape) == 3 else src
            copies.append(
                pltpu.make_async_copy(source, place.at[pl.ds(row, SPAN), :], sem.at[2 * t + k])
            )
    for cp in copies:
        cp.start()
    return copies


def attend_body(sc, own, other, ot_ref, lse_ref, mine, theirs, qs, ks, vs, at, sem):
    copies = gather_rows(sc, own, other, (qs, ks, vs), sem)
    for cp in copies:
        cp.wait()
    lane = lax.broadcasted_iota(jnp.int32, (256, 128), 1)
    key_id = lax.broadcasted_iota(jnp.int32, (256, 256), 0)
    row_id = lax.broadcasted_iota(jnp.int32, (256, 256), 1)
    keep = key_id <= row_id

    def pair(hp, carry):
        cols = pl.ds(pl.multiple_of(hp * 128, 128), 128)
        vt = jnp.transpose(vs[:, cols].astype(F32)).astype(BF)
        for h in range(2):
            for i in range(4):
                n = 256 * (i + 1)
                qm = jnp.where(lane // HEAD_DIM == h, qs[256 * i : n, cols], jnp.zeros((), BF))
                st = dot_nt(ks[0:n, cols], qm)
                diag = jnp.where(keep, st[n - 256 :, :], masked_score)
                st = diag if i == 0 else jnp.concatenate([st[: n - 256, :], diag], axis=0)
                peak = jnp.max(st, axis=0, keepdims=True)
                p = jnp.exp(st - peak)
                total = jnp.sum(p, axis=0, keepdims=True)
                o = dot(vt[h * 64 : h * 64 + 64, :n], p.astype(BF))
                o = o * (1.0 / total)
                row = pl.multiple_of(hp * 128 + h * 64, 64)
                ot_ref[pl.ds(row, 64), 256 * i : n] = o
                lse_ref[pl.ds(hp * 2 + h, 1), 256 * i : n] = peak + jnp.log(total)
        a = jnp.transpose(ot_ref[pl.ds(pl.multiple_of(hp * 128, 128), 128), :]).astype(BF)
        at[:, cols] = a
        return carry

    lax.fori_loop(0, 3, pair, 0)
    row = pl.multiple_of(sc[1] * SPAN, SPAN)
    row_other = pl.multiple_of((1 - sc[1]) * SPAN, SPAN)
    out_other = pltpu.make_async_copy(at.at[pl.ds(row_other, SPAN), :], theirs, sem.at[0])
    out_own = pltpu.make_async_copy(at.at[pl.ds(row, SPAN), :], mine, sem.at[1])
    out_other.start()
    out_own.start()
    out_other.wait()
    out_own.wait()


def attend_call(sc, own, other):
    return call(
        attend_body,
        "attend",
        sc,
        (own, other),
        [hbm(), hbm()],
        [sds((GROUP, SEQ), F32), sds((8, SEQ), F32), sds((SPAN, GROUP)), sds((SPAN, GROUP))],
        [whole((GROUP, SEQ)), whole((8, SEQ)), hbm(), hbm()],
        [pltpu.VMEM((SEQ, GROUP), BF)] * 4 + [pltpu.SemaphoreType.DMA((6,))],
        12,
        (6 * 4 * SEQ * SEQ * 64, 6e6, 4e6),
    )


def proj_body(sc, x_ref, ak_ref, ar_ref, gain_ref, wo, m_ref, n_ref, wo_s, sem):
    copies = []
    for k in range(2):
        head = (sc[0] if k == 0 else 1 - sc[0]) * GROUP
        rows = pl.ds(pl.multiple_of(head, 128), GROUP)
        copies.append(pltpu.make_async_copy(wo.at[rows, :], wo_s.at[k], sem.at[k]))
    for cp in copies:
        cp.start()
    for cp in copies:
        cp.wait()
    for r in range(0, SPAN, 256):
        rr = slice(r, r + 256)
        m = jnp.where(live_mask(sc, r, 256), x_ref[0, rr, :].astype(F32), 0.0)
        m = m + dot(ak_ref[rr, :], wo_s[0]) + dot(ar_ref[rr, :], wo_s[1])
        m_ref[rr, :] = m
        factor = lax.rsqrt(jnp.mean(m * m, axis=-1, keepdims=True) + epsilon)
        n_ref[rr, :] = (m * factor * gain_ref[...]).astype(BF)


def proj_call(sc, tokens, own, other, gain, wo):
    return call(
        proj_body,
        "proj",
        sc,
        (tokens, own, other, gain, wo),
        [whole((1, SPAN, WIDTH))] + [whole((SPAN, GROUP))] * 2 + [whole((1, WIDTH)), far_hbm()],
        [sds((SPAN, WIDTH), F32), sds((SPAN, WIDTH))],
        [whole((SPAN, WIDTH))] * 2,
        [pltpu.VMEM((2, GROUP, WIDTH), BF), pltpu.SemaphoreType.DMA((2,))],
        8,
        (2 * SPAN * WIDTH * WIDTH, 5e6, 1e3),
    )


def place_of(s):
    return (s % 2) * 2 + s // 2


def hidden_cols(sc, s, half):
    return pl.ds(pl.multiple_of(512 * s + 128 * half + 256 * sc[0], 128), 128)


def spread(sc, res_s, first, count, rows, send_ref, keep_ref, to):
    size = send_ref.shape[1]
    for k, ref in enumerate((send_ref, keep_ref)):
        bit = (1 - sc[3]) if k == 0 else sc[3]
        for s in range(4):
            for q in range(count):
                lo = pl.multiple_of(first + (s * count + q) * 2 * rows + bit * rows, 16)
                block, row = divmod(to + q * rows, size)
                ref[2 * place_of(s) + block, row : row + rows, :] = res_s[pl.ds(lo, rows), :].astype(
                    BF
                )


def ffn_body(sc, n_own, n_oth, dy_own, dy_oth, wg, wu, wd, *refs, half):
    (send_ref, keep_ref, h_ref, dg_ref, du_ref, n_s, dy_s, wg_s, wu_s, wd_s, res_a, res_b, sem) = refs
    loads = []
    for k, src in enumerate((n_own, n_oth)):
        loads.append(pltpu.make_async_copy(src, n_s.at[SPAN * k : SPAN * k + SPAN, :], sem.at[k]))
    for k, src in enumerate((dy_own, dy_oth)):
        loads.append(
            pltpu.make_async_copy(src.at[0], dy_s.at[SPAN * k : SPAN * k + SPAN, :], sem.at[2 + k])
        )
    for s in range(4):
        cols = hidden_cols(sc, s, half)
        to = slice(128 * s, 128 * s + 128)
        loads.append(pltpu.make_async_copy(wg.at[:, cols], wg_s.at[:, to], sem.at[4 + s]))
        loads.append(pltpu.make_async_copy(wu.at[:, cols], wu_s.at[:, to], sem.at[8 + s]))
        loads.append(pltpu.make_async_copy(wd.at[cols, :], wd_s.at[to, :], sem.at[12 + s]))
    for cp in loads:
        cp.start()
    for cp in loads:
        cp.wait()
    for r in range(0, SEQ, 256):
        rr = slice(r, r + 256)
        pos = sc[1] if r < SPAN else 1 - sc[1]
        at = pos * SPAN + r % SPAN + lax.broadcasted_iota(jnp.int32, (256, 1), 0)
        dy = jnp.where(at < sc[2], dy_s[rr, :], jnp.zeros((), BF))
        dy_s[rr, :] = dy
        g = dot(n_s[rr, :], wg_s[...])
        u = dot(n_s[rr, :], wu_s[...])
        dh = dot_nt(dy, wd_s[...])
        sg = jax.nn.sigmoid(g)
        gs = g * sg
        h_ref[rr, :] = (gs * u).astype(BF)
        du_ref[rr, :] = (dh * gs).astype(BF)
        dg_ref[rr, :] = (dh * u * (sg + gs * (1.0 - sg))).astype(BF)
    for base, src in ((0, dg_ref), (192, du_ref)):
        for ct in range(2):
            res_a[...] = dot_tn(n_s[...], src[:, 256 * ct : 256 * ct + 256])
            spread(sc, res_a, 0, 2, 48, send_ref, keep_ref, base + 96 * ct)
    for n in range(3):
        res_b[...] = dot_tn(h_ref[...], dy_s[:, 256 * n : 256 * n + 256])
        spread(sc, res_b, 0, 1, 64, send_ref, keep_ref, 384 + 64 * n)


def ffn_call(sc, half, n_own, n_oth, dy_own, dy_oth, wg, wu, wd):
    return call(
        functools.partial(ffn_body, half=half),
        "ffn_first" if half == 0 else "ffn_second",
        sc,
        (n_own, n_oth, dy_own, dy_oth, wg, wu, wd),
        [hbm()] * 4 + [far_hbm()] * 3,
        [sds((8, 288, 256))] * 2 + [sds((SEQ, 512))] * 3,
        [whole((8, 288, 256))] * 2 + [whole((SEQ, 512))] * 3,
        [
            pltpu.VMEM((SEQ, WIDTH), BF),
            pltpu.VMEM((SEQ, WIDTH), BF),
            pltpu.VMEM((WIDTH, 512), BF),
            pltpu.VMEM((WIDTH, 512), BF),
            pltpu.VMEM((512, WIDTH), BF),
            pltpu.VMEM((WIDTH, 256), F32),
            pltpu.VMEM((512, 256), F32),
            pltpu.SemaphoreType.DMA((16,)),
        ],
        26,
        (6 * 2 * SEQ * WIDTH * 512, 14e6, 1e6),
    )


def ffn_out_body(sc, h0, dg0, du0, h1, dg1, du1, wg, wu, wd, acc_ref, accs_ref, dn_ref, dns_ref, *s):
    acts, wg_s, wu_s, wd_s, sem = s
    loads = []
    for half in range(2):
        for k, src in enumerate(((dg0, du0, h0), (dg1, du1, h1))[half]):
            loads.append(pltpu.make_async_copy(src, acts.at[k, half], sem.at[3 * half + k]))
    for half in range(2):
        for q in range(4):
            cols = hidden_cols(sc, q, half)
            to = slice(512 * half + 128 * q, 512 * half + 128 * q + 128)
            i = 6 + 3 * (4 * half + q)
            loads.append(pltpu.make_async_copy(wg.at[:, cols], wg_s.at[:, to], sem.at[i]))
            loads.append(pltpu.make_async_copy(wu.at[:, cols], wu_s.at[:, to], sem.at[i + 1]))
            loads.append(pltpu.make_async_copy(wd.at[cols, :], wd_s.at[to, :], sem.at[i + 2]))
    for cp in loads:
        cp.start()
    for cp in loads:
        cp.wait()
    for r in range(0, SEQ, 256):
        rr = slice(r, r + 256)
        dn = dot_nt(acts[0, 0, rr, :], wg_s[:, :512]) + dot_nt(acts[0, 1, rr, :], wg_s[:, 512:])
        dn = dn + dot_nt(acts[1, 0, rr, :], wu_s[:, :512])
        dn = dn + dot_nt(acts[1, 1, rr, :], wu_s[:, 512:])
        acc = dot(acts[2, 0, rr, :], wd_s[:512, :]) + dot(acts[2, 1, rr, :], wd_s[512:, :])
        if r < SPAN:
            dn_ref[rr, :] = dn
            acc_ref[rr, :] = acc
        else:
            dns_ref[r - SPAN : r - SPAN + 256, :] = dn.astype(BF)
            accs_ref[r - SPAN : r - SPAN + 256, :] = acc.astype(BF)


def ffn_out_call(sc, first, second, wg, wu, wd):
    flat = [whole((SPAN, WIDTH))]
    return call(
        ffn_out_body,
        "ffn_out",
        sc,
        tuple(first) + tuple(second) + (wg, wu, wd),
        [hbm()] * 6 + [far_hbm()] * 3,
        [sds((SPAN, WIDTH), F32), sds((SPAN, WIDTH)), sds((SPAN, WIDTH), F32), sds((SPAN, WIDTH))],
        flat * 4,
        [
            pltpu.VMEM((3, 2, SEQ, 512), BF),
            pltpu.VMEM((WIDTH, SEQ), BF),
            pltpu.VMEM((WIDTH, SEQ), BF),
            pltpu.VMEM((SEQ, WIDTH), BF),
            pltpu.SemaphoreType.DMA((30,)),
        ],
        20,
        (3 * 2 * SEQ * WIDTH * SEQ, 16e6, 0),
    )


def middle_body(sc, dn_ref, got_ref, m_ref, dy_ref, gain_ref, dm_ref, db_ref):
    gain = gain_ref[...]
    for r in range(0, SPAN, 128):
        rr = slice(r, r + 128)
        live = live_mask(sc, r, 128)
        m = m_ref[rr, :]
        factor = lax.rsqrt(jnp.mean(m * m, axis=-1, keepdims=True) + epsilon)
        scaled = (dn_ref[rr, :] + got_ref[rr, :].astype(F32)) * gain
        dm = jnp.where(live, dy_ref[0, rr, :].astype(F32), 0.0) + (
            factor * scaled
            - m * (factor * factor * factor) * jnp.mean(m * scaled, axis=-1, keepdims=True)
        )
        dm_ref[rr, :] = dm
        db_ref[rr, :] = dm.astype(BF)


def middle_call(sc, dn, got, m, dy, gain):
    flat = whole((SPAN, WIDTH))
    return call(
        middle_body,
        "middle",
        sc,
        (dn, got, m, dy, gain),
        [flat, flat, flat, whole((1, SPAN, WIDTH)), whole((1, WIDTH))],
        [sds((SPAN, WIDTH), F32), sds((SPAN, WIDTH))],
        [flat, flat],
        [],
        14,
        (1e6, 8e6, 1e3),
    )


def attend_back_body(
    sc, own, other, ot_ref, lse_ref, dbk, dbr, cos_ref, sin_ref, wo, mine, theirs, *scratch, hp
):
    qs, ks, vs, db, das, wo_s, ds_all, dqt, dkv, sem = scratch
    head = pl.ds(pl.multiple_of(sc[0] * GROUP + hp * 128, 128), 128)
    wo_copy = pltpu.make_async_copy(wo.at[head, :], wo_s, sem.at[8])
    wo_copy.start()
    grads = gather_rows(sc, dbk, dbr, (db,), sem.at[pl.ds(6, 2)])
    cols = slice(hp * 128, hp * 128 + 128)
    copies = gather_rows(sc, own.at[:, :, cols], other.at[:, :, cols], (qs, ks, vs), sem)
    wo_copy.wait()
    for cp in grads:
        cp.wait()
    for r in range(0, SEQ, 256):
        das[r : r + 256, :] = dot_nt(db[r : r + 256, :], wo_s[...]).astype(BF)
    for cp in copies:
        cp.wait()
    lane = lax.broadcasted_iota(jnp.int32, (SEQ, 128), 1)
    key_id = lax.broadcasted_iota(jnp.int32, (256, 256), 0)
    row_id = lax.broadcasted_iota(jnp.int32, (256, 256), 1)
    keep = key_id <= row_id
    kt = jnp.transpose(ks[...].astype(F32)).astype(BF)
    dat = jnp.transpose(das[...].astype(F32))
    for h in range(2):
        qm = jnp.where(lane // HEAD_DIM == h, qs[...], jnp.zeros((), BF))
        dam = jnp.where(lane // HEAD_DIM == h, das[...], jnp.zeros((), BF))
        hs = slice(h * 64, h * 64 + 64)
        delta = jnp.sum(dat[hs, :] * ot_ref[hs, :], axis=0, keepdims=True)
        lse = lse_ref[hp * 2 + h : hp * 2 + h + 1, :]
        for j in range(4):
            lo = 256 * j
            st = dot_nt(ks[lo : lo + 256, :], qm[lo:, :])
            p = jnp.exp(st - lse[:, lo:])
            diag = jnp.where(keep, p[:, :256], 0.0)
            p = diag if j == 3 else jnp.concatenate([diag, p[:, 256:]], axis=1)
            dp = dot_nt(vs[lo : lo + 256, :], dam[lo:, :])
            ds = (p * (dp - delta[:, lo:])).astype(BF)
            dv = dot(p.astype(BF), dam[lo:, :])
            dk = dot(ds, qm[lo:, :])
            dq = dot(kt[hs, lo : lo + 256], ds)
            if h == 0:
                dkv[0, lo : lo + 256, :] = dk
                dkv[1, lo : lo + 256, :] = dv
            else:
                dkv[0, lo : lo + 256, :] += dk
                dkv[1, lo : lo + 256, :] += dv
            if j == 0:
                dqt[hs, :] = dq
            else:
                dqt[hs, lo:] += dq
    dq = jnp.transpose(dqt[...]) * (HEAD_DIM**-0.5)
    back = -sin_ref[...]
    ds_all[0] = turn(dq, cos_ref[...], back).astype(BF)
    ds_all[1] = turn(dkv[0], cos_ref[...], back).astype(BF)
    ds_all[2] = dkv[1].astype(BF)
    row = pl.multiple_of(sc[1] * SPAN, SPAN)
    row_other = pl.multiple_of((1 - sc[1]) * SPAN, SPAN)
    outs = [
        pltpu.make_async_copy(ds_all.at[:, pl.ds(row_other, SPAN), :], theirs, sem.at[0]),
        pltpu.make_async_copy(ds_all.at[:, pl.ds(row, SPAN), :], mine, sem.at[1]),
    ]
    for cp in outs:
        cp.start()
    for cp in outs:
        cp.wait()


def attend_back_call(sc, hp, own, other, ot, lse, dbk, dbr, cosine, sine, wo):
    return call(
        functools.partial(attend_back_body, hp=hp),
        "attend_back",
        sc,
        (own, other, ot, lse, dbk, dbr, cosine, sine, wo),
        [hbm(), hbm(), pl.BlockSpec((128, SEQ), lambda i, sc: (hp, 0)), whole((8, SEQ))]
        + [hbm()] * 2
        + [whole((SEQ, 128))] * 2
        + [far_hbm()],
        [sds((3, SPAN, 128))] * 2,
        [hbm()] * 2,
        [pltpu.VMEM((SEQ, 128), BF)] * 3
        + [
            pltpu.VMEM((SEQ, WIDTH), BF),
            pltpu.VMEM((SEQ, 128), BF),
            pltpu.VMEM((128, WIDTH), BF),
            pltpu.VMEM((3, SEQ, 128), BF),
            pltpu.VMEM((128, SEQ), F32),
            pltpu.VMEM((2, SEQ, 128), F32),
            pltpu.SemaphoreType.DMA((9,)),
        ],
        16,
        (6 * 10 * SEQ * SEQ * 64, 10e6, 4e6),
    )


def square_body(sc, *refs):
    (nk, nr, ak, at, ck, ct, bk, br) = refs[:8]
    parts = refs[8:14]
    (send_ref, keep_ref, n_s, d_s, a_s, c_s, b_s, res, sem) = refs[14:]
    loads = []

    def load(own, other, place):
        for k, src in enumerate((own, other)):
            i = len(loads)
            where = slice(SPAN * k, SPAN * k + SPAN)
            target = place.at[:, where, :] if len(place.shape) == 3 else place.at[where, :]
            loads.append(pltpu.make_async_copy(src, target, sem.at[i]))

    load(nk, nr, n_s)
    for hp in range(3):
        load(parts[hp], parts[3 + hp], d_s.at[:, :, 128 * hp : 128 * hp + 128])
    load(ak, at, a_s)
    load(ck, ct, c_s)
    load(bk, br, b_s)
    for cp in loads:
        cp.start()
    for cp in loads:
        cp.wait()
    own = pl.ds(pl.multiple_of(sc[0] * GROUP, 128), GROUP)
    other = pl.ds(pl.multiple_of((1 - sc[0]) * GROUP, 128), GROUP)
    for t in range(3):
        res[...] = dot_tn(n_s[...], d_s[t])
        spread(sc, res, 0, 2, 48, send_ref, keep_ref, 96 * t)
    res[own, :] = dot_tn(a_s[...], b_s[:, own])
    res[other, :] = dot_tn(c_s[...], b_s[:, own])
    spread(sc, res, 0, 2, 48, send_ref, keep_ref, 288)


def square_call(sc, *args):
    return call(
        square_body,
        "square",
        sc,
        args,
        [hbm()] * 14,
        [sds((8, 192, GROUP))] * 2,
        [whole((8, 192, GROUP))] * 2,
        [
            pltpu.VMEM((SEQ, WIDTH), BF),
            pltpu.VMEM((3, SEQ, GROUP), BF),
            pltpu.VMEM((SEQ, GROUP), BF),
            pltpu.VMEM((SEQ, GROUP), BF),
            pltpu.VMEM((SEQ, WIDTH), BF),
            pltpu.VMEM((WIDTH, GROUP), F32),
            pltpu.SemaphoreType.DMA((14,)),
        ],
        16,
        (4 * 2 * SEQ * WIDTH * GROUP, 12e6, 0),
    )


def input_grad_body(
    sc,
    x_ref,
    gain_ref,
    dm_ref,
    m_ref,
    acc_ref,
    got_ref,
    *refs,
):
    parts = refs[:6]
    wq, wk, wv, lay_ref, o_ref, dk_s, dr_s, ws, sem = refs[6:]
    copies = []
    for t, w in enumerate((wq, wk, wv)):
        copies.append(pltpu.make_async_copy(w, ws.at[t], sem.at[t]))
    for hp in range(3):
        cols = slice(128 * hp, 128 * hp + 128)
        copies.append(pltpu.make_async_copy(parts[hp], dk_s.at[:, :, cols], sem.at[3 + hp]))
        copies.append(pltpu.make_async_copy(parts[3 + hp], dr_s.at[:, :, cols], sem.at[6 + hp]))
    for cp in copies:
        cp.start()
    for r in range(0, SPAN, 256):
        rr = slice(r, r + 256)
        out = m_ref[rr, :] + acc_ref[rr, :] + got_ref[rr, :].astype(F32)
        lay_ref[0, rr, :] = jnp.where(live_mask(sc, r, 256), out, 0.0).astype(BF)
    for cp in copies:
        cp.wait()
    own_cols = pl.multiple_of(sc[0] * GROUP, 128)
    other_cols = pl.multiple_of((1 - sc[0]) * GROUP, 128)
    gain = gain_ref[...]
    for r in range(0, SPAN, 256):
        rr = slice(r, r + 256)
        dn = dot_nt(dk_s[0, rr, :], ws[0, :, pl.ds(own_cols, GROUP)])
        dn = dn + dot_nt(dr_s[0, rr, :], ws[0, :, pl.ds(other_cols, GROUP)])
        for t in (1, 2):
            dn = dn + dot_nt(dk_s[t, rr, :], ws[t, :, pl.ds(own_cols, GROUP)])
            dn = dn + dot_nt(dr_s[t, rr, :], ws[t, :, pl.ds(other_cols, GROUP)])
        live = live_mask(sc, r, 256)
        x = jnp.where(live, x_ref[0, rr, :].astype(F32), 0.0)
        factor = lax.rsqrt(jnp.mean(x * x, axis=-1, keepdims=True) + epsilon)
        scaled = dn * gain
        dx = dm_ref[rr, :] + (
            factor * scaled
            - x * (factor * factor * factor) * jnp.mean(x * scaled, axis=-1, keepdims=True)
        )
        o_ref[0, rr, :] = jnp.where(live, dx, 0.0).astype(BF)


def input_grad_call(sc, tokens, gain, dm, m, acc, got, parts, wq, wk, wv):
    full = whole((1, SPAN, WIDTH))
    flat = whole((SPAN, WIDTH))
    return call(
        input_grad_body,
        "input_grad",
        sc,
        (tokens, gain, dm, m, acc, got) + tuple(parts) + (wq, wk, wv),
        [full, whole((1, WIDTH)), flat, flat, flat, flat] + [hbm()] * 6 + [far_hbm()] * 3,
        [sds((1, SPAN, WIDTH))] * 2,
        [full] * 2,
        [
            pltpu.VMEM((3, SPAN, GROUP), BF),
            pltpu.VMEM((3, SPAN, GROUP), BF),
            pltpu.VMEM((3, WIDTH, WIDTH), BF),
            pltpu.SemaphoreType.DMA((9,)),
        ],
        22,
        (3 * 2 * SPAN * WIDTH * WIDTH, 14e6, 1e3),
    )


def add_pieces(sc, count, picks, arrays, name):
    rows, cols = arrays[0].shape[1:]

    def body(sc_ref, *refs):
        total = refs[0][...].astype(F32)
        for ref in refs[1:-1]:
            total = total + ref[...].astype(F32)
        refs[-1][...] = total.astype(BF)

    def spec(pick):
        return pl.BlockSpec((1, rows, cols), lambda j, sc_ref: (pick(sc_ref, j), 0, 0))

    size = count * rows * cols
    return pl.pallas_call(
        body,
        name=name,
        out_shape=sds((count, rows, cols)),
        grid_spec=pltpu.PrefetchScalarGridSpec(
            num_scalar_prefetch=1,
            grid=(count,),
            in_specs=[spec(pick) for pick in picks],
            out_specs=pl.BlockSpec((1, rows, cols), lambda j, sc_ref: (j, 0, 0)),
        ),
        compiler_params=pltpu.CompilerParams(vmem_limit_bytes=5 * MIB),
        cost_estimate=pl.CostEstimate(
            flops=1000, bytes_accessed=1000, transcendentals=0
        ),
    )(sc, *arrays)


def row_block(rows, cols):
    return pl.BlockSpec((rows, cols), lambda i, sc: (sc[6], 0))


def row_of(column):
    column = jnp.concatenate([column, jnp.zeros((32, 1), F32)], axis=0)
    return jnp.transpose(jnp.broadcast_to(column, (128, 128)))[0:1, :]


def collect(sc, group, full):
    for n in range(8):
        core, k = divmod(n, 4)
        parity = sc[0] if core == 0 else 1 - sc[0]
        first, second = (sc[3], sc[7]) if core == 0 else (sc[7], sc[3])
        first = 1 - first if k in (1, 3) else first
        second = 1 - second if k in (2, 3) else second
        size = group[n].shape[1]
        rows = pl.ds(pl.multiple_of(second * size, 16), size)
        full[parity, first, rows, :] = group[n][0]


def ffn_result_body(sc, *refs):
    groups = (refs[0:8], refs[8:16])
    wg_ref, wu_ref, gain_ref, gate_ref, up_ref, down_ref, gg_ref, full = refs[16:]
    for half, group in enumerate(groups):
        collect(sc, group, full)
        for bit in range(2):
            rows = slice(48 * bit, 48 * bit + 48)
            for parity in range(2):
                for base, ref in ((0, gate_ref), (192, up_ref)):
                    for ct in range(2):
                        lo = pl.multiple_of(base + ct * 96 + sc[0] * 48, 16)
                        block = full[parity, bit, pl.ds(lo, 48), :].astype(F32)
                        for q in range(2):
                            col = 512 * (2 * ct + q) + 128 * half + 256 * parity
                            ref[rows, col : col + 128] = block[:, 128 * q : 128 * q + 128]
            lo = 128 * half + 64 * bit
            for t in range(3):
                down_ref[lo : lo + 64, 256 * t : 256 * t + 256] = full[
                    sc[0], bit, 384 + t * 64 : 448 + t * 64, :
                ].astype(F32)
    gate = jnp.sum(wg_ref[...].astype(F32) * gate_ref[...], axis=-1, keepdims=True)
    up = jnp.sum(wu_ref[...].astype(F32) * up_ref[...], axis=-1, keepdims=True)
    gg_ref[...] = row_of((gate + up) / gain_ref[...])


def ffn_result_call(sc, first, second, wg, wu, gain):
    return call(
        ffn_result_body,
        "ffn_result",
        sc,
        tuple(first) + tuple(second) + (wg, wu, gain),
        [whole((1, 288, 256))] * 16 + [row_block(96, HID)] * 2 + [row_block(96, 1)],
        [sds((96, HID), F32), sds((96, HID), F32), sds((256, WIDTH), F32), sds((1, 128), F32)],
        [whole((96, HID)), whole((96, HID)), whole((256, WIDTH)), whole((1, 128))],
        [pltpu.VMEM((2, 2, 576, 256), BF)],
        12,
        (1e6, 6e6, 0),
    )


def square_result_body(sc, *refs):
    group = refs[:8]
    weights = refs[8:11]
    gain_ref = refs[11]
    outs = refs[12:16]
    gg_ref, full = refs[16:]
    collect(sc, group, full)
    for bit in range(2):
        rows = slice(48 * bit, 48 * bit + 48)
        for parity in range(2):
            cols = slice(GROUP * parity, GROUP * parity + GROUP)
            for t in range(4):
                lo = pl.multiple_of(t * 96 + sc[0] * 48, 16)
                outs[t][rows, cols] = full[parity, bit, pl.ds(lo, 48), :].astype(F32)
    total = jnp.zeros((96, 1), F32)
    for t in range(3):
        total = total + jnp.sum(weights[t][...].astype(F32) * outs[t][...], axis=-1, keepdims=True)
    gg_ref[...] = row_of(total / gain_ref[...])


def square_result_call(sc, group, wq, wk, wv, gain):
    return call(
        square_result_body,
        "square_result",
        sc,
        tuple(group) + (wq, wk, wv, gain),
        [whole((1, 192, GROUP))] * 8 + [row_block(96, WIDTH)] * 3 + [row_block(96, 1)],
        [sds((96, WIDTH), F32)] * 4 + [sds((1, 128), F32)],
        [whole((96, WIDTH))] * 4 + [whole((1, 128))],
        [pltpu.VMEM((2, 2, 384, GROUP), BF)],
        8,
        (1e6, 4e6, 0),
    )


class Chain:
    def __init__(self, sc):
        self.sc = sc

    def next(self, *deps):
        self.sc = after(self.sc, *deps)
        return self.sc


class Reduction:
    def __init__(self, chain, send, keep, name):
        self.chain = chain
        self.parts = [keep]
        self.name = name
        self.send = send
        self.flight = None

    def start(self):
        self.flight = exchange(after(self.send, self.chain.sc), "first")

    def add(self, count, picks, arrays, tag):
        out = add_pieces(self.chain.next(*arrays), count, picks, arrays, self.name + tag)
        self.chain.next(out)
        return out

    def second(self):
        self.parts.append(self.flight)
        pick = lambda t, j: j * 2 + 1 - t[7]
        out = self.add(4, [pick, pick], self.parts, "_b")
        self.flight = exchange(out, "second")

    def near(self):
        self.parts.append(self.flight)
        pick = lambda t, j: (1 - t[4]) * 4 + j * 2 + t[7]
        out = self.add(2, [pick, pick, lambda t, j: (1 - t[4]) * 2 + j], self.parts, "_c")
        self.flight = exchange(out, "near")

    def far(self):
        self.parts.append(self.flight)
        pick = lambda t, j: t[4] * 4 + (1 - t[5]) * 2 + t[7]
        picks = [pick, pick, lambda t, j: t[4] * 2 + 1 - t[5], lambda t, j: 1 - t[5]]
        out = self.add(1, picks, self.parts, "_d")
        self.flight = exchange(out, "far")

    def total(self):
        self.parts.append(self.flight)
        pick = lambda t, j: t[4] * 4 + t[5] * 2 + t[7]
        picks = [pick, pick, lambda t, j: t[4] * 2 + t[5], lambda t, j: t[5], lambda t, j: 0]
        own = self.add(1, picks, self.parts, "_e")
        self.quarters = [own] + [exchange(own, kind) for kind in ("first", "second", "across")]

    def result(self):
        return self.quarters + [exchange(quarter, "core") for quarter in self.quarters]


def fast_step(
    tokens,
    lengths,
    owner,
    w_query,
    w_key,
    w_value,
    w_out,
    w_gate,
    w_up,
    w_down,
    gain_attn,
    gain_mlp,
    cotangent,
):
    batch, seq, core = (lax.axis_index(name) for name in AXES)
    own_pos = jnp.where(core == 0, owner[0, 0], owner[0, 1])
    low, high = batch % 2, batch // 2
    sc = jnp.stack(
        [
            core,
            own_pos,
            lengths[0],
            jnp.where(core == 0, low, high),
            seq % 2,
            seq // 2,
            seq * 2 + core,
            jnp.where(core == 0, high, low),
        ]
    ).astype(jnp.int32)
    tables = position_tables(SEQ)
    cosine, sine = jnp.asarray(tables[0]), jnp.asarray(tables[1])
    gain_row = gain_attn.reshape(1, WIDTH)
    gain_mlp_row = gain_mlp.reshape(1, WIDTH)
    qkv_w = (w_query, w_key, w_value)
    ffn_w = (w_gate, w_up, w_down)
    chain = Chain(sc)

    qkv_send, n1 = qkv_call(chain.sc, tokens, gain_row, cosine, sine, *qkv_w, True)
    qkv_other = exchange(qkv_send, "core")
    (qkv_own,) = qkv_call(chain.next(n1), tokens, gain_row, cosine, sine, *qkv_w, False)
    n1_other = exchange(n1, "core")
    dy_other = exchange(cotangent, "core")
    attn_t, lse, attn_own, attn_send = attend_call(chain.next(qkv_own), qkv_own, qkv_other)
    attn_other = exchange(attn_send, "core")
    attn_rest = exchange(attn_own, "core")
    middle, n2 = proj_call(
        chain.next(lse, n1_other, dy_other), tokens, attn_own, attn_other, gain_mlp_row, w_out
    )
    n2_other = exchange(n2, "core")
    rows = (n2, n2_other, cotangent, dy_other)
    send0, keep0, *acts0 = ffn_call(chain.next(n2, attn_rest), 0, *rows, *ffn_w)
    g0 = Reduction(chain, send0, keep0, "g0")
    g0.start()
    send1, keep1, *acts1 = ffn_call(chain.next(acts0[0]), 1, *rows, *ffn_w)
    g1 = Reduction(chain, send1, keep1, "g1")
    acc, acc_send, dn, dn_send = ffn_out_call(chain.next(acts1[0]), acts0, acts1, *ffn_w)
    dn_other = exchange(dn_send, "core")
    chain.next(dn_send)
    g0.second()
    d_middle, db = middle_call(chain.next(dn_other), dn, dn_other, middle, cotangent, gain_mlp_row)
    db_other = exchange(db, "core")
    acc_other = exchange(after(acc_send, db), "core")
    back = (qkv_own, qkv_other, attn_t, lse, db, db_other, cosine, sine, w_out)
    chain.next(db)
    steps = ((g1.start, g0.near), (g0.far,), (g0.total, g1.second))
    parts_own, parts_send, parts_other = [], [], []
    for hp in range(3):
        d_own, d_send = attend_back_call(chain.sc, hp, *back)
        chain.next(d_own)
        parts_own.append(d_own)
        parts_send.append(d_send)
        parts_other.append(exchange(d_send, "core"))
        for step in steps[hp]:
            step()
    send2, keep2 = square_call(
        chain.sc,
        n1,
        n1_other,
        attn_own,
        attn_send,
        attn_other,
        attn_rest,
        db,
        db_other,
        *parts_own,
        *parts_send,
    )
    g2 = Reduction(chain, send2, keep2, "g2")
    g2.start()
    chain.next(send2)
    g1.near()
    layer_out, input_grad = input_grad_call(
        chain.sc,
        tokens,
        gain_row,
        d_middle,
        middle,
        acc,
        acc_other,
        parts_own + parts_other,
        *qkv_w,
    )
    chain.next(input_grad)
    g1.far()
    g2.second()
    g1.total()
    g2.near()
    g2.far()
    gate, up, down, gain_m = ffn_result_call(
        chain.next(), g0.result(), g1.result(), w_gate, w_up, gain_mlp.reshape(WIDTH, 1)
    )
    chain.next(gain_m)
    g2.total()
    query, key, value, out, gain_a = square_result_call(
        chain.sc, g2.result(), *qkv_w, gain_attn.reshape(WIDTH, 1)
    )
    return (
        layer_out,
        input_grad,
        query,
        key,
        value,
        out,
        gate,
        up,
        down,
        gain_a[0, :96],
        gain_m[0, :96],
    )


def solution(mesh):
    in_specs = (
        P(("batch", "seq"), "seqb", None),
        P(("batch", "seq")),
        P(("batch", "seq"), None),
        P(),
        P(),
        P(),
        P(),
        P(),
        P(),
        P(),
        P(),
        P(),
        P(("batch", "seq"), "seqb", None),
    )
    out_specs = (
        P(("batch", "seq"), "seqb", None),
        P(("batch", "seq"), "seqb", None),
        P(("seq", "seqb"), None),
        P(("seq", "seqb"), None),
        P(("seq", "seqb"), None),
        P(("seq", "seqb"), None),
        P(("seq", "seqb"), None),
        P(("seq", "seqb"), None),
        P(("seq", "seqb"), None),
        P(("seq", "seqb")),
        P(("seq", "seqb")),
    )
    step = fast_step if fast_layout(mesh) else general_step
    return jax.shard_map(step, mesh=mesh, in_specs=in_specs, out_specs=out_specs, check_vma=False)
```

```python
import functools
import math

import jax
import jax.numpy as jnp
import numpy as np
from jax import lax
from jax.experimental import pallas as pl
from jax.experimental.pallas import tpu as pltpu
from jax.sharding import PartitionSpec as P

HEADS = 12
HEAD_DIM = 64


epsilon = 1e-05
rope_base = 10000.0
masked_score = -1e30


def rms_forward(rows, gain):
    factor = lax.rsqrt(jnp.mean(rows * rows, axis=-1, keepdims=True) + epsilon)
    return (rows * factor * gain, factor)


def rms_backward(rows, factor, gain, upstream):
    scaled = upstream * gain
    return factor * scaled - rows * (factor * factor * factor) * jnp.mean(
        rows * scaled, axis=-1, keepdims=True
    )


def rotation_tables(positions):
    half = HEAD_DIM // 2
    freq = rope_base ** (-(2.0 * jnp.arange(half, dtype=jnp.float32)) / HEAD_DIM)
    angles = positions.astype(jnp.float32)[..., None] * freq
    return (jnp.cos(angles), jnp.sin(angles))


def split_heads(rows):
    return rows.reshape(rows.shape[0], rows.shape[1], HEADS, HEAD_DIM)


def rotate(rows, cosine, sine, inverse):
    shaped = split_heads(rows)
    half = HEAD_DIM // 2
    first = shaped[..., :half]
    second = shaped[..., half:]
    cos_part = cosine[:, :, None, :]
    sin_part = sine[:, :, None, :]
    if inverse:
        turned = jnp.concatenate(
            [first * cos_part + second * sin_part, second * cos_part - first * sin_part], axis=-1
        )
    else:
        turned = jnp.concatenate(
            [first * cos_part - second * sin_part, second * cos_part + first * sin_part], axis=-1
        )
    return turned.reshape(rows.shape)


def range_positions(owner, count, span):
    offsets = jnp.arange(span, dtype=jnp.int32)
    return (owner[:, :, None] * span + offsets[None, None, :]).reshape(owner.shape[0], count)


def fold_keys(parts, combine, initial):
    return combine(
        initial,
        (
            lax.all_gather(parts[0], "seqb", axis=1, tiled=True),
            lax.all_gather(parts[1], "seqb", axis=1, tiled=True),
        ),
        jnp.int32(0),
    )


def general_step(
    tokens,
    lengths,
    owner,
    w_query,
    w_key,
    w_value,
    w_out,
    w_gate,
    w_up,
    w_down,
    gain_attn,
    gain_mlp,
    cotangent,
):
    seqs, span, width = tokens.shape
    scale = HEAD_DIM ** (-0.5)
    place = lax.axis_index("seqb")
    own_block = lax.dynamic_slice_in_dim(owner, place, 1, 1)
    local_pos = own_block * span + jnp.arange(span, dtype=jnp.int32)[None, :]
    local_live = local_pos < lengths[:, None]
    live_rows = local_live[:, :, None]
    inputs = jnp.where(live_rows, tokens.astype(jnp.float32), 0.0)
    normed, factor_attn = rms_forward(inputs, gain_attn)
    normed_low = normed.astype(jnp.bfloat16)
    cosine, sine = rotation_tables(local_pos)
    query_pre = jnp.einsum("scd,de->sce", normed_low, w_query, preferred_element_type=jnp.float32)
    key_pre = jnp.einsum("scd,de->sce", normed_low, w_key, preferred_element_type=jnp.float32)
    value_low = jnp.einsum(
        "scd,de->sce", normed_low, w_value, preferred_element_type=jnp.float32
    ).astype(jnp.bfloat16)
    query_rot = rotate(query_pre, cosine, sine, False).astype(jnp.bfloat16)
    key_rot = rotate(key_pre, cosine, sine, False).astype(jnp.bfloat16)
    query_heads = split_heads(query_rot)
    key_heads = split_heads(key_rot)
    value_heads = split_heads(value_low)

    def attend(state, piece, start):
        keys, values = piece
        count = keys.shape[1]
        key_pos = range_positions(owner, count, span)
        key_live = key_pos < lengths[:, None]
        stride = math.gcd(count, 512)

        def attend_one_block(index, inner):
            offset = index * stride
            key_block = split_heads(lax.dynamic_slice_in_dim(keys, offset, stride, 1))
            value_block = split_heads(lax.dynamic_slice_in_dim(values, offset, stride, 1))
            pos_block = lax.dynamic_slice_in_dim(key_pos, offset, stride, 1)
            live_block = lax.dynamic_slice_in_dim(key_live, offset, stride, 1)
            allowed = (
                (pos_block[:, None, :] <= local_pos[:, :, None])
                & live_block[:, None, :]
                & local_live[:, :, None]
            )

            def attend_update(carried):
                peak, total, summed = carried
                scores = (
                    jnp.einsum(
                        "sqhd,skhd->shqk",
                        query_heads,
                        key_block,
                        preferred_element_type=jnp.float32,
                    )
                    * scale
                )
                mask = allowed[:, None, :, :]
                new_peak = jnp.maximum(
                    peak, jnp.max(jnp.where(mask, scores, masked_score), axis=-1)
                )
                weights = jnp.where(mask, jnp.exp(scores - new_peak[..., None]), 0.0)
                factor = jnp.exp(peak - new_peak)
                total = total * factor + jnp.sum(weights, axis=-1)
                term = jnp.einsum(
                    "shqk,skhd->sqhd",
                    weights.astype(jnp.bfloat16),
                    value_block,
                    preferred_element_type=jnp.float32,
                )
                summed = (
                    split_heads(summed) * jnp.transpose(factor, (0, 2, 1))[..., None] + term
                ).reshape(summed.shape)
                return (new_peak, total, summed)

            return lax.cond(jnp.any(allowed), attend_update, lambda carried: carried, inner)

        return lax.fori_loop(0, count // stride, attend_one_block, state)

    start_state = (
        jnp.full((seqs, HEADS, span), masked_score, jnp.float32),
        jnp.zeros((seqs, HEADS, span), jnp.float32),
        jnp.zeros((seqs, span, width), jnp.float32),
    )
    peak, total, summed = fold_keys((key_rot, value_low), attend, start_state)
    safe_total = jnp.where(local_live[:, None, :], total, 1.0)
    attn = split_heads(summed) / jnp.transpose(safe_total, (0, 2, 1))[..., None]
    attn = jnp.where(local_live[:, :, None, None], attn, 0.0).reshape(seqs, span, width)
    log_total = jnp.where(local_live[:, None, :], peak + jnp.log(safe_total), 0.0)
    attn_low = attn.astype(jnp.bfloat16)
    middle = inputs + jnp.einsum("scd,de->sce", attn_low, w_out, preferred_element_type=jnp.float32)
    normed_mlp, factor_mlp = rms_forward(middle, gain_mlp)
    normed_mlp_low = normed_mlp.astype(jnp.bfloat16)
    gate = jnp.einsum("scd,df->scf", normed_mlp_low, w_gate, preferred_element_type=jnp.float32)
    up_proj = jnp.einsum("scd,df->scf", normed_mlp_low, w_up, preferred_element_type=jnp.float32)
    hidden = (jax.nn.silu(gate) * up_proj).astype(jnp.bfloat16)
    out = middle + jnp.einsum("scf,fd->scd", hidden, w_down, preferred_element_type=jnp.float32)
    layer_out = jnp.where(live_rows, out, 0.0).astype(jnp.bfloat16)
    upstream = jnp.where(live_rows, cotangent, jnp.zeros_like(cotangent))
    grad_down = jnp.einsum("scf,scd->fd", hidden, upstream, preferred_element_type=jnp.float32)
    d_hidden = jnp.einsum("scd,fd->scf", upstream, w_down, preferred_element_type=jnp.float32)
    sigmoid_gate = jax.nn.sigmoid(gate)
    d_gate = (d_hidden * up_proj * sigmoid_gate * (1.0 + gate * (1.0 - sigmoid_gate))).astype(
        jnp.bfloat16
    )
    d_up = (d_hidden * gate * sigmoid_gate).astype(jnp.bfloat16)
    grad_gate = jnp.einsum(
        "scd,scf->df", normed_mlp_low, d_gate, preferred_element_type=jnp.float32
    )
    grad_up = jnp.einsum("scd,scf->df", normed_mlp_low, d_up, preferred_element_type=jnp.float32)
    d_normed_mlp = jnp.einsum(
        "scf,df->scd", d_gate, w_gate, preferred_element_type=jnp.float32
    ) + jnp.einsum("scf,df->scd", d_up, w_up, preferred_element_type=jnp.float32)
    grad_gain_mlp = jnp.sum(d_normed_mlp * (middle * factor_mlp), axis=(0, 1))
    d_middle = upstream.astype(jnp.float32) + rms_backward(
        middle, factor_mlp, gain_mlp, d_normed_mlp
    )
    d_branch = d_middle.astype(jnp.bfloat16)
    grad_out = jnp.einsum("scd,sce->de", attn_low, d_branch, preferred_element_type=jnp.float32)
    d_attn = jnp.einsum("sce,de->scd", d_branch, w_out, preferred_element_type=jnp.float32).astype(
        jnp.bfloat16
    )
    first_done = (grad_out, grad_gate, grad_up, grad_down, grad_gain_mlp)
    delta = jnp.sum(split_heads(d_attn.astype(jnp.float32) * attn), axis=-1)
    delta_heads = jnp.transpose(delta, (0, 2, 1))
    grad_heads = split_heads(d_attn)

    def query_grads(state, piece, start):
        keys, values = piece
        count = keys.shape[1]
        key_pos = range_positions(owner, count, span)
        key_live = key_pos < lengths[:, None]
        stride = math.gcd(count, 512)

        def query_one_block(index, inner):
            offset = index * stride
            key_block = split_heads(lax.dynamic_slice_in_dim(keys, offset, stride, 1))
            value_block = split_heads(lax.dynamic_slice_in_dim(values, offset, stride, 1))
            pos_block = lax.dynamic_slice_in_dim(key_pos, offset, stride, 1)
            live_block = lax.dynamic_slice_in_dim(key_live, offset, stride, 1)
            allowed = (
                (pos_block[:, None, :] <= local_pos[:, :, None])
                & live_block[:, None, :]
                & local_live[:, :, None]
            )

            def query_update(carried):
                scores = (
                    jnp.einsum(
                        "sqhd,skhd->shqk",
                        query_heads,
                        key_block,
                        preferred_element_type=jnp.float32,
                    )
                    * scale
                )
                probs = jnp.where(
                    allowed[:, None, :, :], jnp.exp(scores - log_total[..., None]), 0.0
                )
                d_probs = jnp.einsum(
                    "sqhd,skhd->shqk", grad_heads, value_block, preferred_element_type=jnp.float32
                )
                d_scores = (probs * (d_probs - delta_heads[..., None])).astype(jnp.bfloat16)
                term = (
                    jnp.einsum(
                        "shqk,skhd->sqhd", d_scores, key_block, preferred_element_type=jnp.float32
                    )
                    * scale
                )
                return carried + term.reshape(carried.shape)

            return lax.cond(jnp.any(allowed), query_update, lambda carried: carried, inner)

        return lax.fori_loop(0, count // stride, query_one_block, state)

    zero_query = jnp.zeros((seqs, span, width), jnp.float32)
    d_query = fold_keys((key_rot, value_low), query_grads, zero_query)
    lse_all, delta_all = (
        lax.all_gather(jnp.transpose(log_total, (0, 2, 1)), "seqb", axis=1, tiled=True),
        lax.all_gather(delta, "seqb", axis=1, tiled=True),
    )
    zero_rows = jnp.zeros((seqs, span, width), jnp.float32)
    queries = lax.all_gather(query_rot, "seqb", axis=1, tiled=True)
    d_rows = lax.all_gather(d_attn, "seqb", axis=1, tiled=True)
    count = queries.shape[1]
    row_pos = range_positions(owner, count, span)
    row_live = row_pos < lengths[:, None]
    stride = math.gcd(count, 512)

    def key_one_block(index, inner):
        offset = index * stride
        query_block = split_heads(lax.dynamic_slice_in_dim(queries, offset, stride, 1))
        grad_block = split_heads(lax.dynamic_slice_in_dim(d_rows, offset, stride, 1))
        pos_block = lax.dynamic_slice_in_dim(row_pos, offset, stride, 1)
        live_block = lax.dynamic_slice_in_dim(row_live, offset, stride, 1)
        lse_block = jnp.transpose(lax.dynamic_slice_in_dim(lse_all, offset, stride, 1), (0, 2, 1))
        delta_block = jnp.transpose(
            lax.dynamic_slice_in_dim(delta_all, offset, stride, 1), (0, 2, 1)
        )
        allowed = (
            (local_pos[:, None, :] <= pos_block[:, :, None])
            & local_live[:, None, :]
            & live_block[:, :, None]
        )

        def key_update(carried):
            d_key, d_value = carried
            scores = (
                jnp.einsum(
                    "sqhd,skhd->shqk", query_block, key_heads, preferred_element_type=jnp.float32
                )
                * scale
            )
            probs = jnp.where(allowed[:, None, :, :], jnp.exp(scores - lse_block[..., None]), 0.0)
            value_term = jnp.einsum(
                "shqk,sqhd->skhd",
                probs.astype(jnp.bfloat16),
                grad_block,
                preferred_element_type=jnp.float32,
            )
            d_probs = jnp.einsum(
                "sqhd,skhd->shqk", grad_block, value_heads, preferred_element_type=jnp.float32
            )
            d_scores = (probs * (d_probs - delta_block[..., None])).astype(jnp.bfloat16)
            key_term = (
                jnp.einsum(
                    "shqk,sqhd->skhd", d_scores, query_block, preferred_element_type=jnp.float32
                )
                * scale
            )
            return (
                d_key + key_term.reshape(d_key.shape),
                d_value + value_term.reshape(d_value.shape),
            )

        return lax.cond(jnp.any(allowed), key_update, lambda carried: carried, inner)

    d_key, d_value = lax.fori_loop(0, count // stride, key_one_block, (zero_rows, zero_rows))
    d_query_pre = rotate(d_query, cosine, sine, True).astype(jnp.bfloat16)
    d_key_pre = rotate(d_key, cosine, sine, True).astype(jnp.bfloat16)
    d_value_low = d_value.astype(jnp.bfloat16)
    grad_query = jnp.einsum(
        "scd,sce->de", normed_low, d_query_pre, preferred_element_type=jnp.float32
    )
    grad_key = jnp.einsum("scd,sce->de", normed_low, d_key_pre, preferred_element_type=jnp.float32)
    grad_value = jnp.einsum(
        "scd,sce->de", normed_low, d_value_low, preferred_element_type=jnp.float32
    )
    d_normed = jnp.einsum("sce,de->scd", d_query_pre, w_query, preferred_element_type=jnp.float32)
    d_normed = d_normed + jnp.einsum(
        "sce,de->scd", d_key_pre, w_key, preferred_element_type=jnp.float32
    )
    d_normed = d_normed + jnp.einsum(
        "sce,de->scd", d_value_low, w_value, preferred_element_type=jnp.float32
    )
    grad_gain_attn = jnp.sum(d_normed * (inputs * factor_attn), axis=(0, 1))
    d_inputs = d_middle + rms_backward(inputs, factor_attn, gain_attn, d_normed)
    input_grad = jnp.where(live_rows, d_inputs, 0.0).astype(jnp.bfloat16)
    summed_parts = (
        lax.psum_scatter(grad_query, ("seq", "seqb"), scatter_dimension=0, tiled=True),
        lax.psum_scatter(grad_key, ("seq", "seqb"), scatter_dimension=0, tiled=True),
        lax.psum_scatter(grad_value, ("seq", "seqb"), scatter_dimension=0, tiled=True),
        lax.psum_scatter(grad_gain_attn, ("seq", "seqb"), scatter_dimension=0, tiled=True),
        lax.psum_scatter(first_done[0], ("seq", "seqb"), scatter_dimension=0, tiled=True),
        lax.psum_scatter(first_done[1], ("seq", "seqb"), scatter_dimension=0, tiled=True),
        lax.psum_scatter(first_done[2], ("seq", "seqb"), scatter_dimension=0, tiled=True),
        lax.psum_scatter(first_done[3], ("seq", "seqb"), scatter_dimension=0, tiled=True),
        lax.psum_scatter(first_done[4], ("seq", "seqb"), scatter_dimension=0, tiled=True),
    )
    all_done = (
        lax.psum(summed_parts[0].astype(jnp.bfloat16), "batch").astype(jnp.float32),
        lax.psum(summed_parts[1].astype(jnp.bfloat16), "batch").astype(jnp.float32),
        lax.psum(summed_parts[2].astype(jnp.bfloat16), "batch").astype(jnp.float32),
        lax.psum(summed_parts[3].astype(jnp.bfloat16), "batch").astype(jnp.float32),
        lax.psum(summed_parts[4].astype(jnp.bfloat16), "batch").astype(jnp.float32),
        lax.psum(summed_parts[5].astype(jnp.bfloat16), "batch").astype(jnp.float32),
        lax.psum(summed_parts[6].astype(jnp.bfloat16), "batch").astype(jnp.float32),
        lax.psum(summed_parts[7].astype(jnp.bfloat16), "batch").astype(jnp.float32),
        lax.psum(summed_parts[8].astype(jnp.bfloat16), "batch").astype(jnp.float32),
    )
    second_done = (all_done[0], all_done[1], all_done[2], all_done[3])
    first_done = (all_done[4], all_done[5], all_done[6], all_done[7], all_done[8])
    return (
        layer_out,
        input_grad,
        second_done[0],
        second_done[1],
        second_done[2],
        first_done[0],
        first_done[1],
        first_done[2],
        first_done[3],
        second_done[3],
        first_done[4],
    )


AXES = ("batch", "seq", "seqb")
BF = jnp.bfloat16
F32 = jnp.float32
MIB = 1 << 20
COST = 1e6
ADD_COST = 2e9
KERNEL_US = {
    "qkv_other": 4,
    "qkv_own": 4,
    "attend": 9,
    "proj": 3,
    "ffn_first": 8,
    "ffn_second": 8,
    "ffn_out": 9,
    "middle": 1.4,
    "attend_back": 14,
    "square": 5,
    "input_grad": 6.5,
    "ffn_result": 2,
    "square_result": 2,
}


def fast_layout(mesh):
    return mesh.shape["batch"] == 4 and mesh.shape["seq"] == 4 and mesh.shape["seqb"] == 2


def exchange(rows, kind):
    pairs = []
    for b in range(4):
        for s in range(4):
            for c in range(2):
                first = 1 if c == 0 else 2
                target = {
                    "core": (b, s, 1 - c),
                    "first": (b ^ first, s, c),
                    "second": (b ^ (3 - first), s, c),
                    "near": (b, s ^ 1, c),
                    "far": (b, s ^ 2, c),
                    "across": (b ^ 3, s, c),
                }[kind]
                pairs.append((b * 8 + s * 2 + c, target[0] * 8 + target[1] * 2 + target[2]))
    return lax.ppermute(rows, AXES, pairs)


def dot(a, b):
    return lax.dot_general(a, b, (((1,), (0,)), ((), ())), preferred_element_type=F32)


def dot_nt(a, b):
    return lax.dot_general(a, b, (((1,), (1,)), ((), ())), preferred_element_type=F32)


def position_tables(count):
    half = HEAD_DIM // 2
    freq = rope_base ** (-(2.0 * np.arange(half)) / HEAD_DIM)
    angles = np.arange(count)[:, None] * freq[None, :]
    cosine, sine = np.cos(angles), np.sin(angles)
    return (
        np.concatenate([cosine, cosine, cosine, cosine], 1).astype(np.float32),
        np.concatenate([-sine, sine, -sine, sine], 1).astype(np.float32),
    )


def swap_halves(u):
    lane = lax.broadcasted_iota(jnp.int32, u.shape, 1) % HEAD_DIM
    return jnp.where(lane < HEAD_DIM // 2, pltpu.roll(u, 96, 1), pltpu.roll(u, 32, 1))


def turn(rows, cosine, sine):
    parts = []
    for g in range(rows.shape[1] // 128):
        u = rows[:, g * 128 : (g + 1) * 128]
        parts.append(u * cosine + swap_halves(u) * sine)
    return parts[0] if len(parts) == 1 else jnp.concatenate(parts, axis=1)


def live_mask(sc, row0, count):
    span_pos = sc[1] * SPAN + row0 + lax.broadcasted_iota(jnp.int32, (count, 1), 0)
    return span_pos < sc[2]


SPAN = 512
SEQ = 1024
WIDTH = 768
GROUP = 384
HID = 2048


def hbm():
    return pl.BlockSpec(memory_space=pl.ANY)


def far_hbm():
    return pl.BlockSpec(memory_space=pltpu.HBM)


def after(sc, *deps):
    return lax.optimization_barrier((sc,) + deps)[0]


def dot_tn(a, b):
    return lax.dot_general(a, b, (((0,), (0,)), ((), ())), preferred_element_type=F32)


def whole(shape):
    return pl.BlockSpec(shape, lambda i, sc: (0,) * len(shape))


def call(body, name, sc, args, in_specs, out_shapes, out_specs, scratch, vmem, cost):
    flops, moved, trans = cost
    args = [
        pltpu.with_memory_space_constraint(a, pltpu.HBM) if spec.memory_space is pltpu.HBM else a
        for a, spec in zip(args, in_specs)
    ]
    return pl.pallas_call(
        body,
        name=name,
        out_shape=out_shapes,
        grid_spec=pltpu.PrefetchScalarGridSpec(
            num_scalar_prefetch=1,
            grid=(1,),
            in_specs=in_specs,
            out_specs=out_specs,
            scratch_shapes=scratch,
        ),
        compiler_params=pltpu.CompilerParams(vmem_limit_bytes=vmem * MIB),
        cost_estimate=pl.CostEstimate(
            flops=int(COST * KERNEL_US[name]), bytes_accessed=1000, transcendentals=0
        ),
    )(sc, *args)


def sds(shape, dtype=BF):
    return jax.ShapeDtypeStruct(shape, dtype)


def qkv_body(sc, x_hbm, cos_hbm, sin_hbm, gain_ref, wq, wk, wv, *rest, flip):
    if flip:
        o_ref, n_ref, xs, cs, ss, ws, sem = rest
    else:
        o_ref, xs, cs, ss, ws, sem = rest
    col = (1 - sc[0]) if flip else sc[0]
    col = pl.multiple_of(col * GROUP, 128)
    row = pl.multiple_of(sc[1] * SPAN, SPAN)
    x_copy = pltpu.make_async_copy(x_hbm.at[0], xs, sem.at[3])
    x_copy.start()
    copies = [
        pltpu.make_async_copy(w.at[:, pl.ds(col, GROUP)], ws.at[t], sem.at[t])
        for t, w in enumerate((wq, wk, wv))
    ]
    tables = [
        pltpu.make_async_copy(cos_hbm.at[pl.ds(row, SPAN), :], cs, sem.at[4]),
        pltpu.make_async_copy(sin_hbm.at[pl.ds(row, SPAN), :], ss, sem.at[5]),
    ]
    for cp in [copies[0]] + tables + copies[1:]:
        cp.start()
    x_copy.wait()
    normed = []
    for r in range(0, SPAN, 256):
        x = jnp.where(live_mask(sc, r, 256), xs[r : r + 256, :].astype(F32), 0.0)
        factor = lax.rsqrt(jnp.mean(x * x, axis=-1, keepdims=True) + epsilon)
        n1 = (x * factor * gain_ref[...]).astype(BF)
        if flip:
            n_ref[r : r + 256, :] = n1
        normed.append(n1)
    copies[0].wait()
    for cp in tables:
        cp.wait()
    for t in range(3):
        if t:
            copies[t].wait()
        for i, r in enumerate(range(0, SPAN, 256)):
            y = dot(normed[i], ws[t])
            if t < 2:
                y = turn(y, cs[r : r + 256, :], ss[r : r + 256, :])
            if t == 0:
                y = y * (HEAD_DIM**-0.5)
            o_ref[t, r : r + 256, :] = y.astype(BF)


def qkv_call(sc, tokens, gain, cosine, sine, wq, wk, wv, flip):
    out_shapes = [sds((3, SPAN, GROUP))]
    out_specs = [whole((3, SPAN, GROUP))]
    if flip:
        out_shapes.append(sds((SPAN, WIDTH)))
        out_specs.append(whole((SPAN, WIDTH)))
    return call(
        functools.partial(qkv_body, flip=flip),
        "qkv_other" if flip else "qkv_own",
        sc,
        (tokens, cosine, sine, gain, wq, wk, wv),
        [far_hbm(), far_hbm(), far_hbm(), whole((1, WIDTH)), far_hbm(), far_hbm(), far_hbm()],
        out_shapes,
        out_specs,
        [
            pltpu.VMEM((SPAN, WIDTH), BF),
            pltpu.VMEM((SPAN, 128), F32),
            pltpu.VMEM((SPAN, 128), F32),
            pltpu.VMEM((3, WIDTH, GROUP), BF),
            pltpu.SemaphoreType.DMA((6,)),
        ],
        9,
        (3 * 2 * SPAN * WIDTH * GROUP, 5e6, 1e3),
    )


def gather_rows(sc, own, other, places, sem):
    copies = []
    for t, place in enumerate(places):
        for k, src in enumerate((own, other)):
            pos = sc[1] if k == 0 else 1 - sc[1]
            row = pl.multiple_of(pos * SPAN, SPAN)
            source = src.at[t] if len(src.shape) == 3 else src
            copies.append(
                pltpu.make_async_copy(source, place.at[pl.ds(row, SPAN), :], sem.at[2 * t + k])
            )
    for cp in copies:
        cp.start()
    return copies


def attend_body(sc, own, other, ot_ref, lse_ref, mine, theirs, qs, ks, vs, at, sem):
    copies = gather_rows(sc, own, other, (qs, ks, vs), sem)
    for cp in copies:
        cp.wait()
    lane = lax.broadcasted_iota(jnp.int32, (256, 128), 1)
    key_id = lax.broadcasted_iota(jnp.int32, (256, 256), 0)
    row_id = lax.broadcasted_iota(jnp.int32, (256, 256), 1)
    keep = key_id <= row_id

    def pair(hp, carry):
        base = pl.multiple_of(hp * 128, 128)
        cols = pl.ds(base, 128)
        vt = jnp.transpose(vs[:, cols].astype(F32)).astype(BF)

        def scores(i, h):
            n = 256 * (i + 1)
            qm = jnp.where(lane // HEAD_DIM == h, qs[256 * i : n, cols], jnp.zeros((), BF))
            return dot_nt(ks[0:n, cols], qm)

        def soften(i, h, st):
            n = 256 * (i + 1)
            diag = jnp.where(keep, st[n - 256 :, :], masked_score)
            st = diag if i == 0 else jnp.concatenate([st[: n - 256, :], diag], axis=0)
            peak = jnp.max(st, axis=0, keepdims=True)
            p = jnp.exp(st - peak)
            return p.astype(BF), peak, jnp.sum(p, axis=0, keepdims=True)

        def finish(i, h, p, peak, total):
            n = 256 * (i + 1)
            o = dot(vt[h * 64 : h * 64 + 64, :n], p) * (1.0 / total)
            ot_ref[pl.ds(pl.multiple_of(hp * 128 + h * 64, 64), 64), 256 * i : n] = o
            lse_ref[pl.ds(hp * 2 + h, 1), 256 * i : n] = peak + jnp.log(total)

        tasks = [(i, h) for i in range(4) for h in range(2)]
        st, waiting = scores(*tasks[0]), None
        for k, task in enumerate(tasks):
            ahead = scores(*tasks[k + 1]) if k + 1 < len(tasks) else None
            parts = soften(*task, st)
            if waiting is not None:
                finish(*waiting)
            waiting, st = task + parts, ahead
        finish(*waiting)
        at[:, cols] = jnp.transpose(ot_ref[cols, :]).astype(BF)
        return carry

    lax.fori_loop(0, 3, pair, 0)
    row = pl.multiple_of(sc[1] * SPAN, SPAN)
    row_other = pl.multiple_of((1 - sc[1]) * SPAN, SPAN)
    out_other = pltpu.make_async_copy(at.at[pl.ds(row_other, SPAN), :], theirs, sem.at[0])
    out_own = pltpu.make_async_copy(at.at[pl.ds(row, SPAN), :], mine, sem.at[1])
    out_other.start()
    out_own.start()
    out_other.wait()
    out_own.wait()


def attend_call(sc, own, other):
    return call(
        attend_body,
        "attend",
        sc,
        (own, other),
        [hbm(), hbm()],
        [sds((GROUP, SEQ), F32), sds((8, SEQ), F32), sds((SPAN, GROUP)), sds((SPAN, GROUP))],
        [whole((GROUP, SEQ)), whole((8, SEQ)), hbm(), hbm()],
        [pltpu.VMEM((SEQ, GROUP), BF)] * 4 + [pltpu.SemaphoreType.DMA((24,))],
        12,
        (6 * 4 * SEQ * SEQ * 64, 6e6, 4e6),
    )


def proj_body(sc, x_ref, ak_ref, ar_ref, gain_ref, wo, m_ref, n_ref, wo_s, sem):
    copies = []
    for k in range(2):
        head = (sc[0] if k == 0 else 1 - sc[0]) * GROUP
        rows = pl.ds(pl.multiple_of(head, 128), GROUP)
        copies.append(pltpu.make_async_copy(wo.at[rows, :], wo_s.at[k], sem.at[k]))
    for cp in copies:
        cp.start()
    for cp in copies:
        cp.wait()
    for r in range(0, SPAN, 256):
        rr = slice(r, r + 256)
        m = jnp.where(live_mask(sc, r, 256), x_ref[0, rr, :].astype(F32), 0.0)
        m = m + dot(ak_ref[rr, :], wo_s[0]) + dot(ar_ref[rr, :], wo_s[1])
        m_ref[rr, :] = m
        factor = lax.rsqrt(jnp.mean(m * m, axis=-1, keepdims=True) + epsilon)
        n_ref[rr, :] = (m * factor * gain_ref[...]).astype(BF)


def proj_call(sc, tokens, own, other, gain, wo):
    return call(
        proj_body,
        "proj",
        sc,
        (tokens, own, other, gain, wo),
        [whole((1, SPAN, WIDTH))] + [whole((SPAN, GROUP))] * 2 + [whole((1, WIDTH)), far_hbm()],
        [sds((SPAN, WIDTH), F32), sds((SPAN, WIDTH))],
        [whole((SPAN, WIDTH))] * 2,
        [pltpu.VMEM((2, GROUP, WIDTH), BF), pltpu.SemaphoreType.DMA((2,))],
        8,
        (2 * SPAN * WIDTH * WIDTH, 5e6, 1e3),
    )


def place_of(s):
    return (s % 2) * 2 + s // 2


def hidden_cols(sc, s, half):
    return pl.ds(pl.multiple_of(512 * s + 128 * half + 256 * sc[0], 128), 128)


def spread(sc, res_s, first, count, rows, send_ref, keep_ref, to):
    size = send_ref.shape[1]
    for k, ref in enumerate((send_ref, keep_ref)):
        bit = (1 - sc[3]) if k == 0 else sc[3]
        for s in range(4):
            for q in range(count):
                lo = pl.multiple_of(first + (s * count + q) * 2 * rows + bit * rows, 16)
                block, row = divmod(to + q * rows, size)
                ref[2 * place_of(s) + block, row : row + rows, :] = res_s[pl.ds(lo, rows), :].astype(
                    BF
                )


def ffn_body(sc, n_own, n_oth, dy_own, dy_oth, wg, wu, wd, *refs, half):
    (send_ref, keep_ref, h_ref, dg_ref, du_ref, n_s, dy_s, wg_s, wu_s, wd_s, res_a, res_b, sem) = refs
    loads = []
    for k, src in enumerate((n_own, n_oth)):
        loads.append(pltpu.make_async_copy(src, n_s.at[SPAN * k : SPAN * k + SPAN, :], sem.at[k]))
    for k, src in enumerate((dy_own, dy_oth)):
        loads.append(
            pltpu.make_async_copy(src.at[0], dy_s.at[SPAN * k : SPAN * k + SPAN, :], sem.at[2 + k])
        )
    for s in range(4):
        cols = hidden_cols(sc, s, half)
        to = slice(128 * s, 128 * s + 128)
        loads.append(pltpu.make_async_copy(wg.at[:, cols], wg_s.at[:, to], sem.at[4 + s]))
        loads.append(pltpu.make_async_copy(wu.at[:, cols], wu_s.at[:, to], sem.at[8 + s]))
        loads.append(pltpu.make_async_copy(wd.at[cols, :], wd_s.at[to, :], sem.at[12 + s]))
    for cp in loads:
        cp.start()
    for cp in loads:
        cp.wait()
    for r in range(0, SEQ, 256):
        rr = slice(r, r + 256)
        pos = sc[1] if r < SPAN else 1 - sc[1]
        at = pos * SPAN + r % SPAN + lax.broadcasted_iota(jnp.int32, (256, 1), 0)
        dy = jnp.where(at < sc[2], dy_s[rr, :], jnp.zeros((), BF))
        dy_s[rr, :] = dy
        g = dot(n_s[rr, :], wg_s[...])
        u = dot(n_s[rr, :], wu_s[...])
        dh = dot_nt(dy, wd_s[...])
        sg = jax.nn.sigmoid(g)
        gs = g * sg
        h_ref[rr, :] = (gs * u).astype(BF)
        du_ref[rr, :] = (dh * gs).astype(BF)
        dg_ref[rr, :] = (dh * u * (sg + gs * (1.0 - sg))).astype(BF)
    for base, src in ((0, dg_ref), (192, du_ref)):
        for ct in range(2):
            res_a[...] = dot_tn(n_s[...], src[:, 256 * ct : 256 * ct + 256])
            spread(sc, res_a, 0, 2, 48, send_ref, keep_ref, base + 96 * ct)
    for n in range(3):
        res_b[...] = dot_tn(h_ref[...], dy_s[:, 256 * n : 256 * n + 256])
        spread(sc, res_b, 0, 1, 64, send_ref, keep_ref, 384 + 64 * n)


def ffn_call(sc, half, n_own, n_oth, dy_own, dy_oth, wg, wu, wd):
    return call(
        functools.partial(ffn_body, half=half),
        "ffn_first" if half == 0 else "ffn_second",
        sc,
        (n_own, n_oth, dy_own, dy_oth, wg, wu, wd),
        [hbm()] * 4 + [far_hbm()] * 3,
        [sds((8, 288, 256))] * 2 + [sds((SEQ, 512))] * 3,
        [whole((8, 288, 256))] * 2 + [whole((SEQ, 512))] * 3,
        [
            pltpu.VMEM((SEQ, WIDTH), BF),
            pltpu.VMEM((SEQ, WIDTH), BF),
            pltpu.VMEM((WIDTH, 512), BF),
            pltpu.VMEM((WIDTH, 512), BF),
            pltpu.VMEM((512, WIDTH), BF),
            pltpu.VMEM((WIDTH, 256), F32),
            pltpu.VMEM((512, 256), F32),
            pltpu.SemaphoreType.DMA((16,)),
        ],
        26,
        (6 * 2 * SEQ * WIDTH * 512, 14e6, 1e6),
    )


def ffn_out_body(sc, h0, dg0, du0, h1, dg1, du1, wg, wu, wd, acc_ref, accs_ref, dn_ref, dns_ref, *s):
    acts, wg_s, wu_s, wd_s, sem = s
    loads = []
    for half in range(2):
        for k, src in enumerate(((dg0, du0, h0), (dg1, du1, h1))[half]):
            loads.append(pltpu.make_async_copy(src, acts.at[k, half], sem.at[3 * half + k]))
    for half in range(2):
        for q in range(4):
            cols = hidden_cols(sc, q, half)
            to = slice(512 * half + 128 * q, 512 * half + 128 * q + 128)
            i = 6 + 3 * (4 * half + q)
            loads.append(pltpu.make_async_copy(wg.at[:, cols], wg_s.at[:, to], sem.at[i]))
            loads.append(pltpu.make_async_copy(wu.at[:, cols], wu_s.at[:, to], sem.at[i + 1]))
            loads.append(pltpu.make_async_copy(wd.at[cols, :], wd_s.at[to, :], sem.at[i + 2]))
    for cp in loads:
        cp.start()
    for cp in loads:
        cp.wait()
    for r in range(0, SEQ, 256):
        rr = slice(r, r + 256)
        dn = dot_nt(acts[0, 0, rr, :], wg_s[:, :512]) + dot_nt(acts[0, 1, rr, :], wg_s[:, 512:])
        dn = dn + dot_nt(acts[1, 0, rr, :], wu_s[:, :512])
        dn = dn + dot_nt(acts[1, 1, rr, :], wu_s[:, 512:])
        acc = dot(acts[2, 0, rr, :], wd_s[:512, :]) + dot(acts[2, 1, rr, :], wd_s[512:, :])
        if r < SPAN:
            dn_ref[rr, :] = dn
            acc_ref[rr, :] = acc
        else:
            dns_ref[r - SPAN : r - SPAN + 256, :] = dn.astype(BF)
            accs_ref[r - SPAN : r - SPAN + 256, :] = acc.astype(BF)


def ffn_out_call(sc, first, second, wg, wu, wd):
    flat = [whole((SPAN, WIDTH))]
    return call(
        ffn_out_body,
        "ffn_out",
        sc,
        tuple(first) + tuple(second) + (wg, wu, wd),
        [hbm()] * 6 + [far_hbm()] * 3,
        [sds((SPAN, WIDTH), F32), sds((SPAN, WIDTH)), sds((SPAN, WIDTH), F32), sds((SPAN, WIDTH))],
        flat * 4,
        [
            pltpu.VMEM((3, 2, SEQ, 512), BF),
            pltpu.VMEM((WIDTH, SEQ), BF),
            pltpu.VMEM((WIDTH, SEQ), BF),
            pltpu.VMEM((SEQ, WIDTH), BF),
            pltpu.SemaphoreType.DMA((30,)),
        ],
        20,
        (3 * 2 * SEQ * WIDTH * SEQ, 16e6, 0),
    )


def middle_body(sc, dn_ref, got_ref, m_ref, dy_ref, gain_ref, dm_ref, db_ref):
    gain = gain_ref[...]
    for r in range(0, SPAN, 128):
        rr = slice(r, r + 128)
        live = live_mask(sc, r, 128)
        m = m_ref[rr, :]
        factor = lax.rsqrt(jnp.mean(m * m, axis=-1, keepdims=True) + epsilon)
        scaled = (dn_ref[rr, :] + got_ref[rr, :].astype(F32)) * gain
        dm = jnp.where(live, dy_ref[0, rr, :].astype(F32), 0.0) + (
            factor * scaled
            - m * (factor * factor * factor) * jnp.mean(m * scaled, axis=-1, keepdims=True)
        )
        dm_ref[rr, :] = dm
        db_ref[rr, :] = dm.astype(BF)


def middle_call(sc, dn, got, m, dy, gain):
    flat = whole((SPAN, WIDTH))
    return call(
        middle_body,
        "middle",
        sc,
        (dn, got, m, dy, gain),
        [flat, flat, flat, whole((1, SPAN, WIDTH)), whole((1, WIDTH))],
        [sds((SPAN, WIDTH), F32), sds((SPAN, WIDTH))],
        [flat, flat],
        [],
        14,
        (1e6, 8e6, 1e3),
    )


def attend_back_body(sc, own, other, ot, lse, dbk, dbr, cos_hbm, sin_hbm, wo, mine, theirs, *scratch):
    qs, ks, vs, db, das, wo_s, ds_all, dqt, dkv, ot_s, lse_s, cs, ss, sem = scratch
    head = pl.ds(pl.multiple_of(sc[0] * GROUP, 128), GROUP)
    wo_copy = pltpu.make_async_copy(wo.at[head, :], wo_s, sem.at[18])
    wo_copy.start()
    grads = gather_rows(sc, dbk, dbr, (db,), sem.at[pl.ds(19, 2)])
    loads = gather_rows(sc, own, other, (qs, ks, vs), sem.at[pl.ds(0, 6)])
    small = [
        pltpu.make_async_copy(src, to, sem.at[24 + n])
        for n, (src, to) in enumerate(((lse, lse_s), (cos_hbm, cs), (sin_hbm, ss), (ot, ot_s)))
    ]
    for cp in small:
        cp.start()
    wo_copy.wait()
    for cp in grads:
        cp.wait()

    def spread_grads(r, carry):
        rows = pl.ds(pl.multiple_of(r * 256, 256), 256)
        das[rows, :] = dot_nt(db[rows, :], wo_s[...]).astype(BF)
        return carry

    lax.fori_loop(0, 4, spread_grads, 0)
    for cp in loads + small:
        cp.wait()
    lane = lax.broadcasted_iota(jnp.int32, (SEQ, 128), 1)
    key_id = lax.broadcasted_iota(jnp.int32, (256, 256), 0)
    row_id = lax.broadcasted_iota(jnp.int32, (256, 256), 1)
    keep = key_id <= row_id

    def pair(hp, carry):
        base = pl.multiple_of(hp * 128, 128)
        cols = pl.ds(base, 128)
        kt = jnp.transpose(ks[:, cols].astype(F32)).astype(BF)
        dat = jnp.transpose(das[:, cols].astype(F32))
        qm, dam, delta, lses = [], [], [], []
        for h in range(2):
            qm.append(jnp.where(lane // HEAD_DIM == h, qs[:, cols], jnp.zeros((), BF)))
            dam.append(jnp.where(lane // HEAD_DIM == h, das[:, cols], jnp.zeros((), BF)))
            rows = pl.ds(pl.multiple_of(base + 64 * h, 64), 64)
            product = dat[64 * h : 64 * h + 64, :] * ot_s[rows, :]
            delta.append(jnp.sum(product, axis=0, keepdims=True))
            lses.append(lse_s[pl.ds(2 * hp + h, 1), :])

        def scores(i, h):
            n = 256 * (i + 1)
            rows = slice(256 * i, n)
            return dot_nt(ks[:n, cols], qm[h][rows, :]), dot_nt(vs[:n, cols], dam[h][rows, :])

        def soften(i, h, st, dp):
            n = 256 * (i + 1)
            rows = slice(256 * i, n)
            p = jnp.exp(st - lses[h][:, rows])
            diag = jnp.where(keep, p[n - 256 :, :], 0.0)
            p = diag if i == 0 else jnp.concatenate([p[: n - 256, :], diag], axis=0)
            return p.astype(BF), (p * (dp - delta[h][:, rows])).astype(BF)

        def finish(i, h, p, ds):
            n = 256 * (i + 1)
            rows = slice(256 * i, n)
            half = slice(64 * h, 64 * h + 64)
            dv = dot(p, dam[h][rows, :])
            dk = dot(ds, qm[h][rows, :])
            dqt[half, rows] = dot(kt[half, :n], ds)
            if (i, h) == (3, 0):
                dkv[0] = dk
                dkv[1] = dv
            else:
                dkv[0, :n] += dk
                dkv[1, :n] += dv

        tasks = [(i, h) for i in (3, 2, 1, 0) for h in range(2)]
        now, waiting = scores(*tasks[0]), None
        for k, task in enumerate(tasks):
            ahead = scores(*tasks[k + 1]) if k + 1 < len(tasks) else None
            parts = soften(*task, *now)
            if waiting is not None:
                finish(*waiting)
            waiting, now = task + parts, ahead
        finish(*waiting)
        dq = jnp.transpose(dqt[...]) * (HEAD_DIM**-0.5)
        ds_all[0, :, cols] = turn(dq, cs[...], -ss[...]).astype(BF)
        ds_all[1, :, cols] = turn(dkv[0], cs[...], -ss[...]).astype(BF)
        ds_all[2, :, cols] = dkv[1].astype(BF)
        return carry

    lax.fori_loop(0, 3, pair, 0)
    row = pl.multiple_of(sc[1] * SPAN, SPAN)
    row_other = pl.multiple_of((1 - sc[1]) * SPAN, SPAN)
    stores = [
        pltpu.make_async_copy(ds_all.at[:, pl.ds(row_other, SPAN), :], theirs, sem.at[28]),
        pltpu.make_async_copy(ds_all.at[:, pl.ds(row, SPAN), :], mine, sem.at[29]),
    ]
    for cp in stores:
        cp.start()
    for cp in stores:
        cp.wait()


def attend_back_call(sc, own, other, ot, lse, dbk, dbr, cosine, sine, wo):
    return call(
        attend_back_body,
        "attend_back",
        sc,
        (own, other, ot, lse, dbk, dbr, cosine, sine, wo),
        [hbm()] * 6 + [far_hbm()] * 3,
        [sds((3, SPAN, GROUP))] * 2,
        [hbm()] * 2,
        [pltpu.VMEM((SEQ, GROUP), BF)] * 3
        + [
            pltpu.VMEM((SEQ, WIDTH), BF),
            pltpu.VMEM((SEQ, GROUP), BF),
            pltpu.VMEM((GROUP, WIDTH), BF),
            pltpu.VMEM((3, SEQ, GROUP), BF),
            pltpu.VMEM((128, SEQ), F32),
            pltpu.VMEM((2, SEQ, 128), F32),
            pltpu.VMEM((GROUP, SEQ), F32),
            pltpu.VMEM((8, SEQ), F32),
            pltpu.VMEM((SEQ, 128), F32),
            pltpu.VMEM((SEQ, 128), F32),
            pltpu.SemaphoreType.DMA((33,)),
        ],
        26,
        (6 * 10 * SEQ * SEQ * 64, 10e6, 4e6),
    )


def over_rows(own, other, d_own, d_other):
    return dot_tn(own, d_own) + dot_tn(other, d_other)


def square_body(sc, nk, nr, ak, at, ck, ct, bk, br, dk, dr, sa_ref, ka_ref, sb_ref, kb_ref, res):
    own = pl.ds(pl.multiple_of(sc[0] * GROUP, 128), GROUP)
    other = pl.ds(pl.multiple_of((1 - sc[0]) * GROUP, 128), GROUP)
    res[0, own, :] = over_rows(ak[...], at[...], bk[:, own], br[:, own])
    res[0, other, :] = over_rows(ck[...], ct[...], bk[:, own], br[:, own])
    spread(sc, res.at[0], 0, 2, 48, sa_ref, ka_ref, 0)
    for n, t in enumerate((2, 0, 1)):
        place = res.at[(n + 1) % 2]
        place[...] = over_rows(nk[...], nr[...], dk[t], dr[t])
        if n == 0:
            spread(sc, place, 0, 2, 48, sa_ref, ka_ref, 96)
        else:
            spread(sc, place, 0, 2, 48, sb_ref, kb_ref, 96 * t)


def square_call(sc, *args):
    flat = [whole((SPAN, WIDTH))] * 2
    return call(
        square_body,
        "square",
        sc,
        args,
        flat + [whole((SPAN, GROUP))] * 4 + flat + [whole((3, SPAN, GROUP))] * 2,
        [sds((8, 96, GROUP))] * 4,
        [whole((8, 96, GROUP))] * 4,
        [pltpu.VMEM((2, WIDTH, GROUP), F32)],
        16,
        (4 * 2 * SEQ * WIDTH * GROUP, 12e6, 0),
    )


def input_grad_body(
    sc,
    x_ref,
    gain_ref,
    dm_ref,
    m_ref,
    acc_ref,
    got_ref,
    *refs,
):
    dk, dr, wq, wk, wv, lay_ref, o_ref, dk_s, dr_s, ws, sem = refs
    copies = []
    for t, w in enumerate((wq, wk, wv)):
        copies.append(pltpu.make_async_copy(w, ws.at[t], sem.at[t]))
    copies.append(pltpu.make_async_copy(dk, dk_s, sem.at[3]))
    copies.append(pltpu.make_async_copy(dr, dr_s, sem.at[4]))
    for cp in copies:
        cp.start()
    for r in range(0, SPAN, 256):
        rr = slice(r, r + 256)
        out = m_ref[rr, :] + acc_ref[rr, :] + got_ref[rr, :].astype(F32)
        lay_ref[0, rr, :] = jnp.where(live_mask(sc, r, 256), out, 0.0).astype(BF)
    for cp in copies:
        cp.wait()
    own_cols = pl.multiple_of(sc[0] * GROUP, 128)
    other_cols = pl.multiple_of((1 - sc[0]) * GROUP, 128)
    gain = gain_ref[...]
    for r in range(0, SPAN, 256):
        rr = slice(r, r + 256)
        dn = dot_nt(dk_s[0, rr, :], ws[0, :, pl.ds(own_cols, GROUP)])
        dn = dn + dot_nt(dr_s[0, rr, :], ws[0, :, pl.ds(other_cols, GROUP)])
        for t in (1, 2):
            dn = dn + dot_nt(dk_s[t, rr, :], ws[t, :, pl.ds(own_cols, GROUP)])
            dn = dn + dot_nt(dr_s[t, rr, :], ws[t, :, pl.ds(other_cols, GROUP)])
        live = live_mask(sc, r, 256)
        x = jnp.where(live, x_ref[0, rr, :].astype(F32), 0.0)
        factor = lax.rsqrt(jnp.mean(x * x, axis=-1, keepdims=True) + epsilon)
        scaled = dn * gain
        dx = dm_ref[rr, :] + (
            factor * scaled
            - x * (factor * factor * factor) * jnp.mean(x * scaled, axis=-1, keepdims=True)
        )
        o_ref[0, rr, :] = jnp.where(live, dx, 0.0).astype(BF)


def input_grad_call(sc, tokens, gain, dm, m, acc, got, dk, dr, wq, wk, wv):
    full = whole((1, SPAN, WIDTH))
    flat = whole((SPAN, WIDTH))
    return call(
        input_grad_body,
        "input_grad",
        sc,
        (tokens, gain, dm, m, acc, got, dk, dr, wq, wk, wv),
        [full, whole((1, WIDTH)), flat, flat, flat, flat] + [hbm()] * 2 + [far_hbm()] * 3,
        [sds((1, SPAN, WIDTH))] * 2,
        [full] * 2,
        [
            pltpu.VMEM((3, SPAN, GROUP), BF),
            pltpu.VMEM((3, SPAN, GROUP), BF),
            pltpu.VMEM((3, WIDTH, WIDTH), BF),
            pltpu.SemaphoreType.DMA((5,)),
        ],
        22,
        (3 * 2 * SPAN * WIDTH * WIDTH, 14e6, 1e3),
    )


def add_pieces(sc, count, sums, name):
    rows, cols = sums[0][0][0].shape[1:]
    arrays = [array for stack in sums for array, _ in stack]
    picks = [pick for stack in sums for _, pick in stack]

    def body(sc_ref, *refs):
        at = 0
        for n, stack in enumerate(sums):
            total = refs[at][0].astype(F32)
            for ref in refs[at + 1 : at + len(stack)]:
                total = total + ref[0].astype(F32)
            refs[-1][0, n * rows : (n + 1) * rows, :] = total.astype(BF)
            at += len(stack)

    def spec(pick):
        block, row = pick
        return pl.BlockSpec((1, rows, cols), lambda j, sc_ref: (block(sc_ref, j), row, 0))

    high = rows * len(sums)
    return pl.pallas_call(
        body,
        name=name,
        out_shape=sds((count, high, cols)),
        grid_spec=pltpu.PrefetchScalarGridSpec(
            num_scalar_prefetch=1,
            grid=(count,),
            in_specs=[spec(pick) for pick in picks],
            out_specs=pl.BlockSpec((1, high, cols), lambda j, sc_ref: (j, 0, 0)),
        ),
        compiler_params=pltpu.CompilerParams(vmem_limit_bytes=6 * MIB),
        cost_estimate=pl.CostEstimate(
            flops=int(0 if name == "g0_b" else ADD_COST), bytes_accessed=1000, transcendentals=0
        ),
    )(sc, *arrays)


def row_block(rows, cols):
    return pl.BlockSpec((rows, cols), lambda i, sc: (sc[6], 0))


def row_of(column):
    column = jnp.concatenate([column, jnp.zeros((32, 1), F32)], axis=0)
    return jnp.transpose(jnp.broadcast_to(column, (128, 128)))[0:1, :]


def collect_halves(sc, group, full):
    for n in range(4):
        core, k = divmod(n, 2)
        parity = sc[0] if core == 0 else 1 - sc[0]
        first = sc[3] if core == 0 else sc[7]
        first = 1 - first if k == 1 else first
        for h in range(2):
            full[parity, first, 288 * h : 288 * h + 288, :] = group[n][h]


def collect(sc, group, full, row, size):
    for n in range(8):
        core, k = divmod(n, 4)
        parity = sc[0] if core == 0 else 1 - sc[0]
        first, second = (sc[3], sc[7]) if core == 0 else (sc[7], sc[3])
        first = 1 - first if k in (1, 3) else first
        second = 1 - second if k in (2, 3) else second
        rows = pl.ds(pl.multiple_of(second * size, 16), size)
        full[parity, first, rows, :] = group[n][0, row : row + size, :]


def ffn_result_body(sc, *refs):
    wg_ref, wu_ref, gain_ref, gate_ref, up_ref, down_ref, gg_ref, full = refs[12:]
    collect_halves(sc, refs[:4], full.at[0])
    collect(sc, refs[4:12], full.at[1], 0, 288)
    for half in range(2):
        for bit in range(2):
            rows = slice(48 * bit, 48 * bit + 48)
            for parity in range(2):
                for base, ref in ((0, gate_ref), (192, up_ref)):
                    for ct in range(2):
                        lo = pl.multiple_of(base + ct * 96 + sc[0] * 48, 16)
                        block = full[half, parity, bit, pl.ds(lo, 48), :].astype(F32)
                        for q in range(2):
                            col = 512 * (2 * ct + q) + 128 * half + 256 * parity
                            ref[rows, col : col + 128] = block[:, 128 * q : 128 * q + 128]
            lo = 128 * half + 64 * bit
            for t in range(3):
                down_ref[lo : lo + 64, 256 * t : 256 * t + 256] = full[
                    half, sc[0], bit, 384 + t * 64 : 448 + t * 64, :
                ].astype(F32)
    gate = jnp.sum(wg_ref[...].astype(F32) * gate_ref[...], axis=-1, keepdims=True)
    up = jnp.sum(wu_ref[...].astype(F32) * up_ref[...], axis=-1, keepdims=True)
    gg_ref[...] = row_of((gate + up) / gain_ref[...])


def ffn_result_call(sc, first, second, wg, wu, gain):
    return call(
        ffn_result_body,
        "ffn_result",
        sc,
        tuple(first) + tuple(second) + (wg, wu, gain),
        [whole((2, 288, 256))] * 4 + [whole((1, 288, 256))] * 8 + [row_block(96, HID)] * 2 + [row_block(96, 1)],
        [sds((96, HID), F32), sds((96, HID), F32), sds((256, WIDTH), F32), sds((1, 128), F32)],
        [whole((96, HID)), whole((96, HID)), whole((256, WIDTH)), whole((1, 128))],
        [pltpu.VMEM((2, 2, 2, 576, 256), BF)],
        14,
        (1e6, 6e6, 0),
    )


def square_result_body(sc, *refs):
    group = refs[:8]
    weights = refs[8:11]
    gain_ref = refs[11]
    outs = refs[12:16]
    gg_ref, full = refs[16:]
    order = ((3, 2), (0, 1))
    for n in range(2):
        collect(sc, group, full.at[n], 96 * n, 96)
        for bit in range(2):
            rows = slice(48 * bit, 48 * bit + 48)
            for parity in range(2):
                cols = slice(GROUP * parity, GROUP * parity + GROUP)
                for t in range(2):
                    lo = pl.multiple_of(t * 96 + sc[0] * 48, 16)
                    block = full[n, parity, bit, pl.ds(lo, 48), :]
                    outs[order[n][t]][rows, cols] = block.astype(F32)
    total = jnp.zeros((96, 1), F32)
    for t in range(3):
        total = total + jnp.sum(weights[t][...].astype(F32) * outs[t][...], axis=-1, keepdims=True)
    gg_ref[...] = row_of(total / gain_ref[...])


def square_result_call(sc, group, wq, wk, wv, gain):
    return call(
        square_result_body,
        "square_result",
        sc,
        tuple(group) + (wq, wk, wv, gain),
        [whole((1, 192, GROUP))] * 8 + [row_block(96, WIDTH)] * 3 + [row_block(96, 1)],
        [sds((96, WIDTH), F32)] * 4 + [sds((1, 128), F32)],
        [whole((96, WIDTH))] * 4 + [whole((1, 128))],
        [pltpu.VMEM((2, 2, 2, 192, GROUP), BF)],
        8,
        (1e6, 4e6, 0),
    )


class Chain:
    def __init__(self, sc):
        self.sc = sc

    def next(self, *deps):
        self.sc = after(self.sc, *deps)
        return self.sc


class Reduction:
    def __init__(self, chain, send, keep, name):
        self.chain = chain
        self.send = send
        self.name = name
        self.stacks = [[[keep, 0]]]
        self.flight = None

    def start(self):
        self.fly(after(self.send, self.chain.sc), "first")

    def fly(self, rows, kind):
        self.flight = exchange(rows, kind)

    def land(self):
        if self.flight is not None:
            for n, stack in enumerate(self.stacks):
                stack.append([self.flight, n])
        self.flight = None

    def add(self, count, picks, tag):
        self.land()
        sums = []
        for stack in self.stacks:
            blocks = ([picks[0]] + picks)[-len(stack) :]
            sums.append([(array, (pick, row)) for (array, row), pick in zip(stack, blocks)])
        arrays = [array for stack in sums for array, _ in stack]
        out = add_pieces(self.chain.next(*arrays), count, sums, self.name + tag)
        self.chain.next(out)
        return out

    def second(self):
        pick = lambda t, j: j * 2 + 1 - t[7]
        self.fly(self.add(4, [pick], "_b"), "second")

    def near(self):
        pick = lambda t, j: (1 - t[4]) * 4 + j * 2 + t[7]
        self.fly(self.add(2, [pick, lambda t, j: (1 - t[4]) * 2 + j], "_c"), "near")

    def far(self):
        pick = lambda t, j: t[4] * 4 + (1 - t[5]) * 2 + t[7]
        picks = [pick, lambda t, j: t[4] * 2 + 1 - t[5], lambda t, j: 1 - t[5]]
        self.fly(self.add(1, picks, "_d"), "far")

    def total(self):
        pick = lambda t, j: t[4] * 4 + t[5] * 2 + t[7]
        picks = [pick, lambda t, j: t[4] * 2 + t[5], lambda t, j: t[5], lambda t, j: 0]
        own = self.add(1, picks, "_e")
        self.quarters = [own] + [exchange(own, kind) for kind in ("first", "second", "across")]

    def result(self):
        return self.quarters + [exchange(quarter, "core") for quarter in self.quarters]


class Straight(Reduction):
    def near(self):
        pick = lambda t, j: (1 - t[4]) * 4 + j
        self.fly(self.add(4, [pick], "_b"), "near")

    def far(self):
        pick = lambda t, j: t[4] * 4 + (1 - t[5]) * 2 + j
        self.fly(self.add(2, [pick, lambda t, j: (1 - t[5]) * 2 + j], "_c"), "far")

    def second(self):
        pick = lambda t, j: t[4] * 4 + t[5] * 2 + j
        own = self.add(2, [pick, lambda t, j: t[5] * 2 + j, lambda t, j: j], "_d")
        self.stacks = [[[own, 0]]]
        self.fly(own, "second")

    def total(self):
        own = self.add(2, [lambda t, j: j], "_e")
        self.quarters = [own, exchange(own, "first")]


def join(first, second):
    both = Reduction(first.chain, None, None, first.name + second.name)
    first.land()
    second.land()
    both.stacks = first.stacks + second.stacks
    return both


def fast_step(
    tokens,
    lengths,
    owner,
    w_query,
    w_key,
    w_value,
    w_out,
    w_gate,
    w_up,
    w_down,
    gain_attn,
    gain_mlp,
    cotangent,
):
    batch, seq, core = (lax.axis_index(name) for name in AXES)
    own_pos = jnp.where(core == 0, owner[0, 0], owner[0, 1])
    low, high = batch % 2, batch // 2
    sc = jnp.stack(
        [
            core,
            own_pos,
            lengths[0],
            jnp.where(core == 0, low, high),
            seq % 2,
            seq // 2,
            seq * 2 + core,
            jnp.where(core == 0, high, low),
        ]
    ).astype(jnp.int32)
    tables = position_tables(SEQ)
    cosine, sine = jnp.asarray(tables[0]), jnp.asarray(tables[1])
    gain_row = gain_attn.reshape(1, WIDTH)
    gain_mlp_row = gain_mlp.reshape(1, WIDTH)
    qkv_w = (w_query, w_key, w_value)
    ffn_w = (w_gate, w_up, w_down)
    chain = Chain(sc)

    qkv_send, n1 = qkv_call(chain.sc, tokens, gain_row, cosine, sine, *qkv_w, True)
    qkv_other = exchange(qkv_send, "core")
    (qkv_own,) = qkv_call(chain.next(n1), tokens, gain_row, cosine, sine, *qkv_w, False)
    n1_other = exchange(n1, "core")
    dy_other = exchange(cotangent, "core")
    attn_t, lse, attn_own, attn_send = attend_call(chain.next(qkv_own), qkv_own, qkv_other)
    attn_other = exchange(attn_send, "core")
    attn_rest = exchange(attn_own, "core")
    middle, n2 = proj_call(
        chain.next(lse, n1_other, dy_other), tokens, attn_own, attn_other, gain_mlp_row, w_out
    )
    n2_other = exchange(n2, "core")
    rows = (n2, n2_other, cotangent, dy_other)
    send0, keep0, *acts0 = ffn_call(chain.next(n2, attn_rest), 0, *rows, *ffn_w)
    g0 = Straight(chain, send0, keep0, "g0")
    g0.start()
    send1, keep1, *acts1 = ffn_call(chain.next(acts0[0]), 1, *rows, *ffn_w)
    g1 = Reduction(chain, send1, keep1, "g1")
    g1.start()
    acc, acc_send, dn, dn_send = ffn_out_call(chain.next(acts1[0]), acts0, acts1, *ffn_w)
    dn_other = exchange(dn_send, "core")
    chain.next(dn_send)
    g0.near()
    d_middle, db = middle_call(chain.next(dn_other), dn, dn_other, middle, cotangent, gain_mlp_row)
    db_other = exchange(db, "core")
    acc_other = exchange(after(acc_send, db_other), "core")
    d_own, d_send = attend_back_call(
        chain.next(db), qkv_own, qkv_other, attn_t, lse, db, db_other, cosine, sine, w_out
    )
    d_other = exchange(d_send, "core")
    chain.next(d_own, g0.flight, g1.flight)
    g1.second()
    g0.far()
    attn = (attn_own, attn_send, attn_other, attn_rest)
    send2, keep2, send3, keep3 = square_call(
        chain.sc, n1, n1_other, *attn, db, db_other, d_own, d_send
    )
    g2 = Reduction(chain, send2, keep2, "g2")
    g3 = Reduction(chain, send3, keep3, "g3")
    g2.start()
    g3.start()
    chain.next(send3)
    layer_out, input_grad = input_grad_call(
        chain.next(acc_other, d_other),
        tokens,
        gain_row,
        d_middle,
        middle,
        acc,
        acc_other,
        d_own,
        d_other,
        *qkv_w,
    )
    chain.next(input_grad)
    g2.second()
    g1.near()
    g3.second()
    g2.near()
    g0.second()
    g3.near()
    g1.far()
    g2.far()
    g3.far()
    g0.total()
    g1.total()
    g23 = join(g2, g3)
    g23.total()
    gate, up, down, gain_m = ffn_result_call(
        chain.sc, g0.result(), g1.result(), w_gate, w_up, gain_mlp.reshape(WIDTH, 1)
    )
    chain.next(gain_m)
    query, key, value, out, gain_a = square_result_call(
        chain.sc, g23.result(), *qkv_w, gain_attn.reshape(WIDTH, 1)
    )
    return (
        layer_out,
        input_grad,
        query,
        key,
        value,
        out,
        gate,
        up,
        down,
        gain_a[0, :96],
        gain_m[0, :96],
    )


def solution(mesh):
    in_specs = (
        P(("batch", "seq"), "seqb", None),
        P(("batch", "seq")),
        P(("batch", "seq"), None),
        P(),
        P(),
        P(),
        P(),
        P(),
        P(),
        P(),
        P(),
        P(),
        P(("batch", "seq"), "seqb", None),
    )
    out_specs = (
        P(("batch", "seq"), "seqb", None),
        P(("batch", "seq"), "seqb", None),
        P(("seq", "seqb"), None),
        P(("seq", "seqb"), None),
        P(("seq", "seqb"), None),
        P(("seq", "seqb"), None),
        P(("seq", "seqb"), None),
        P(("seq", "seqb"), None),
        P(("seq", "seqb"), None),
        P(("seq", "seqb")),
        P(("seq", "seqb")),
    )
    step = fast_step if fast_layout(mesh) else general_step
    return jax.shard_map(step, mesh=mesh, in_specs=in_specs, out_specs=out_specs, check_vma=False)
```

```python
import functools
import math

import jax
import jax.numpy as jnp
import numpy as np
from jax import lax
from jax.experimental import pallas as pl
from jax.experimental.pallas import tpu as pltpu
from jax.sharding import PartitionSpec as P

HEADS = 12
HEAD_DIM = 64


epsilon = 1e-05
rope_base = 10000.0
masked_score = -1e30


def rms_forward(rows, gain):
    factor = lax.rsqrt(jnp.mean(rows * rows, axis=-1, keepdims=True) + epsilon)
    return (rows * factor * gain, factor)


def rms_backward(rows, factor, gain, upstream):
    scaled = upstream * gain
    return factor * scaled - rows * (factor * factor * factor) * jnp.mean(
        rows * scaled, axis=-1, keepdims=True
    )


def rotation_tables(positions):
    half = HEAD_DIM // 2
    freq = rope_base ** (-(2.0 * jnp.arange(half, dtype=jnp.float32)) / HEAD_DIM)
    angles = positions.astype(jnp.float32)[..., None] * freq
    return (jnp.cos(angles), jnp.sin(angles))


def split_heads(rows):
    return rows.reshape(rows.shape[0], rows.shape[1], HEADS, HEAD_DIM)


def rotate(rows, cosine, sine, inverse):
    shaped = split_heads(rows)
    half = HEAD_DIM // 2
    first = shaped[..., :half]
    second = shaped[..., half:]
    cos_part = cosine[:, :, None, :]
    sin_part = sine[:, :, None, :]
    if inverse:
        turned = jnp.concatenate(
            [first * cos_part + second * sin_part, second * cos_part - first * sin_part], axis=-1
        )
    else:
        turned = jnp.concatenate(
            [first * cos_part - second * sin_part, second * cos_part + first * sin_part], axis=-1
        )
    return turned.reshape(rows.shape)


def range_positions(owner, count, span):
    offsets = jnp.arange(span, dtype=jnp.int32)
    return (owner[:, :, None] * span + offsets[None, None, :]).reshape(owner.shape[0], count)


def fold_keys(parts, combine, initial):
    return combine(
        initial,
        (
            lax.all_gather(parts[0], "seqb", axis=1, tiled=True),
            lax.all_gather(parts[1], "seqb", axis=1, tiled=True),
        ),
        jnp.int32(0),
    )


def general_step(
    tokens,
    lengths,
    owner,
    w_query,
    w_key,
    w_value,
    w_out,
    w_gate,
    w_up,
    w_down,
    gain_attn,
    gain_mlp,
    cotangent,
):
    seqs, span, width = tokens.shape
    scale = HEAD_DIM ** (-0.5)
    place = lax.axis_index("seqb")
    own_block = lax.dynamic_slice_in_dim(owner, place, 1, 1)
    local_pos = own_block * span + jnp.arange(span, dtype=jnp.int32)[None, :]
    local_live = local_pos < lengths[:, None]
    live_rows = local_live[:, :, None]
    inputs = jnp.where(live_rows, tokens.astype(jnp.float32), 0.0)
    normed, factor_attn = rms_forward(inputs, gain_attn)
    normed_low = normed.astype(jnp.bfloat16)
    cosine, sine = rotation_tables(local_pos)
    query_pre = jnp.einsum("scd,de->sce", normed_low, w_query, preferred_element_type=jnp.float32)
    key_pre = jnp.einsum("scd,de->sce", normed_low, w_key, preferred_element_type=jnp.float32)
    value_low = jnp.einsum(
        "scd,de->sce", normed_low, w_value, preferred_element_type=jnp.float32
    ).astype(jnp.bfloat16)
    query_rot = rotate(query_pre, cosine, sine, False).astype(jnp.bfloat16)
    key_rot = rotate(key_pre, cosine, sine, False).astype(jnp.bfloat16)
    query_heads = split_heads(query_rot)
    key_heads = split_heads(key_rot)
    value_heads = split_heads(value_low)

    def attend(state, piece, start):
        keys, values = piece
        count = keys.shape[1]
        key_pos = range_positions(owner, count, span)
        key_live = key_pos < lengths[:, None]
        stride = math.gcd(count, 512)

        def attend_one_block(index, inner):
            offset = index * stride
            key_block = split_heads(lax.dynamic_slice_in_dim(keys, offset, stride, 1))
            value_block = split_heads(lax.dynamic_slice_in_dim(values, offset, stride, 1))
            pos_block = lax.dynamic_slice_in_dim(key_pos, offset, stride, 1)
            live_block = lax.dynamic_slice_in_dim(key_live, offset, stride, 1)
            allowed = (
                (pos_block[:, None, :] <= local_pos[:, :, None])
                & live_block[:, None, :]
                & local_live[:, :, None]
            )

            def attend_update(carried):
                peak, total, summed = carried
                scores = (
                    jnp.einsum(
                        "sqhd,skhd->shqk",
                        query_heads,
                        key_block,
                        preferred_element_type=jnp.float32,
                    )
                    * scale
                )
                mask = allowed[:, None, :, :]
                new_peak = jnp.maximum(
                    peak, jnp.max(jnp.where(mask, scores, masked_score), axis=-1)
                )
                weights = jnp.where(mask, jnp.exp(scores - new_peak[..., None]), 0.0)
                factor = jnp.exp(peak - new_peak)
                total = total * factor + jnp.sum(weights, axis=-1)
                term = jnp.einsum(
                    "shqk,skhd->sqhd",
                    weights.astype(jnp.bfloat16),
                    value_block,
                    preferred_element_type=jnp.float32,
                )
                summed = (
                    split_heads(summed) * jnp.transpose(factor, (0, 2, 1))[..., None] + term
                ).reshape(summed.shape)
                return (new_peak, total, summed)

            return lax.cond(jnp.any(allowed), attend_update, lambda carried: carried, inner)

        return lax.fori_loop(0, count // stride, attend_one_block, state)

    start_state = (
        jnp.full((seqs, HEADS, span), masked_score, jnp.float32),
        jnp.zeros((seqs, HEADS, span), jnp.float32),
        jnp.zeros((seqs, span, width), jnp.float32),
    )
    peak, total, summed = fold_keys((key_rot, value_low), attend, start_state)
    safe_total = jnp.where(local_live[:, None, :], total, 1.0)
    attn = split_heads(summed) / jnp.transpose(safe_total, (0, 2, 1))[..., None]
    attn = jnp.where(local_live[:, :, None, None], attn, 0.0).reshape(seqs, span, width)
    log_total = jnp.where(local_live[:, None, :], peak + jnp.log(safe_total), 0.0)
    attn_low = attn.astype(jnp.bfloat16)
    middle = inputs + jnp.einsum("scd,de->sce", attn_low, w_out, preferred_element_type=jnp.float32)
    normed_mlp, factor_mlp = rms_forward(middle, gain_mlp)
    normed_mlp_low = normed_mlp.astype(jnp.bfloat16)
    gate = jnp.einsum("scd,df->scf", normed_mlp_low, w_gate, preferred_element_type=jnp.float32)
    up_proj = jnp.einsum("scd,df->scf", normed_mlp_low, w_up, preferred_element_type=jnp.float32)
    hidden = (jax.nn.silu(gate) * up_proj).astype(jnp.bfloat16)
    out = middle + jnp.einsum("scf,fd->scd", hidden, w_down, preferred_element_type=jnp.float32)
    layer_out = jnp.where(live_rows, out, 0.0).astype(jnp.bfloat16)
    upstream = jnp.where(live_rows, cotangent, jnp.zeros_like(cotangent))
    grad_down = jnp.einsum("scf,scd->fd", hidden, upstream, preferred_element_type=jnp.float32)
    d_hidden = jnp.einsum("scd,fd->scf", upstream, w_down, preferred_element_type=jnp.float32)
    sigmoid_gate = jax.nn.sigmoid(gate)
    d_gate = (d_hidden * up_proj * sigmoid_gate * (1.0 + gate * (1.0 - sigmoid_gate))).astype(
        jnp.bfloat16
    )
    d_up = (d_hidden * gate * sigmoid_gate).astype(jnp.bfloat16)
    grad_gate = jnp.einsum(
        "scd,scf->df", normed_mlp_low, d_gate, preferred_element_type=jnp.float32
    )
    grad_up = jnp.einsum("scd,scf->df", normed_mlp_low, d_up, preferred_element_type=jnp.float32)
    d_normed_mlp = jnp.einsum(
        "scf,df->scd", d_gate, w_gate, preferred_element_type=jnp.float32
    ) + jnp.einsum("scf,df->scd", d_up, w_up, preferred_element_type=jnp.float32)
    grad_gain_mlp = jnp.sum(d_normed_mlp * (middle * factor_mlp), axis=(0, 1))
    d_middle = upstream.astype(jnp.float32) + rms_backward(
        middle, factor_mlp, gain_mlp, d_normed_mlp
    )
    d_branch = d_middle.astype(jnp.bfloat16)
    grad_out = jnp.einsum("scd,sce->de", attn_low, d_branch, preferred_element_type=jnp.float32)
    d_attn = jnp.einsum("sce,de->scd", d_branch, w_out, preferred_element_type=jnp.float32).astype(
        jnp.bfloat16
    )
    first_done = (grad_out, grad_gate, grad_up, grad_down, grad_gain_mlp)
    delta = jnp.sum(split_heads(d_attn.astype(jnp.float32) * attn), axis=-1)
    delta_heads = jnp.transpose(delta, (0, 2, 1))
    grad_heads = split_heads(d_attn)

    def query_grads(state, piece, start):
        keys, values = piece
        count = keys.shape[1]
        key_pos = range_positions(owner, count, span)
        key_live = key_pos < lengths[:, None]
        stride = math.gcd(count, 512)

        def query_one_block(index, inner):
            offset = index * stride
            key_block = split_heads(lax.dynamic_slice_in_dim(keys, offset, stride, 1))
            value_block = split_heads(lax.dynamic_slice_in_dim(values, offset, stride, 1))
            pos_block = lax.dynamic_slice_in_dim(key_pos, offset, stride, 1)
            live_block = lax.dynamic_slice_in_dim(key_live, offset, stride, 1)
            allowed = (
                (pos_block[:, None, :] <= local_pos[:, :, None])
                & live_block[:, None, :]
                & local_live[:, :, None]
            )

            def query_update(carried):
                scores = (
                    jnp.einsum(
                        "sqhd,skhd->shqk",
                        query_heads,
                        key_block,
                        preferred_element_type=jnp.float32,
                    )
                    * scale
                )
                probs = jnp.where(
                    allowed[:, None, :, :], jnp.exp(scores - log_total[..., None]), 0.0
                )
                d_probs = jnp.einsum(
                    "sqhd,skhd->shqk", grad_heads, value_block, preferred_element_type=jnp.float32
                )
                d_scores = (probs * (d_probs - delta_heads[..., None])).astype(jnp.bfloat16)
                term = (
                    jnp.einsum(
                        "shqk,skhd->sqhd", d_scores, key_block, preferred_element_type=jnp.float32
                    )
                    * scale
                )
                return carried + term.reshape(carried.shape)

            return lax.cond(jnp.any(allowed), query_update, lambda carried: carried, inner)

        return lax.fori_loop(0, count // stride, query_one_block, state)

    zero_query = jnp.zeros((seqs, span, width), jnp.float32)
    d_query = fold_keys((key_rot, value_low), query_grads, zero_query)
    lse_all, delta_all = (
        lax.all_gather(jnp.transpose(log_total, (0, 2, 1)), "seqb", axis=1, tiled=True),
        lax.all_gather(delta, "seqb", axis=1, tiled=True),
    )
    zero_rows = jnp.zeros((seqs, span, width), jnp.float32)
    queries = lax.all_gather(query_rot, "seqb", axis=1, tiled=True)
    d_rows = lax.all_gather(d_attn, "seqb", axis=1, tiled=True)
    count = queries.shape[1]
    row_pos = range_positions(owner, count, span)
    row_live = row_pos < lengths[:, None]
    stride = math.gcd(count, 512)

    def key_one_block(index, inner):
        offset = index * stride
        query_block = split_heads(lax.dynamic_slice_in_dim(queries, offset, stride, 1))
        grad_block = split_heads(lax.dynamic_slice_in_dim(d_rows, offset, stride, 1))
        pos_block = lax.dynamic_slice_in_dim(row_pos, offset, stride, 1)
        live_block = lax.dynamic_slice_in_dim(row_live, offset, stride, 1)
        lse_block = jnp.transpose(lax.dynamic_slice_in_dim(lse_all, offset, stride, 1), (0, 2, 1))
        delta_block = jnp.transpose(
            lax.dynamic_slice_in_dim(delta_all, offset, stride, 1), (0, 2, 1)
        )
        allowed = (
            (local_pos[:, None, :] <= pos_block[:, :, None])
            & local_live[:, None, :]
            & live_block[:, :, None]
        )

        def key_update(carried):
            d_key, d_value = carried
            scores = (
                jnp.einsum(
                    "sqhd,skhd->shqk", query_block, key_heads, preferred_element_type=jnp.float32
                )
                * scale
            )
            probs = jnp.where(allowed[:, None, :, :], jnp.exp(scores - lse_block[..., None]), 0.0)
            value_term = jnp.einsum(
                "shqk,sqhd->skhd",
                probs.astype(jnp.bfloat16),
                grad_block,
                preferred_element_type=jnp.float32,
            )
            d_probs = jnp.einsum(
                "sqhd,skhd->shqk", grad_block, value_heads, preferred_element_type=jnp.float32
            )
            d_scores = (probs * (d_probs - delta_block[..., None])).astype(jnp.bfloat16)
            key_term = (
                jnp.einsum(
                    "shqk,sqhd->skhd", d_scores, query_block, preferred_element_type=jnp.float32
                )
                * scale
            )
            return (
                d_key + key_term.reshape(d_key.shape),
                d_value + value_term.reshape(d_value.shape),
            )

        return lax.cond(jnp.any(allowed), key_update, lambda carried: carried, inner)

    d_key, d_value = lax.fori_loop(0, count // stride, key_one_block, (zero_rows, zero_rows))
    d_query_pre = rotate(d_query, cosine, sine, True).astype(jnp.bfloat16)
    d_key_pre = rotate(d_key, cosine, sine, True).astype(jnp.bfloat16)
    d_value_low = d_value.astype(jnp.bfloat16)
    grad_query = jnp.einsum(
        "scd,sce->de", normed_low, d_query_pre, preferred_element_type=jnp.float32
    )
    grad_key = jnp.einsum("scd,sce->de", normed_low, d_key_pre, preferred_element_type=jnp.float32)
    grad_value = jnp.einsum(
        "scd,sce->de", normed_low, d_value_low, preferred_element_type=jnp.float32
    )
    d_normed = jnp.einsum("sce,de->scd", d_query_pre, w_query, preferred_element_type=jnp.float32)
    d_normed = d_normed + jnp.einsum(
        "sce,de->scd", d_key_pre, w_key, preferred_element_type=jnp.float32
    )
    d_normed = d_normed + jnp.einsum(
        "sce,de->scd", d_value_low, w_value, preferred_element_type=jnp.float32
    )
    grad_gain_attn = jnp.sum(d_normed * (inputs * factor_attn), axis=(0, 1))
    d_inputs = d_middle + rms_backward(inputs, factor_attn, gain_attn, d_normed)
    input_grad = jnp.where(live_rows, d_inputs, 0.0).astype(jnp.bfloat16)
    summed_parts = (
        lax.psum_scatter(grad_query, ("seq", "seqb"), scatter_dimension=0, tiled=True),
        lax.psum_scatter(grad_key, ("seq", "seqb"), scatter_dimension=0, tiled=True),
        lax.psum_scatter(grad_value, ("seq", "seqb"), scatter_dimension=0, tiled=True),
        lax.psum_scatter(grad_gain_attn, ("seq", "seqb"), scatter_dimension=0, tiled=True),
        lax.psum_scatter(first_done[0], ("seq", "seqb"), scatter_dimension=0, tiled=True),
        lax.psum_scatter(first_done[1], ("seq", "seqb"), scatter_dimension=0, tiled=True),
        lax.psum_scatter(first_done[2], ("seq", "seqb"), scatter_dimension=0, tiled=True),
        lax.psum_scatter(first_done[3], ("seq", "seqb"), scatter_dimension=0, tiled=True),
        lax.psum_scatter(first_done[4], ("seq", "seqb"), scatter_dimension=0, tiled=True),
    )
    all_done = (
        lax.psum(summed_parts[0].astype(jnp.bfloat16), "batch").astype(jnp.float32),
        lax.psum(summed_parts[1].astype(jnp.bfloat16), "batch").astype(jnp.float32),
        lax.psum(summed_parts[2].astype(jnp.bfloat16), "batch").astype(jnp.float32),
        lax.psum(summed_parts[3].astype(jnp.bfloat16), "batch").astype(jnp.float32),
        lax.psum(summed_parts[4].astype(jnp.bfloat16), "batch").astype(jnp.float32),
        lax.psum(summed_parts[5].astype(jnp.bfloat16), "batch").astype(jnp.float32),
        lax.psum(summed_parts[6].astype(jnp.bfloat16), "batch").astype(jnp.float32),
        lax.psum(summed_parts[7].astype(jnp.bfloat16), "batch").astype(jnp.float32),
        lax.psum(summed_parts[8].astype(jnp.bfloat16), "batch").astype(jnp.float32),
    )
    second_done = (all_done[0], all_done[1], all_done[2], all_done[3])
    first_done = (all_done[4], all_done[5], all_done[6], all_done[7], all_done[8])
    return (
        layer_out,
        input_grad,
        second_done[0],
        second_done[1],
        second_done[2],
        first_done[0],
        first_done[1],
        first_done[2],
        first_done[3],
        second_done[3],
        first_done[4],
    )


AXES = ("batch", "seq", "seqb")
BF = jnp.bfloat16
F32 = jnp.float32
MIB = 1 << 20
COST = 1e6
ADD_COST = 2e9
KERNEL_US = {
    "qkv_other": 4,
    "qkv_own": 4,
    "attend": 9,
    "proj": 3,
    "ffn_first": 8,
    "ffn_second": 8,
    "ffn_out": 9,
    "middle": 1.4,
    "attend_back": 14,
    "square": 5,
    "input_grad": 6.5,
    "ffn_result": 2,
    "square_result": 2,
}


def fast_layout(mesh):
    return mesh.shape["batch"] == 4 and mesh.shape["seq"] == 4 and mesh.shape["seqb"] == 2


def exchange(rows, kind):
    pairs = []
    for b in range(4):
        for s in range(4):
            for c in range(2):
                first = 1 if c == 0 else 2
                target = {
                    "core": (b, s, 1 - c),
                    "first": (b ^ first, s, c),
                    "second": (b ^ (3 - first), s, c),
                    "near": (b, s ^ 1, c),
                    "far": (b, s ^ 2, c),
                    "across": (b ^ 3, s, c),
                }[kind]
                pairs.append((b * 8 + s * 2 + c, target[0] * 8 + target[1] * 2 + target[2]))
    return lax.ppermute(rows, AXES, pairs)


def dot(a, b):
    return lax.dot_general(a, b, (((1,), (0,)), ((), ())), preferred_element_type=F32)


def dot_nt(a, b):
    return lax.dot_general(a, b, (((1,), (1,)), ((), ())), preferred_element_type=F32)


def position_tables(count):
    half = HEAD_DIM // 2
    freq = rope_base ** (-(2.0 * np.arange(half)) / HEAD_DIM)
    angles = np.arange(count)[:, None] * freq[None, :]
    cosine, sine = np.cos(angles), np.sin(angles)
    return (
        np.concatenate([cosine, cosine, cosine, cosine], 1).astype(np.float32),
        np.concatenate([-sine, sine, -sine, sine], 1).astype(np.float32),
    )


def swap_halves(u):
    lane = lax.broadcasted_iota(jnp.int32, u.shape, 1) % HEAD_DIM
    return jnp.where(lane < HEAD_DIM // 2, pltpu.roll(u, 96, 1), pltpu.roll(u, 32, 1))


def turn(rows, cosine, sine):
    parts = []
    for g in range(rows.shape[1] // 128):
        u = rows[:, g * 128 : (g + 1) * 128]
        parts.append(u * cosine + swap_halves(u) * sine)
    return parts[0] if len(parts) == 1 else jnp.concatenate(parts, axis=1)


def live_mask(sc, row0, count):
    span_pos = sc[1] * SPAN + row0 + lax.broadcasted_iota(jnp.int32, (count, 1), 0)
    return span_pos < sc[2]


SPAN = 512
SEQ = 1024
WIDTH = 768
GROUP = 384
HID = 2048


def hbm():
    return pl.BlockSpec(memory_space=pl.ANY)


def far_hbm():
    return pl.BlockSpec(memory_space=pltpu.HBM)


def after(sc, *deps):
    return lax.optimization_barrier((sc,) + deps)[0]


def dot_tn(a, b):
    return lax.dot_general(a, b, (((0,), (0,)), ((), ())), preferred_element_type=F32)


def whole(shape):
    return pl.BlockSpec(shape, lambda i, sc: (0,) * len(shape))


def call(body, name, sc, args, in_specs, out_shapes, out_specs, scratch, vmem, cost):
    flops, moved, trans = cost
    args = [
        pltpu.with_memory_space_constraint(a, pltpu.HBM) if spec.memory_space is pltpu.HBM else a
        for a, spec in zip(args, in_specs)
    ]
    return pl.pallas_call(
        body,
        name=name,
        out_shape=out_shapes,
        grid_spec=pltpu.PrefetchScalarGridSpec(
            num_scalar_prefetch=1,
            grid=(1,),
            in_specs=in_specs,
            out_specs=out_specs,
            scratch_shapes=scratch,
        ),
        compiler_params=pltpu.CompilerParams(vmem_limit_bytes=vmem * MIB),
        cost_estimate=pl.CostEstimate(
            flops=int(COST * KERNEL_US[name]), bytes_accessed=1000, transcendentals=0
        ),
    )(sc, *args)


def sds(shape, dtype=BF):
    return jax.ShapeDtypeStruct(shape, dtype)


def qkv_body(sc, *refs, flip):
    if flip:
        x_hbm, cos_hbm, sin_hbm, gain_ref, wq, wk, wv, o_ref, n_ref, xs, cs, ss, ws, sem = refs
    else:
        n_ref, cos_hbm, sin_hbm, wq, wk, wv, o_ref, cs, ss, ws, sem = refs
    col = (1 - sc[0]) if flip else sc[0]
    col = pl.multiple_of(col * GROUP, 128)
    row = pl.multiple_of(sc[1] * SPAN, SPAN)
    copies = [
        pltpu.make_async_copy(w.at[:, pl.ds(col, GROUP)], ws.at[t], sem.at[t])
        for t, w in enumerate((wq, wk, wv))
    ]
    tables = [
        pltpu.make_async_copy(cos_hbm.at[pl.ds(row, SPAN), :], cs, sem.at[4]),
        pltpu.make_async_copy(sin_hbm.at[pl.ds(row, SPAN), :], ss, sem.at[5]),
    ]
    if flip:
        x_copy = pltpu.make_async_copy(x_hbm.at[0], xs, sem.at[3])
        x_copy.start()
    for cp in [copies[2]] + copies[:2] + tables:
        cp.start()
    if flip:
        x_copy.wait()
        for r in range(0, SPAN, 256):
            x = jnp.where(live_mask(sc, r, 256), xs[r : r + 256, :].astype(F32), 0.0)
            factor = lax.rsqrt(jnp.mean(x * x, axis=-1, keepdims=True) + epsilon)
            n_ref[r : r + 256, :] = (x * factor * gain_ref[...]).astype(BF)
    for t in (2, 0, 1):
        copies[t].wait()
        if t == 0:
            for cp in tables:
                cp.wait()
        for r in range(0, SPAN, 256):
            y = dot(n_ref[r : r + 256, :], ws[t])
            if t < 2:
                y = turn(y, cs[r : r + 256, :], ss[r : r + 256, :])
            if t == 0:
                y = y * (HEAD_DIM**-0.5)
            o_ref[t, r : r + 256, :] = y.astype(BF)


def qkv_call(sc, rows, gain, cosine, sine, wq, wk, wv, flip):
    out_shapes = [sds((3, SPAN, GROUP))]
    out_specs = [whole((3, SPAN, GROUP))]
    scratch = [
        pltpu.VMEM((SPAN, 128), F32),
        pltpu.VMEM((SPAN, 128), F32),
        pltpu.VMEM((3, WIDTH, GROUP), BF),
        pltpu.SemaphoreType.DMA((6,)),
    ]
    if flip:
        out_shapes.append(sds((SPAN, WIDTH)))
        out_specs.append(whole((SPAN, WIDTH)))
        args = (rows, cosine, sine, gain, wq, wk, wv)
        specs = [far_hbm()] * 3 + [whole((1, WIDTH))] + [far_hbm()] * 3
        scratch = [pltpu.VMEM((SPAN, WIDTH), BF)] + scratch
    else:
        args = (rows, cosine, sine, wq, wk, wv)
        specs = [whole((SPAN, WIDTH))] + [far_hbm()] * 5
    return call(
        functools.partial(qkv_body, flip=flip),
        "qkv_other" if flip else "qkv_own",
        sc,
        args,
        specs,
        out_shapes,
        out_specs,
        scratch,
        9,
        (3 * 2 * SPAN * WIDTH * GROUP, 5e6, 1e3),
    )


def gather_rows(sc, own, other, places, sem):
    copies = []
    for t, place in enumerate(places):
        for k, src in enumerate((own, other)):
            pos = sc[1] if k == 0 else 1 - sc[1]
            row = pl.multiple_of(pos * SPAN, SPAN)
            source = src.at[t] if len(src.shape) == 3 else src
            copies.append(
                pltpu.make_async_copy(source, place.at[pl.ds(row, SPAN), :], sem.at[2 * t + k])
            )
    for cp in copies:
        cp.start()
    return copies


def attend_body(sc, own, other, wo, wg, wu, wd, *refs):
    (ot_ref, lse_ref, mine, theirs, wo_v, wg_v, wu_v, wd_v, qs, ks, vs, at, sem, wsem) = refs
    copies = gather_rows(sc, own, other, (qs, ks, vs), sem)
    fetch = []

    def bring(src, place):
        fetch.append(pltpu.make_async_copy(src, place, wsem.at[len(fetch)]))
        fetch[-1].start()

    for k in range(2):
        head = (sc[0] if k == 0 else 1 - sc[0]) * GROUP
        rows = pl.ds(pl.multiple_of(head, 128), GROUP)
        bring(wo.at[rows, :], wo_v.at[GROUP * k : GROUP * k + GROUP, :])
    for half in range(2):
        for s in range(4):
            cols = hidden_cols(sc, s, half)
            to = slice(512 * half + 128 * s, 512 * half + 128 * s + 128)
            bring(wg.at[:, cols], wg_v.at[:, to])
            bring(wu.at[:, cols], wu_v.at[:, to])
            bring(wd.at[cols, :], wd_v.at[to, :])
    for cp in copies:
        cp.wait()
    lane = lax.broadcasted_iota(jnp.int32, (256, 128), 1)
    key_id = lax.broadcasted_iota(jnp.int32, (256, 256), 0)
    row_id = lax.broadcasted_iota(jnp.int32, (256, 256), 1)
    keep = key_id <= row_id

    def pair(hp, carry):
        base = pl.multiple_of(hp * 128, 128)
        cols = pl.ds(base, 128)
        vt = jnp.transpose(vs[:, cols].astype(F32)).astype(BF)

        def scores(i, h):
            n = 256 * (i + 1)
            qm = jnp.where(lane // HEAD_DIM == h, qs[256 * i : n, cols], jnp.zeros((), BF))
            return dot_nt(ks[0:n, cols], qm)

        def soften(i, h, st):
            n = 256 * (i + 1)
            diag = jnp.where(keep, st[n - 256 :, :], masked_score)
            st = diag if i == 0 else jnp.concatenate([st[: n - 256, :], diag], axis=0)
            peak = jnp.max(st, axis=0, keepdims=True)
            p = jnp.exp(st - peak)
            return p.astype(BF), peak, jnp.sum(p, axis=0, keepdims=True)

        def finish(i, h, p, peak, total):
            n = 256 * (i + 1)
            o = dot(vt[h * 64 : h * 64 + 64, :n], p) * (1.0 / total)
            ot_ref[pl.ds(pl.multiple_of(hp * 128 + h * 64, 64), 64), 256 * i : n] = o
            lse_ref[pl.ds(hp * 2 + h, 1), 256 * i : n] = peak + jnp.log(total)

        tasks = [(i, h) for i in range(4) for h in range(2)]
        st, waiting = scores(*tasks[0]), None
        for k, task in enumerate(tasks):
            ahead = scores(*tasks[k + 1]) if k + 1 < len(tasks) else None
            parts = soften(*task, st)
            if waiting is not None:
                finish(*waiting)
            waiting, st = task + parts, ahead
        finish(*waiting)
        at[:, cols] = jnp.transpose(ot_ref[cols, :]).astype(BF)
        return carry

    lax.fori_loop(0, 3, pair, 0)
    row = pl.multiple_of(sc[1] * SPAN, SPAN)
    row_other = pl.multiple_of((1 - sc[1]) * SPAN, SPAN)
    out_other = pltpu.make_async_copy(at.at[pl.ds(row_other, SPAN), :], theirs, sem.at[0])
    out_own = pltpu.make_async_copy(at.at[pl.ds(row, SPAN), :], mine, sem.at[1])
    out_other.start()
    out_own.start()
    out_other.wait()
    out_own.wait()
    for cp in fetch:
        cp.wait()


def attend_call(sc, own, other, wo, wg, wu, wd):
    return call(
        attend_body,
        "attend",
        sc,
        (own, other, wo, wg, wu, wd),
        [hbm(), hbm()] + [far_hbm()] * 4,
        [sds((GROUP, SEQ), F32), sds((8, SEQ), F32), sds((SPAN, GROUP)), sds((SPAN, GROUP))]
        + [sds((WIDTH, WIDTH)), sds((WIDTH, SEQ)), sds((WIDTH, SEQ)), sds((SEQ, WIDTH))],
        [whole((GROUP, SEQ)), whole((8, SEQ))] + [hbm()] * 6,
        [pltpu.VMEM((SEQ, GROUP), BF)] * 4
        + [pltpu.SemaphoreType.DMA((6,)), pltpu.SemaphoreType.DMA((26,))],
        12,
        (6 * 4 * SEQ * SEQ * 64, 6e6, 4e6),
    )


def proj_body(sc, x_ref, ak_ref, ar_ref, gain_ref, wo_ref, m_ref, n_ref):
    for r in range(0, SPAN, 256):
        rr = slice(r, r + 256)
        m = jnp.where(live_mask(sc, r, 256), x_ref[0, rr, :].astype(F32), 0.0)
        m = m + dot(ak_ref[rr, :], wo_ref[:GROUP, :]) + dot(ar_ref[rr, :], wo_ref[GROUP:, :])
        m_ref[rr, :] = m
        factor = lax.rsqrt(jnp.mean(m * m, axis=-1, keepdims=True) + epsilon)
        n_ref[rr, :] = (m * factor * gain_ref[...]).astype(BF)


def proj_call(sc, tokens, own, other, gain, wo):
    return call(
        proj_body,
        "proj",
        sc,
        (tokens, own, other, gain, wo),
        [whole((1, SPAN, WIDTH))]
        + [whole((SPAN, GROUP))] * 2
        + [whole((1, WIDTH)), whole((WIDTH, WIDTH))],
        [sds((SPAN, WIDTH), F32), sds((SPAN, WIDTH))],
        [whole((SPAN, WIDTH))] * 2,
        [],
        8,
        (2 * SPAN * WIDTH * WIDTH, 5e6, 1e3),
    )


def over_rows(own, other, d_own, d_other):
    return dot_tn(own, d_own) + dot_tn(other, d_other)


def place_of(s):
    return (s % 2) * 2 + s // 2


def hidden_cols(sc, s, half):
    return pl.ds(pl.multiple_of(512 * s + 128 * half + 256 * sc[0], 128), 128)


def spread(sc, res_s, first, count, rows, send_ref, keep_ref, to):
    size = send_ref.shape[1]
    for k, ref in enumerate((send_ref, keep_ref)):
        bit = (1 - sc[3]) if k == 0 else sc[3]
        for s in range(4):
            for q in range(count):
                lo = pl.multiple_of(first + (s * count + q) * 2 * rows + bit * rows, 16)
                block, row = divmod(to + q * rows, size)
                ref[2 * place_of(s) + block, row : row + rows, :] = res_s[pl.ds(lo, rows), :].astype(
                    BF
                )


def ffn_body(sc, n_own, n_oth, dy_own, dy_oth, wg_s, wu_s, wd_s, *refs):
    (send_ref, keep_ref, h_ref, dg_ref, du_ref, dy_s, res_a, res_b) = refs
    for r in range(0, SEQ, 256):
        pos = sc[1] if r < SPAN else 1 - sc[1]
        at = pos * SPAN + r % SPAN + lax.broadcasted_iota(jnp.int32, (256, 1), 0)
        src = dy_own if r < SPAN else dy_oth
        lo = r % SPAN
        dy_s[r : r + 256, :] = jnp.where(at < sc[2], src[0, lo : lo + 256, :], jnp.zeros((), BF))

    def products(r):
        src = n_own if r < SPAN else n_oth
        rows = src[r % SPAN : r % SPAN + 256, :]
        return dot(rows, wg_s[...]), dot(rows, wu_s[...]), dot_nt(dy_s[r : r + 256, :], wd_s[...])

    ahead = products(0)
    for r in range(0, SEQ, 256):
        g, u, dh = ahead
        if r + 256 < SEQ:
            ahead = products(r + 256)
        rr = slice(r, r + 256)
        sg = jax.nn.sigmoid(g)
        gs = g * sg
        h_ref[rr, :] = (gs * u).astype(BF)
        du_ref[rr, :] = (dh * gs).astype(BF)
        dg_ref[rr, :] = (dh * u * (sg + gs * (1.0 - sg))).astype(BF)
    lower, upper = slice(0, SPAN), slice(SPAN, SEQ)
    for k, (base, src) in enumerate(((0, dg_ref), (192, du_ref))):
        for ct in range(2):
            cols = slice(256 * ct, 256 * ct + 256)
            place = res_a.at[ct]
            place[...] = over_rows(n_own[...], n_oth[...], src[lower, cols], src[upper, cols])
            spread(sc, place, 0, 2, 48, send_ref, keep_ref, base + 96 * ct)
    for n in range(3):
        place = res_b.at[n % 2]
        place[...] = dot_tn(h_ref[...], dy_s[:, 256 * n : 256 * n + 256])
        spread(sc, place, 0, 1, 64, send_ref, keep_ref, 384 + 64 * n)


def ffn_call(sc, half, n_own, n_oth, dy_own, dy_oth, wg, wu, wd):
    flat, full = whole((SPAN, WIDTH)), whole((1, SPAN, WIDTH))
    wide = pl.BlockSpec((WIDTH, 512), lambda i, sc: (0, half))
    return call(
        ffn_body,
        "ffn_first" if half == 0 else "ffn_second",
        sc,
        (n_own, n_oth, dy_own, dy_oth, wg, wu, wd),
        [flat, flat, full, full, wide, wide, pl.BlockSpec((512, WIDTH), lambda i, sc: (half, 0))],
        [sds((8, 288, 256))] * 2 + [sds((SEQ, 512))] * 3,
        [whole((8, 288, 256))] * 2 + [whole((SEQ, 512))] * 3,
        [
            pltpu.VMEM((SEQ, WIDTH), BF),
            pltpu.VMEM((2, WIDTH, 256), F32),
            pltpu.VMEM((2, 512, 256), F32),
        ],
        26,
        (6 * 2 * SEQ * WIDTH * 512, 14e6, 1e6),
    )


def ffn_out_body(sc, h0, dg0, du0, h1, dg1, du1, wg, wu, wd, acc_ref, accs_ref, dn_ref, dns_ref):
    for r in (512, 768, 0, 256):
        rr = slice(r, r + 256)
        dn = dot_nt(dg0[rr, :], wg[:, :512]) + dot_nt(dg1[rr, :], wg[:, 512:])
        dn = dn + dot_nt(du0[rr, :], wu[:, :512]) + dot_nt(du1[rr, :], wu[:, 512:])
        acc = dot(h0[rr, :], wd[:512, :]) + dot(h1[rr, :], wd[512:, :])
        if r < SPAN:
            dn_ref[rr, :] = dn
            acc_ref[rr, :] = acc
        else:
            dns_ref[r - SPAN : r - SPAN + 256, :] = dn.astype(BF)
            accs_ref[r - SPAN : r - SPAN + 256, :] = acc.astype(BF)


def ffn_out_call(sc, first, second, wg, wu, wd):
    flat = [whole((SPAN, WIDTH))]
    return call(
        ffn_out_body,
        "ffn_out",
        sc,
        tuple(first) + tuple(second) + (wg, wu, wd),
        [whole((SEQ, 512))] * 6 + [whole((WIDTH, SEQ))] * 2 + [whole((SEQ, WIDTH))],
        [sds((SPAN, WIDTH), F32), sds((SPAN, WIDTH)), sds((SPAN, WIDTH), F32), sds((SPAN, WIDTH))],
        flat * 4,
        [],
        24,
        (3 * 2 * SEQ * WIDTH * SEQ, 16e6, 0),
    )


def middle_body(sc, dn_ref, got_ref, m_ref, dy_ref, gain_ref, dm_ref, db_ref):
    gain = gain_ref[...]
    for r in range(0, SPAN, 128):
        rr = slice(r, r + 128)
        live = live_mask(sc, r, 128)
        m = m_ref[rr, :]
        factor = lax.rsqrt(jnp.mean(m * m, axis=-1, keepdims=True) + epsilon)
        scaled = (dn_ref[rr, :] + got_ref[rr, :].astype(F32)) * gain
        dm = jnp.where(live, dy_ref[0, rr, :].astype(F32), 0.0) + (
            factor * scaled
            - m * (factor * factor * factor) * jnp.mean(m * scaled, axis=-1, keepdims=True)
        )
        dm_ref[rr, :] = dm
        db_ref[rr, :] = dm.astype(BF)


def middle_call(sc, dn, got, m, dy, gain):
    flat = whole((SPAN, WIDTH))
    return call(
        middle_body,
        "middle",
        sc,
        (dn, got, m, dy, gain),
        [flat, flat, flat, whole((1, SPAN, WIDTH)), whole((1, WIDTH))],
        [sds((SPAN, WIDTH), F32), sds((SPAN, WIDTH))],
        [flat, flat],
        [],
        14,
        (1e6, 8e6, 1e3),
    )


def attend_back_body(sc, own, other, ot_s, lse_s, dbk, dbr, wo_s, cos_hbm, sin_hbm, *refs):
    wq, wk, wv, mine, theirs, ws, qs, ks, vs, das, ds_all, dqt, dkv, cs, ss, sem = refs
    loads = gather_rows(sc, own, other, (qs, ks, vs), sem.at[pl.ds(0, 6)])
    small = [
        pltpu.make_async_copy(src, to, sem.at[6 + n])
        for n, (src, to) in enumerate(((cos_hbm, cs), (sin_hbm, ss)))
    ]
    fetch = [
        pltpu.make_async_copy(w, ws.at[t], sem.at[10 + t]) for t, w in enumerate((wq, wk, wv))
    ]
    for cp in small + fetch:
        cp.start()
    for k, src in enumerate((dbk, dbr)):
        pos = sc[1] if k == 0 else 1 - sc[1]
        for r in range(0, SPAN, 256):
            rows = pl.ds(pl.multiple_of(pos * SPAN + r, 256), 256)
            das[rows, :] = dot_nt(src[r : r + 256, :], wo_s[...]).astype(BF)
    for cp in loads:
        cp.wait()
    for cp in small:
        cp.wait()
    lane = lax.broadcasted_iota(jnp.int32, (SEQ, 128), 1)
    key_id = lax.broadcasted_iota(jnp.int32, (256, 256), 0)
    row_id = lax.broadcasted_iota(jnp.int32, (256, 256), 1)
    keep = key_id <= row_id

    def pair(hp, carry):
        base = pl.multiple_of(hp * 128, 128)
        cols = pl.ds(base, 128)
        kt = jnp.transpose(ks[:, cols].astype(F32)).astype(BF)
        dat = jnp.transpose(das[:, cols].astype(F32))
        qm, dam, delta, lses = [], [], [], []
        for h in range(2):
            qm.append(jnp.where(lane // HEAD_DIM == h, qs[:, cols], jnp.zeros((), BF)))
            dam.append(jnp.where(lane // HEAD_DIM == h, das[:, cols], jnp.zeros((), BF)))
            rows = pl.ds(pl.multiple_of(base + 64 * h, 64), 64)
            product = dat[64 * h : 64 * h + 64, :] * ot_s[rows, :]
            delta.append(jnp.sum(product, axis=0, keepdims=True))
            lses.append(lse_s[pl.ds(2 * hp + h, 1), :])

        def scores(i, h):
            n = 256 * (i + 1)
            rows = slice(256 * i, n)
            return dot_nt(ks[:n, cols], qm[h][rows, :]), dot_nt(vs[:n, cols], dam[h][rows, :])

        def soften(i, h, st, dp):
            n = 256 * (i + 1)
            rows = slice(256 * i, n)
            p = jnp.exp(st - lses[h][:, rows])
            diag = jnp.where(keep, p[n - 256 :, :], 0.0)
            p = diag if i == 0 else jnp.concatenate([p[: n - 256, :], diag], axis=0)
            return p.astype(BF), (p * (dp - delta[h][:, rows])).astype(BF)

        def finish(i, h, p, ds):
            n = 256 * (i + 1)
            rows = slice(256 * i, n)
            half = slice(64 * h, 64 * h + 64)
            dv = dot(p, dam[h][rows, :])
            dk = dot(ds, qm[h][rows, :])
            dqt[half, rows] = dot(kt[half, :n], ds)
            if (i, h) == (3, 0):
                dkv[0] = dk
                dkv[1] = dv
            else:
                dkv[0, :n] += dk
                dkv[1, :n] += dv

        tasks = [(i, h) for i in (3, 2, 1, 0) for h in range(2)]
        now, waiting = scores(*tasks[0]), None
        for k, task in enumerate(tasks):
            ahead = scores(*tasks[k + 1]) if k + 1 < len(tasks) else None
            parts = soften(*task, *now)
            if waiting is not None:
                finish(*waiting)
            waiting, now = task + parts, ahead
        finish(*waiting)
        dq = jnp.transpose(dqt[...]) * (HEAD_DIM**-0.5)
        ds_all[0, :, cols] = turn(dq, cs[...], -ss[...]).astype(BF)
        ds_all[1, :, cols] = turn(dkv[0], cs[...], -ss[...]).astype(BF)
        ds_all[2, :, cols] = dkv[1].astype(BF)
        return carry

    lax.fori_loop(0, 3, pair, 0)
    row = pl.multiple_of(sc[1] * SPAN, SPAN)
    row_other = pl.multiple_of((1 - sc[1]) * SPAN, SPAN)
    stores = [
        pltpu.make_async_copy(ds_all.at[:, pl.ds(row_other, SPAN), :], theirs, sem.at[8]),
        pltpu.make_async_copy(ds_all.at[:, pl.ds(row, SPAN), :], mine, sem.at[9]),
    ]
    for cp in stores:
        cp.start()
    for cp in stores + fetch:
        cp.wait()


def attend_back_call(sc, own, other, ot, lse, dbk, dbr, wo, cosine, sine, wq, wk, wv):
    return call(
        attend_back_body,
        "attend_back",
        sc,
        (own, other, ot, lse, dbk, dbr, wo, cosine, sine, wq, wk, wv),
        [hbm(), hbm(), whole((GROUP, SEQ)), whole((8, SEQ))]
        + [whole((SPAN, WIDTH))] * 2
        + [whole((GROUP, WIDTH))]
        + [far_hbm()] * 5,
        [sds((3, SPAN, GROUP))] * 2 + [sds((3, WIDTH, WIDTH))],
        [hbm()] * 3,
        [pltpu.VMEM((SEQ, GROUP), BF)] * 4
        + [
            pltpu.VMEM((3, SEQ, GROUP), BF),
            pltpu.VMEM((128, SEQ), F32),
            pltpu.VMEM((2, SEQ, 128), F32),
            pltpu.VMEM((SEQ, 128), F32),
            pltpu.VMEM((SEQ, 128), F32),
            pltpu.SemaphoreType.DMA((13,)),
        ],
        22,
        (6 * 10 * SEQ * SEQ * 64, 10e6, 4e6),
    )


def square_body(sc, nk, nr, ak, at, ck, ct, bk, br, dk, dr, sa_ref, ka_ref, sb_ref, kb_ref, res):
    own = pl.ds(pl.multiple_of(sc[0] * GROUP, 128), GROUP)
    other = pl.ds(pl.multiple_of((1 - sc[0]) * GROUP, 128), GROUP)
    res[0, own, :] = over_rows(ak[...], at[...], bk[:, own], br[:, own])
    res[0, other, :] = over_rows(ck[...], ct[...], bk[:, own], br[:, own])
    spread(sc, res.at[0], 0, 2, 48, sa_ref, ka_ref, 0)
    for n, t in enumerate((2, 0, 1)):
        place = res.at[(n + 1) % 2]
        place[...] = over_rows(nk[...], nr[...], dk[t], dr[t])
        if n == 0:
            spread(sc, place, 0, 2, 48, sa_ref, ka_ref, 96)
        else:
            spread(sc, place, 0, 2, 48, sb_ref, kb_ref, 96 * t)


def square_call(sc, *args):
    flat = [whole((SPAN, WIDTH))] * 2
    return call(
        square_body,
        "square",
        sc,
        args,
        flat + [whole((SPAN, GROUP))] * 4 + flat + [whole((3, SPAN, GROUP))] * 2,
        [sds((8, 96, GROUP))] * 4,
        [whole((8, 96, GROUP))] * 4,
        [pltpu.VMEM((2, WIDTH, GROUP), F32)],
        16,
        (4 * 2 * SEQ * WIDTH * GROUP, 12e6, 0),
    )


def input_grad_body(sc, x_ref, gain_ref, dm_ref, m_ref, acc_ref, got_ref, dk_s, dr_s, ws, *refs):
    lay_ref, o_ref = refs
    for r in range(0, SPAN, 256):
        rr = slice(r, r + 256)
        out = m_ref[rr, :] + acc_ref[rr, :] + got_ref[rr, :].astype(F32)
        lay_ref[0, rr, :] = jnp.where(live_mask(sc, r, 256), out, 0.0).astype(BF)
    own_cols = pl.multiple_of(sc[0] * GROUP, 128)
    other_cols = pl.multiple_of((1 - sc[0]) * GROUP, 128)
    gain = gain_ref[...]
    for r in range(0, SPAN, 256):
        rr = slice(r, r + 256)
        dn = dot_nt(dk_s[0, rr, :], ws[0, :, pl.ds(own_cols, GROUP)])
        dn = dn + dot_nt(dr_s[0, rr, :], ws[0, :, pl.ds(other_cols, GROUP)])
        for t in (1, 2):
            dn = dn + dot_nt(dk_s[t, rr, :], ws[t, :, pl.ds(own_cols, GROUP)])
            dn = dn + dot_nt(dr_s[t, rr, :], ws[t, :, pl.ds(other_cols, GROUP)])
        live = live_mask(sc, r, 256)
        x = jnp.where(live, x_ref[0, rr, :].astype(F32), 0.0)
        factor = lax.rsqrt(jnp.mean(x * x, axis=-1, keepdims=True) + epsilon)
        scaled = dn * gain
        dx = dm_ref[rr, :] + (
            factor * scaled
            - x * (factor * factor * factor) * jnp.mean(x * scaled, axis=-1, keepdims=True)
        )
        o_ref[0, rr, :] = jnp.where(live, dx, 0.0).astype(BF)


def input_grad_call(sc, tokens, gain, dm, m, acc, got, dk, dr, ws):
    full = whole((1, SPAN, WIDTH))
    flat = whole((SPAN, WIDTH))
    return call(
        input_grad_body,
        "input_grad",
        sc,
        (tokens, gain, dm, m, acc, got, dk, dr, ws),
        [full, whole((1, WIDTH)), flat, flat, flat, flat]
        + [whole((3, SPAN, GROUP))] * 2
        + [whole((3, WIDTH, WIDTH))],
        [sds((1, SPAN, WIDTH))] * 2,
        [full] * 2,
        [],
        20,
        (3 * 2 * SPAN * WIDTH * WIDTH, 14e6, 1e3),
    )


def add_pieces(sc, count, sums, name):
    rows, cols = sums[0][0][0].shape[1:]
    arrays = [array for stack in sums for array, _ in stack]
    picks = [pick for stack in sums for _, pick in stack]

    def body(sc_ref, *refs):
        at = 0
        for n, stack in enumerate(sums):
            total = refs[at][0].astype(F32)
            for ref in refs[at + 1 : at + len(stack)]:
                total = total + ref[0].astype(F32)
            refs[-1][0, n * rows : (n + 1) * rows, :] = total.astype(BF)
            at += len(stack)

    def spec(pick):
        block, row = pick
        return pl.BlockSpec((1, rows, cols), lambda j, sc_ref: (block(sc_ref, j), row, 0))

    high = rows * len(sums)
    return pl.pallas_call(
        body,
        name=name,
        out_shape=sds((count, high, cols)),
        grid_spec=pltpu.PrefetchScalarGridSpec(
            num_scalar_prefetch=1,
            grid=(count,),
            in_specs=[spec(pick) for pick in picks],
            out_specs=pl.BlockSpec((1, high, cols), lambda j, sc_ref: (j, 0, 0)),
        ),
        compiler_params=pltpu.CompilerParams(vmem_limit_bytes=6 * MIB),
        cost_estimate=pl.CostEstimate(
            flops=int(0 if name == "g0_b" else ADD_COST), bytes_accessed=1000, transcendentals=0
        ),
    )(sc, *arrays)


def row_block(rows, cols):
    return pl.BlockSpec((rows, cols), lambda i, sc: (sc[6], 0))


def row_of(column):
    column = jnp.concatenate([column, jnp.zeros((32, 1), F32)], axis=0)
    return jnp.transpose(jnp.broadcast_to(column, (128, 128)))[0:1, :]


def collect_halves(sc, group, full):
    for n in range(4):
        core, k = divmod(n, 2)
        parity = sc[0] if core == 0 else 1 - sc[0]
        first = sc[3] if core == 0 else sc[7]
        first = 1 - first if k == 1 else first
        for h in range(2):
            full[parity, first, 288 * h : 288 * h + 288, :] = group[n][h]


def collect(sc, group, full, row, size):
    for n in range(8):
        core, k = divmod(n, 4)
        parity = sc[0] if core == 0 else 1 - sc[0]
        first, second = (sc[3], sc[7]) if core == 0 else (sc[7], sc[3])
        first = 1 - first if k in (1, 3) else first
        second = 1 - second if k in (2, 3) else second
        rows = pl.ds(pl.multiple_of(second * size, 16), size)
        full[parity, first, rows, :] = group[n][0, row : row + size, :]


def ffn_result_body(sc, *refs):
    wg_ref, wu_ref, gain_ref, gate_ref, up_ref, down_ref, gg_ref, full = refs[12:]
    collect_halves(sc, refs[:4], full.at[0])
    collect(sc, refs[4:12], full.at[1], 0, 288)
    for half in range(2):
        for bit in range(2):
            rows = slice(48 * bit, 48 * bit + 48)
            for parity in range(2):
                for base, ref in ((0, gate_ref), (192, up_ref)):
                    for ct in range(2):
                        lo = pl.multiple_of(base + ct * 96 + sc[0] * 48, 16)
                        block = full[half, parity, bit, pl.ds(lo, 48), :].astype(F32)
                        for q in range(2):
                            col = 512 * (2 * ct + q) + 128 * half + 256 * parity
                            ref[rows, col : col + 128] = block[:, 128 * q : 128 * q + 128]
            lo = 128 * half + 64 * bit
            for t in range(3):
                down_ref[lo : lo + 64, 256 * t : 256 * t + 256] = full[
                    half, sc[0], bit, 384 + t * 64 : 448 + t * 64, :
                ].astype(F32)
    gate = jnp.sum(wg_ref[...].astype(F32) * gate_ref[...], axis=-1, keepdims=True)
    up = jnp.sum(wu_ref[...].astype(F32) * up_ref[...], axis=-1, keepdims=True)
    gg_ref[...] = row_of((gate + up) / gain_ref[...])


def ffn_result_call(sc, first, second, wg, wu, gain):
    return call(
        ffn_result_body,
        "ffn_result",
        sc,
        tuple(first) + tuple(second) + (wg, wu, gain),
        [whole((2, 288, 256))] * 4 + [whole((1, 288, 256))] * 8 + [row_block(96, HID)] * 2 + [row_block(96, 1)],
        [sds((96, HID), F32), sds((96, HID), F32), sds((256, WIDTH), F32), sds((1, 128), F32)],
        [whole((96, HID)), whole((96, HID)), whole((256, WIDTH)), whole((1, 128))],
        [pltpu.VMEM((2, 2, 2, 576, 256), BF)],
        14,
        (1e6, 6e6, 0),
    )


def square_result_body(sc, *refs):
    group = refs[:8]
    weights = refs[8:11]
    gain_ref = refs[11]
    outs = refs[12:16]
    gg_ref, full = refs[16:]
    order = ((3, 2), (0, 1))
    for n in range(2):
        collect(sc, group, full.at[n], 96 * n, 96)
        for bit in range(2):
            rows = slice(48 * bit, 48 * bit + 48)
            for parity in range(2):
                cols = slice(GROUP * parity, GROUP * parity + GROUP)
                for t in range(2):
                    lo = pl.multiple_of(t * 96 + sc[0] * 48, 16)
                    block = full[n, parity, bit, pl.ds(lo, 48), :]
                    outs[order[n][t]][rows, cols] = block.astype(F32)
    total = jnp.zeros((96, 1), F32)
    for t in range(3):
        total = total + jnp.sum(weights[t][...].astype(F32) * outs[t][...], axis=-1, keepdims=True)
    gg_ref[...] = row_of(total / gain_ref[...])


def square_result_call(sc, group, wq, wk, wv, gain):
    return call(
        square_result_body,
        "square_result",
        sc,
        tuple(group) + (wq, wk, wv, gain),
        [whole((1, 192, GROUP))] * 8 + [row_block(96, WIDTH)] * 3 + [row_block(96, 1)],
        [sds((96, WIDTH), F32)] * 4 + [sds((1, 128), F32)],
        [whole((96, WIDTH))] * 4 + [whole((1, 128))],
        [pltpu.VMEM((2, 2, 2, 192, GROUP), BF)],
        8,
        (1e6, 4e6, 0),
    )


class Chain:
    def __init__(self, sc):
        self.sc = sc

    def next(self, *deps):
        self.sc = after(self.sc, *deps)
        return self.sc


class Reduction:
    def __init__(self, chain, send, keep, name):
        self.chain = chain
        self.send = send
        self.name = name
        self.stacks = [[[keep, 0]]]
        self.flight = None

    def start(self):
        self.fly(after(self.send, self.chain.sc), "first")

    def fly(self, rows, kind):
        self.flight = exchange(rows, kind)

    def land(self):
        if self.flight is not None:
            for n, stack in enumerate(self.stacks):
                stack.append([self.flight, n])
        self.flight = None

    def add(self, count, picks, tag):
        self.land()
        sums = []
        for stack in self.stacks:
            blocks = ([picks[0]] + picks)[-len(stack) :]
            sums.append([(array, (pick, row)) for (array, row), pick in zip(stack, blocks)])
        arrays = [array for stack in sums for array, _ in stack]
        out = add_pieces(self.chain.next(*arrays), count, sums, self.name + tag)
        self.chain.next(out)
        return out

    def second(self):
        pick = lambda t, j: j * 2 + 1 - t[7]
        self.fly(self.add(4, [pick], "_b"), "second")

    def near(self):
        pick = lambda t, j: (1 - t[4]) * 4 + j * 2 + t[7]
        self.fly(self.add(2, [pick, lambda t, j: (1 - t[4]) * 2 + j], "_c"), "near")

    def far(self):
        pick = lambda t, j: t[4] * 4 + (1 - t[5]) * 2 + t[7]
        picks = [pick, lambda t, j: t[4] * 2 + 1 - t[5], lambda t, j: 1 - t[5]]
        self.fly(self.add(1, picks, "_d"), "far")

    def total(self):
        pick = lambda t, j: t[4] * 4 + t[5] * 2 + t[7]
        picks = [pick, lambda t, j: t[4] * 2 + t[5], lambda t, j: t[5], lambda t, j: 0]
        own = self.add(1, picks, "_e")
        self.quarters = [own] + [exchange(own, kind) for kind in ("first", "second", "across")]

    def result(self):
        return self.quarters + [exchange(quarter, "core") for quarter in self.quarters]


class Straight(Reduction):
    def near(self):
        pick = lambda t, j: (1 - t[4]) * 4 + j
        self.fly(self.add(4, [pick], "_b"), "near")

    def far(self):
        pick = lambda t, j: t[4] * 4 + (1 - t[5]) * 2 + j
        self.fly(self.add(2, [pick, lambda t, j: (1 - t[5]) * 2 + j], "_c"), "far")

    def second(self):
        pick = lambda t, j: t[4] * 4 + t[5] * 2 + j
        own = self.add(2, [pick, lambda t, j: t[5] * 2 + j, lambda t, j: j], "_d")
        self.stacks = [[[own, 0]]]
        self.fly(own, "second")

    def total(self):
        own = self.add(2, [lambda t, j: j], "_e")
        self.quarters = [own, exchange(own, "first")]


def join(first, second):
    both = Reduction(first.chain, None, None, first.name + second.name)
    first.land()
    second.land()
    both.stacks = first.stacks + second.stacks
    return both


def fast_step(
    tokens,
    lengths,
    owner,
    w_query,
    w_key,
    w_value,
    w_out,
    w_gate,
    w_up,
    w_down,
    gain_attn,
    gain_mlp,
    cotangent,
):
    batch, seq, core = (lax.axis_index(name) for name in AXES)
    low, high = batch % 2, batch // 2
    swap = core == 0
    slot = jnp.arange(8, dtype=jnp.int32)
    fixed = (
        core,
        core,
        0,
        jnp.where(swap, low, high),
        seq % 2,
        seq // 2,
        seq * 2 + core,
        jnp.where(swap, high, low),
    )
    sc = jnp.zeros((8,), jnp.int32)
    for n, value in enumerate(fixed):
        sc = jnp.where(slot == n, value, sc)
    first_pos = jnp.broadcast_to(owner[0, :1], (8,))
    sc = jnp.where(slot == 1, jnp.where(swap, first_pos, 1 - first_pos), sc)
    sc = jnp.where(slot == 2, jnp.broadcast_to(lengths, (8,)), sc)
    tables = position_tables(SEQ)
    cosine, sine = jnp.asarray(tables[0]), jnp.asarray(tables[1])
    gain_row = gain_attn.reshape(1, WIDTH)
    gain_mlp_row = gain_mlp.reshape(1, WIDTH)
    qkv_w = (w_query, w_key, w_value)
    ffn_w = (w_gate, w_up, w_down)
    chain = Chain(sc)

    qkv_send, n1 = qkv_call(chain.sc, tokens, gain_row, cosine, sine, *qkv_w, True)
    qkv_other = exchange(qkv_send, "core")
    (qkv_own,) = qkv_call(chain.next(n1), n1, gain_row, cosine, sine, *qkv_w, False)
    n1_other = exchange(n1, "core")
    dy_other = exchange(cotangent, "core")
    attn_t, lse, attn_own, attn_send, wo_v, *ffn_v = attend_call(
        chain.next(qkv_own), qkv_own, qkv_other, w_out, *ffn_w
    )
    attn_other = exchange(attn_send, "core")
    attn_rest = exchange(attn_own, "core")
    middle, n2 = proj_call(
        chain.next(lse, n1_other, dy_other), tokens, attn_own, attn_other, gain_mlp_row, wo_v
    )
    n2_other = exchange(n2, "core")
    rows = (n2, n2_other, cotangent, dy_other)
    send0, keep0, *acts0 = ffn_call(chain.next(n2, attn_rest), 0, *rows, *ffn_v)
    g0 = Straight(chain, send0, keep0, "g0")
    g0.start()
    send1, keep1, *acts1 = ffn_call(chain.next(acts0[0]), 1, *rows, *ffn_v)
    g1 = Reduction(chain, send1, keep1, "g1")
    g1.start()
    acc, acc_send, dn, dn_send = ffn_out_call(chain.next(acts1[0]), acts0, acts1, *ffn_v)
    dn_other = exchange(dn_send, "core")
    chain.next(dn_send)
    g0.near()
    d_middle, db = middle_call(chain.next(dn_other), dn, dn_other, middle, cotangent, gain_mlp_row)
    db_other = exchange(db, "core")
    acc_other = exchange(after(acc_send, db_other), "core")
    d_own, d_send, qkv_v = attend_back_call(
        chain.next(db),
        qkv_own,
        qkv_other,
        attn_t,
        lse,
        db,
        db_other,
        wo_v,
        cosine,
        sine,
        *qkv_w,
    )
    d_other = exchange(d_send, "core")
    chain.next(d_own, g0.flight, g1.flight)
    g1.second()
    g0.far()
    attn = (attn_own, attn_send, attn_other, attn_rest)
    send2, keep2, send3, keep3 = square_call(
        chain.sc, n1, n1_other, *attn, db, db_other, d_own, d_send
    )
    g2 = Reduction(chain, send2, keep2, "g2")
    g3 = Reduction(chain, send3, keep3, "g3")
    g2.start()
    g3.start()
    chain.next(send3)
    layer_out, input_grad = input_grad_call(
        chain.next(acc_other, d_other),
        tokens,
        gain_row,
        d_middle,
        middle,
        acc,
        acc_other,
        d_own,
        d_other,
        qkv_v,
    )
    chain.next(input_grad)
    g2.second()
    g1.near()
    g3.second()
    g2.near()
    g0.second()
    g3.near()
    g1.far()
    g2.far()
    g3.far()
    g0.total()
    g1.total()
    g23 = join(g2, g3)
    g23.total()
    gate, up, down, gain_m = ffn_result_call(
        chain.sc, g0.result(), g1.result(), w_gate, w_up, gain_mlp.reshape(WIDTH, 1)
    )
    chain.next(gain_m)
    query, key, value, out, gain_a = square_result_call(
        chain.sc, g23.result(), *qkv_w, gain_attn.reshape(WIDTH, 1)
    )
    return (
        layer_out,
        input_grad,
        query,
        key,
        value,
        out,
        gate,
        up,
        down,
        gain_a[0, :96],
        gain_m[0, :96],
    )


def solution(mesh):
    in_specs = (
        P(("batch", "seq"), "seqb", None),
        P(("batch", "seq")),
        P(("batch", "seq"), None),
        P(),
        P(),
        P(),
        P(),
        P(),
        P(),
        P(),
        P(),
        P(),
        P(("batch", "seq"), "seqb", None),
    )
    out_specs = (
        P(("batch", "seq"), "seqb", None),
        P(("batch", "seq"), "seqb", None),
        P(("seq", "seqb"), None),
        P(("seq", "seqb"), None),
        P(("seq", "seqb"), None),
        P(("seq", "seqb"), None),
        P(("seq", "seqb"), None),
        P(("seq", "seqb"), None),
        P(("seq", "seqb"), None),
        P(("seq", "seqb")),
        P(("seq", "seqb")),
    )
    step = fast_step if fast_layout(mesh) else general_step
    return jax.shard_map(step, mesh=mesh, in_specs=in_specs, out_specs=out_specs, check_vma=False)
```

```python
import functools
import math

import jax
import jax.numpy as jnp
import numpy as np
from jax import lax
from jax.experimental import pallas as pl
from jax.experimental.pallas import tpu as pltpu
from jax.sharding import PartitionSpec as P

HEADS = 12
HEAD_DIM = 64


epsilon = 1e-05
rope_base = 10000.0
masked_score = -1e30


def rms_forward(rows, gain):
    factor = lax.rsqrt(jnp.mean(rows * rows, axis=-1, keepdims=True) + epsilon)
    return (rows * factor * gain, factor)


def rms_backward(rows, factor, gain, upstream):
    scaled = upstream * gain
    return factor * scaled - rows * (factor * factor * factor) * jnp.mean(
        rows * scaled, axis=-1, keepdims=True
    )


def rotation_tables(positions):
    half = HEAD_DIM // 2
    freq = rope_base ** (-(2.0 * jnp.arange(half, dtype=jnp.float32)) / HEAD_DIM)
    angles = positions.astype(jnp.float32)[..., None] * freq
    return (jnp.cos(angles), jnp.sin(angles))


def split_heads(rows):
    return rows.reshape(rows.shape[0], rows.shape[1], HEADS, HEAD_DIM)


def rotate(rows, cosine, sine, inverse):
    shaped = split_heads(rows)
    half = HEAD_DIM // 2
    first = shaped[..., :half]
    second = shaped[..., half:]
    cos_part = cosine[:, :, None, :]
    sin_part = sine[:, :, None, :]
    if inverse:
        turned = jnp.concatenate(
            [first * cos_part + second * sin_part, second * cos_part - first * sin_part], axis=-1
        )
    else:
        turned = jnp.concatenate(
            [first * cos_part - second * sin_part, second * cos_part + first * sin_part], axis=-1
        )
    return turned.reshape(rows.shape)


def range_positions(owner, count, span):
    offsets = jnp.arange(span, dtype=jnp.int32)
    return (owner[:, :, None] * span + offsets[None, None, :]).reshape(owner.shape[0], count)


def fold_keys(parts, combine, initial):
    return combine(
        initial,
        (
            lax.all_gather(parts[0], "seqb", axis=1, tiled=True),
            lax.all_gather(parts[1], "seqb", axis=1, tiled=True),
        ),
        jnp.int32(0),
    )


def general_step(
    tokens,
    lengths,
    owner,
    w_query,
    w_key,
    w_value,
    w_out,
    w_gate,
    w_up,
    w_down,
    gain_attn,
    gain_mlp,
    cotangent,
):
    seqs, span, width = tokens.shape
    scale = HEAD_DIM ** (-0.5)
    place = lax.axis_index("seqb")
    own_block = lax.dynamic_slice_in_dim(owner, place, 1, 1)
    local_pos = own_block * span + jnp.arange(span, dtype=jnp.int32)[None, :]
    local_live = local_pos < lengths[:, None]
    live_rows = local_live[:, :, None]
    inputs = jnp.where(live_rows, tokens.astype(jnp.float32), 0.0)
    normed, factor_attn = rms_forward(inputs, gain_attn)
    normed_low = normed.astype(jnp.bfloat16)
    cosine, sine = rotation_tables(local_pos)
    query_pre = jnp.einsum("scd,de->sce", normed_low, w_query, preferred_element_type=jnp.float32)
    key_pre = jnp.einsum("scd,de->sce", normed_low, w_key, preferred_element_type=jnp.float32)
    value_low = jnp.einsum(
        "scd,de->sce", normed_low, w_value, preferred_element_type=jnp.float32
    ).astype(jnp.bfloat16)
    query_rot = rotate(query_pre, cosine, sine, False).astype(jnp.bfloat16)
    key_rot = rotate(key_pre, cosine, sine, False).astype(jnp.bfloat16)
    query_heads = split_heads(query_rot)
    key_heads = split_heads(key_rot)
    value_heads = split_heads(value_low)

    def attend(state, piece, start):
        keys, values = piece
        count = keys.shape[1]
        key_pos = range_positions(owner, count, span)
        key_live = key_pos < lengths[:, None]
        stride = math.gcd(count, 512)

        def attend_one_block(index, inner):
            offset = index * stride
            key_block = split_heads(lax.dynamic_slice_in_dim(keys, offset, stride, 1))
            value_block = split_heads(lax.dynamic_slice_in_dim(values, offset, stride, 1))
            pos_block = lax.dynamic_slice_in_dim(key_pos, offset, stride, 1)
            live_block = lax.dynamic_slice_in_dim(key_live, offset, stride, 1)
            allowed = (
                (pos_block[:, None, :] <= local_pos[:, :, None])
                & live_block[:, None, :]
                & local_live[:, :, None]
            )

            def attend_update(carried):
                peak, total, summed = carried
                scores = (
                    jnp.einsum(
                        "sqhd,skhd->shqk",
                        query_heads,
                        key_block,
                        preferred_element_type=jnp.float32,
                    )
                    * scale
                )
                mask = allowed[:, None, :, :]
                new_peak = jnp.maximum(
                    peak, jnp.max(jnp.where(mask, scores, masked_score), axis=-1)
                )
                weights = jnp.where(mask, jnp.exp(scores - new_peak[..., None]), 0.0)
                factor = jnp.exp(peak - new_peak)
                total = total * factor + jnp.sum(weights, axis=-1)
                term = jnp.einsum(
                    "shqk,skhd->sqhd",
                    weights.astype(jnp.bfloat16),
                    value_block,
                    preferred_element_type=jnp.float32,
                )
                summed = (
                    split_heads(summed) * jnp.transpose(factor, (0, 2, 1))[..., None] + term
                ).reshape(summed.shape)
                return (new_peak, total, summed)

            return lax.cond(jnp.any(allowed), attend_update, lambda carried: carried, inner)

        return lax.fori_loop(0, count // stride, attend_one_block, state)

    start_state = (
        jnp.full((seqs, HEADS, span), masked_score, jnp.float32),
        jnp.zeros((seqs, HEADS, span), jnp.float32),
        jnp.zeros((seqs, span, width), jnp.float32),
    )
    peak, total, summed = fold_keys((key_rot, value_low), attend, start_state)
    safe_total = jnp.where(local_live[:, None, :], total, 1.0)
    attn = split_heads(summed) / jnp.transpose(safe_total, (0, 2, 1))[..., None]
    attn = jnp.where(local_live[:, :, None, None], attn, 0.0).reshape(seqs, span, width)
    log_total = jnp.where(local_live[:, None, :], peak + jnp.log(safe_total), 0.0)
    attn_low = attn.astype(jnp.bfloat16)
    middle = inputs + jnp.einsum("scd,de->sce", attn_low, w_out, preferred_element_type=jnp.float32)
    normed_mlp, factor_mlp = rms_forward(middle, gain_mlp)
    normed_mlp_low = normed_mlp.astype(jnp.bfloat16)
    gate = jnp.einsum("scd,df->scf", normed_mlp_low, w_gate, preferred_element_type=jnp.float32)
    up_proj = jnp.einsum("scd,df->scf", normed_mlp_low, w_up, preferred_element_type=jnp.float32)
    hidden = (jax.nn.silu(gate) * up_proj).astype(jnp.bfloat16)
    out = middle + jnp.einsum("scf,fd->scd", hidden, w_down, preferred_element_type=jnp.float32)
    layer_out = jnp.where(live_rows, out, 0.0).astype(jnp.bfloat16)
    upstream = jnp.where(live_rows, cotangent, jnp.zeros_like(cotangent))
    grad_down = jnp.einsum("scf,scd->fd", hidden, upstream, preferred_element_type=jnp.float32)
    d_hidden = jnp.einsum("scd,fd->scf", upstream, w_down, preferred_element_type=jnp.float32)
    sigmoid_gate = jax.nn.sigmoid(gate)
    d_gate = (d_hidden * up_proj * sigmoid_gate * (1.0 + gate * (1.0 - sigmoid_gate))).astype(
        jnp.bfloat16
    )
    d_up = (d_hidden * gate * sigmoid_gate).astype(jnp.bfloat16)
    grad_gate = jnp.einsum(
        "scd,scf->df", normed_mlp_low, d_gate, preferred_element_type=jnp.float32
    )
    grad_up = jnp.einsum("scd,scf->df", normed_mlp_low, d_up, preferred_element_type=jnp.float32)
    d_normed_mlp = jnp.einsum(
        "scf,df->scd", d_gate, w_gate, preferred_element_type=jnp.float32
    ) + jnp.einsum("scf,df->scd", d_up, w_up, preferred_element_type=jnp.float32)
    grad_gain_mlp = jnp.sum(d_normed_mlp * (middle * factor_mlp), axis=(0, 1))
    d_middle = upstream.astype(jnp.float32) + rms_backward(
        middle, factor_mlp, gain_mlp, d_normed_mlp
    )
    d_branch = d_middle.astype(jnp.bfloat16)
    grad_out = jnp.einsum("scd,sce->de", attn_low, d_branch, preferred_element_type=jnp.float32)
    d_attn = jnp.einsum("sce,de->scd", d_branch, w_out, preferred_element_type=jnp.float32).astype(
        jnp.bfloat16
    )
    first_done = (grad_out, grad_gate, grad_up, grad_down, grad_gain_mlp)
    delta = jnp.sum(split_heads(d_attn.astype(jnp.float32) * attn), axis=-1)
    delta_heads = jnp.transpose(delta, (0, 2, 1))
    grad_heads = split_heads(d_attn)

    def query_grads(state, piece, start):
        keys, values = piece
        count = keys.shape[1]
        key_pos = range_positions(owner, count, span)
        key_live = key_pos < lengths[:, None]
        stride = math.gcd(count, 512)

        def query_one_block(index, inner):
            offset = index * stride
            key_block = split_heads(lax.dynamic_slice_in_dim(keys, offset, stride, 1))
            value_block = split_heads(lax.dynamic_slice_in_dim(values, offset, stride, 1))
            pos_block = lax.dynamic_slice_in_dim(key_pos, offset, stride, 1)
            live_block = lax.dynamic_slice_in_dim(key_live, offset, stride, 1)
            allowed = (
                (pos_block[:, None, :] <= local_pos[:, :, None])
                & live_block[:, None, :]
                & local_live[:, :, None]
            )

            def query_update(carried):
                scores = (
                    jnp.einsum(
                        "sqhd,skhd->shqk",
                        query_heads,
                        key_block,
                        preferred_element_type=jnp.float32,
                    )
                    * scale
                )
                probs = jnp.where(
                    allowed[:, None, :, :], jnp.exp(scores - log_total[..., None]), 0.0
                )
                d_probs = jnp.einsum(
                    "sqhd,skhd->shqk", grad_heads, value_block, preferred_element_type=jnp.float32
                )
                d_scores = (probs * (d_probs - delta_heads[..., None])).astype(jnp.bfloat16)
                term = (
                    jnp.einsum(
                        "shqk,skhd->sqhd", d_scores, key_block, preferred_element_type=jnp.float32
                    )
                    * scale
                )
                return carried + term.reshape(carried.shape)

            return lax.cond(jnp.any(allowed), query_update, lambda carried: carried, inner)

        return lax.fori_loop(0, count // stride, query_one_block, state)

    zero_query = jnp.zeros((seqs, span, width), jnp.float32)
    d_query = fold_keys((key_rot, value_low), query_grads, zero_query)
    lse_all, delta_all = (
        lax.all_gather(jnp.transpose(log_total, (0, 2, 1)), "seqb", axis=1, tiled=True),
        lax.all_gather(delta, "seqb", axis=1, tiled=True),
    )
    zero_rows = jnp.zeros((seqs, span, width), jnp.float32)
    queries = lax.all_gather(query_rot, "seqb", axis=1, tiled=True)
    d_rows = lax.all_gather(d_attn, "seqb", axis=1, tiled=True)
    count = queries.shape[1]
    row_pos = range_positions(owner, count, span)
    row_live = row_pos < lengths[:, None]
    stride = math.gcd(count, 512)

    def key_one_block(index, inner):
        offset = index * stride
        query_block = split_heads(lax.dynamic_slice_in_dim(queries, offset, stride, 1))
        grad_block = split_heads(lax.dynamic_slice_in_dim(d_rows, offset, stride, 1))
        pos_block = lax.dynamic_slice_in_dim(row_pos, offset, stride, 1)
        live_block = lax.dynamic_slice_in_dim(row_live, offset, stride, 1)
        lse_block = jnp.transpose(lax.dynamic_slice_in_dim(lse_all, offset, stride, 1), (0, 2, 1))
        delta_block = jnp.transpose(
            lax.dynamic_slice_in_dim(delta_all, offset, stride, 1), (0, 2, 1)
        )
        allowed = (
            (local_pos[:, None, :] <= pos_block[:, :, None])
            & local_live[:, None, :]
            & live_block[:, :, None]
        )

        def key_update(carried):
            d_key, d_value = carried
            scores = (
                jnp.einsum(
                    "sqhd,skhd->shqk", query_block, key_heads, preferred_element_type=jnp.float32
                )
                * scale
            )
            probs = jnp.where(allowed[:, None, :, :], jnp.exp(scores - lse_block[..., None]), 0.0)
            value_term = jnp.einsum(
                "shqk,sqhd->skhd",
                probs.astype(jnp.bfloat16),
                grad_block,
                preferred_element_type=jnp.float32,
            )
            d_probs = jnp.einsum(
                "sqhd,skhd->shqk", grad_block, value_heads, preferred_element_type=jnp.float32
            )
            d_scores = (probs * (d_probs - delta_block[..., None])).astype(jnp.bfloat16)
            key_term = (
                jnp.einsum(
                    "shqk,sqhd->skhd", d_scores, query_block, preferred_element_type=jnp.float32
                )
                * scale
            )
            return (
                d_key + key_term.reshape(d_key.shape),
                d_value + value_term.reshape(d_value.shape),
            )

        return lax.cond(jnp.any(allowed), key_update, lambda carried: carried, inner)

    d_key, d_value = lax.fori_loop(0, count // stride, key_one_block, (zero_rows, zero_rows))
    d_query_pre = rotate(d_query, cosine, sine, True).astype(jnp.bfloat16)
    d_key_pre = rotate(d_key, cosine, sine, True).astype(jnp.bfloat16)
    d_value_low = d_value.astype(jnp.bfloat16)
    grad_query = jnp.einsum(
        "scd,sce->de", normed_low, d_query_pre, preferred_element_type=jnp.float32
    )
    grad_key = jnp.einsum("scd,sce->de", normed_low, d_key_pre, preferred_element_type=jnp.float32)
    grad_value = jnp.einsum(
        "scd,sce->de", normed_low, d_value_low, preferred_element_type=jnp.float32
    )
    d_normed = jnp.einsum("sce,de->scd", d_query_pre, w_query, preferred_element_type=jnp.float32)
    d_normed = d_normed + jnp.einsum(
        "sce,de->scd", d_key_pre, w_key, preferred_element_type=jnp.float32
    )
    d_normed = d_normed + jnp.einsum(
        "sce,de->scd", d_value_low, w_value, preferred_element_type=jnp.float32
    )
    grad_gain_attn = jnp.sum(d_normed * (inputs * factor_attn), axis=(0, 1))
    d_inputs = d_middle + rms_backward(inputs, factor_attn, gain_attn, d_normed)
    input_grad = jnp.where(live_rows, d_inputs, 0.0).astype(jnp.bfloat16)
    summed_parts = (
        lax.psum_scatter(grad_query, ("seq", "seqb"), scatter_dimension=0, tiled=True),
        lax.psum_scatter(grad_key, ("seq", "seqb"), scatter_dimension=0, tiled=True),
        lax.psum_scatter(grad_value, ("seq", "seqb"), scatter_dimension=0, tiled=True),
        lax.psum_scatter(grad_gain_attn, ("seq", "seqb"), scatter_dimension=0, tiled=True),
        lax.psum_scatter(first_done[0], ("seq", "seqb"), scatter_dimension=0, tiled=True),
        lax.psum_scatter(first_done[1], ("seq", "seqb"), scatter_dimension=0, tiled=True),
        lax.psum_scatter(first_done[2], ("seq", "seqb"), scatter_dimension=0, tiled=True),
        lax.psum_scatter(first_done[3], ("seq", "seqb"), scatter_dimension=0, tiled=True),
        lax.psum_scatter(first_done[4], ("seq", "seqb"), scatter_dimension=0, tiled=True),
    )
    all_done = (
        lax.psum(summed_parts[0].astype(jnp.bfloat16), "batch").astype(jnp.float32),
        lax.psum(summed_parts[1].astype(jnp.bfloat16), "batch").astype(jnp.float32),
        lax.psum(summed_parts[2].astype(jnp.bfloat16), "batch").astype(jnp.float32),
        lax.psum(summed_parts[3].astype(jnp.bfloat16), "batch").astype(jnp.float32),
        lax.psum(summed_parts[4].astype(jnp.bfloat16), "batch").astype(jnp.float32),
        lax.psum(summed_parts[5].astype(jnp.bfloat16), "batch").astype(jnp.float32),
        lax.psum(summed_parts[6].astype(jnp.bfloat16), "batch").astype(jnp.float32),
        lax.psum(summed_parts[7].astype(jnp.bfloat16), "batch").astype(jnp.float32),
        lax.psum(summed_parts[8].astype(jnp.bfloat16), "batch").astype(jnp.float32),
    )
    second_done = (all_done[0], all_done[1], all_done[2], all_done[3])
    first_done = (all_done[4], all_done[5], all_done[6], all_done[7], all_done[8])
    return (
        layer_out,
        input_grad,
        second_done[0],
        second_done[1],
        second_done[2],
        first_done[0],
        first_done[1],
        first_done[2],
        first_done[3],
        second_done[3],
        first_done[4],
    )


AXES = ("batch", "seq", "seqb")
BF = jnp.bfloat16
F32 = jnp.float32
MIB = 1 << 20
COST = 1e6
ADD_COST = 2e9
KERNEL_US = {
    "qkv_other": 4,
    "qkv_own": 4,
    "attend": 9,
    "proj": 3,
    "ffn_first": 8,
    "ffn_second": 8,
    "ffn_out": 9,
    "middle": 1.4,
    "attend_back": 14,
    "square": 5,
    "input_grad": 6.5,
    "ffn_result": 2,
    "square_result": 2,
}


def fast_layout(mesh):
    return mesh.shape["batch"] == 4 and mesh.shape["seq"] == 4 and mesh.shape["seqb"] == 2


def exchange(rows, kind):
    pairs = []
    for b in range(4):
        for s in range(4):
            for c in range(2):
                first = 1 if c == 0 else 2
                target = {
                    "core": (b, s, 1 - c),
                    "first": (b ^ first, s, c),
                    "second": (b ^ (3 - first), s, c),
                    "near": (b, s ^ 1, c),
                    "far": (b, s ^ 2, c),
                    "across": (b ^ 3, s, c),
                }[kind]
                pairs.append((b * 8 + s * 2 + c, target[0] * 8 + target[1] * 2 + target[2]))
    return lax.ppermute(rows, AXES, pairs)


def dot(a, b):
    return lax.dot_general(a, b, (((1,), (0,)), ((), ())), preferred_element_type=F32)


def dot_nt(a, b):
    return lax.dot_general(a, b, (((1,), (1,)), ((), ())), preferred_element_type=F32)


def position_tables(count):
    half = HEAD_DIM // 2
    freq = rope_base ** (-(2.0 * np.arange(half)) / HEAD_DIM)
    angles = np.arange(count)[:, None] * freq[None, :]
    cosine, sine = np.cos(angles), np.sin(angles)
    return (
        np.concatenate([cosine, cosine, cosine, cosine], 1).astype(np.float32),
        np.concatenate([-sine, sine, -sine, sine], 1).astype(np.float32),
    )


def swap_halves(u):
    lane = lax.broadcasted_iota(jnp.int32, u.shape, 1) % HEAD_DIM
    return jnp.where(lane < HEAD_DIM // 2, pltpu.roll(u, 96, 1), pltpu.roll(u, 32, 1))


def turn(rows, cosine, sine):
    parts = []
    for g in range(rows.shape[1] // 128):
        u = rows[:, g * 128 : (g + 1) * 128]
        parts.append(u * cosine + swap_halves(u) * sine)
    return parts[0] if len(parts) == 1 else jnp.concatenate(parts, axis=1)


def live_mask(sc, row0, count):
    span_pos = sc[1] * SPAN + row0 + lax.broadcasted_iota(jnp.int32, (count, 1), 0)
    return span_pos < sc[2]


SPAN = 512
SEQ = 1024
WIDTH = 768
GROUP = 384
HID = 2048


def hbm():
    return pl.BlockSpec(memory_space=pl.ANY)


def far_hbm():
    return pl.BlockSpec(memory_space=pltpu.HBM)


def after(sc, *deps):
    return lax.optimization_barrier((sc,) + deps)[0]


def dot_tn(a, b):
    return lax.dot_general(a, b, (((0,), (0,)), ((), ())), preferred_element_type=F32)


def whole(shape):
    return pl.BlockSpec(shape, lambda i, sc: (0,) * len(shape))


def call(body, name, sc, args, in_specs, out_shapes, out_specs, scratch, vmem, cost):
    flops, moved, trans = cost
    args = [
        pltpu.with_memory_space_constraint(a, pltpu.HBM) if spec.memory_space is pltpu.HBM else a
        for a, spec in zip(args, in_specs)
    ]
    return pl.pallas_call(
        body,
        name=name,
        out_shape=out_shapes,
        grid_spec=pltpu.PrefetchScalarGridSpec(
            num_scalar_prefetch=1,
            grid=(1,),
            in_specs=in_specs,
            out_specs=out_specs,
            scratch_shapes=scratch,
        ),
        compiler_params=pltpu.CompilerParams(vmem_limit_bytes=vmem * MIB),
        cost_estimate=pl.CostEstimate(
            flops=int(COST * KERNEL_US[name]), bytes_accessed=1000, transcendentals=0
        ),
    )(sc, *args)


def sds(shape, dtype=BF):
    return jax.ShapeDtypeStruct(shape, dtype)


def qkv_body(sc, *refs, flip):
    if flip:
        x_hbm, cos_hbm, sin_hbm, gain_ref, wq, wk, wv, o_ref, n_ref, xs, cs, ss, ws, sem = refs
    else:
        n_ref, cos_hbm, sin_hbm, wq, wk, wv, o_ref, cs, ss, ws, sem = refs
    col = (1 - sc[0]) if flip else sc[0]
    col = pl.multiple_of(col * GROUP, 128)
    row = pl.multiple_of(sc[1] * SPAN, SPAN)
    copies = [
        pltpu.make_async_copy(w.at[:, pl.ds(col, GROUP)], ws.at[t], sem.at[t])
        for t, w in enumerate((wq, wk, wv))
    ]
    tables = [
        pltpu.make_async_copy(cos_hbm.at[pl.ds(row, SPAN), :], cs, sem.at[4]),
        pltpu.make_async_copy(sin_hbm.at[pl.ds(row, SPAN), :], ss, sem.at[5]),
    ]
    if flip:
        x_copy = pltpu.make_async_copy(x_hbm.at[0], xs, sem.at[3])
        x_copy.start()
    for cp in [copies[2]] + copies[:2] + tables:
        cp.start()
    if flip:
        x_copy.wait()
        for r in range(0, SPAN, 256):
            x = jnp.where(live_mask(sc, r, 256), xs[r : r + 256, :].astype(F32), 0.0)
            factor = lax.rsqrt(jnp.mean(x * x, axis=-1, keepdims=True) + epsilon)
            n_ref[r : r + 256, :] = (x * factor * gain_ref[...]).astype(BF)
    for t in (2, 0, 1):
        copies[t].wait()
        if t == 0:
            for cp in tables:
                cp.wait()
        for r in range(0, SPAN, 256):
            y = dot(n_ref[r : r + 256, :], ws[t])
            if t < 2:
                y = turn(y, cs[r : r + 256, :], ss[r : r + 256, :])
            if t == 0:
                y = y * (HEAD_DIM**-0.5)
            o_ref[t, r : r + 256, :] = y.astype(BF)


def qkv_call(sc, rows, gain, cosine, sine, wq, wk, wv, flip):
    out_shapes = [sds((3, SPAN, GROUP))]
    out_specs = [whole((3, SPAN, GROUP))]
    scratch = [
        pltpu.VMEM((SPAN, 128), F32),
        pltpu.VMEM((SPAN, 128), F32),
        pltpu.VMEM((3, WIDTH, GROUP), BF),
        pltpu.SemaphoreType.DMA((6,)),
    ]
    if flip:
        out_shapes.append(sds((SPAN, WIDTH)))
        out_specs.append(whole((SPAN, WIDTH)))
        args = (rows, cosine, sine, gain, wq, wk, wv)
        specs = [far_hbm()] * 3 + [whole((1, WIDTH))] + [far_hbm()] * 3
        scratch = [pltpu.VMEM((SPAN, WIDTH), BF)] + scratch
    else:
        args = (rows, cosine, sine, wq, wk, wv)
        specs = [whole((SPAN, WIDTH))] + [far_hbm()] * 5
    return call(
        functools.partial(qkv_body, flip=flip),
        "qkv_other" if flip else "qkv_own",
        sc,
        args,
        specs,
        out_shapes,
        out_specs,
        scratch,
        9,
        (3 * 2 * SPAN * WIDTH * GROUP, 5e6, 1e3),
    )


def gather_rows(sc, own, other, places, sem):
    copies = []
    for t, place in enumerate(places):
        for k, src in enumerate((own, other)):
            pos = sc[1] if k == 0 else 1 - sc[1]
            row = pl.multiple_of(pos * SPAN, SPAN)
            source = src.at[t] if len(src.shape) == 3 else src
            copies.append(
                pltpu.make_async_copy(source, place.at[pl.ds(row, SPAN), :], sem.at[2 * t + k])
            )
    for cp in copies:
        cp.start()
    return copies


def attend_body(sc, own, other, wo, wg, wu, wd, *refs):
    (ot_ref, lse_ref, mine, theirs, wo_v, wg_v, wu_v, wd_v, qs, ks, vs, at, sem, wsem) = refs
    copies = gather_rows(sc, own, other, (qs, ks, vs), sem)
    fetch = []

    def bring(src, place):
        fetch.append(pltpu.make_async_copy(src, place, wsem.at[len(fetch)]))
        fetch[-1].start()

    for k in range(2):
        head = (sc[0] if k == 0 else 1 - sc[0]) * GROUP
        rows = pl.ds(pl.multiple_of(head, 128), GROUP)
        bring(wo.at[rows, :], wo_v.at[GROUP * k : GROUP * k + GROUP, :])
    for half in range(2):
        for s in range(4):
            cols = hidden_cols(sc, s, half)
            to = slice(512 * half + 128 * s, 512 * half + 128 * s + 128)
            bring(wg.at[:, cols], wg_v.at[:, to])
            bring(wu.at[:, cols], wu_v.at[:, to])
            bring(wd.at[cols, :], wd_v.at[to, :])
    for cp in copies:
        cp.wait()
    lane = lax.broadcasted_iota(jnp.int32, (256, 128), 1)
    key_id = lax.broadcasted_iota(jnp.int32, (256, 256), 0)
    row_id = lax.broadcasted_iota(jnp.int32, (256, 256), 1)
    keep = key_id <= row_id

    def pair(hp, carry):
        base = pl.multiple_of(hp * 128, 128)
        cols = pl.ds(base, 128)
        vt = jnp.transpose(vs[:, cols].astype(F32)).astype(BF)

        def scores(i, h):
            n = 256 * (i + 1)
            qm = jnp.where(lane // HEAD_DIM == h, qs[256 * i : n, cols], jnp.zeros((), BF))
            return dot_nt(ks[0:n, cols], qm)

        def soften(i, h, st):
            n = 256 * (i + 1)
            diag = jnp.where(keep, st[n - 256 :, :], masked_score)
            st = diag if i == 0 else jnp.concatenate([st[: n - 256, :], diag], axis=0)
            peak = jnp.max(st, axis=0, keepdims=True)
            p = jnp.exp(st - peak)
            return p.astype(BF), peak, jnp.sum(p, axis=0, keepdims=True)

        def finish(i, h, p, peak, total):
            n = 256 * (i + 1)
            o = dot(vt[h * 64 : h * 64 + 64, :n], p) * (1.0 / total)
            ot_ref[pl.ds(pl.multiple_of(hp * 128 + h * 64, 64), 64), 256 * i : n] = o
            lse_ref[pl.ds(hp * 2 + h, 1), 256 * i : n] = peak + jnp.log(total)

        tasks = [(i, h) for i in range(4) for h in range(2)]
        st, waiting = scores(*tasks[0]), None
        for k, task in enumerate(tasks):
            ahead = scores(*tasks[k + 1]) if k + 1 < len(tasks) else None
            parts = soften(*task, st)
            if waiting is not None:
                finish(*waiting)
            waiting, st = task + parts, ahead
        finish(*waiting)
        at[:, cols] = jnp.transpose(ot_ref[cols, :]).astype(BF)
        return carry

    lax.fori_loop(0, 3, pair, 0)
    row = pl.multiple_of(sc[1] * SPAN, SPAN)
    row_other = pl.multiple_of((1 - sc[1]) * SPAN, SPAN)
    out_other = pltpu.make_async_copy(at.at[pl.ds(row_other, SPAN), :], theirs, sem.at[0])
    out_own = pltpu.make_async_copy(at.at[pl.ds(row, SPAN), :], mine, sem.at[1])
    out_other.start()
    out_own.start()
    out_other.wait()
    out_own.wait()
    for cp in fetch:
        cp.wait()


def attend_call(sc, own, other, wo, wg, wu, wd):
    return call(
        attend_body,
        "attend",
        sc,
        (own, other, wo, wg, wu, wd),
        [hbm(), hbm()] + [far_hbm()] * 4,
        [sds((GROUP, SEQ), F32), sds((8, SEQ), F32), sds((SPAN, GROUP)), sds((SPAN, GROUP))]
        + [sds((WIDTH, WIDTH)), sds((WIDTH, SEQ)), sds((WIDTH, SEQ)), sds((SEQ, WIDTH))],
        [whole((GROUP, SEQ)), whole((8, SEQ))] + [hbm()] * 6,
        [pltpu.VMEM((SEQ, GROUP), BF)] * 4
        + [pltpu.SemaphoreType.DMA((6,)), pltpu.SemaphoreType.DMA((26,))],
        12,
        (6 * 4 * SEQ * SEQ * 64, 6e6, 4e6),
    )


def proj_body(sc, x_ref, ak_ref, ar_ref, gain_ref, wo_ref, m_ref, n_ref):
    for r in range(0, SPAN, 256):
        rr = slice(r, r + 256)
        m = jnp.where(live_mask(sc, r, 256), x_ref[0, rr, :].astype(F32), 0.0)
        m = m + dot(ak_ref[rr, :], wo_ref[:GROUP, :]) + dot(ar_ref[rr, :], wo_ref[GROUP:, :])
        m_ref[rr, :] = m
        factor = lax.rsqrt(jnp.mean(m * m, axis=-1, keepdims=True) + epsilon)
        n_ref[rr, :] = (m * factor * gain_ref[...]).astype(BF)


def proj_call(sc, tokens, own, other, gain, wo):
    return call(
        proj_body,
        "proj",
        sc,
        (tokens, own, other, gain, wo),
        [whole((1, SPAN, WIDTH))]
        + [whole((SPAN, GROUP))] * 2
        + [whole((1, WIDTH)), whole((WIDTH, WIDTH))],
        [sds((SPAN, WIDTH), F32), sds((SPAN, WIDTH))],
        [whole((SPAN, WIDTH))] * 2,
        [],
        8,
        (2 * SPAN * WIDTH * WIDTH, 5e6, 1e3),
    )


def over_rows(own, other, d_own, d_other):
    return dot_tn(own, d_own) + dot_tn(other, d_other)


def place_of(s):
    return (s % 2) * 2 + s // 2


def hidden_cols(sc, s, half):
    return pl.ds(pl.multiple_of(512 * s + 128 * half + 256 * sc[0], 128), 128)


def spread(sc, res_s, first, count, rows, send_ref, keep_ref, to):
    size = send_ref.shape[1]
    for k, ref in enumerate((send_ref, keep_ref)):
        bit = (1 - sc[3]) if k == 0 else sc[3]
        for s in range(4):
            for q in range(count):
                lo = pl.multiple_of(first + (s * count + q) * 2 * rows + bit * rows, 16)
                block, row = divmod(to + q * rows, size)
                ref[2 * place_of(s) + block, row : row + rows, :] = res_s[pl.ds(lo, rows), :].astype(
                    BF
                )


def ffn_body(sc, n_own, n_oth, dy_own, dy_oth, wg_s, wu_s, wd_s, *refs):
    (send_ref, keep_ref, h_ref, dg_ref, du_ref, dy_s, res_a, res_b) = refs
    for r in range(0, SEQ, 256):
        pos = sc[1] if r < SPAN else 1 - sc[1]
        at = pos * SPAN + r % SPAN + lax.broadcasted_iota(jnp.int32, (256, 1), 0)
        src = dy_own if r < SPAN else dy_oth
        lo = r % SPAN
        dy_s[r : r + 256, :] = jnp.where(at < sc[2], src[0, lo : lo + 256, :], jnp.zeros((), BF))

    def products(r):
        src = n_own if r < SPAN else n_oth
        rows = src[r % SPAN : r % SPAN + 256, :]
        return dot(rows, wg_s[...]), dot(rows, wu_s[...]), dot_nt(dy_s[r : r + 256, :], wd_s[...])

    ahead = products(0)
    for r in range(0, SEQ, 256):
        g, u, dh = ahead
        if r + 256 < SEQ:
            ahead = products(r + 256)
        rr = slice(r, r + 256)
        sg = jax.nn.sigmoid(g)
        gs = g * sg
        h_ref[rr, :] = (gs * u).astype(BF)
        du_ref[rr, :] = (dh * gs).astype(BF)
        dg_ref[rr, :] = (dh * u * (sg + gs * (1.0 - sg))).astype(BF)
    lower, upper = slice(0, SPAN), slice(SPAN, SEQ)
    for k, (base, src) in enumerate(((0, dg_ref), (192, du_ref))):
        for ct in range(2):
            cols = slice(256 * ct, 256 * ct + 256)
            place = res_a.at[ct]
            place[...] = over_rows(n_own[...], n_oth[...], src[lower, cols], src[upper, cols])
            spread(sc, place, 0, 2, 48, send_ref, keep_ref, base + 96 * ct)
    for n in range(3):
        place = res_b.at[n % 2]
        place[...] = dot_tn(h_ref[...], dy_s[:, 256 * n : 256 * n + 256])
        spread(sc, place, 0, 1, 64, send_ref, keep_ref, 384 + 64 * n)


def ffn_call(sc, half, n_own, n_oth, dy_own, dy_oth, wg, wu, wd):
    flat, full = whole((SPAN, WIDTH)), whole((1, SPAN, WIDTH))
    wide = pl.BlockSpec((WIDTH, 512), lambda i, sc: (0, half))
    return call(
        ffn_body,
        "ffn_first" if half == 0 else "ffn_second",
        sc,
        (n_own, n_oth, dy_own, dy_oth, wg, wu, wd),
        [flat, flat, full, full, wide, wide, pl.BlockSpec((512, WIDTH), lambda i, sc: (half, 0))],
        [sds((8, 288, 256))] * 2 + [sds((SEQ, 512))] * 3,
        [whole((8, 288, 256))] * 2 + [whole((SEQ, 512))] * 3,
        [
            pltpu.VMEM((SEQ, WIDTH), BF),
            pltpu.VMEM((2, WIDTH, 256), F32),
            pltpu.VMEM((2, 512, 256), F32),
        ],
        26,
        (6 * 2 * SEQ * WIDTH * 512, 14e6, 1e6),
    )


def ffn_out_body(sc, h0, dg0, du0, h1, dg1, du1, wg, wu, wd, acc_ref, accs_ref, dn_ref, dns_ref):
    for r in (512, 768, 0, 256):
        rr = slice(r, r + 256)
        dn = dot_nt(dg0[rr, :], wg[:, :512]) + dot_nt(dg1[rr, :], wg[:, 512:])
        dn = dn + dot_nt(du0[rr, :], wu[:, :512]) + dot_nt(du1[rr, :], wu[:, 512:])
        acc = dot(h0[rr, :], wd[:512, :]) + dot(h1[rr, :], wd[512:, :])
        if r < SPAN:
            dn_ref[rr, :] = dn
            acc_ref[rr, :] = acc
        else:
            dns_ref[r - SPAN : r - SPAN + 256, :] = dn.astype(BF)
            accs_ref[r - SPAN : r - SPAN + 256, :] = acc.astype(BF)


def ffn_out_call(sc, first, second, wg, wu, wd):
    flat = [whole((SPAN, WIDTH))]
    return call(
        ffn_out_body,
        "ffn_out",
        sc,
        tuple(first) + tuple(second) + (wg, wu, wd),
        [whole((SEQ, 512))] * 6 + [whole((WIDTH, SEQ))] * 2 + [whole((SEQ, WIDTH))],
        [sds((SPAN, WIDTH), F32), sds((SPAN, WIDTH)), sds((SPAN, WIDTH), F32), sds((SPAN, WIDTH))],
        flat * 4,
        [],
        24,
        (3 * 2 * SEQ * WIDTH * SEQ, 16e6, 0),
    )


def middle_body(sc, dn_ref, got_ref, m_ref, dy_ref, gain_ref, dm_ref, db_ref):
    gain = gain_ref[...]
    for r in range(0, SPAN, 128):
        rr = slice(r, r + 128)
        live = live_mask(sc, r, 128)
        m = m_ref[rr, :]
        factor = lax.rsqrt(jnp.mean(m * m, axis=-1, keepdims=True) + epsilon)
        scaled = (dn_ref[rr, :] + got_ref[rr, :].astype(F32)) * gain
        dm = jnp.where(live, dy_ref[0, rr, :].astype(F32), 0.0) + (
            factor * scaled
            - m * (factor * factor * factor) * jnp.mean(m * scaled, axis=-1, keepdims=True)
        )
        dm_ref[rr, :] = dm
        db_ref[rr, :] = dm.astype(BF)


def middle_call(sc, dn, got, m, dy, gain):
    flat = whole((SPAN, WIDTH))
    return call(
        middle_body,
        "middle",
        sc,
        (dn, got, m, dy, gain),
        [flat, flat, flat, whole((1, SPAN, WIDTH)), whole((1, WIDTH))],
        [sds((SPAN, WIDTH), F32), sds((SPAN, WIDTH))],
        [flat, flat],
        [],
        14,
        (1e6, 8e6, 1e3),
    )


def attend_back_body(sc, own, other, ot_s, lse_s, dbk, dbr, wo_s, cos_hbm, sin_hbm, *refs):
    wq, wk, wv, mine, theirs, ws, qs, ks, vs, das, ds_all, dqt, dkv, cs, ss, sem = refs
    loads = gather_rows(sc, own, other, (qs, ks, vs), sem.at[pl.ds(0, 6)])
    small = [
        pltpu.make_async_copy(src, to, sem.at[6 + n])
        for n, (src, to) in enumerate(((cos_hbm, cs), (sin_hbm, ss)))
    ]
    fetch = [
        pltpu.make_async_copy(w, ws.at[t], sem.at[10 + t]) for t, w in enumerate((wq, wk, wv))
    ]
    for cp in small + fetch:
        cp.start()
    for k, src in enumerate((dbk, dbr)):
        pos = sc[1] if k == 0 else 1 - sc[1]
        for r in range(0, SPAN, 256):
            rows = pl.ds(pl.multiple_of(pos * SPAN + r, 256), 256)
            das[rows, :] = dot_nt(src[r : r + 256, :], wo_s[...]).astype(BF)
    for cp in loads:
        cp.wait()
    for cp in small:
        cp.wait()
    lane = lax.broadcasted_iota(jnp.int32, (SEQ, 128), 1)
    key_id = lax.broadcasted_iota(jnp.int32, (256, 256), 0)
    row_id = lax.broadcasted_iota(jnp.int32, (256, 256), 1)
    keep = key_id <= row_id

    def pair(hp, carry):
        base = pl.multiple_of(hp * 128, 128)
        cols = pl.ds(base, 128)
        kt = jnp.transpose(ks[:, cols].astype(F32)).astype(BF)
        dat = jnp.transpose(das[:, cols].astype(F32))
        qm, dam, delta, lses = [], [], [], []
        for h in range(2):
            qm.append(jnp.where(lane // HEAD_DIM == h, qs[:, cols], jnp.zeros((), BF)))
            dam.append(jnp.where(lane // HEAD_DIM == h, das[:, cols], jnp.zeros((), BF)))
            rows = pl.ds(pl.multiple_of(base + 64 * h, 64), 64)
            product = dat[64 * h : 64 * h + 64, :] * ot_s[rows, :]
            delta.append(jnp.sum(product, axis=0, keepdims=True))
            lses.append(lse_s[pl.ds(2 * hp + h, 1), :])

        def scores(i, h):
            n = 256 * (i + 1)
            rows = slice(256 * i, n)
            return dot_nt(ks[:n, cols], qm[h][rows, :]), dot_nt(vs[:n, cols], dam[h][rows, :])

        def soften(i, h, st, dp):
            n = 256 * (i + 1)
            rows = slice(256 * i, n)
            p = jnp.exp(st - lses[h][:, rows])
            diag = jnp.where(keep, p[n - 256 :, :], 0.0)
            p = diag if i == 0 else jnp.concatenate([p[: n - 256, :], diag], axis=0)
            return p.astype(BF), (p * (dp - delta[h][:, rows])).astype(BF)

        def finish(i, h, p, ds):
            n = 256 * (i + 1)
            rows = slice(256 * i, n)
            half = slice(64 * h, 64 * h + 64)
            dv = dot(p, dam[h][rows, :])
            dk = dot(ds, qm[h][rows, :])
            dqt[half, rows] = dot(kt[half, :n], ds)
            if (i, h) == (3, 0):
                dkv[0] = dk
                dkv[1] = dv
            else:
                dkv[0, :n] += dk
                dkv[1, :n] += dv

        tasks = [(i, h) for i in (3, 2, 1, 0) for h in range(2)]
        now, waiting = scores(*tasks[0]), None
        for k, task in enumerate(tasks):
            ahead = scores(*tasks[k + 1]) if k + 1 < len(tasks) else None
            parts = soften(*task, *now)
            if waiting is not None:
                finish(*waiting)
            waiting, now = task + parts, ahead
        finish(*waiting)
        dq = jnp.transpose(dqt[...]) * (HEAD_DIM**-0.5)
        ds_all[0, :, cols] = turn(dq, cs[...], -ss[...]).astype(BF)
        ds_all[1, :, cols] = turn(dkv[0], cs[...], -ss[...]).astype(BF)
        ds_all[2, :, cols] = dkv[1].astype(BF)
        return carry

    lax.fori_loop(0, 3, pair, 0)
    row = pl.multiple_of(sc[1] * SPAN, SPAN)
    row_other = pl.multiple_of((1 - sc[1]) * SPAN, SPAN)
    stores = [
        pltpu.make_async_copy(ds_all.at[:, pl.ds(row_other, SPAN), :], theirs, sem.at[8]),
        pltpu.make_async_copy(ds_all.at[:, pl.ds(row, SPAN), :], mine, sem.at[9]),
    ]
    for cp in stores:
        cp.start()
    for cp in stores + fetch:
        cp.wait()


def attend_back_call(sc, own, other, ot, lse, dbk, dbr, wo, cosine, sine, wq, wk, wv):
    return call(
        attend_back_body,
        "attend_back",
        sc,
        (own, other, ot, lse, dbk, dbr, wo, cosine, sine, wq, wk, wv),
        [hbm(), hbm(), whole((GROUP, SEQ)), whole((8, SEQ))]
        + [whole((SPAN, WIDTH))] * 2
        + [whole((GROUP, WIDTH))]
        + [far_hbm()] * 5,
        [sds((3, SPAN, GROUP))] * 2 + [sds((3, WIDTH, WIDTH))],
        [hbm()] * 3,
        [pltpu.VMEM((SEQ, GROUP), BF)] * 4
        + [
            pltpu.VMEM((3, SEQ, GROUP), BF),
            pltpu.VMEM((128, SEQ), F32),
            pltpu.VMEM((2, SEQ, 128), F32),
            pltpu.VMEM((SEQ, 128), F32),
            pltpu.VMEM((SEQ, 128), F32),
            pltpu.SemaphoreType.DMA((13,)),
        ],
        22,
        (6 * 10 * SEQ * SEQ * 64, 10e6, 4e6),
    )


def square_body(sc, nk, nr, ak, at, ck, ct, bk, br, dk, dr, sa_ref, ka_ref, sb_ref, kb_ref, res):
    own = pl.ds(pl.multiple_of(sc[0] * GROUP, 128), GROUP)
    other = pl.ds(pl.multiple_of((1 - sc[0]) * GROUP, 128), GROUP)
    res[0, own, :] = over_rows(ak[...], at[...], bk[:, own], br[:, own])
    res[0, other, :] = over_rows(ck[...], ct[...], bk[:, own], br[:, own])
    spread(sc, res.at[0], 0, 2, 48, sa_ref, ka_ref, 0)
    for n, t in enumerate((2, 0, 1)):
        place = res.at[(n + 1) % 2]
        place[...] = over_rows(nk[...], nr[...], dk[t], dr[t])
        if n == 0:
            spread(sc, place, 0, 2, 48, sa_ref, ka_ref, 96)
        else:
            spread(sc, place, 0, 2, 48, sb_ref, kb_ref, 96 * t)


def square_call(sc, *args):
    flat = [whole((SPAN, WIDTH))] * 2
    return call(
        square_body,
        "square",
        sc,
        args,
        flat + [whole((SPAN, GROUP))] * 4 + flat + [whole((3, SPAN, GROUP))] * 2,
        [sds((8, 96, GROUP))] * 4,
        [whole((8, 96, GROUP))] * 4,
        [pltpu.VMEM((2, WIDTH, GROUP), F32)],
        16,
        (4 * 2 * SEQ * WIDTH * GROUP, 12e6, 0),
    )


def input_grad_body(sc, x_ref, gain_ref, dm_ref, m_ref, acc_ref, got_ref, dk_s, dr_s, ws, *refs):
    lay_ref, o_ref = refs
    for r in range(0, SPAN, 256):
        rr = slice(r, r + 256)
        out = m_ref[rr, :] + acc_ref[rr, :] + got_ref[rr, :].astype(F32)
        lay_ref[0, rr, :] = jnp.where(live_mask(sc, r, 256), out, 0.0).astype(BF)
    own_cols = pl.multiple_of(sc[0] * GROUP, 128)
    other_cols = pl.multiple_of((1 - sc[0]) * GROUP, 128)
    gain = gain_ref[...]
    for r in range(0, SPAN, 256):
        rr = slice(r, r + 256)
        dn = dot_nt(dk_s[0, rr, :], ws[0, :, pl.ds(own_cols, GROUP)])
        dn = dn + dot_nt(dr_s[0, rr, :], ws[0, :, pl.ds(other_cols, GROUP)])
        for t in (1, 2):
            dn = dn + dot_nt(dk_s[t, rr, :], ws[t, :, pl.ds(own_cols, GROUP)])
            dn = dn + dot_nt(dr_s[t, rr, :], ws[t, :, pl.ds(other_cols, GROUP)])
        live = live_mask(sc, r, 256)
        x = jnp.where(live, x_ref[0, rr, :].astype(F32), 0.0)
        factor = lax.rsqrt(jnp.mean(x * x, axis=-1, keepdims=True) + epsilon)
        scaled = dn * gain
        dx = dm_ref[rr, :] + (
            factor * scaled
            - x * (factor * factor * factor) * jnp.mean(x * scaled, axis=-1, keepdims=True)
        )
        o_ref[0, rr, :] = jnp.where(live, dx, 0.0).astype(BF)


def input_grad_call(sc, tokens, gain, dm, m, acc, got, dk, dr, ws):
    full = whole((1, SPAN, WIDTH))
    flat = whole((SPAN, WIDTH))
    return call(
        input_grad_body,
        "input_grad",
        sc,
        (tokens, gain, dm, m, acc, got, dk, dr, ws),
        [full, whole((1, WIDTH)), flat, flat, flat, flat]
        + [whole((3, SPAN, GROUP))] * 2
        + [whole((3, WIDTH, WIDTH))],
        [sds((1, SPAN, WIDTH))] * 2,
        [full] * 2,
        [],
        20,
        (3 * 2 * SPAN * WIDTH * WIDTH, 14e6, 1e3),
    )


def add_pieces(sc, count, sums, name):
    rows, cols = sums[0][0][0].shape[1:]
    arrays = [array for stack in sums for array, _ in stack]
    picks = [pick for stack in sums for _, pick in stack]

    def body(sc_ref, *refs):
        at = 0
        for n, stack in enumerate(sums):
            total = refs[at][0].astype(F32)
            for ref in refs[at + 1 : at + len(stack)]:
                total = total + ref[0].astype(F32)
            refs[-1][0, n * rows : (n + 1) * rows, :] = total.astype(BF)
            at += len(stack)

    def spec(pick):
        block, row = pick
        return pl.BlockSpec((1, rows, cols), lambda j, sc_ref: (block(sc_ref, j), row, 0))

    high = rows * len(sums)
    return pl.pallas_call(
        body,
        name=name,
        out_shape=sds((count, high, cols)),
        grid_spec=pltpu.PrefetchScalarGridSpec(
            num_scalar_prefetch=1,
            grid=(count,),
            in_specs=[spec(pick) for pick in picks],
            out_specs=pl.BlockSpec((1, high, cols), lambda j, sc_ref: (j, 0, 0)),
        ),
        compiler_params=pltpu.CompilerParams(vmem_limit_bytes=6 * MIB),
        cost_estimate=pl.CostEstimate(
            flops=int(0 if name == "g0_b" else ADD_COST), bytes_accessed=1000, transcendentals=0
        ),
    )(sc, *arrays)


def row_block(rows, cols):
    return pl.BlockSpec((rows, cols), lambda i, sc: (sc[6], 0))


def row_of(column):
    column = jnp.concatenate([column, jnp.zeros((32, 1), F32)], axis=0)
    return jnp.transpose(jnp.broadcast_to(column, (128, 128)))[0, :96]


def collect_halves(sc, group, full):
    for n in range(4):
        core, k = divmod(n, 2)
        parity = sc[0] if core == 0 else 1 - sc[0]
        first = sc[3] if core == 0 else sc[7]
        first = 1 - first if k == 1 else first
        for h in range(2):
            full[parity, first, 288 * h : 288 * h + 288, :] = group[n][h]


def collect(sc, group, full, row, size):
    for n in range(8):
        core, k = divmod(n, 4)
        parity = sc[0] if core == 0 else 1 - sc[0]
        first, second = (sc[3], sc[7]) if core == 0 else (sc[7], sc[3])
        first = 1 - first if k in (1, 3) else first
        second = 1 - second if k in (2, 3) else second
        rows = pl.ds(pl.multiple_of(second * size, 16), size)
        full[parity, first, rows, :] = group[n][0, row : row + size, :]


def ffn_result_body(sc, *refs):
    wg_ref, wu_ref, gain_ref, gate_ref, up_ref, down_ref, gg_ref, full = refs[12:]
    collect_halves(sc, refs[:4], full.at[0])
    collect(sc, refs[4:12], full.at[1], 0, 288)
    for half in range(2):
        for bit in range(2):
            rows = slice(48 * bit, 48 * bit + 48)
            for parity in range(2):
                for base, ref in ((0, gate_ref), (192, up_ref)):
                    for ct in range(2):
                        lo = pl.multiple_of(base + ct * 96 + sc[0] * 48, 16)
                        block = full[half, parity, bit, pl.ds(lo, 48), :].astype(F32)
                        for q in range(2):
                            col = 512 * (2 * ct + q) + 128 * half + 256 * parity
                            ref[rows, col : col + 128] = block[:, 128 * q : 128 * q + 128]
            lo = 128 * half + 64 * bit
            for t in range(3):
                down_ref[lo : lo + 64, 256 * t : 256 * t + 256] = full[
                    half, sc[0], bit, 384 + t * 64 : 448 + t * 64, :
                ].astype(F32)
    gate = jnp.sum(wg_ref[...].astype(F32) * gate_ref[...], axis=-1, keepdims=True)
    up = jnp.sum(wu_ref[...].astype(F32) * up_ref[...], axis=-1, keepdims=True)
    gg_ref[...] = row_of((gate + up) / gain_ref[...])


def ffn_result_call(sc, first, second, wg, wu, gain):
    return call(
        ffn_result_body,
        "ffn_result",
        sc,
        tuple(first) + tuple(second) + (wg, wu, gain),
        [whole((2, 288, 256))] * 4 + [whole((1, 288, 256))] * 8 + [row_block(96, HID)] * 2 + [row_block(96, 1)],
        [sds((96, HID), F32), sds((96, HID), F32), sds((256, WIDTH), F32), sds((96,), F32)],
        [whole((96, HID)), whole((96, HID)), whole((256, WIDTH)), whole((96,))],
        [pltpu.VMEM((2, 2, 2, 576, 256), BF)],
        14,
        (1e6, 6e6, 0),
    )


def square_result_body(sc, *refs):
    group = refs[:8]
    weights = refs[8:11]
    gain_ref = refs[11]
    outs = refs[12:16]
    gg_ref, full = refs[16:]
    order = ((3, 2), (0, 1))
    for n in range(2):
        collect(sc, group, full.at[n], 96 * n, 96)
        for bit in range(2):
            rows = slice(48 * bit, 48 * bit + 48)
            for parity in range(2):
                cols = slice(GROUP * parity, GROUP * parity + GROUP)
                for t in range(2):
                    lo = pl.multiple_of(t * 96 + sc[0] * 48, 16)
                    block = full[n, parity, bit, pl.ds(lo, 48), :]
                    outs[order[n][t]][rows, cols] = block.astype(F32)
    total = jnp.zeros((96, 1), F32)
    for t in range(3):
        total = total + jnp.sum(weights[t][...].astype(F32) * outs[t][...], axis=-1, keepdims=True)
    gg_ref[...] = row_of(total / gain_ref[...])


def square_result_call(sc, group, wq, wk, wv, gain):
    return call(
        square_result_body,
        "square_result",
        sc,
        tuple(group) + (wq, wk, wv, gain),
        [whole((1, 192, GROUP))] * 8 + [row_block(96, WIDTH)] * 3 + [row_block(96, 1)],
        [sds((96, WIDTH), F32)] * 4 + [sds((96,), F32)],
        [whole((96, WIDTH))] * 4 + [whole((96,))],
        [pltpu.VMEM((2, 2, 2, 192, GROUP), BF)],
        8,
        (1e6, 4e6, 0),
    )


class Chain:
    def __init__(self, sc):
        self.sc = sc

    def next(self, *deps):
        self.sc = after(self.sc, *deps)
        return self.sc


class Reduction:
    def __init__(self, chain, send, keep, name):
        self.chain = chain
        self.send = send
        self.name = name
        self.stacks = [[[keep, 0]]]
        self.flight = None

    def start(self):
        self.fly(after(self.send, self.chain.sc), "first")

    def fly(self, rows, kind):
        self.flight = exchange(rows, kind)

    def land(self):
        if self.flight is not None:
            for n, stack in enumerate(self.stacks):
                stack.append([self.flight, n])
        self.flight = None

    def add(self, count, picks, tag):
        self.land()
        sums = []
        for stack in self.stacks:
            blocks = ([picks[0]] + picks)[-len(stack) :]
            sums.append([(array, (pick, row)) for (array, row), pick in zip(stack, blocks)])
        arrays = [array for stack in sums for array, _ in stack]
        out = add_pieces(self.chain.next(*arrays), count, sums, self.name + tag)
        self.chain.next(out)
        return out

    def second(self):
        pick = lambda t, j: j * 2 + 1 - t[7]
        self.fly(self.add(4, [pick], "_b"), "second")

    def near(self):
        pick = lambda t, j: (1 - t[4]) * 4 + j * 2 + t[7]
        self.fly(self.add(2, [pick, lambda t, j: (1 - t[4]) * 2 + j], "_c"), "near")

    def far(self):
        pick = lambda t, j: t[4] * 4 + (1 - t[5]) * 2 + t[7]
        picks = [pick, lambda t, j: t[4] * 2 + 1 - t[5], lambda t, j: 1 - t[5]]
        self.fly(self.add(1, picks, "_d"), "far")

    def total(self):
        pick = lambda t, j: t[4] * 4 + t[5] * 2 + t[7]
        picks = [pick, lambda t, j: t[4] * 2 + t[5], lambda t, j: t[5], lambda t, j: 0]
        own = self.add(1, picks, "_e")
        self.quarters = [own] + [exchange(own, kind) for kind in ("first", "second", "across")]

    def result(self):
        late = [after(quarter, self.chain.sc) for quarter in self.quarters]
        return self.quarters + [exchange(quarter, "core") for quarter in late]


class Straight(Reduction):
    def near(self):
        pick = lambda t, j: (1 - t[4]) * 4 + j
        self.fly(self.add(4, [pick], "_b"), "near")

    def far(self):
        pick = lambda t, j: t[4] * 4 + (1 - t[5]) * 2 + j
        self.fly(self.add(2, [pick, lambda t, j: (1 - t[5]) * 2 + j], "_c"), "far")

    def second(self):
        pick = lambda t, j: t[4] * 4 + t[5] * 2 + j
        own = self.add(2, [pick, lambda t, j: t[5] * 2 + j, lambda t, j: j], "_d")
        self.stacks = [[[own, 0]]]
        self.fly(own, "second")

    def total(self):
        own = self.add(2, [lambda t, j: j], "_e")
        self.quarters = [own, exchange(own, "first")]


def join(first, second):
    both = Reduction(first.chain, None, None, first.name + second.name)
    first.land()
    second.land()
    both.stacks = first.stacks + second.stacks
    return both


def fast_step(
    tokens,
    lengths,
    owner,
    w_query,
    w_key,
    w_value,
    w_out,
    w_gate,
    w_up,
    w_down,
    gain_attn,
    gain_mlp,
    cotangent,
):
    batch, seq, core = (lax.axis_index(name) for name in AXES)
    low, high = batch % 2, batch // 2
    swap = core == 0
    slot = jnp.arange(8, dtype=jnp.int32)
    fixed = (
        core,
        core,
        0,
        jnp.where(swap, low, high),
        seq % 2,
        seq // 2,
        seq * 2 + core,
        jnp.where(swap, high, low),
    )
    sc = jnp.zeros((8,), jnp.int32)
    for n, value in enumerate(fixed):
        sc = jnp.where(slot == n, value, sc)
    first_pos = jnp.broadcast_to(owner[0, :1], (8,))
    sc = jnp.where(slot == 1, jnp.where(swap, first_pos, 1 - first_pos), sc)
    sc = jnp.where(slot == 2, jnp.broadcast_to(lengths, (8,)), sc)
    tables = position_tables(SEQ)
    cosine, sine = jnp.asarray(tables[0]), jnp.asarray(tables[1])
    gain_row = gain_attn.reshape(1, WIDTH)
    gain_mlp_row = gain_mlp.reshape(1, WIDTH)
    qkv_w = (w_query, w_key, w_value)
    ffn_w = (w_gate, w_up, w_down)
    chain = Chain(sc)

    qkv_send, n1 = qkv_call(chain.sc, tokens, gain_row, cosine, sine, *qkv_w, True)
    qkv_other = exchange(qkv_send, "core")
    (qkv_own,) = qkv_call(chain.next(n1), n1, gain_row, cosine, sine, *qkv_w, False)
    n1_other = exchange(n1, "core")
    dy_other = exchange(cotangent, "core")
    attn_t, lse, attn_own, attn_send, wo_v, *ffn_v = attend_call(
        chain.next(qkv_own), qkv_own, qkv_other, w_out, *ffn_w
    )
    attn_other = exchange(attn_send, "core")
    attn_rest = exchange(attn_own, "core")
    middle, n2 = proj_call(
        chain.next(lse, n1_other, dy_other), tokens, attn_own, attn_other, gain_mlp_row, wo_v
    )
    n2_other = exchange(n2, "core")
    rows = (n2, n2_other, cotangent, dy_other)
    send0, keep0, *acts0 = ffn_call(chain.next(n2, attn_rest), 0, *rows, *ffn_v)
    g0 = Straight(chain, send0, keep0, "g0")
    g0.start()
    send1, keep1, *acts1 = ffn_call(chain.next(acts0[0]), 1, *rows, *ffn_v)
    g1 = Reduction(chain, send1, keep1, "g1")
    g1.start()
    acc, acc_send, dn, dn_send = ffn_out_call(chain.next(acts1[0]), acts0, acts1, *ffn_v)
    dn_other = exchange(dn_send, "core")
    chain.next(dn_send)
    g0.near()
    d_middle, db = middle_call(chain.next(dn_other), dn, dn_other, middle, cotangent, gain_mlp_row)
    db_other = exchange(db, "core")
    acc_other = exchange(after(acc_send, db_other), "core")
    d_own, d_send, qkv_v = attend_back_call(
        chain.next(db),
        qkv_own,
        qkv_other,
        attn_t,
        lse,
        db,
        db_other,
        wo_v,
        cosine,
        sine,
        *qkv_w,
    )
    d_other = exchange(d_send, "core")
    chain.next(d_own, g0.flight, g1.flight)
    g1.second()
    g0.far()
    attn = (attn_own, attn_send, attn_other, attn_rest)
    send2, keep2, send3, keep3 = square_call(
        chain.sc, n1, n1_other, *attn, db, db_other, d_own, d_send
    )
    g2 = Reduction(chain, send2, keep2, "g2")
    g3 = Reduction(chain, send3, keep3, "g3")
    g2.start()
    g3.start()
    chain.next(send3)
    layer_out, input_grad = input_grad_call(
        chain.next(acc_other, d_other),
        tokens,
        gain_row,
        d_middle,
        middle,
        acc,
        acc_other,
        d_own,
        d_other,
        qkv_v,
    )
    chain.next(input_grad)
    g0.second()
    g1.near()
    g2.second()
    g1.far()
    g3.second()
    g2.near()
    g0.total()
    g3.near()
    g2.far()
    g3.far()
    g1.total()
    g23 = join(g2, g3)
    g23.total()
    first, second, third = g0.result(), g1.result(), g23.result()
    chain.next(*g23.quarters)
    gate, up, down, gain_m = ffn_result_call(
        chain.sc, first, second, w_gate, w_up, gain_mlp.reshape(WIDTH, 1)
    )
    chain.next(gain_m)
    query, key, value, out, gain_a = square_result_call(
        chain.sc, third, *qkv_w, gain_attn.reshape(WIDTH, 1)
    )
    return (
        layer_out,
        input_grad,
        query,
        key,
        value,
        out,
        gate,
        up,
        down,
        gain_a,
        gain_m,
    )


def solution(mesh):
    in_specs = (
        P(("batch", "seq"), "seqb", None),
        P(("batch", "seq")),
        P(("batch", "seq"), None),
        P(),
        P(),
        P(),
        P(),
        P(),
        P(),
        P(),
        P(),
        P(),
        P(("batch", "seq"), "seqb", None),
    )
    out_specs = (
        P(("batch", "seq"), "seqb", None),
        P(("batch", "seq"), "seqb", None),
        P(("seq", "seqb"), None),
        P(("seq", "seqb"), None),
        P(("seq", "seqb"), None),
        P(("seq", "seqb"), None),
        P(("seq", "seqb"), None),
        P(("seq", "seqb"), None),
        P(("seq", "seqb"), None),
        P(("seq", "seqb")),
        P(("seq", "seqb")),
    )
    step = fast_step if fast_layout(mesh) else general_step
    return jax.shard_map(step, mesh=mesh, in_specs=in_specs, out_specs=out_specs, check_vma=False)
```

```python
import functools
import math

import jax
import jax.numpy as jnp
import numpy as np
from jax import lax
from jax.experimental import pallas as pl
from jax.experimental.pallas import tpu as pltpu
from jax.sharding import PartitionSpec as P

HEADS = 12
HEAD_DIM = 64


epsilon = 1e-05
rope_base = 10000.0
masked_score = -1e30


def rms_forward(rows, gain):
    factor = lax.rsqrt(jnp.mean(rows * rows, axis=-1, keepdims=True) + epsilon)
    return (rows * factor * gain, factor)


def rms_backward(rows, factor, gain, upstream):
    scaled = upstream * gain
    return factor * scaled - rows * (factor * factor * factor) * jnp.mean(
        rows * scaled, axis=-1, keepdims=True
    )


def rotation_tables(positions):
    half = HEAD_DIM // 2
    freq = rope_base ** (-(2.0 * jnp.arange(half, dtype=jnp.float32)) / HEAD_DIM)
    angles = positions.astype(jnp.float32)[..., None] * freq
    return (jnp.cos(angles), jnp.sin(angles))


def split_heads(rows):
    return rows.reshape(rows.shape[0], rows.shape[1], HEADS, HEAD_DIM)


def rotate(rows, cosine, sine, inverse):
    shaped = split_heads(rows)
    half = HEAD_DIM // 2
    first = shaped[..., :half]
    second = shaped[..., half:]
    cos_part = cosine[:, :, None, :]
    sin_part = sine[:, :, None, :]
    if inverse:
        turned = jnp.concatenate(
            [first * cos_part + second * sin_part, second * cos_part - first * sin_part], axis=-1
        )
    else:
        turned = jnp.concatenate(
            [first * cos_part - second * sin_part, second * cos_part + first * sin_part], axis=-1
        )
    return turned.reshape(rows.shape)


def range_positions(owner, count, span):
    offsets = jnp.arange(span, dtype=jnp.int32)
    return (owner[:, :, None] * span + offsets[None, None, :]).reshape(owner.shape[0], count)


def fold_keys(parts, combine, initial):
    return combine(
        initial,
        (
            lax.all_gather(parts[0], "seqb", axis=1, tiled=True),
            lax.all_gather(parts[1], "seqb", axis=1, tiled=True),
        ),
        jnp.int32(0),
    )


def general_step(
    tokens,
    lengths,
    owner,
    w_query,
    w_key,
    w_value,
    w_out,
    w_gate,
    w_up,
    w_down,
    gain_attn,
    gain_mlp,
    cotangent,
):
    seqs, span, width = tokens.shape
    scale = HEAD_DIM ** (-0.5)
    place = lax.axis_index("seqb")
    own_block = lax.dynamic_slice_in_dim(owner, place, 1, 1)
    local_pos = own_block * span + jnp.arange(span, dtype=jnp.int32)[None, :]
    local_live = local_pos < lengths[:, None]
    live_rows = local_live[:, :, None]
    inputs = jnp.where(live_rows, tokens.astype(jnp.float32), 0.0)
    normed, factor_attn = rms_forward(inputs, gain_attn)
    normed_low = normed.astype(jnp.bfloat16)
    cosine, sine = rotation_tables(local_pos)
    query_pre = jnp.einsum("scd,de->sce", normed_low, w_query, preferred_element_type=jnp.float32)
    key_pre = jnp.einsum("scd,de->sce", normed_low, w_key, preferred_element_type=jnp.float32)
    value_low = jnp.einsum(
        "scd,de->sce", normed_low, w_value, preferred_element_type=jnp.float32
    ).astype(jnp.bfloat16)
    query_rot = rotate(query_pre, cosine, sine, False).astype(jnp.bfloat16)
    key_rot = rotate(key_pre, cosine, sine, False).astype(jnp.bfloat16)
    query_heads = split_heads(query_rot)
    key_heads = split_heads(key_rot)
    value_heads = split_heads(value_low)

    def attend(state, piece, start):
        keys, values = piece
        count = keys.shape[1]
        key_pos = range_positions(owner, count, span)
        key_live = key_pos < lengths[:, None]
        stride = math.gcd(count, 512)

        def attend_one_block(index, inner):
            offset = index * stride
            key_block = split_heads(lax.dynamic_slice_in_dim(keys, offset, stride, 1))
            value_block = split_heads(lax.dynamic_slice_in_dim(values, offset, stride, 1))
            pos_block = lax.dynamic_slice_in_dim(key_pos, offset, stride, 1)
            live_block = lax.dynamic_slice_in_dim(key_live, offset, stride, 1)
            allowed = (
                (pos_block[:, None, :] <= local_pos[:, :, None])
                & live_block[:, None, :]
                & local_live[:, :, None]
            )

            def attend_update(carried):
                peak, total, summed = carried
                scores = (
                    jnp.einsum(
                        "sqhd,skhd->shqk",
                        query_heads,
                        key_block,
                        preferred_element_type=jnp.float32,
                    )
                    * scale
                )
                mask = allowed[:, None, :, :]
                new_peak = jnp.maximum(
                    peak, jnp.max(jnp.where(mask, scores, masked_score), axis=-1)
                )
                weights = jnp.where(mask, jnp.exp(scores - new_peak[..., None]), 0.0)
                factor = jnp.exp(peak - new_peak)
                total = total * factor + jnp.sum(weights, axis=-1)
                term = jnp.einsum(
                    "shqk,skhd->sqhd",
                    weights.astype(jnp.bfloat16),
                    value_block,
                    preferred_element_type=jnp.float32,
                )
                summed = (
                    split_heads(summed) * jnp.transpose(factor, (0, 2, 1))[..., None] + term
                ).reshape(summed.shape)
                return (new_peak, total, summed)

            return lax.cond(jnp.any(allowed), attend_update, lambda carried: carried, inner)

        return lax.fori_loop(0, count // stride, attend_one_block, state)

    start_state = (
        jnp.full((seqs, HEADS, span), masked_score, jnp.float32),
        jnp.zeros((seqs, HEADS, span), jnp.float32),
        jnp.zeros((seqs, span, width), jnp.float32),
    )
    peak, total, summed = fold_keys((key_rot, value_low), attend, start_state)
    safe_total = jnp.where(local_live[:, None, :], total, 1.0)
    attn = split_heads(summed) / jnp.transpose(safe_total, (0, 2, 1))[..., None]
    attn = jnp.where(local_live[:, :, None, None], attn, 0.0).reshape(seqs, span, width)
    log_total = jnp.where(local_live[:, None, :], peak + jnp.log(safe_total), 0.0)
    attn_low = attn.astype(jnp.bfloat16)
    middle = inputs + jnp.einsum("scd,de->sce", attn_low, w_out, preferred_element_type=jnp.float32)
    normed_mlp, factor_mlp = rms_forward(middle, gain_mlp)
    normed_mlp_low = normed_mlp.astype(jnp.bfloat16)
    gate = jnp.einsum("scd,df->scf", normed_mlp_low, w_gate, preferred_element_type=jnp.float32)
    up_proj = jnp.einsum("scd,df->scf", normed_mlp_low, w_up, preferred_element_type=jnp.float32)
    hidden = (jax.nn.silu(gate) * up_proj).astype(jnp.bfloat16)
    out = middle + jnp.einsum("scf,fd->scd", hidden, w_down, preferred_element_type=jnp.float32)
    layer_out = jnp.where(live_rows, out, 0.0).astype(jnp.bfloat16)
    upstream = jnp.where(live_rows, cotangent, jnp.zeros_like(cotangent))
    grad_down = jnp.einsum("scf,scd->fd", hidden, upstream, preferred_element_type=jnp.float32)
    d_hidden = jnp.einsum("scd,fd->scf", upstream, w_down, preferred_element_type=jnp.float32)
    sigmoid_gate = jax.nn.sigmoid(gate)
    d_gate = (d_hidden * up_proj * sigmoid_gate * (1.0 + gate * (1.0 - sigmoid_gate))).astype(
        jnp.bfloat16
    )
    d_up = (d_hidden * gate * sigmoid_gate).astype(jnp.bfloat16)
    grad_gate = jnp.einsum(
        "scd,scf->df", normed_mlp_low, d_gate, preferred_element_type=jnp.float32
    )
    grad_up = jnp.einsum("scd,scf->df", normed_mlp_low, d_up, preferred_element_type=jnp.float32)
    d_normed_mlp = jnp.einsum(
        "scf,df->scd", d_gate, w_gate, preferred_element_type=jnp.float32
    ) + jnp.einsum("scf,df->scd", d_up, w_up, preferred_element_type=jnp.float32)
    grad_gain_mlp = jnp.sum(d_normed_mlp * (middle * factor_mlp), axis=(0, 1))
    d_middle = upstream.astype(jnp.float32) + rms_backward(
        middle, factor_mlp, gain_mlp, d_normed_mlp
    )
    d_branch = d_middle.astype(jnp.bfloat16)
    grad_out = jnp.einsum("scd,sce->de", attn_low, d_branch, preferred_element_type=jnp.float32)
    d_attn = jnp.einsum("sce,de->scd", d_branch, w_out, preferred_element_type=jnp.float32).astype(
        jnp.bfloat16
    )
    first_done = (grad_out, grad_gate, grad_up, grad_down, grad_gain_mlp)
    delta = jnp.sum(split_heads(d_attn.astype(jnp.float32) * attn), axis=-1)
    delta_heads = jnp.transpose(delta, (0, 2, 1))
    grad_heads = split_heads(d_attn)

    def query_grads(state, piece, start):
        keys, values = piece
        count = keys.shape[1]
        key_pos = range_positions(owner, count, span)
        key_live = key_pos < lengths[:, None]
        stride = math.gcd(count, 512)

        def query_one_block(index, inner):
            offset = index * stride
            key_block = split_heads(lax.dynamic_slice_in_dim(keys, offset, stride, 1))
            value_block = split_heads(lax.dynamic_slice_in_dim(values, offset, stride, 1))
            pos_block = lax.dynamic_slice_in_dim(key_pos, offset, stride, 1)
            live_block = lax.dynamic_slice_in_dim(key_live, offset, stride, 1)
            allowed = (
                (pos_block[:, None, :] <= local_pos[:, :, None])
                & live_block[:, None, :]
                & local_live[:, :, None]
            )

            def query_update(carried):
                scores = (
                    jnp.einsum(
                        "sqhd,skhd->shqk",
                        query_heads,
                        key_block,
                        preferred_element_type=jnp.float32,
                    )
                    * scale
                )
                probs = jnp.where(
                    allowed[:, None, :, :], jnp.exp(scores - log_total[..., None]), 0.0
                )
                d_probs = jnp.einsum(
                    "sqhd,skhd->shqk", grad_heads, value_block, preferred_element_type=jnp.float32
                )
                d_scores = (probs * (d_probs - delta_heads[..., None])).astype(jnp.bfloat16)
                term = (
                    jnp.einsum(
                        "shqk,skhd->sqhd", d_scores, key_block, preferred_element_type=jnp.float32
                    )
                    * scale
                )
                return carried + term.reshape(carried.shape)

            return lax.cond(jnp.any(allowed), query_update, lambda carried: carried, inner)

        return lax.fori_loop(0, count // stride, query_one_block, state)

    zero_query = jnp.zeros((seqs, span, width), jnp.float32)
    d_query = fold_keys((key_rot, value_low), query_grads, zero_query)
    lse_all, delta_all = (
        lax.all_gather(jnp.transpose(log_total, (0, 2, 1)), "seqb", axis=1, tiled=True),
        lax.all_gather(delta, "seqb", axis=1, tiled=True),
    )
    zero_rows = jnp.zeros((seqs, span, width), jnp.float32)
    queries = lax.all_gather(query_rot, "seqb", axis=1, tiled=True)
    d_rows = lax.all_gather(d_attn, "seqb", axis=1, tiled=True)
    count = queries.shape[1]
    row_pos = range_positions(owner, count, span)
    row_live = row_pos < lengths[:, None]
    stride = math.gcd(count, 512)

    def key_one_block(index, inner):
        offset = index * stride
        query_block = split_heads(lax.dynamic_slice_in_dim(queries, offset, stride, 1))
        grad_block = split_heads(lax.dynamic_slice_in_dim(d_rows, offset, stride, 1))
        pos_block = lax.dynamic_slice_in_dim(row_pos, offset, stride, 1)
        live_block = lax.dynamic_slice_in_dim(row_live, offset, stride, 1)
        lse_block = jnp.transpose(lax.dynamic_slice_in_dim(lse_all, offset, stride, 1), (0, 2, 1))
        delta_block = jnp.transpose(
            lax.dynamic_slice_in_dim(delta_all, offset, stride, 1), (0, 2, 1)
        )
        allowed = (
            (local_pos[:, None, :] <= pos_block[:, :, None])
            & local_live[:, None, :]
            & live_block[:, :, None]
        )

        def key_update(carried):
            d_key, d_value = carried
            scores = (
                jnp.einsum(
                    "sqhd,skhd->shqk", query_block, key_heads, preferred_element_type=jnp.float32
                )
                * scale
            )
            probs = jnp.where(allowed[:, None, :, :], jnp.exp(scores - lse_block[..., None]), 0.0)
            value_term = jnp.einsum(
                "shqk,sqhd->skhd",
                probs.astype(jnp.bfloat16),
                grad_block,
                preferred_element_type=jnp.float32,
            )
            d_probs = jnp.einsum(
                "sqhd,skhd->shqk", grad_block, value_heads, preferred_element_type=jnp.float32
            )
            d_scores = (probs * (d_probs - delta_block[..., None])).astype(jnp.bfloat16)
            key_term = (
                jnp.einsum(
                    "shqk,sqhd->skhd", d_scores, query_block, preferred_element_type=jnp.float32
                )
                * scale
            )
            return (
                d_key + key_term.reshape(d_key.shape),
                d_value + value_term.reshape(d_value.shape),
            )

        return lax.cond(jnp.any(allowed), key_update, lambda carried: carried, inner)

    d_key, d_value = lax.fori_loop(0, count // stride, key_one_block, (zero_rows, zero_rows))
    d_query_pre = rotate(d_query, cosine, sine, True).astype(jnp.bfloat16)
    d_key_pre = rotate(d_key, cosine, sine, True).astype(jnp.bfloat16)
    d_value_low = d_value.astype(jnp.bfloat16)
    grad_query = jnp.einsum(
        "scd,sce->de", normed_low, d_query_pre, preferred_element_type=jnp.float32
    )
    grad_key = jnp.einsum("scd,sce->de", normed_low, d_key_pre, preferred_element_type=jnp.float32)
    grad_value = jnp.einsum(
        "scd,sce->de", normed_low, d_value_low, preferred_element_type=jnp.float32
    )
    d_normed = jnp.einsum("sce,de->scd", d_query_pre, w_query, preferred_element_type=jnp.float32)
    d_normed = d_normed + jnp.einsum(
        "sce,de->scd", d_key_pre, w_key, preferred_element_type=jnp.float32
    )
    d_normed = d_normed + jnp.einsum(
        "sce,de->scd", d_value_low, w_value, preferred_element_type=jnp.float32
    )
    grad_gain_attn = jnp.sum(d_normed * (inputs * factor_attn), axis=(0, 1))
    d_inputs = d_middle + rms_backward(inputs, factor_attn, gain_attn, d_normed)
    input_grad = jnp.where(live_rows, d_inputs, 0.0).astype(jnp.bfloat16)
    summed_parts = (
        lax.psum_scatter(grad_query, ("seq", "seqb"), scatter_dimension=0, tiled=True),
        lax.psum_scatter(grad_key, ("seq", "seqb"), scatter_dimension=0, tiled=True),
        lax.psum_scatter(grad_value, ("seq", "seqb"), scatter_dimension=0, tiled=True),
        lax.psum_scatter(grad_gain_attn, ("seq", "seqb"), scatter_dimension=0, tiled=True),
        lax.psum_scatter(first_done[0], ("seq", "seqb"), scatter_dimension=0, tiled=True),
        lax.psum_scatter(first_done[1], ("seq", "seqb"), scatter_dimension=0, tiled=True),
        lax.psum_scatter(first_done[2], ("seq", "seqb"), scatter_dimension=0, tiled=True),
        lax.psum_scatter(first_done[3], ("seq", "seqb"), scatter_dimension=0, tiled=True),
        lax.psum_scatter(first_done[4], ("seq", "seqb"), scatter_dimension=0, tiled=True),
    )
    all_done = (
        lax.psum(summed_parts[0].astype(jnp.bfloat16), "batch").astype(jnp.float32),
        lax.psum(summed_parts[1].astype(jnp.bfloat16), "batch").astype(jnp.float32),
        lax.psum(summed_parts[2].astype(jnp.bfloat16), "batch").astype(jnp.float32),
        lax.psum(summed_parts[3].astype(jnp.bfloat16), "batch").astype(jnp.float32),
        lax.psum(summed_parts[4].astype(jnp.bfloat16), "batch").astype(jnp.float32),
        lax.psum(summed_parts[5].astype(jnp.bfloat16), "batch").astype(jnp.float32),
        lax.psum(summed_parts[6].astype(jnp.bfloat16), "batch").astype(jnp.float32),
        lax.psum(summed_parts[7].astype(jnp.bfloat16), "batch").astype(jnp.float32),
        lax.psum(summed_parts[8].astype(jnp.bfloat16), "batch").astype(jnp.float32),
    )
    second_done = (all_done[0], all_done[1], all_done[2], all_done[3])
    first_done = (all_done[4], all_done[5], all_done[6], all_done[7], all_done[8])
    return (
        layer_out,
        input_grad,
        second_done[0],
        second_done[1],
        second_done[2],
        first_done[0],
        first_done[1],
        first_done[2],
        first_done[3],
        second_done[3],
        first_done[4],
    )


AXES = ("batch", "seq", "seqb")
BF = jnp.bfloat16
F32 = jnp.float32
MIB = 1 << 20
COST = 1e6
ADD_COST = 2e9
KERNEL_US = {
    "qkv_other": 4,
    "qkv_own": 4,
    "attend": 9,
    "proj": 3,
    "ffn_first": 8,
    "ffn_second": 8,
    "ffn_out": 9,
    "middle": 1.4,
    "attend_back": 14,
    "square": 5,
    "input_grad": 6.5,
    "ffn_result": 2,
    "square_result": 2,
}


def fast_layout(mesh):
    return mesh.shape["batch"] == 4 and mesh.shape["seq"] == 4 and mesh.shape["seqb"] == 2


def exchange(rows, kind):
    pairs = []
    for b in range(4):
        for s in range(4):
            for c in range(2):
                first = 1 if c == 0 else 2
                target = {
                    "core": (b, s, 1 - c),
                    "first": (b ^ first, s, c),
                    "second": (b ^ (3 - first), s, c),
                    "near": (b, s ^ 1, c),
                    "far": (b, s ^ 2, c),
                    "across": (b ^ 3, s, c),
                }[kind]
                pairs.append((b * 8 + s * 2 + c, target[0] * 8 + target[1] * 2 + target[2]))
    return lax.ppermute(rows, AXES, pairs)


def dot(a, b):
    return lax.dot_general(a, b, (((1,), (0,)), ((), ())), preferred_element_type=F32)


def dot_nt(a, b):
    return lax.dot_general(a, b, (((1,), (1,)), ((), ())), preferred_element_type=F32)


def position_tables(count):
    half = HEAD_DIM // 2
    freq = rope_base ** (-(2.0 * np.arange(half)) / HEAD_DIM)
    angles = np.arange(count)[:, None] * freq[None, :]
    cosine, sine = np.cos(angles), np.sin(angles)
    return (
        np.concatenate([cosine, cosine, cosine, cosine], 1).astype(np.float32),
        np.concatenate([-sine, sine, -sine, sine], 1).astype(np.float32),
    )


def swap_halves(u):
    lane = lax.broadcasted_iota(jnp.int32, u.shape, 1) % HEAD_DIM
    return jnp.where(lane < HEAD_DIM // 2, pltpu.roll(u, 96, 1), pltpu.roll(u, 32, 1))


def turn(rows, cosine, sine):
    parts = []
    for g in range(rows.shape[1] // 128):
        u = rows[:, g * 128 : (g + 1) * 128]
        parts.append(u * cosine + swap_halves(u) * sine)
    return parts[0] if len(parts) == 1 else jnp.concatenate(parts, axis=1)


def live_mask(sc, row0, count):
    span_pos = sc[1] * SPAN + row0 + lax.broadcasted_iota(jnp.int32, (count, 1), 0)
    return span_pos < sc[2]


SPAN = 512
SEQ = 1024
WIDTH = 768
GROUP = 384
HID = 2048


def hbm():
    return pl.BlockSpec(memory_space=pl.ANY)


def far_hbm():
    return pl.BlockSpec(memory_space=pltpu.HBM)


def after(sc, *deps):
    return lax.optimization_barrier((sc,) + deps)[0]


def dot_tn(a, b):
    return lax.dot_general(a, b, (((0,), (0,)), ((), ())), preferred_element_type=F32)


def whole(shape):
    return pl.BlockSpec(shape, lambda i, sc: (0,) * len(shape))


def call(body, name, sc, args, in_specs, out_shapes, out_specs, scratch, vmem, cost):
    flops, moved, trans = cost
    args = [
        pltpu.with_memory_space_constraint(a, pltpu.HBM) if spec.memory_space is pltpu.HBM else a
        for a, spec in zip(args, in_specs)
    ]
    return pl.pallas_call(
        body,
        name=name,
        out_shape=out_shapes,
        grid_spec=pltpu.PrefetchScalarGridSpec(
            num_scalar_prefetch=1,
            grid=(1,),
            in_specs=in_specs,
            out_specs=out_specs,
            scratch_shapes=scratch,
        ),
        compiler_params=pltpu.CompilerParams(vmem_limit_bytes=vmem * MIB),
        cost_estimate=pl.CostEstimate(
            flops=int(COST * KERNEL_US[name]), bytes_accessed=1000, transcendentals=0
        ),
    )(sc, *args)


def sds(shape, dtype=BF):
    return jax.ShapeDtypeStruct(shape, dtype)


def project(o_ref, n_ref, cs, ss, weight, t):
    for r in range(0, SPAN, 256):
        y = dot(n_ref[r : r + 256, :], weight)
        if t < 2:
            y = turn(y, cs[r : r + 256, :], ss[r : r + 256, :])
        if t == 0:
            y = y * (HEAD_DIM**-0.5)
        o_ref[t, r : r + 256, :] = y.astype(BF)


def qkv_other_body(
    sc, x_hbm, cos_hbm, sin_hbm, gain_ref, wq, wk, wv, o_ref, n_ref, cs, ss, own_w, xs, ws, sem
):
    col = pl.multiple_of((1 - sc[0]) * GROUP, 128)
    own_col = pl.multiple_of(sc[0] * GROUP, 128)
    row = pl.multiple_of(sc[1] * SPAN, SPAN)
    weights = (wq, wk, wv)
    rows = [
        pltpu.make_async_copy(x_hbm.at[0, r : r + 256, :], xs.at[r : r + 256, :], sem.at[n])
        for n, r in enumerate((0, 256))
    ]
    copies = [
        pltpu.make_async_copy(w.at[:, pl.ds(col, GROUP)], ws.at[t], sem.at[2 + t])
        for t, w in enumerate(weights)
    ]
    tables = [
        pltpu.make_async_copy(cos_hbm.at[pl.ds(row, SPAN), :], cs, sem.at[5]),
        pltpu.make_async_copy(sin_hbm.at[pl.ds(row, SPAN), :], ss, sem.at[6]),
    ]
    later = [
        pltpu.make_async_copy(w.at[:, pl.ds(own_col, GROUP)], own_w.at[t], sem.at[7 + t])
        for t, w in enumerate(weights)
    ]
    for cp in rows + [copies[2]] + copies[:2] + tables + later:
        cp.start()
    for n, r in enumerate((0, 256)):
        rows[n].wait()
        x = jnp.where(live_mask(sc, r, 256), xs[r : r + 256, :].astype(F32), 0.0)
        factor = lax.rsqrt(jnp.mean(x * x, axis=-1, keepdims=True) + epsilon)
        n_ref[r : r + 256, :] = (x * factor * gain_ref[...]).astype(BF)
    for t in (2, 0, 1):
        copies[t].wait()
        if t == 0:
            for cp in tables:
                cp.wait()
        project(o_ref, n_ref, cs, ss, ws[t], t)
    for cp in later:
        cp.wait()


def qkv_own_body(sc, n_ref, cs, ss, ws, o_ref):
    for t in (2, 0, 1):
        project(o_ref, n_ref, cs, ss, ws[t], t)


def qkv_other_call(sc, tokens, gain, cosine, sine, wq, wk, wv):
    table = sds((SPAN, 128), F32)
    return call(
        qkv_other_body,
        "qkv_other",
        sc,
        (tokens, cosine, sine, gain, wq, wk, wv),
        [far_hbm()] * 3 + [whole((1, WIDTH))] + [far_hbm()] * 3,
        [sds((3, SPAN, GROUP)), sds((SPAN, WIDTH)), table, table, sds((3, WIDTH, GROUP))],
        [whole((3, SPAN, GROUP)), whole((SPAN, WIDTH))] + [whole((SPAN, 128))] * 2 + [hbm()],
        [
            pltpu.VMEM((SPAN, WIDTH), BF),
            pltpu.VMEM((3, WIDTH, GROUP), BF),
            pltpu.SemaphoreType.DMA((10,)),
        ],
        9,
        (3 * 2 * SPAN * WIDTH * GROUP, 5e6, 1e3),
    )


def qkv_own_call(sc, n1, cs, ss, ws):
    return call(
        qkv_own_body,
        "qkv_own",
        sc,
        (n1, cs, ss, ws),
        [whole((SPAN, WIDTH))] + [whole((SPAN, 128))] * 2 + [whole((3, WIDTH, GROUP))],
        sds((3, SPAN, GROUP)),
        whole((3, SPAN, GROUP)),
        [],
        9,
        (3 * 2 * SPAN * WIDTH * GROUP, 5e6, 1e3),
    )


def gather_rows(sc, own, other, places, sem):
    copies = []
    for t, place in enumerate(places):
        for k, src in enumerate((own, other)):
            pos = sc[1] if k == 0 else 1 - sc[1]
            row = pl.multiple_of(pos * SPAN, SPAN)
            source = src.at[t] if len(src.shape) == 3 else src
            copies.append(
                pltpu.make_async_copy(source, place.at[pl.ds(row, SPAN), :], sem.at[2 * t + k])
            )
    for cp in copies:
        cp.start()
    return copies


def pair_loads(sc, own, other, places, sem, hp):
    cols = pl.ds(hp * 128 if isinstance(hp, int) else pl.multiple_of(hp * 128, 128), 128)
    copies = []
    for t, place in enumerate(places):
        for k, src in enumerate((own, other)):
            pos = sc[1] if k == 0 else 1 - sc[1]
            rows = pl.ds(pl.multiple_of(pos * SPAN, SPAN), SPAN)
            copies.append(
                pltpu.make_async_copy(
                    src.at[t, :, cols], place.at[rows, cols], sem.at[6 * hp + 2 * t + k]
                )
            )
    return copies


def attend_body(sc, own, other, wo, wg, wu, wd, *refs):
    (ot_ref, lse_ref, mine, theirs, wo_v, wg_v, wu_v, wd_v, qs, ks, vs, at, sem, wsem) = refs
    for n in range(3):
        for cp in pair_loads(sc, own, other, (qs, ks, vs), sem, n):
            cp.start()
    fetch = []

    def bring(src, place):
        fetch.append(pltpu.make_async_copy(src, place, wsem.at[len(fetch)]))
        fetch[-1].start()

    for k in range(2):
        head = (sc[0] if k == 0 else 1 - sc[0]) * GROUP
        rows = pl.ds(pl.multiple_of(head, 128), GROUP)
        bring(wo.at[rows, :], wo_v.at[GROUP * k : GROUP * k + GROUP, :])
    for half in range(2):
        for s in range(4):
            cols = hidden_cols(sc, s, half)
            to = slice(512 * half + 128 * s, 512 * half + 128 * s + 128)
            bring(wg.at[:, cols], wg_v.at[:, to])
            bring(wu.at[:, cols], wu_v.at[:, to])
            bring(wd.at[cols, :], wd_v.at[to, :])
    lane = lax.broadcasted_iota(jnp.int32, (256, 128), 1)
    key_id = lax.broadcasted_iota(jnp.int32, (256, 256), 0)
    row_id = lax.broadcasted_iota(jnp.int32, (256, 256), 1)
    keep = key_id <= row_id

    def pair(hp, carry):
        base = pl.multiple_of(hp * 128, 128)
        cols = pl.ds(base, 128)
        for cp in pair_loads(sc, own, other, (qs, ks, vs), sem, hp):
            cp.wait()
        vt = jnp.transpose(vs[:, cols].astype(F32)).astype(BF)

        def scores(i, h):
            n = 256 * (i + 1)
            qm = jnp.where(lane // HEAD_DIM == h, qs[256 * i : n, cols], jnp.zeros((), BF))
            return dot_nt(ks[0:n, cols], qm)

        def soften(i, h, st):
            n = 256 * (i + 1)
            diag = jnp.where(keep, st[n - 256 :, :], masked_score)
            st = diag if i == 0 else jnp.concatenate([st[: n - 256, :], diag], axis=0)
            peak = jnp.max(st, axis=0, keepdims=True)
            p = jnp.exp(st - peak)
            return p.astype(BF), peak, jnp.sum(p, axis=0, keepdims=True)

        def finish(i, h, p, peak, total):
            n = 256 * (i + 1)
            o = dot(vt[h * 64 : h * 64 + 64, :n], p) * (1.0 / total)
            ot_ref[pl.ds(pl.multiple_of(hp * 128 + h * 64, 64), 64), 256 * i : n] = o
            lse_ref[pl.ds(hp * 2 + h, 1), 256 * i : n] = peak + jnp.log(total)

        tasks = [(i, h) for i in range(4) for h in range(2)]
        st, waiting = scores(*tasks[0]), None
        for k, task in enumerate(tasks):
            ahead = scores(*tasks[k + 1]) if k + 1 < len(tasks) else None
            parts = soften(*task, st)
            if waiting is not None:
                finish(*waiting)
            waiting, st = task + parts, ahead
        finish(*waiting)
        at[:, cols] = jnp.transpose(ot_ref[cols, :]).astype(BF)
        return carry

    lax.fori_loop(0, 3, pair, 0)
    row = pl.multiple_of(sc[1] * SPAN, SPAN)
    row_other = pl.multiple_of((1 - sc[1]) * SPAN, SPAN)
    out_other = pltpu.make_async_copy(at.at[pl.ds(row_other, SPAN), :], theirs, sem.at[18])
    out_own = pltpu.make_async_copy(at.at[pl.ds(row, SPAN), :], mine, sem.at[19])
    out_other.start()
    out_own.start()
    out_other.wait()
    out_own.wait()
    for cp in fetch:
        cp.wait()


def attend_call(sc, own, other, wo, wg, wu, wd):
    return call(
        attend_body,
        "attend",
        sc,
        (own, other, wo, wg, wu, wd),
        [hbm(), hbm()] + [far_hbm()] * 4,
        [sds((GROUP, SEQ), F32), sds((8, SEQ), F32), sds((SPAN, GROUP)), sds((SPAN, GROUP))]
        + [sds((WIDTH, WIDTH)), sds((WIDTH, SEQ)), sds((WIDTH, SEQ)), sds((SEQ, WIDTH))],
        [whole((GROUP, SEQ)), whole((8, SEQ))] + [hbm()] * 6,
        [pltpu.VMEM((SEQ, GROUP), BF)] * 4
        + [pltpu.SemaphoreType.DMA((20,)), pltpu.SemaphoreType.DMA((26,))],
        12,
        (6 * 4 * SEQ * SEQ * 64, 6e6, 4e6),
    )


def proj_body(sc, x_ref, ak_ref, ar_ref, gain_ref, wo_ref, m_ref, n_ref):
    for r in range(0, SPAN, 256):
        rr = slice(r, r + 256)
        m = jnp.where(live_mask(sc, r, 256), x_ref[0, rr, :].astype(F32), 0.0)
        m = m + dot(ak_ref[rr, :], wo_ref[:GROUP, :]) + dot(ar_ref[rr, :], wo_ref[GROUP:, :])
        m_ref[rr, :] = m
        factor = lax.rsqrt(jnp.mean(m * m, axis=-1, keepdims=True) + epsilon)
        n_ref[rr, :] = (m * factor * gain_ref[...]).astype(BF)


def proj_call(sc, tokens, own, other, gain, wo):
    return call(
        proj_body,
        "proj",
        sc,
        (tokens, own, other, gain, wo),
        [whole((1, SPAN, WIDTH))]
        + [whole((SPAN, GROUP))] * 2
        + [whole((1, WIDTH)), whole((WIDTH, WIDTH))],
        [sds((SPAN, WIDTH), F32), sds((SPAN, WIDTH))],
        [whole((SPAN, WIDTH))] * 2,
        [],
        8,
        (2 * SPAN * WIDTH * WIDTH, 5e6, 1e3),
    )


def over_rows(own, other, d_own, d_other):
    return dot_tn(own, d_own) + dot_tn(other, d_other)


def place_of(s):
    return (s % 2) * 2 + s // 2


def hidden_cols(sc, s, half):
    return pl.ds(pl.multiple_of(512 * s + 128 * half + 256 * sc[0], 128), 128)


def spread(sc, res_s, first, count, rows, send_ref, keep_ref, to):
    size = send_ref.shape[1]
    for k, ref in enumerate((send_ref, keep_ref)):
        bit = (1 - sc[3]) if k == 0 else sc[3]
        for s in range(4):
            for q in range(count):
                lo = pl.multiple_of(first + (s * count + q) * 2 * rows + bit * rows, 16)
                block, row = divmod(to + q * rows, size)
                ref[2 * place_of(s) + block, row : row + rows, :] = res_s[pl.ds(lo, rows), :].astype(
                    BF
                )


def ffn_body(sc, n_own, n_oth, dy_own, dy_oth, wg_s, wu_s, wd_s, *refs):
    (send_ref, keep_ref, h_ref, dg_ref, du_ref, dy_s, res_a, res_b) = refs
    for r in range(0, SEQ, 256):
        pos = sc[1] if r < SPAN else 1 - sc[1]
        at = pos * SPAN + r % SPAN + lax.broadcasted_iota(jnp.int32, (256, 1), 0)
        src = dy_own if r < SPAN else dy_oth
        lo = r % SPAN
        dy_s[r : r + 256, :] = jnp.where(at < sc[2], src[0, lo : lo + 256, :], jnp.zeros((), BF))

    def products(r):
        src = n_own if r < SPAN else n_oth
        rows = src[r % SPAN : r % SPAN + 256, :]
        return dot(rows, wg_s[...]), dot(rows, wu_s[...]), dot_nt(dy_s[r : r + 256, :], wd_s[...])

    ahead = products(0)
    for r in range(0, SEQ, 256):
        g, u, dh = ahead
        if r + 256 < SEQ:
            ahead = products(r + 256)
        rr = slice(r, r + 256)
        sg = jax.nn.sigmoid(g)
        gs = g * sg
        h_ref[rr, :] = (gs * u).astype(BF)
        du_ref[rr, :] = (dh * gs).astype(BF)
        dg_ref[rr, :] = (dh * u * (sg + gs * (1.0 - sg))).astype(BF)
    lower, upper = slice(0, SPAN), slice(SPAN, SEQ)
    for k, (base, src) in enumerate(((0, dg_ref), (192, du_ref))):
        for ct in range(2):
            cols = slice(256 * ct, 256 * ct + 256)
            place = res_a.at[ct]
            place[...] = over_rows(n_own[...], n_oth[...], src[lower, cols], src[upper, cols])
            spread(sc, place, 0, 2, 48, send_ref, keep_ref, base + 96 * ct)
    for n in range(3):
        place = res_b.at[n % 2]
        place[...] = dot_tn(h_ref[...], dy_s[:, 256 * n : 256 * n + 256])
        spread(sc, place, 0, 1, 64, send_ref, keep_ref, 384 + 64 * n)


def ffn_call(sc, half, n_own, n_oth, dy_own, dy_oth, wg, wu, wd):
    flat, full = whole((SPAN, WIDTH)), whole((1, SPAN, WIDTH))
    wide = pl.BlockSpec((WIDTH, 512), lambda i, sc: (0, half))
    return call(
        ffn_body,
        "ffn_first" if half == 0 else "ffn_second",
        sc,
        (n_own, n_oth, dy_own, dy_oth, wg, wu, wd),
        [flat, flat, full, full, wide, wide, pl.BlockSpec((512, WIDTH), lambda i, sc: (half, 0))],
        [sds((8, 288, 256))] * 2 + [sds((SEQ, 512))] * 3,
        [whole((8, 288, 256))] * 2 + [whole((SEQ, 512))] * 3,
        [
            pltpu.VMEM((SEQ, WIDTH), BF),
            pltpu.VMEM((2, WIDTH, 256), F32),
            pltpu.VMEM((2, 512, 256), F32),
        ],
        26,
        (6 * 2 * SEQ * WIDTH * 512, 14e6, 1e6),
    )


def ffn_out_body(sc, h0, dg0, du0, h1, dg1, du1, wg, wu, wd, acc_ref, accs_ref, dn_ref, dns_ref):
    for r in (512, 768, 0, 256):
        rr = slice(r, r + 256)
        dn = dot_nt(dg0[rr, :], wg[:, :512]) + dot_nt(dg1[rr, :], wg[:, 512:])
        dn = dn + dot_nt(du0[rr, :], wu[:, :512]) + dot_nt(du1[rr, :], wu[:, 512:])
        acc = dot(h0[rr, :], wd[:512, :]) + dot(h1[rr, :], wd[512:, :])
        if r < SPAN:
            dn_ref[rr, :] = dn
            acc_ref[rr, :] = acc
        else:
            dns_ref[r - SPAN : r - SPAN + 256, :] = dn.astype(BF)
            accs_ref[r - SPAN : r - SPAN + 256, :] = acc.astype(BF)


def ffn_out_call(sc, first, second, wg, wu, wd):
    flat = [whole((SPAN, WIDTH))]
    return call(
        ffn_out_body,
        "ffn_out",
        sc,
        tuple(first) + tuple(second) + (wg, wu, wd),
        [whole((SEQ, 512))] * 6 + [whole((WIDTH, SEQ))] * 2 + [whole((SEQ, WIDTH))],
        [sds((SPAN, WIDTH), F32), sds((SPAN, WIDTH)), sds((SPAN, WIDTH), F32), sds((SPAN, WIDTH))],
        flat * 4,
        [],
        24,
        (3 * 2 * SEQ * WIDTH * SEQ, 16e6, 0),
    )


def middle_body(sc, dn_ref, got_ref, m_ref, dy_ref, gain_ref, dm_ref, db_ref):
    gain = gain_ref[...]
    for r in range(0, SPAN, 128):
        rr = slice(r, r + 128)
        live = live_mask(sc, r, 128)
        m = m_ref[rr, :]
        factor = lax.rsqrt(jnp.mean(m * m, axis=-1, keepdims=True) + epsilon)
        scaled = (dn_ref[rr, :] + got_ref[rr, :].astype(F32)) * gain
        dm = jnp.where(live, dy_ref[0, rr, :].astype(F32), 0.0) + (
            factor * scaled
            - m * (factor * factor * factor) * jnp.mean(m * scaled, axis=-1, keepdims=True)
        )
        dm_ref[rr, :] = dm
        db_ref[rr, :] = dm.astype(BF)


def middle_call(sc, dn, got, m, dy, gain):
    flat = whole((SPAN, WIDTH))
    return call(
        middle_body,
        "middle",
        sc,
        (dn, got, m, dy, gain),
        [flat, flat, flat, whole((1, SPAN, WIDTH)), whole((1, WIDTH))],
        [sds((SPAN, WIDTH), F32), sds((SPAN, WIDTH))],
        [flat, flat],
        [],
        14,
        (1e6, 8e6, 1e3),
    )


def attend_back_body(sc, own, other, ot_s, lse_s, dbk, dbr, wo_s, cos_hbm, sin_hbm, *refs):
    wq, wk, wv, mine, theirs, ws, qs, ks, vs, das, ds_all, dqt, dkv, cs, ss, sem, load_sem = refs
    for n in range(3):
        for cp in pair_loads(sc, own, other, (qs, ks, vs), load_sem, n):
            cp.start()
    small = [
        pltpu.make_async_copy(src, to, sem.at[6 + n])
        for n, (src, to) in enumerate(((cos_hbm, cs), (sin_hbm, ss)))
    ]
    fetch = [
        pltpu.make_async_copy(w, ws.at[t], sem.at[10 + t]) for t, w in enumerate((wq, wk, wv))
    ]
    for cp in small + fetch:
        cp.start()
    for k, src in enumerate((dbk, dbr)):
        pos = sc[1] if k == 0 else 1 - sc[1]
        for r in range(0, SPAN, 256):
            rows = pl.ds(pl.multiple_of(pos * SPAN + r, 256), 256)
            das[rows, :] = dot_nt(src[r : r + 256, :], wo_s[...]).astype(BF)
    for cp in small:
        cp.wait()
    lane = lax.broadcasted_iota(jnp.int32, (SEQ, 128), 1)
    key_id = lax.broadcasted_iota(jnp.int32, (256, 256), 0)
    row_id = lax.broadcasted_iota(jnp.int32, (256, 256), 1)
    keep = key_id <= row_id

    def pair(hp, carry):
        base = pl.multiple_of(hp * 128, 128)
        cols = pl.ds(base, 128)
        for cp in pair_loads(sc, own, other, (qs, ks, vs), load_sem, hp):
            cp.wait()
        kt = jnp.transpose(ks[:, cols].astype(F32)).astype(BF)
        dat = jnp.transpose(das[:, cols].astype(F32))
        qm, dam, delta, lses = [], [], [], []
        for h in range(2):
            qm.append(jnp.where(lane // HEAD_DIM == h, qs[:, cols], jnp.zeros((), BF)))
            dam.append(jnp.where(lane // HEAD_DIM == h, das[:, cols], jnp.zeros((), BF)))
            rows = pl.ds(pl.multiple_of(base + 64 * h, 64), 64)
            product = dat[64 * h : 64 * h + 64, :] * ot_s[rows, :]
            delta.append(jnp.sum(product, axis=0, keepdims=True))
            lses.append(lse_s[pl.ds(2 * hp + h, 1), :])

        def scores(i, h):
            n = 256 * (i + 1)
            rows = slice(256 * i, n)
            return dot_nt(ks[:n, cols], qm[h][rows, :]), dot_nt(vs[:n, cols], dam[h][rows, :])

        def soften(i, h, st, dp):
            n = 256 * (i + 1)
            rows = slice(256 * i, n)
            p = jnp.exp(st - lses[h][:, rows])
            diag = jnp.where(keep, p[n - 256 :, :], 0.0)
            p = diag if i == 0 else jnp.concatenate([p[: n - 256, :], diag], axis=0)
            return p.astype(BF), (p * (dp - delta[h][:, rows])).astype(BF)

        def finish(i, h, p, ds):
            n = 256 * (i + 1)
            rows = slice(256 * i, n)
            half = slice(64 * h, 64 * h + 64)
            dv = dot(p, dam[h][rows, :])
            dk = dot(ds, qm[h][rows, :])
            dqt[half, rows] = dot(kt[half, :n], ds)
            if (i, h) == (3, 0):
                dkv[0] = dk
                dkv[1] = dv
            else:
                dkv[0, :n] += dk
                dkv[1, :n] += dv

        tasks = [(i, h) for i in (3, 2, 1, 0) for h in range(2)]
        now, waiting = scores(*tasks[0]), None
        for k, task in enumerate(tasks):
            ahead = scores(*tasks[k + 1]) if k + 1 < len(tasks) else None
            parts = soften(*task, *now)
            if waiting is not None:
                finish(*waiting)
            waiting, now = task + parts, ahead
        finish(*waiting)
        dq = jnp.transpose(dqt[...]) * (HEAD_DIM**-0.5)
        ds_all[0, :, cols] = turn(dq, cs[...], -ss[...]).astype(BF)
        ds_all[1, :, cols] = turn(dkv[0], cs[...], -ss[...]).astype(BF)
        ds_all[2, :, cols] = dkv[1].astype(BF)
        return carry

    lax.fori_loop(0, 3, pair, 0)
    row = pl.multiple_of(sc[1] * SPAN, SPAN)
    row_other = pl.multiple_of((1 - sc[1]) * SPAN, SPAN)
    stores = [
        pltpu.make_async_copy(ds_all.at[:, pl.ds(row_other, SPAN), :], theirs, sem.at[8]),
        pltpu.make_async_copy(ds_all.at[:, pl.ds(row, SPAN), :], mine, sem.at[9]),
    ]
    for cp in stores:
        cp.start()
    for cp in stores + fetch:
        cp.wait()


def attend_back_call(sc, own, other, ot, lse, dbk, dbr, wo, cosine, sine, wq, wk, wv):
    return call(
        attend_back_body,
        "attend_back",
        sc,
        (own, other, ot, lse, dbk, dbr, wo, cosine, sine, wq, wk, wv),
        [hbm(), hbm(), whole((GROUP, SEQ)), whole((8, SEQ))]
        + [whole((SPAN, WIDTH))] * 2
        + [whole((GROUP, WIDTH))]
        + [far_hbm()] * 5,
        [sds((3, SPAN, GROUP))] * 2 + [sds((3, WIDTH, WIDTH))],
        [hbm()] * 3,
        [pltpu.VMEM((SEQ, GROUP), BF)] * 4
        + [
            pltpu.VMEM((3, SEQ, GROUP), BF),
            pltpu.VMEM((128, SEQ), F32),
            pltpu.VMEM((2, SEQ, 128), F32),
            pltpu.VMEM((SEQ, 128), F32),
            pltpu.VMEM((SEQ, 128), F32),
            pltpu.SemaphoreType.DMA((13,)),
            pltpu.SemaphoreType.DMA((18,)),
        ],
        22,
        (6 * 10 * SEQ * SEQ * 64, 10e6, 4e6),
    )


def square_body(sc, nk, nr, ak, at, ck, ct, bk, br, dk, dr, sa_ref, ka_ref, sb_ref, kb_ref, res):
    own = pl.ds(pl.multiple_of(sc[0] * GROUP, 128), GROUP)
    other = pl.ds(pl.multiple_of((1 - sc[0]) * GROUP, 128), GROUP)
    res[0, own, :] = over_rows(ak[...], at[...], bk[:, own], br[:, own])
    res[0, other, :] = over_rows(ck[...], ct[...], bk[:, own], br[:, own])
    spread(sc, res.at[0], 0, 2, 48, sa_ref, ka_ref, 0)
    for n, t in enumerate((2, 0, 1)):
        place = res.at[(n + 1) % 2]
        place[...] = over_rows(nk[...], nr[...], dk[t], dr[t])
        if n == 0:
            spread(sc, place, 0, 2, 48, sa_ref, ka_ref, 96)
        else:
            spread(sc, place, 0, 2, 48, sb_ref, kb_ref, 96 * t)


def square_call(sc, *args):
    flat = [whole((SPAN, WIDTH))] * 2
    return call(
        square_body,
        "square",
        sc,
        args,
        flat + [whole((SPAN, GROUP))] * 4 + flat + [whole((3, SPAN, GROUP))] * 2,
        [sds((8, 96, GROUP))] * 4,
        [whole((8, 96, GROUP))] * 4,
        [pltpu.VMEM((2, WIDTH, GROUP), F32)],
        16,
        (4 * 2 * SEQ * WIDTH * GROUP, 12e6, 0),
    )


def input_grad_body(sc, x_ref, gain_ref, dm_ref, m_ref, acc_ref, got_ref, dk_s, dr_s, ws, *refs):
    lay_ref, o_ref = refs
    for r in range(0, SPAN, 256):
        rr = slice(r, r + 256)
        out = m_ref[rr, :] + acc_ref[rr, :] + got_ref[rr, :].astype(F32)
        lay_ref[0, rr, :] = jnp.where(live_mask(sc, r, 256), out, 0.0).astype(BF)
    own_cols = pl.multiple_of(sc[0] * GROUP, 128)
    other_cols = pl.multiple_of((1 - sc[0]) * GROUP, 128)
    gain = gain_ref[...]
    for r in range(0, SPAN, 256):
        rr = slice(r, r + 256)
        dn = dot_nt(dk_s[0, rr, :], ws[0, :, pl.ds(own_cols, GROUP)])
        dn = dn + dot_nt(dr_s[0, rr, :], ws[0, :, pl.ds(other_cols, GROUP)])
        for t in (1, 2):
            dn = dn + dot_nt(dk_s[t, rr, :], ws[t, :, pl.ds(own_cols, GROUP)])
            dn = dn + dot_nt(dr_s[t, rr, :], ws[t, :, pl.ds(other_cols, GROUP)])
        live = live_mask(sc, r, 256)
        x = jnp.where(live, x_ref[0, rr, :].astype(F32), 0.0)
        factor = lax.rsqrt(jnp.mean(x * x, axis=-1, keepdims=True) + epsilon)
        scaled = dn * gain
        dx = dm_ref[rr, :] + (
            factor * scaled
            - x * (factor * factor * factor) * jnp.mean(x * scaled, axis=-1, keepdims=True)
        )
        o_ref[0, rr, :] = jnp.where(live, dx, 0.0).astype(BF)


def input_grad_call(sc, tokens, gain, dm, m, acc, got, dk, dr, ws):
    full = whole((1, SPAN, WIDTH))
    flat = whole((SPAN, WIDTH))
    return call(
        input_grad_body,
        "input_grad",
        sc,
        (tokens, gain, dm, m, acc, got, dk, dr, ws),
        [full, whole((1, WIDTH)), flat, flat, flat, flat]
        + [whole((3, SPAN, GROUP))] * 2
        + [whole((3, WIDTH, WIDTH))],
        [sds((1, SPAN, WIDTH))] * 2,
        [full] * 2,
        [],
        20,
        (3 * 2 * SPAN * WIDTH * WIDTH, 14e6, 1e3),
    )


def add_pieces(sc, count, sums, name):
    rows, cols = sums[0][0][0].shape[1:]
    arrays = [array for stack in sums for array, _ in stack]
    picks = [pick for stack in sums for _, pick in stack]

    def body(sc_ref, *refs):
        at = 0
        for n, stack in enumerate(sums):
            total = refs[at][0].astype(F32)
            for ref in refs[at + 1 : at + len(stack)]:
                total = total + ref[0].astype(F32)
            refs[-1][0, n * rows : (n + 1) * rows, :] = total.astype(BF)
            at += len(stack)

    def spec(pick):
        block, row = pick
        return pl.BlockSpec((1, rows, cols), lambda j, sc_ref: (block(sc_ref, j), row, 0))

    high = rows * len(sums)
    return pl.pallas_call(
        body,
        name=name,
        out_shape=sds((count, high, cols)),
        grid_spec=pltpu.PrefetchScalarGridSpec(
            num_scalar_prefetch=1,
            grid=(count,),
            in_specs=[spec(pick) for pick in picks],
            out_specs=pl.BlockSpec((1, high, cols), lambda j, sc_ref: (j, 0, 0)),
        ),
        compiler_params=pltpu.CompilerParams(vmem_limit_bytes=6 * MIB),
        cost_estimate=pl.CostEstimate(
            flops=int(0 if name == "g0_b" else ADD_COST), bytes_accessed=1000, transcendentals=0
        ),
    )(sc, *arrays)


def row_block(rows, cols):
    return pl.BlockSpec((rows, cols), lambda i, sc: (sc[6], 0))


def row_of(column):
    column = jnp.concatenate([column, jnp.zeros((32, 1), F32)], axis=0)
    return jnp.transpose(jnp.broadcast_to(column, (128, 128)))[0, :96]


def collect_halves(sc, group, full):
    for n in range(4):
        core, k = divmod(n, 2)
        parity = sc[0] if core == 0 else 1 - sc[0]
        first = sc[3] if core == 0 else sc[7]
        first = 1 - first if k == 1 else first
        for h in range(2):
            full[parity, first, 288 * h : 288 * h + 288, :] = group[n][h]


def collect(sc, group, full, row, size):
    for n in range(8):
        core, k = divmod(n, 4)
        parity = sc[0] if core == 0 else 1 - sc[0]
        first, second = (sc[3], sc[7]) if core == 0 else (sc[7], sc[3])
        first = 1 - first if k in (1, 3) else first
        second = 1 - second if k in (2, 3) else second
        rows = pl.ds(pl.multiple_of(second * size, 16), size)
        full[parity, first, rows, :] = group[n][0, row : row + size, :]


def ffn_result_body(sc, *refs):
    wg_ref, wu_ref, gain_ref, gate_ref, up_ref, down_ref, gg_ref, full = refs[12:]
    collect_halves(sc, refs[:4], full.at[0])
    collect(sc, refs[4:12], full.at[1], 0, 288)
    for half in range(2):
        for bit in range(2):
            rows = slice(48 * bit, 48 * bit + 48)
            for parity in range(2):
                for base, ref in ((0, gate_ref), (192, up_ref)):
                    for ct in range(2):
                        lo = pl.multiple_of(base + ct * 96 + sc[0] * 48, 16)
                        block = full[half, parity, bit, pl.ds(lo, 48), :].astype(F32)
                        for q in range(2):
                            col = 512 * (2 * ct + q) + 128 * half + 256 * parity
                            ref[rows, col : col + 128] = block[:, 128 * q : 128 * q + 128]
            lo = 128 * half + 64 * bit
            for t in range(3):
                down_ref[lo : lo + 64, 256 * t : 256 * t + 256] = full[
                    half, sc[0], bit, 384 + t * 64 : 448 + t * 64, :
                ].astype(F32)
    gate = jnp.sum(wg_ref[...].astype(F32) * gate_ref[...], axis=-1, keepdims=True)
    up = jnp.sum(wu_ref[...].astype(F32) * up_ref[...], axis=-1, keepdims=True)
    gg_ref[...] = row_of((gate + up) / gain_ref[...])


def ffn_result_call(sc, first, second, wg, wu, gain):
    return call(
        ffn_result_body,
        "ffn_result",
        sc,
        tuple(first) + tuple(second) + (wg, wu, gain),
        [whole((2, 288, 256))] * 4 + [whole((1, 288, 256))] * 8 + [row_block(96, HID)] * 2 + [row_block(96, 1)],
        [sds((96, HID), F32), sds((96, HID), F32), sds((256, WIDTH), F32), sds((96,), F32)],
        [whole((96, HID)), whole((96, HID)), whole((256, WIDTH)), whole((96,))],
        [pltpu.VMEM((2, 2, 2, 576, 256), BF)],
        14,
        (1e6, 6e6, 0),
    )


def square_result_body(sc, *refs):
    group = refs[:8]
    weights = refs[8:11]
    gain_ref = refs[11]
    outs = refs[12:16]
    gg_ref, full = refs[16:]
    order = ((3, 2), (0, 1))
    for n in range(2):
        collect(sc, group, full.at[n], 96 * n, 96)
        for bit in range(2):
            rows = slice(48 * bit, 48 * bit + 48)
            for parity in range(2):
                cols = slice(GROUP * parity, GROUP * parity + GROUP)
                for t in range(2):
                    lo = pl.multiple_of(t * 96 + sc[0] * 48, 16)
                    block = full[n, parity, bit, pl.ds(lo, 48), :]
                    outs[order[n][t]][rows, cols] = block.astype(F32)
    total = jnp.zeros((96, 1), F32)
    for t in range(3):
        total = total + jnp.sum(weights[t][...].astype(F32) * outs[t][...], axis=-1, keepdims=True)
    gg_ref[...] = row_of(total / gain_ref[...])


def square_result_call(sc, group, wq, wk, wv, gain):
    return call(
        square_result_body,
        "square_result",
        sc,
        tuple(group) + (wq, wk, wv, gain),
        [whole((1, 192, GROUP))] * 8 + [row_block(96, WIDTH)] * 3 + [row_block(96, 1)],
        [sds((96, WIDTH), F32)] * 4 + [sds((96,), F32)],
        [whole((96, WIDTH))] * 4 + [whole((96,))],
        [pltpu.VMEM((2, 2, 2, 192, GROUP), BF)],
        8,
        (1e6, 4e6, 0),
    )


class Chain:
    def __init__(self, sc):
        self.sc = sc

    def next(self, *deps):
        self.sc = after(self.sc, *deps)
        return self.sc


class Reduction:
    def __init__(self, chain, send, keep, name):
        self.chain = chain
        self.send = send
        self.name = name
        self.stacks = [[[keep, 0]]]
        self.flight = None

    def start(self):
        self.fly(after(self.send, self.chain.sc), "first")

    def fly(self, rows, kind):
        self.flight = exchange(rows, kind)

    def land(self):
        if self.flight is not None:
            for n, stack in enumerate(self.stacks):
                stack.append([self.flight, n])
        self.flight = None

    def add(self, count, picks, tag):
        self.land()
        sums = []
        for stack in self.stacks:
            blocks = ([picks[0]] + picks)[-len(stack) :]
            sums.append([(array, (pick, row)) for (array, row), pick in zip(stack, blocks)])
        arrays = [array for stack in sums for array, _ in stack]
        out = add_pieces(self.chain.next(*arrays), count, sums, self.name + tag)
        self.chain.next(out)
        return out

    def second(self):
        pick = lambda t, j: j * 2 + 1 - t[7]
        self.fly(self.add(4, [pick], "_b"), "second")

    def near(self):
        pick = lambda t, j: (1 - t[4]) * 4 + j * 2 + t[7]
        self.fly(self.add(2, [pick, lambda t, j: (1 - t[4]) * 2 + j], "_c"), "near")

    def far(self):
        pick = lambda t, j: t[4] * 4 + (1 - t[5]) * 2 + t[7]
        picks = [pick, lambda t, j: t[4] * 2 + 1 - t[5], lambda t, j: 1 - t[5]]
        self.fly(self.add(1, picks, "_d"), "far")

    def total(self):
        pick = lambda t, j: t[4] * 4 + t[5] * 2 + t[7]
        picks = [pick, lambda t, j: t[4] * 2 + t[5], lambda t, j: t[5], lambda t, j: 0]
        own = self.add(1, picks, "_e")
        self.quarters = [own] + [exchange(own, kind) for kind in ("first", "second", "across")]

    def result(self):
        late = [after(quarter, self.chain.sc) for quarter in self.quarters]
        return self.quarters + [exchange(quarter, "core") for quarter in late]


class Straight(Reduction):
    def near(self):
        pick = lambda t, j: (1 - t[4]) * 4 + j
        self.fly(self.add(4, [pick], "_b"), "near")

    def far(self):
        pick = lambda t, j: t[4] * 4 + (1 - t[5]) * 2 + j
        self.fly(self.add(2, [pick, lambda t, j: (1 - t[5]) * 2 + j], "_c"), "far")

    def second(self):
        pick = lambda t, j: t[4] * 4 + t[5] * 2 + j
        own = self.add(2, [pick, lambda t, j: t[5] * 2 + j, lambda t, j: j], "_d")
        self.stacks = [[[own, 0]]]
        self.fly(own, "second")

    def total(self):
        own = self.add(2, [lambda t, j: j], "_e")
        self.quarters = [own, exchange(own, "first")]


def join(first, second):
    both = Reduction(first.chain, None, None, first.name + second.name)
    first.land()
    second.land()
    both.stacks = first.stacks + second.stacks
    return both


def fast_step(
    tokens,
    lengths,
    owner,
    w_query,
    w_key,
    w_value,
    w_out,
    w_gate,
    w_up,
    w_down,
    gain_attn,
    gain_mlp,
    cotangent,
):
    batch, seq, core = (lax.axis_index(name) for name in AXES)
    low, high = batch % 2, batch // 2
    swap = core == 0
    slot = jnp.arange(8, dtype=jnp.int32)
    fixed = (
        core,
        core,
        0,
        jnp.where(swap, low, high),
        seq % 2,
        seq // 2,
        seq * 2 + core,
        jnp.where(swap, high, low),
    )
    sc = jnp.zeros((8,), jnp.int32)
    for n, value in enumerate(fixed):
        sc = jnp.where(slot == n, value, sc)
    first_pos = jnp.broadcast_to(owner[0, :1], (8,))
    sc = jnp.where(slot == 1, jnp.where(swap, first_pos, 1 - first_pos), sc)
    sc = jnp.where(slot == 2, jnp.broadcast_to(lengths, (8,)), sc)
    tables = position_tables(SEQ)
    cosine, sine = jnp.asarray(tables[0]), jnp.asarray(tables[1])
    gain_row = gain_attn.reshape(1, WIDTH)
    gain_mlp_row = gain_mlp.reshape(1, WIDTH)
    qkv_w = (w_query, w_key, w_value)
    ffn_w = (w_gate, w_up, w_down)
    chain = Chain(sc)

    qkv_send, n1, cs_v, ss_v, w_v = qkv_other_call(chain.sc, tokens, gain_row, cosine, sine, *qkv_w)
    qkv_other = exchange(qkv_send, "core")
    qkv_own = qkv_own_call(chain.next(n1), n1, cs_v, ss_v, w_v)
    n1_other = exchange(n1, "core")
    dy_other = exchange(cotangent, "core")
    attn_t, lse, attn_own, attn_send, wo_v, *ffn_v = attend_call(
        chain.next(qkv_own), qkv_own, qkv_other, w_out, *ffn_w
    )
    attn_other = exchange(attn_send, "core")
    attn_rest = exchange(attn_own, "core")
    middle, n2 = proj_call(
        chain.next(lse, n1_other, dy_other), tokens, attn_own, attn_other, gain_mlp_row, wo_v
    )
    n2_other = exchange(n2, "core")
    rows = (n2, n2_other, cotangent, dy_other)
    send0, keep0, *acts0 = ffn_call(chain.next(n2, attn_rest), 0, *rows, *ffn_v)
    g0 = Straight(chain, send0, keep0, "g0")
    g0.start()
    send1, keep1, *acts1 = ffn_call(chain.next(acts0[0]), 1, *rows, *ffn_v)
    g1 = Reduction(chain, send1, keep1, "g1")
    g1.start()
    acc, acc_send, dn, dn_send = ffn_out_call(chain.next(acts1[0]), acts0, acts1, *ffn_v)
    dn_other = exchange(dn_send, "core")
    chain.next(dn_send)
    d_middle, db = middle_call(
        chain.next(dn_other, g0.flight), dn, dn_other, middle, cotangent, gain_mlp_row
    )
    chain.next(db)
    g0.near()
    db_other = exchange(db, "core")
    acc_other = exchange(after(acc_send, db_other), "core")
    d_own, d_send, qkv_v = attend_back_call(
        chain.sc,
        qkv_own,
        qkv_other,
        attn_t,
        lse,
        db,
        db_other,
        wo_v,
        cosine,
        sine,
        *qkv_w,
    )
    d_other = exchange(d_send, "core")
    chain.next(d_own, g0.flight, g1.flight)
    g1.second()
    g0.far()
    attn = (attn_own, attn_send, attn_other, attn_rest)
    send2, keep2, send3, keep3 = square_call(
        chain.sc, n1, n1_other, *attn, db, db_other, d_own, d_send
    )
    g2 = Reduction(chain, send2, keep2, "g2")
    g3 = Reduction(chain, send3, keep3, "g3")
    g2.start()
    g3.start()
    chain.next(send3)
    layer_out, input_grad = input_grad_call(
        chain.next(acc_other, d_other),
        tokens,
        gain_row,
        d_middle,
        middle,
        acc,
        acc_other,
        d_own,
        d_other,
        qkv_v,
    )
    chain.next(input_grad)
    g0.second()
    g1.near()
    g2.second()
    g1.far()
    g3.second()
    g2.near()
    g0.total()
    g3.near()
    g2.far()
    g3.far()
    g1.total()
    g23 = join(g2, g3)
    g23.total()
    first = g0.result()
    second = g1.result()
    third = g23.result()
    gate, up, down, gain_m = ffn_result_call(
        chain.sc, first, second, w_gate, w_up, gain_mlp.reshape(WIDTH, 1)
    )
    chain.next(gain_m)
    query, key, value, out, gain_a = square_result_call(
        chain.sc, third, *qkv_w, gain_attn.reshape(WIDTH, 1)
    )
    return (
        layer_out,
        input_grad,
        query,
        key,
        value,
        out,
        gate,
        up,
        down,
        gain_a,
        gain_m,
    )


def solution(mesh):
    in_specs = (
        P(("batch", "seq"), "seqb", None),
        P(("batch", "seq")),
        P(("batch", "seq"), None),
        P(),
        P(),
        P(),
        P(),
        P(),
        P(),
        P(),
        P(),
        P(),
        P(("batch", "seq"), "seqb", None),
    )
    out_specs = (
        P(("batch", "seq"), "seqb", None),
        P(("batch", "seq"), "seqb", None),
        P(("seq", "seqb"), None),
        P(("seq", "seqb"), None),
        P(("seq", "seqb"), None),
        P(("seq", "seqb"), None),
        P(("seq", "seqb"), None),
        P(("seq", "seqb"), None),
        P(("seq", "seqb"), None),
        P(("seq", "seqb")),
        P(("seq", "seqb")),
    )
    step = fast_step if fast_layout(mesh) else general_step
    return jax.shard_map(step, mesh=mesh, in_specs=in_specs, out_specs=out_specs, check_vma=False)
```

```python
import functools
import math

import jax
import jax.numpy as jnp
import numpy as np
from jax import lax
from jax.experimental import pallas as pl
from jax.experimental.pallas import tpu as pltpu
from jax.sharding import PartitionSpec as P

HEADS = 12
HEAD_DIM = 64


epsilon = 1e-05
rope_base = 10000.0
masked_score = -1e30


def rms_forward(rows, gain):
    factor = lax.rsqrt(jnp.mean(rows * rows, axis=-1, keepdims=True) + epsilon)
    return (rows * factor * gain, factor)


def rms_backward(rows, factor, gain, upstream):
    scaled = upstream * gain
    return factor * scaled - rows * (factor * factor * factor) * jnp.mean(
        rows * scaled, axis=-1, keepdims=True
    )


def rotation_tables(positions):
    half = HEAD_DIM // 2
    freq = rope_base ** (-(2.0 * jnp.arange(half, dtype=jnp.float32)) / HEAD_DIM)
    angles = positions.astype(jnp.float32)[..., None] * freq
    return (jnp.cos(angles), jnp.sin(angles))


def split_heads(rows):
    return rows.reshape(rows.shape[0], rows.shape[1], HEADS, HEAD_DIM)


def rotate(rows, cosine, sine, inverse):
    shaped = split_heads(rows)
    half = HEAD_DIM // 2
    first = shaped[..., :half]
    second = shaped[..., half:]
    cos_part = cosine[:, :, None, :]
    sin_part = sine[:, :, None, :]
    if inverse:
        turned = jnp.concatenate(
            [first * cos_part + second * sin_part, second * cos_part - first * sin_part], axis=-1
        )
    else:
        turned = jnp.concatenate(
            [first * cos_part - second * sin_part, second * cos_part + first * sin_part], axis=-1
        )
    return turned.reshape(rows.shape)


def range_positions(owner, count, span):
    offsets = jnp.arange(span, dtype=jnp.int32)
    return (owner[:, :, None] * span + offsets[None, None, :]).reshape(owner.shape[0], count)


def fold_keys(parts, combine, initial):
    return combine(
        initial,
        (
            lax.all_gather(parts[0], "seqb", axis=1, tiled=True),
            lax.all_gather(parts[1], "seqb", axis=1, tiled=True),
        ),
        jnp.int32(0),
    )


def general_step(
    tokens,
    lengths,
    owner,
    w_query,
    w_key,
    w_value,
    w_out,
    w_gate,
    w_up,
    w_down,
    gain_attn,
    gain_mlp,
    cotangent,
):
    seqs, span, width = tokens.shape
    scale = HEAD_DIM ** (-0.5)
    place = lax.axis_index("seqb")
    own_block = lax.dynamic_slice_in_dim(owner, place, 1, 1)
    local_pos = own_block * span + jnp.arange(span, dtype=jnp.int32)[None, :]
    local_live = local_pos < lengths[:, None]
    live_rows = local_live[:, :, None]
    inputs = jnp.where(live_rows, tokens.astype(jnp.float32), 0.0)
    normed, factor_attn = rms_forward(inputs, gain_attn)
    normed_low = normed.astype(jnp.bfloat16)
    cosine, sine = rotation_tables(local_pos)
    query_pre = jnp.einsum("scd,de->sce", normed_low, w_query, preferred_element_type=jnp.float32)
    key_pre = jnp.einsum("scd,de->sce", normed_low, w_key, preferred_element_type=jnp.float32)
    value_low = jnp.einsum(
        "scd,de->sce", normed_low, w_value, preferred_element_type=jnp.float32
    ).astype(jnp.bfloat16)
    query_rot = rotate(query_pre, cosine, sine, False).astype(jnp.bfloat16)
    key_rot = rotate(key_pre, cosine, sine, False).astype(jnp.bfloat16)
    query_heads = split_heads(query_rot)
    key_heads = split_heads(key_rot)
    value_heads = split_heads(value_low)

    def attend(state, piece, start):
        keys, values = piece
        count = keys.shape[1]
        key_pos = range_positions(owner, count, span)
        key_live = key_pos < lengths[:, None]
        stride = math.gcd(count, 512)

        def attend_one_block(index, inner):
            offset = index * stride
            key_block = split_heads(lax.dynamic_slice_in_dim(keys, offset, stride, 1))
            value_block = split_heads(lax.dynamic_slice_in_dim(values, offset, stride, 1))
            pos_block = lax.dynamic_slice_in_dim(key_pos, offset, stride, 1)
            live_block = lax.dynamic_slice_in_dim(key_live, offset, stride, 1)
            allowed = (
                (pos_block[:, None, :] <= local_pos[:, :, None])
                & live_block[:, None, :]
                & local_live[:, :, None]
            )

            def attend_update(carried):
                peak, total, summed = carried
                scores = (
                    jnp.einsum(
                        "sqhd,skhd->shqk",
                        query_heads,
                        key_block,
                        preferred_element_type=jnp.float32,
                    )
                    * scale
                )
                mask = allowed[:, None, :, :]
                new_peak = jnp.maximum(
                    peak, jnp.max(jnp.where(mask, scores, masked_score), axis=-1)
                )
                weights = jnp.where(mask, jnp.exp(scores - new_peak[..., None]), 0.0)
                factor = jnp.exp(peak - new_peak)
                total = total * factor + jnp.sum(weights, axis=-1)
                term = jnp.einsum(
                    "shqk,skhd->sqhd",
                    weights.astype(jnp.bfloat16),
                    value_block,
                    preferred_element_type=jnp.float32,
                )
                summed = (
                    split_heads(summed) * jnp.transpose(factor, (0, 2, 1))[..., None] + term
                ).reshape(summed.shape)
                return (new_peak, total, summed)

            return lax.cond(jnp.any(allowed), attend_update, lambda carried: carried, inner)

        return lax.fori_loop(0, count // stride, attend_one_block, state)

    start_state = (
        jnp.full((seqs, HEADS, span), masked_score, jnp.float32),
        jnp.zeros((seqs, HEADS, span), jnp.float32),
        jnp.zeros((seqs, span, width), jnp.float32),
    )
    peak, total, summed = fold_keys((key_rot, value_low), attend, start_state)
    safe_total = jnp.where(local_live[:, None, :], total, 1.0)
    attn = split_heads(summed) / jnp.transpose(safe_total, (0, 2, 1))[..., None]
    attn = jnp.where(local_live[:, :, None, None], attn, 0.0).reshape(seqs, span, width)
    log_total = jnp.where(local_live[:, None, :], peak + jnp.log(safe_total), 0.0)
    attn_low = attn.astype(jnp.bfloat16)
    middle = inputs + jnp.einsum("scd,de->sce", attn_low, w_out, preferred_element_type=jnp.float32)
    normed_mlp, factor_mlp = rms_forward(middle, gain_mlp)
    normed_mlp_low = normed_mlp.astype(jnp.bfloat16)
    gate = jnp.einsum("scd,df->scf", normed_mlp_low, w_gate, preferred_element_type=jnp.float32)
    up_proj = jnp.einsum("scd,df->scf", normed_mlp_low, w_up, preferred_element_type=jnp.float32)
    hidden = (jax.nn.silu(gate) * up_proj).astype(jnp.bfloat16)
    out = middle + jnp.einsum("scf,fd->scd", hidden, w_down, preferred_element_type=jnp.float32)
    layer_out = jnp.where(live_rows, out, 0.0).astype(jnp.bfloat16)
    upstream = jnp.where(live_rows, cotangent, jnp.zeros_like(cotangent))
    grad_down = jnp.einsum("scf,scd->fd", hidden, upstream, preferred_element_type=jnp.float32)
    d_hidden = jnp.einsum("scd,fd->scf", upstream, w_down, preferred_element_type=jnp.float32)
    sigmoid_gate = jax.nn.sigmoid(gate)
    d_gate = (d_hidden * up_proj * sigmoid_gate * (1.0 + gate * (1.0 - sigmoid_gate))).astype(
        jnp.bfloat16
    )
    d_up = (d_hidden * gate * sigmoid_gate).astype(jnp.bfloat16)
    grad_gate = jnp.einsum(
        "scd,scf->df", normed_mlp_low, d_gate, preferred_element_type=jnp.float32
    )
    grad_up = jnp.einsum("scd,scf->df", normed_mlp_low, d_up, preferred_element_type=jnp.float32)
    d_normed_mlp = jnp.einsum(
        "scf,df->scd", d_gate, w_gate, preferred_element_type=jnp.float32
    ) + jnp.einsum("scf,df->scd", d_up, w_up, preferred_element_type=jnp.float32)
    grad_gain_mlp = jnp.sum(d_normed_mlp * (middle * factor_mlp), axis=(0, 1))
    d_middle = upstream.astype(jnp.float32) + rms_backward(
        middle, factor_mlp, gain_mlp, d_normed_mlp
    )
    d_branch = d_middle.astype(jnp.bfloat16)
    grad_out = jnp.einsum("scd,sce->de", attn_low, d_branch, preferred_element_type=jnp.float32)
    d_attn = jnp.einsum("sce,de->scd", d_branch, w_out, preferred_element_type=jnp.float32).astype(
        jnp.bfloat16
    )
    first_done = (grad_out, grad_gate, grad_up, grad_down, grad_gain_mlp)
    delta = jnp.sum(split_heads(d_attn.astype(jnp.float32) * attn), axis=-1)
    delta_heads = jnp.transpose(delta, (0, 2, 1))
    grad_heads = split_heads(d_attn)

    def query_grads(state, piece, start):
        keys, values = piece
        count = keys.shape[1]
        key_pos = range_positions(owner, count, span)
        key_live = key_pos < lengths[:, None]
        stride = math.gcd(count, 512)

        def query_one_block(index, inner):
            offset = index * stride
            key_block = split_heads(lax.dynamic_slice_in_dim(keys, offset, stride, 1))
            value_block = split_heads(lax.dynamic_slice_in_dim(values, offset, stride, 1))
            pos_block = lax.dynamic_slice_in_dim(key_pos, offset, stride, 1)
            live_block = lax.dynamic_slice_in_dim(key_live, offset, stride, 1)
            allowed = (
                (pos_block[:, None, :] <= local_pos[:, :, None])
                & live_block[:, None, :]
                & local_live[:, :, None]
            )

            def query_update(carried):
                scores = (
                    jnp.einsum(
                        "sqhd,skhd->shqk",
                        query_heads,
                        key_block,
                        preferred_element_type=jnp.float32,
                    )
                    * scale
                )
                probs = jnp.where(
                    allowed[:, None, :, :], jnp.exp(scores - log_total[..., None]), 0.0
                )
                d_probs = jnp.einsum(
                    "sqhd,skhd->shqk", grad_heads, value_block, preferred_element_type=jnp.float32
                )
                d_scores = (probs * (d_probs - delta_heads[..., None])).astype(jnp.bfloat16)
                term = (
                    jnp.einsum(
                        "shqk,skhd->sqhd", d_scores, key_block, preferred_element_type=jnp.float32
                    )
                    * scale
                )
                return carried + term.reshape(carried.shape)

            return lax.cond(jnp.any(allowed), query_update, lambda carried: carried, inner)

        return lax.fori_loop(0, count // stride, query_one_block, state)

    zero_query = jnp.zeros((seqs, span, width), jnp.float32)
    d_query = fold_keys((key_rot, value_low), query_grads, zero_query)
    lse_all, delta_all = (
        lax.all_gather(jnp.transpose(log_total, (0, 2, 1)), "seqb", axis=1, tiled=True),
        lax.all_gather(delta, "seqb", axis=1, tiled=True),
    )
    zero_rows = jnp.zeros((seqs, span, width), jnp.float32)
    queries = lax.all_gather(query_rot, "seqb", axis=1, tiled=True)
    d_rows = lax.all_gather(d_attn, "seqb", axis=1, tiled=True)
    count = queries.shape[1]
    row_pos = range_positions(owner, count, span)
    row_live = row_pos < lengths[:, None]
    stride = math.gcd(count, 512)

    def key_one_block(index, inner):
        offset = index * stride
        query_block = split_heads(lax.dynamic_slice_in_dim(queries, offset, stride, 1))
        grad_block = split_heads(lax.dynamic_slice_in_dim(d_rows, offset, stride, 1))
        pos_block = lax.dynamic_slice_in_dim(row_pos, offset, stride, 1)
        live_block = lax.dynamic_slice_in_dim(row_live, offset, stride, 1)
        lse_block = jnp.transpose(lax.dynamic_slice_in_dim(lse_all, offset, stride, 1), (0, 2, 1))
        delta_block = jnp.transpose(
            lax.dynamic_slice_in_dim(delta_all, offset, stride, 1), (0, 2, 1)
        )
        allowed = (
            (local_pos[:, None, :] <= pos_block[:, :, None])
            & local_live[:, None, :]
            & live_block[:, :, None]
        )

        def key_update(carried):
            d_key, d_value = carried
            scores = (
                jnp.einsum(
                    "sqhd,skhd->shqk", query_block, key_heads, preferred_element_type=jnp.float32
                )
                * scale
            )
            probs = jnp.where(allowed[:, None, :, :], jnp.exp(scores - lse_block[..., None]), 0.0)
            value_term = jnp.einsum(
                "shqk,sqhd->skhd",
                probs.astype(jnp.bfloat16),
                grad_block,
                preferred_element_type=jnp.float32,
            )
            d_probs = jnp.einsum(
                "sqhd,skhd->shqk", grad_block, value_heads, preferred_element_type=jnp.float32
            )
            d_scores = (probs * (d_probs - delta_block[..., None])).astype(jnp.bfloat16)
            key_term = (
                jnp.einsum(
                    "shqk,sqhd->skhd", d_scores, query_block, preferred_element_type=jnp.float32
                )
                * scale
            )
            return (
                d_key + key_term.reshape(d_key.shape),
                d_value + value_term.reshape(d_value.shape),
            )

        return lax.cond(jnp.any(allowed), key_update, lambda carried: carried, inner)

    d_key, d_value = lax.fori_loop(0, count // stride, key_one_block, (zero_rows, zero_rows))
    d_query_pre = rotate(d_query, cosine, sine, True).astype(jnp.bfloat16)
    d_key_pre = rotate(d_key, cosine, sine, True).astype(jnp.bfloat16)
    d_value_low = d_value.astype(jnp.bfloat16)
    grad_query = jnp.einsum(
        "scd,sce->de", normed_low, d_query_pre, preferred_element_type=jnp.float32
    )
    grad_key = jnp.einsum("scd,sce->de", normed_low, d_key_pre, preferred_element_type=jnp.float32)
    grad_value = jnp.einsum(
        "scd,sce->de", normed_low, d_value_low, preferred_element_type=jnp.float32
    )
    d_normed = jnp.einsum("sce,de->scd", d_query_pre, w_query, preferred_element_type=jnp.float32)
    d_normed = d_normed + jnp.einsum(
        "sce,de->scd", d_key_pre, w_key, preferred_element_type=jnp.float32
    )
    d_normed = d_normed + jnp.einsum(
        "sce,de->scd", d_value_low, w_value, preferred_element_type=jnp.float32
    )
    grad_gain_attn = jnp.sum(d_normed * (inputs * factor_attn), axis=(0, 1))
    d_inputs = d_middle + rms_backward(inputs, factor_attn, gain_attn, d_normed)
    input_grad = jnp.where(live_rows, d_inputs, 0.0).astype(jnp.bfloat16)
    summed_parts = (
        lax.psum_scatter(grad_query, ("seq", "seqb"), scatter_dimension=0, tiled=True),
        lax.psum_scatter(grad_key, ("seq", "seqb"), scatter_dimension=0, tiled=True),
        lax.psum_scatter(grad_value, ("seq", "seqb"), scatter_dimension=0, tiled=True),
        lax.psum_scatter(grad_gain_attn, ("seq", "seqb"), scatter_dimension=0, tiled=True),
        lax.psum_scatter(first_done[0], ("seq", "seqb"), scatter_dimension=0, tiled=True),
        lax.psum_scatter(first_done[1], ("seq", "seqb"), scatter_dimension=0, tiled=True),
        lax.psum_scatter(first_done[2], ("seq", "seqb"), scatter_dimension=0, tiled=True),
        lax.psum_scatter(first_done[3], ("seq", "seqb"), scatter_dimension=0, tiled=True),
        lax.psum_scatter(first_done[4], ("seq", "seqb"), scatter_dimension=0, tiled=True),
    )
    all_done = (
        lax.psum(summed_parts[0].astype(jnp.bfloat16), "batch").astype(jnp.float32),
        lax.psum(summed_parts[1].astype(jnp.bfloat16), "batch").astype(jnp.float32),
        lax.psum(summed_parts[2].astype(jnp.bfloat16), "batch").astype(jnp.float32),
        lax.psum(summed_parts[3].astype(jnp.bfloat16), "batch").astype(jnp.float32),
        lax.psum(summed_parts[4].astype(jnp.bfloat16), "batch").astype(jnp.float32),
        lax.psum(summed_parts[5].astype(jnp.bfloat16), "batch").astype(jnp.float32),
        lax.psum(summed_parts[6].astype(jnp.bfloat16), "batch").astype(jnp.float32),
        lax.psum(summed_parts[7].astype(jnp.bfloat16), "batch").astype(jnp.float32),
        lax.psum(summed_parts[8].astype(jnp.bfloat16), "batch").astype(jnp.float32),
    )
    second_done = (all_done[0], all_done[1], all_done[2], all_done[3])
    first_done = (all_done[4], all_done[5], all_done[6], all_done[7], all_done[8])
    return (
        layer_out,
        input_grad,
        second_done[0],
        second_done[1],
        second_done[2],
        first_done[0],
        first_done[1],
        first_done[2],
        first_done[3],
        second_done[3],
        first_done[4],
    )


AXES = ("batch", "seq", "seqb")
BF = jnp.bfloat16
F32 = jnp.float32
MIB = 1 << 20
COST = 1e6
ADD_COST = 2e9
KERNEL_US = {
    "qkv_other": 4,
    "qkv_own": 4,
    "attend": 9,
    "proj": 3,
    "ffn_first": 8,
    "ffn_second": 8,
    "ffn_out": 9,
    "middle": 1.4,
    "attend_back": 14,
    "square": 5,
    "input_grad": 6.5,
    "ffn_result": 2,
    "square_result": 2,
}


def fast_layout(mesh):
    return mesh.shape["batch"] == 4 and mesh.shape["seq"] == 4 and mesh.shape["seqb"] == 2


def exchange(rows, kind):
    pairs = []
    for b in range(4):
        for s in range(4):
            for c in range(2):
                first = 1 if c == 0 else 2
                target = {
                    "core": (b, s, 1 - c),
                    "first": (b ^ first, s, c),
                    "second": (b ^ (3 - first), s, c),
                    "near": (b, s ^ 1, c),
                    "far": (b, s ^ 2, c),
                    "across": (b ^ 3, s, c),
                }[kind]
                pairs.append((b * 8 + s * 2 + c, target[0] * 8 + target[1] * 2 + target[2]))
    return lax.ppermute(rows, AXES, pairs)


def dot(a, b):
    return lax.dot_general(a, b, (((1,), (0,)), ((), ())), preferred_element_type=F32)


def dot_nt(a, b):
    return lax.dot_general(a, b, (((1,), (1,)), ((), ())), preferred_element_type=F32)


def position_tables(count):
    half = HEAD_DIM // 2
    freq = rope_base ** (-(2.0 * np.arange(half)) / HEAD_DIM)
    angles = np.arange(count)[:, None] * freq[None, :]
    cosine, sine = np.cos(angles), np.sin(angles)
    return (
        np.concatenate([cosine, cosine, cosine, cosine], 1).astype(np.float32),
        np.concatenate([-sine, sine, -sine, sine], 1).astype(np.float32),
    )


def swap_halves(u):
    lane = lax.broadcasted_iota(jnp.int32, u.shape, 1) % HEAD_DIM
    return jnp.where(lane < HEAD_DIM // 2, pltpu.roll(u, 96, 1), pltpu.roll(u, 32, 1))


def turn(rows, cosine, sine):
    parts = []
    for g in range(rows.shape[1] // 128):
        u = rows[:, g * 128 : (g + 1) * 128]
        parts.append(u * cosine + swap_halves(u) * sine)
    return parts[0] if len(parts) == 1 else jnp.concatenate(parts, axis=1)


def live_mask(sc, row0, count):
    span_pos = sc[1] * SPAN + row0 + lax.broadcasted_iota(jnp.int32, (count, 1), 0)
    return span_pos < sc[2]


SPAN = 512
SEQ = 1024
WIDTH = 768
GROUP = 384
HID = 2048


def hbm():
    return pl.BlockSpec(memory_space=pl.ANY)


def far_hbm():
    return pl.BlockSpec(memory_space=pltpu.HBM)


def after(sc, *deps):
    return lax.optimization_barrier((sc,) + deps)[0]


def dot_tn(a, b):
    return lax.dot_general(a, b, (((0,), (0,)), ((), ())), preferred_element_type=F32)


def whole(shape):
    return pl.BlockSpec(shape, lambda i, sc: (0,) * len(shape))


def call(body, name, sc, args, in_specs, out_shapes, out_specs, scratch, vmem, cost):
    flops, moved, trans = cost
    args = [
        pltpu.with_memory_space_constraint(a, pltpu.HBM) if spec.memory_space is pltpu.HBM else a
        for a, spec in zip(args, in_specs)
    ]
    return pl.pallas_call(
        body,
        name=name,
        out_shape=out_shapes,
        grid_spec=pltpu.PrefetchScalarGridSpec(
            num_scalar_prefetch=1,
            grid=(1,),
            in_specs=in_specs,
            out_specs=out_specs,
            scratch_shapes=scratch,
        ),
        compiler_params=pltpu.CompilerParams(vmem_limit_bytes=vmem * MIB),
        cost_estimate=pl.CostEstimate(
            flops=int(COST * KERNEL_US[name]), bytes_accessed=1000, transcendentals=0
        ),
    )(sc, *args)


def sds(shape, dtype=BF):
    return jax.ShapeDtypeStruct(shape, dtype)


def project(o_ref, n_ref, cs, ss, weight, t):
    for r in range(0, SPAN, 256):
        y = dot(n_ref[r : r + 256, :], weight)
        if t < 2:
            y = turn(y, cs[r : r + 256, :], ss[r : r + 256, :])
        if t == 0:
            y = y * (HEAD_DIM**-0.5)
        o_ref[t, r : r + 256, :] = y.astype(BF)


def qkv_other_body(
    sc, x_hbm, cos_hbm, sin_hbm, gain, wq, wk, wv, o_ref, n_ref, cs, ss, own_w, xs, ws, gain_s, sem
):
    col = pl.multiple_of((1 - sc[0]) * GROUP, 128)
    own_col = pl.multiple_of(sc[0] * GROUP, 128)
    row = pl.multiple_of(sc[1] * SPAN, SPAN)
    weights = (wq, wk, wv)
    rows = [
        pltpu.make_async_copy(x_hbm.at[0, r : r + 256, :], xs.at[r : r + 256, :], sem.at[n])
        for n, r in enumerate((0, 256))
    ]
    copies = [
        pltpu.make_async_copy(w.at[:, pl.ds(col, GROUP)], ws.at[t], sem.at[2 + t])
        for t, w in enumerate(weights)
    ]
    tables = [
        pltpu.make_async_copy(cos_hbm.at[pl.ds(row, SPAN), :], cs, sem.at[5]),
        pltpu.make_async_copy(sin_hbm.at[pl.ds(row, SPAN), :], ss, sem.at[6]),
    ]
    later = [
        pltpu.make_async_copy(w.at[:, pl.ds(own_col, GROUP)], own_w.at[t], sem.at[7 + t])
        for t, w in enumerate(weights)
    ]
    gain_copy = pltpu.make_async_copy(gain, gain_s, sem.at[10])
    for cp in rows + [gain_copy, copies[2]] + copies[:2] + tables + later:
        cp.start()
    gain_copy.wait()
    gain_row = gain_s[...][None, :]
    for n, r in enumerate((0, 256)):
        rows[n].wait()
        x = jnp.where(live_mask(sc, r, 256), xs[r : r + 256, :].astype(F32), 0.0)
        factor = lax.rsqrt(jnp.mean(x * x, axis=-1, keepdims=True) + epsilon)
        n_ref[r : r + 256, :] = (x * factor * gain_row).astype(BF)
    for t in (2, 0, 1):
        copies[t].wait()
        if t == 0:
            for cp in tables:
                cp.wait()
        project(o_ref, n_ref, cs, ss, ws[t], t)
    for cp in later:
        cp.wait()


def qkv_own_body(sc, n_ref, cs, ss, ws, o_ref):
    for t in (2, 0, 1):
        project(o_ref, n_ref, cs, ss, ws[t], t)


def qkv_other_call(sc, tokens, gain, cosine, sine, wq, wk, wv):
    table = sds((SPAN, 128), F32)
    return call(
        qkv_other_body,
        "qkv_other",
        sc,
        (tokens, cosine, sine, gain, wq, wk, wv),
        [far_hbm()] * 7,
        [sds((3, SPAN, GROUP)), sds((SPAN, WIDTH)), table, table, sds((3, WIDTH, GROUP))],
        [whole((3, SPAN, GROUP)), whole((SPAN, WIDTH))] + [whole((SPAN, 128))] * 2 + [hbm()],
        [
            pltpu.VMEM((SPAN, WIDTH), BF),
            pltpu.VMEM((3, WIDTH, GROUP), BF),
            pltpu.VMEM((WIDTH,), F32),
            pltpu.SemaphoreType.DMA((11,)),
        ],
        9,
        (3 * 2 * SPAN * WIDTH * GROUP, 5e6, 1e3),
    )


def qkv_own_call(sc, n1, cs, ss, ws):
    return call(
        qkv_own_body,
        "qkv_own",
        sc,
        (n1, cs, ss, ws),
        [whole((SPAN, WIDTH))] + [whole((SPAN, 128))] * 2 + [whole((3, WIDTH, GROUP))],
        sds((3, SPAN, GROUP)),
        whole((3, SPAN, GROUP)),
        [],
        9,
        (3 * 2 * SPAN * WIDTH * GROUP, 5e6, 1e3),
    )


def gather_rows(sc, own, other, places, sem):
    copies = []
    for t, place in enumerate(places):
        for k, src in enumerate((own, other)):
            pos = sc[1] if k == 0 else 1 - sc[1]
            row = pl.multiple_of(pos * SPAN, SPAN)
            source = src.at[t] if len(src.shape) == 3 else src
            copies.append(
                pltpu.make_async_copy(source, place.at[pl.ds(row, SPAN), :], sem.at[2 * t + k])
            )
    for cp in copies:
        cp.start()
    return copies


def pair_loads(sc, own, other, places, sem, hp):
    cols = pl.ds(hp * 128 if isinstance(hp, int) else pl.multiple_of(hp * 128, 128), 128)
    copies = []
    for t, place in enumerate(places):
        for k, src in enumerate((own, other)):
            pos = sc[1] if k == 0 else 1 - sc[1]
            rows = pl.ds(pl.multiple_of(pos * SPAN, SPAN), SPAN)
            copies.append(
                pltpu.make_async_copy(
                    src.at[t, :, cols], place.at[rows, cols], sem.at[6 * hp + 2 * t + k]
                )
            )
    return copies


def attend_body(sc, own, other, wo, wg, wu, wd, *refs):
    (ot_ref, lse_ref, mine, theirs, wo_v, wg_v, wu_v, wd_v, qs, ks, vs, at, sem, wsem) = refs
    for n in range(3):
        for cp in pair_loads(sc, own, other, (qs, ks, vs), sem, n):
            cp.start()
    fetch = []

    def bring(src, place):
        fetch.append(pltpu.make_async_copy(src, place, wsem.at[len(fetch)]))
        fetch[-1].start()

    for k in range(2):
        head = (sc[0] if k == 0 else 1 - sc[0]) * GROUP
        rows = pl.ds(pl.multiple_of(head, 128), GROUP)
        bring(wo.at[rows, :], wo_v.at[GROUP * k : GROUP * k + GROUP, :])
    for half in range(2):
        for s in range(4):
            cols = hidden_cols(sc, s, half)
            to = slice(512 * half + 128 * s, 512 * half + 128 * s + 128)
            bring(wg.at[:, cols], wg_v.at[:, to])
            bring(wu.at[:, cols], wu_v.at[:, to])
            bring(wd.at[cols, :], wd_v.at[to, :])
    lane = lax.broadcasted_iota(jnp.int32, (256, 128), 1)
    key_id = lax.broadcasted_iota(jnp.int32, (256, 256), 0)
    row_id = lax.broadcasted_iota(jnp.int32, (256, 256), 1)
    keep = key_id <= row_id

    def pair(hp, carry):
        base = pl.multiple_of(hp * 128, 128)
        cols = pl.ds(base, 128)
        for cp in pair_loads(sc, own, other, (qs, ks, vs), sem, hp):
            cp.wait()
        vt = jnp.transpose(vs[:, cols].astype(F32)).astype(BF)

        def scores(i, h):
            n = 256 * (i + 1)
            qm = jnp.where(lane // HEAD_DIM == h, qs[256 * i : n, cols], jnp.zeros((), BF))
            return dot_nt(ks[0:n, cols], qm)

        def soften(i, h, st):
            n = 256 * (i + 1)
            diag = jnp.where(keep, st[n - 256 :, :], masked_score)
            st = diag if i == 0 else jnp.concatenate([st[: n - 256, :], diag], axis=0)
            peak = jnp.max(st, axis=0, keepdims=True)
            p = jnp.exp(st - peak)
            return p.astype(BF), peak, jnp.sum(p, axis=0, keepdims=True)

        def finish(i, h, p, peak, total):
            n = 256 * (i + 1)
            o = dot(vt[h * 64 : h * 64 + 64, :n], p) * (1.0 / total)
            ot_ref[pl.ds(pl.multiple_of(hp * 128 + h * 64, 64), 64), 256 * i : n] = o
            lse_ref[pl.ds(hp * 2 + h, 1), 256 * i : n] = peak + jnp.log(total)

        tasks = [(i, h) for i in range(4) for h in range(2)]
        st, waiting = scores(*tasks[0]), None
        for k, task in enumerate(tasks):
            ahead = scores(*tasks[k + 1]) if k + 1 < len(tasks) else None
            parts = soften(*task, st)
            if waiting is not None:
                finish(*waiting)
            waiting, st = task + parts, ahead
        finish(*waiting)
        at[:, cols] = jnp.transpose(ot_ref[cols, :]).astype(BF)
        return carry

    lax.fori_loop(0, 3, pair, 0)
    row = pl.multiple_of(sc[1] * SPAN, SPAN)
    row_other = pl.multiple_of((1 - sc[1]) * SPAN, SPAN)
    out_other = pltpu.make_async_copy(at.at[pl.ds(row_other, SPAN), :], theirs, sem.at[18])
    out_own = pltpu.make_async_copy(at.at[pl.ds(row, SPAN), :], mine, sem.at[19])
    out_other.start()
    out_own.start()
    out_other.wait()
    out_own.wait()
    for cp in fetch:
        cp.wait()


def attend_call(sc, own, other, wo, wg, wu, wd):
    return call(
        attend_body,
        "attend",
        sc,
        (own, other, wo, wg, wu, wd),
        [hbm(), hbm()] + [far_hbm()] * 4,
        [sds((GROUP, SEQ), F32), sds((8, SEQ), F32), sds((SPAN, GROUP)), sds((SPAN, GROUP))]
        + [sds((WIDTH, WIDTH)), sds((WIDTH, SEQ)), sds((WIDTH, SEQ)), sds((SEQ, WIDTH))],
        [whole((GROUP, SEQ)), whole((8, SEQ))] + [hbm()] * 6,
        [pltpu.VMEM((SEQ, GROUP), BF)] * 4
        + [pltpu.SemaphoreType.DMA((20,)), pltpu.SemaphoreType.DMA((26,))],
        12,
        (6 * 4 * SEQ * SEQ * 64, 6e6, 4e6),
    )


def proj_body(sc, x_ref, ak_ref, ar_ref, gain_ref, wo_ref, m_ref, n_ref):
    for r in range(0, SPAN, 256):
        rr = slice(r, r + 256)
        m = jnp.where(live_mask(sc, r, 256), x_ref[0, rr, :].astype(F32), 0.0)
        m = m + dot(ak_ref[rr, :], wo_ref[:GROUP, :]) + dot(ar_ref[rr, :], wo_ref[GROUP:, :])
        m_ref[rr, :] = m
        factor = lax.rsqrt(jnp.mean(m * m, axis=-1, keepdims=True) + epsilon)
        n_ref[rr, :] = (m * factor * gain_ref[...]).astype(BF)


def proj_call(sc, tokens, own, other, gain, wo):
    return call(
        proj_body,
        "proj",
        sc,
        (tokens, own, other, gain, wo),
        [whole((1, SPAN, WIDTH))]
        + [whole((SPAN, GROUP))] * 2
        + [whole((1, WIDTH)), whole((WIDTH, WIDTH))],
        [sds((SPAN, WIDTH), F32), sds((SPAN, WIDTH))],
        [whole((SPAN, WIDTH))] * 2,
        [],
        8,
        (2 * SPAN * WIDTH * WIDTH, 5e6, 1e3),
    )


def over_rows(own, other, d_own, d_other):
    return dot_tn(own, d_own) + dot_tn(other, d_other)


def place_of(s):
    return (s % 2) * 2 + s // 2


def hidden_cols(sc, s, half):
    return pl.ds(pl.multiple_of(512 * s + 128 * half + 256 * sc[0], 128), 128)


def spread(sc, res_s, first, count, rows, send_ref, keep_ref, to):
    size = send_ref.shape[1]
    for k, ref in enumerate((send_ref, keep_ref)):
        bit = (1 - sc[3]) if k == 0 else sc[3]
        for s in range(4):
            for q in range(count):
                lo = pl.multiple_of(first + (s * count + q) * 2 * rows + bit * rows, 16)
                block, row = divmod(to + q * rows, size)
                ref[2 * place_of(s) + block, row : row + rows, :] = res_s[pl.ds(lo, rows), :].astype(
                    BF
                )


def ffn_body(sc, n_own, n_oth, dy_own, dy_oth, wg_s, wu_s, wd_s, *refs):
    (send_ref, keep_ref, h_ref, dg_ref, du_ref, dy_s, res_a, res_b) = refs
    for r in range(0, SEQ, 256):
        pos = sc[1] if r < SPAN else 1 - sc[1]
        at = pos * SPAN + r % SPAN + lax.broadcasted_iota(jnp.int32, (256, 1), 0)
        src = dy_own if r < SPAN else dy_oth
        lo = r % SPAN
        dy_s[r : r + 256, :] = jnp.where(at < sc[2], src[0, lo : lo + 256, :], jnp.zeros((), BF))

    def products(r):
        src = n_own if r < SPAN else n_oth
        rows = src[r % SPAN : r % SPAN + 256, :]
        return dot(rows, wg_s[...]), dot(rows, wu_s[...]), dot_nt(dy_s[r : r + 256, :], wd_s[...])

    ahead = products(0)
    for r in range(0, SEQ, 256):
        g, u, dh = ahead
        if r + 256 < SEQ:
            ahead = products(r + 256)
        rr = slice(r, r + 256)
        sg = jax.nn.sigmoid(g)
        gs = g * sg
        h_ref[rr, :] = (gs * u).astype(BF)
        du_ref[rr, :] = (dh * gs).astype(BF)
        dg_ref[rr, :] = (dh * u * (sg + gs * (1.0 - sg))).astype(BF)
    lower, upper = slice(0, SPAN), slice(SPAN, SEQ)
    for k, (base, src) in enumerate(((0, dg_ref), (192, du_ref))):
        for ct in range(2):
            cols = slice(256 * ct, 256 * ct + 256)
            place = res_a.at[ct]
            place[...] = over_rows(n_own[...], n_oth[...], src[lower, cols], src[upper, cols])
            spread(sc, place, 0, 2, 48, send_ref, keep_ref, base + 96 * ct)
    for n in range(3):
        place = res_b.at[n % 2]
        place[...] = dot_tn(h_ref[...], dy_s[:, 256 * n : 256 * n + 256])
        spread(sc, place, 0, 1, 64, send_ref, keep_ref, 384 + 64 * n)


def ffn_call(sc, half, n_own, n_oth, dy_own, dy_oth, wg, wu, wd):
    flat, full = whole((SPAN, WIDTH)), whole((1, SPAN, WIDTH))
    wide = pl.BlockSpec((WIDTH, 512), lambda i, sc: (0, half))
    return call(
        ffn_body,
        "ffn_first" if half == 0 else "ffn_second",
        sc,
        (n_own, n_oth, dy_own, dy_oth, wg, wu, wd),
        [flat, flat, full, full, wide, wide, pl.BlockSpec((512, WIDTH), lambda i, sc: (half, 0))],
        [sds((8, 288, 256))] * 2 + [sds((SEQ, 512))] * 3,
        [whole((8, 288, 256))] * 2 + [whole((SEQ, 512))] * 3,
        [
            pltpu.VMEM((SEQ, WIDTH), BF),
            pltpu.VMEM((2, WIDTH, 256), F32),
            pltpu.VMEM((2, 512, 256), F32),
        ],
        26,
        (6 * 2 * SEQ * WIDTH * 512, 14e6, 1e6),
    )


def ffn_out_body(sc, h0, dg0, du0, h1, dg1, du1, wg, wu, wd, acc_ref, accs_ref, dn_ref, dns_ref):
    for r in (512, 768, 0, 256):
        rr = slice(r, r + 256)
        dn = dot_nt(dg0[rr, :], wg[:, :512]) + dot_nt(dg1[rr, :], wg[:, 512:])
        dn = dn + dot_nt(du0[rr, :], wu[:, :512]) + dot_nt(du1[rr, :], wu[:, 512:])
        acc = dot(h0[rr, :], wd[:512, :]) + dot(h1[rr, :], wd[512:, :])
        if r < SPAN:
            dn_ref[rr, :] = dn
            acc_ref[rr, :] = acc
        else:
            dns_ref[r - SPAN : r - SPAN + 256, :] = dn.astype(BF)
            accs_ref[r - SPAN : r - SPAN + 256, :] = acc.astype(BF)


def ffn_out_call(sc, first, second, wg, wu, wd):
    flat = [whole((SPAN, WIDTH))]
    return call(
        ffn_out_body,
        "ffn_out",
        sc,
        tuple(first) + tuple(second) + (wg, wu, wd),
        [whole((SEQ, 512))] * 6 + [whole((WIDTH, SEQ))] * 2 + [whole((SEQ, WIDTH))],
        [sds((SPAN, WIDTH), F32), sds((SPAN, WIDTH)), sds((SPAN, WIDTH), F32), sds((SPAN, WIDTH))],
        flat * 4,
        [],
        24,
        (3 * 2 * SEQ * WIDTH * SEQ, 16e6, 0),
    )


def middle_body(sc, dn_ref, got_ref, m_ref, dy_ref, gain_ref, dm_ref, db_ref):
    gain = gain_ref[...]
    for r in range(0, SPAN, 128):
        rr = slice(r, r + 128)
        live = live_mask(sc, r, 128)
        m = m_ref[rr, :]
        factor = lax.rsqrt(jnp.mean(m * m, axis=-1, keepdims=True) + epsilon)
        scaled = (dn_ref[rr, :] + got_ref[rr, :].astype(F32)) * gain
        dm = jnp.where(live, dy_ref[0, rr, :].astype(F32), 0.0) + (
            factor * scaled
            - m * (factor * factor * factor) * jnp.mean(m * scaled, axis=-1, keepdims=True)
        )
        dm_ref[rr, :] = dm
        db_ref[rr, :] = dm.astype(BF)


def middle_call(sc, dn, got, m, dy, gain):
    flat = whole((SPAN, WIDTH))
    return call(
        middle_body,
        "middle",
        sc,
        (dn, got, m, dy, gain),
        [flat, flat, flat, whole((1, SPAN, WIDTH)), whole((1, WIDTH))],
        [sds((SPAN, WIDTH), F32), sds((SPAN, WIDTH))],
        [flat, flat],
        [],
        14,
        (1e6, 8e6, 1e3),
    )


def attend_back_body(sc, own, other, ot_s, lse_s, dbk, dbr, wo_s, cos_hbm, sin_hbm, *refs):
    wq, wk, wv, mine, theirs, ws, qs, ks, vs, das, ds_all, dqt, dkv, cs, ss, sem, load_sem = refs
    for n in range(3):
        for cp in pair_loads(sc, own, other, (qs, ks, vs), load_sem, n):
            cp.start()
    small = [
        pltpu.make_async_copy(src, to, sem.at[6 + n])
        for n, (src, to) in enumerate(((cos_hbm, cs), (sin_hbm, ss)))
    ]
    fetch = [
        pltpu.make_async_copy(w, ws.at[t], sem.at[10 + t]) for t, w in enumerate((wq, wk, wv))
    ]
    for cp in small + fetch:
        cp.start()
    for k, src in enumerate((dbk, dbr)):
        pos = sc[1] if k == 0 else 1 - sc[1]
        for r in range(0, SPAN, 256):
            rows = pl.ds(pl.multiple_of(pos * SPAN + r, 256), 256)
            das[rows, :] = dot_nt(src[r : r + 256, :], wo_s[...]).astype(BF)
    for cp in small:
        cp.wait()
    lane = lax.broadcasted_iota(jnp.int32, (SEQ, 128), 1)
    key_id = lax.broadcasted_iota(jnp.int32, (256, 256), 0)
    row_id = lax.broadcasted_iota(jnp.int32, (256, 256), 1)
    keep = key_id <= row_id

    def pair(hp, carry):
        base = pl.multiple_of(hp * 128, 128)
        cols = pl.ds(base, 128)
        for cp in pair_loads(sc, own, other, (qs, ks, vs), load_sem, hp):
            cp.wait()
        kt = jnp.transpose(ks[:, cols].astype(F32)).astype(BF)
        dat = jnp.transpose(das[:, cols].astype(F32))
        qm, dam, delta, lses = [], [], [], []
        for h in range(2):
            qm.append(jnp.where(lane // HEAD_DIM == h, qs[:, cols], jnp.zeros((), BF)))
            dam.append(jnp.where(lane // HEAD_DIM == h, das[:, cols], jnp.zeros((), BF)))
            rows = pl.ds(pl.multiple_of(base + 64 * h, 64), 64)
            product = dat[64 * h : 64 * h + 64, :] * ot_s[rows, :]
            delta.append(jnp.sum(product, axis=0, keepdims=True))
            lses.append(lse_s[pl.ds(2 * hp + h, 1), :])

        def scores(i, h):
            n = 256 * (i + 1)
            rows = slice(256 * i, n)
            return dot_nt(ks[:n, cols], qm[h][rows, :]), dot_nt(vs[:n, cols], dam[h][rows, :])

        def soften(i, h, st, dp):
            n = 256 * (i + 1)
            rows = slice(256 * i, n)
            p = jnp.exp(st - lses[h][:, rows])
            diag = jnp.where(keep, p[n - 256 :, :], 0.0)
            p = diag if i == 0 else jnp.concatenate([p[: n - 256, :], diag], axis=0)
            return p.astype(BF), (p * (dp - delta[h][:, rows])).astype(BF)

        def finish(i, h, p, ds):
            n = 256 * (i + 1)
            rows = slice(256 * i, n)
            half = slice(64 * h, 64 * h + 64)
            dv = dot(p, dam[h][rows, :])
            dk = dot(ds, qm[h][rows, :])
            dqt[half, rows] = dot(kt[half, :n], ds)
            if (i, h) == (3, 0):
                dkv[0] = dk
                dkv[1] = dv
            else:
                dkv[0, :n] += dk
                dkv[1, :n] += dv

        tasks = [(i, h) for i in (3, 2, 1, 0) for h in range(2)]
        now, waiting = scores(*tasks[0]), None
        for k, task in enumerate(tasks):
            ahead = scores(*tasks[k + 1]) if k + 1 < len(tasks) else None
            parts = soften(*task, *now)
            if waiting is not None:
                finish(*waiting)
            waiting, now = task + parts, ahead
        finish(*waiting)
        dq = jnp.transpose(dqt[...]) * (HEAD_DIM**-0.5)
        ds_all[0, :, cols] = turn(dq, cs[...], -ss[...]).astype(BF)
        ds_all[1, :, cols] = turn(dkv[0], cs[...], -ss[...]).astype(BF)
        ds_all[2, :, cols] = dkv[1].astype(BF)
        return carry

    lax.fori_loop(0, 3, pair, 0)
    row = pl.multiple_of(sc[1] * SPAN, SPAN)
    row_other = pl.multiple_of((1 - sc[1]) * SPAN, SPAN)
    stores = [
        pltpu.make_async_copy(ds_all.at[:, pl.ds(row_other, SPAN), :], theirs, sem.at[8]),
        pltpu.make_async_copy(ds_all.at[:, pl.ds(row, SPAN), :], mine, sem.at[9]),
    ]
    for cp in stores:
        cp.start()
    for cp in stores + fetch:
        cp.wait()


def attend_back_call(sc, own, other, ot, lse, dbk, dbr, wo, cosine, sine, wq, wk, wv):
    return call(
        attend_back_body,
        "attend_back",
        sc,
        (own, other, ot, lse, dbk, dbr, wo, cosine, sine, wq, wk, wv),
        [hbm(), hbm(), whole((GROUP, SEQ)), whole((8, SEQ))]
        + [whole((SPAN, WIDTH))] * 2
        + [whole((GROUP, WIDTH))]
        + [far_hbm()] * 5,
        [sds((3, SPAN, GROUP))] * 2 + [sds((3, WIDTH, WIDTH))],
        [hbm()] * 3,
        [pltpu.VMEM((SEQ, GROUP), BF)] * 4
        + [
            pltpu.VMEM((3, SEQ, GROUP), BF),
            pltpu.VMEM((128, SEQ), F32),
            pltpu.VMEM((2, SEQ, 128), F32),
            pltpu.VMEM((SEQ, 128), F32),
            pltpu.VMEM((SEQ, 128), F32),
            pltpu.SemaphoreType.DMA((13,)),
            pltpu.SemaphoreType.DMA((18,)),
        ],
        22,
        (6 * 10 * SEQ * SEQ * 64, 10e6, 4e6),
    )


def square_body(sc, nk, nr, ak, at, ck, ct, bk, br, dk, dr, sa_ref, ka_ref, sb_ref, kb_ref, res):
    own = pl.ds(pl.multiple_of(sc[0] * GROUP, 128), GROUP)
    other = pl.ds(pl.multiple_of((1 - sc[0]) * GROUP, 128), GROUP)
    res[0, own, :] = over_rows(ak[...], at[...], bk[:, own], br[:, own])
    res[0, other, :] = over_rows(ck[...], ct[...], bk[:, own], br[:, own])
    spread(sc, res.at[0], 0, 2, 48, sa_ref, ka_ref, 0)
    for n, t in enumerate((2, 0, 1)):
        place = res.at[(n + 1) % 2]
        place[...] = over_rows(nk[...], nr[...], dk[t], dr[t])
        if n == 0:
            spread(sc, place, 0, 2, 48, sa_ref, ka_ref, 96)
        else:
            spread(sc, place, 0, 2, 48, sb_ref, kb_ref, 96 * t)


def square_call(sc, *args):
    flat = [whole((SPAN, WIDTH))] * 2
    return call(
        square_body,
        "square",
        sc,
        args,
        flat + [whole((SPAN, GROUP))] * 4 + flat + [whole((3, SPAN, GROUP))] * 2,
        [sds((8, 96, GROUP))] * 4,
        [whole((8, 96, GROUP))] * 4,
        [pltpu.VMEM((2, WIDTH, GROUP), F32)],
        16,
        (4 * 2 * SEQ * WIDTH * GROUP, 12e6, 0),
    )


def input_grad_body(sc, x_ref, gain_ref, dm_ref, m_ref, acc_ref, got_ref, dk_s, dr_s, ws, *refs):
    lay_ref, o_ref = refs
    for r in range(0, SPAN, 256):
        rr = slice(r, r + 256)
        out = m_ref[rr, :] + acc_ref[rr, :] + got_ref[rr, :].astype(F32)
        lay_ref[0, rr, :] = jnp.where(live_mask(sc, r, 256), out, 0.0).astype(BF)
    own_cols = pl.multiple_of(sc[0] * GROUP, 128)
    other_cols = pl.multiple_of((1 - sc[0]) * GROUP, 128)
    gain = gain_ref[...]
    for r in range(0, SPAN, 256):
        rr = slice(r, r + 256)
        dn = dot_nt(dk_s[0, rr, :], ws[0, :, pl.ds(own_cols, GROUP)])
        dn = dn + dot_nt(dr_s[0, rr, :], ws[0, :, pl.ds(other_cols, GROUP)])
        for t in (1, 2):
            dn = dn + dot_nt(dk_s[t, rr, :], ws[t, :, pl.ds(own_cols, GROUP)])
            dn = dn + dot_nt(dr_s[t, rr, :], ws[t, :, pl.ds(other_cols, GROUP)])
        live = live_mask(sc, r, 256)
        x = jnp.where(live, x_ref[0, rr, :].astype(F32), 0.0)
        factor = lax.rsqrt(jnp.mean(x * x, axis=-1, keepdims=True) + epsilon)
        scaled = dn * gain
        dx = dm_ref[rr, :] + (
            factor * scaled
            - x * (factor * factor * factor) * jnp.mean(x * scaled, axis=-1, keepdims=True)
        )
        o_ref[0, rr, :] = jnp.where(live, dx, 0.0).astype(BF)


def input_grad_call(sc, tokens, gain, dm, m, acc, got, dk, dr, ws):
    full = whole((1, SPAN, WIDTH))
    flat = whole((SPAN, WIDTH))
    return call(
        input_grad_body,
        "input_grad",
        sc,
        (tokens, gain, dm, m, acc, got, dk, dr, ws),
        [full, whole((1, WIDTH)), flat, flat, flat, flat]
        + [whole((3, SPAN, GROUP))] * 2
        + [whole((3, WIDTH, WIDTH))],
        [sds((1, SPAN, WIDTH))] * 2,
        [full] * 2,
        [],
        20,
        (3 * 2 * SPAN * WIDTH * WIDTH, 14e6, 1e3),
    )


def add_pieces(sc, count, sums, name):
    rows, cols = sums[0][0][0].shape[1:]
    arrays = [array for stack in sums for array, _ in stack]
    picks = [pick for stack in sums for _, pick in stack]

    def body(sc_ref, *refs):
        at = 0
        for n, stack in enumerate(sums):
            total = refs[at][0].astype(F32)
            for ref in refs[at + 1 : at + len(stack)]:
                total = total + ref[0].astype(F32)
            refs[-1][0, n * rows : (n + 1) * rows, :] = total.astype(BF)
            at += len(stack)

    def spec(pick):
        block, row = pick
        return pl.BlockSpec((1, rows, cols), lambda j, sc_ref: (block(sc_ref, j), row, 0))

    high = rows * len(sums)
    return pl.pallas_call(
        body,
        name=name,
        out_shape=sds((count, high, cols)),
        grid_spec=pltpu.PrefetchScalarGridSpec(
            num_scalar_prefetch=1,
            grid=(count,),
            in_specs=[spec(pick) for pick in picks],
            out_specs=pl.BlockSpec((1, high, cols), lambda j, sc_ref: (j, 0, 0)),
        ),
        compiler_params=pltpu.CompilerParams(vmem_limit_bytes=6 * MIB),
        cost_estimate=pl.CostEstimate(
            flops=int(0 if name == "g0_b" else ADD_COST), bytes_accessed=1000, transcendentals=0
        ),
    )(sc, *arrays)


def row_block(rows, cols):
    return pl.BlockSpec((rows, cols), lambda i, sc: (sc[6], 0))


def row_of(column):
    column = jnp.concatenate([column, jnp.zeros((32, 1), F32)], axis=0)
    return jnp.transpose(jnp.broadcast_to(column, (128, 128)))[0, :96]


def collect_halves(sc, group, full):
    for n in range(4):
        core, k = divmod(n, 2)
        parity = sc[0] if core == 0 else 1 - sc[0]
        first = sc[3] if core == 0 else sc[7]
        first = 1 - first if k == 1 else first
        for h in range(2):
            full[parity, first, 288 * h : 288 * h + 288, :] = group[n][h]


def collect(sc, group, full, row, size):
    for n in range(8):
        core, k = divmod(n, 4)
        parity = sc[0] if core == 0 else 1 - sc[0]
        first, second = (sc[3], sc[7]) if core == 0 else (sc[7], sc[3])
        first = 1 - first if k in (1, 3) else first
        second = 1 - second if k in (2, 3) else second
        rows = pl.ds(pl.multiple_of(second * size, 16), size)
        full[parity, first, rows, :] = group[n][0, row : row + size, :]


def ffn_result_body(sc, *refs):
    wg_ref, wu_ref, gain_ref, gate_ref, up_ref, down_ref, gg_ref, full = refs[12:]
    collect_halves(sc, refs[:4], full.at[0])
    collect(sc, refs[4:12], full.at[1], 0, 288)
    for half in range(2):
        for bit in range(2):
            rows = slice(48 * bit, 48 * bit + 48)
            for parity in range(2):
                for base, ref in ((0, gate_ref), (192, up_ref)):
                    for ct in range(2):
                        lo = pl.multiple_of(base + ct * 96 + sc[0] * 48, 16)
                        block = full[half, parity, bit, pl.ds(lo, 48), :].astype(F32)
                        for q in range(2):
                            col = 512 * (2 * ct + q) + 128 * half + 256 * parity
                            ref[rows, col : col + 128] = block[:, 128 * q : 128 * q + 128]
            lo = 128 * half + 64 * bit
            for t in range(3):
                down_ref[lo : lo + 64, 256 * t : 256 * t + 256] = full[
                    half, sc[0], bit, 384 + t * 64 : 448 + t * 64, :
                ].astype(F32)
    gate = jnp.sum(wg_ref[...].astype(F32) * gate_ref[...], axis=-1, keepdims=True)
    up = jnp.sum(wu_ref[...].astype(F32) * up_ref[...], axis=-1, keepdims=True)
    gg_ref[...] = row_of((gate + up) / gain_ref[...])


def ffn_result_call(sc, first, second, wg, wu, gain):
    return call(
        ffn_result_body,
        "ffn_result",
        sc,
        tuple(first) + tuple(second) + (wg, wu, gain),
        [whole((2, 288, 256))] * 4 + [whole((1, 288, 256))] * 8 + [row_block(96, HID)] * 2 + [row_block(96, 1)],
        [sds((96, HID), F32), sds((96, HID), F32), sds((256, WIDTH), F32), sds((96,), F32)],
        [whole((96, HID)), whole((96, HID)), whole((256, WIDTH)), whole((96,))],
        [pltpu.VMEM((2, 2, 2, 576, 256), BF)],
        14,
        (1e6, 6e6, 0),
    )


def square_result_body(sc, *refs):
    group = refs[:8]
    weights = refs[8:11]
    gain_ref = refs[11]
    outs = refs[12:16]
    gg_ref, full = refs[16:]
    order = ((3, 2), (0, 1))
    for n in range(2):
        collect(sc, group, full.at[n], 96 * n, 96)
        for bit in range(2):
            rows = slice(48 * bit, 48 * bit + 48)
            for parity in range(2):
                cols = slice(GROUP * parity, GROUP * parity + GROUP)
                for t in range(2):
                    lo = pl.multiple_of(t * 96 + sc[0] * 48, 16)
                    block = full[n, parity, bit, pl.ds(lo, 48), :]
                    outs[order[n][t]][rows, cols] = block.astype(F32)
    total = jnp.zeros((96, 1), F32)
    for t in range(3):
        total = total + jnp.sum(weights[t][...].astype(F32) * outs[t][...], axis=-1, keepdims=True)
    gg_ref[...] = row_of(total / gain_ref[...])


def square_result_call(sc, group, wq, wk, wv, gain):
    return call(
        square_result_body,
        "square_result",
        sc,
        tuple(group) + (wq, wk, wv, gain),
        [whole((1, 192, GROUP))] * 8 + [row_block(96, WIDTH)] * 3 + [row_block(96, 1)],
        [sds((96, WIDTH), F32)] * 4 + [sds((96,), F32)],
        [whole((96, WIDTH))] * 4 + [whole((96,))],
        [pltpu.VMEM((2, 2, 2, 192, GROUP), BF)],
        8,
        (1e6, 4e6, 0),
    )


class Chain:
    def __init__(self, sc):
        self.sc = sc

    def next(self, *deps):
        self.sc = after(self.sc, *deps)
        return self.sc


class Reduction:
    def __init__(self, chain, send, keep, name):
        self.chain = chain
        self.send = send
        self.name = name
        self.stacks = [[[keep, 0]]]
        self.flight = None

    def start(self):
        self.fly(after(self.send, self.chain.sc), "first")

    def fly(self, rows, kind):
        self.flight = exchange(rows, kind)

    def land(self):
        if self.flight is not None:
            for n, stack in enumerate(self.stacks):
                stack.append([self.flight, n])
        self.flight = None

    def add(self, count, picks, tag):
        self.land()
        sums = []
        for stack in self.stacks:
            blocks = ([picks[0]] + picks)[-len(stack) :]
            sums.append([(array, (pick, row)) for (array, row), pick in zip(stack, blocks)])
        arrays = [array for stack in sums for array, _ in stack]
        out = add_pieces(self.chain.next(*arrays), count, sums, self.name + tag)
        self.chain.next(out)
        return out

    def second(self):
        pick = lambda t, j: j * 2 + 1 - t[7]
        self.fly(self.add(4, [pick], "_b"), "second")

    def near(self):
        pick = lambda t, j: (1 - t[4]) * 4 + j * 2 + t[7]
        self.fly(self.add(2, [pick, lambda t, j: (1 - t[4]) * 2 + j], "_c"), "near")

    def far(self):
        pick = lambda t, j: t[4] * 4 + (1 - t[5]) * 2 + t[7]
        picks = [pick, lambda t, j: t[4] * 2 + 1 - t[5], lambda t, j: 1 - t[5]]
        self.fly(self.add(1, picks, "_d"), "far")

    def total(self):
        pick = lambda t, j: t[4] * 4 + t[5] * 2 + t[7]
        picks = [pick, lambda t, j: t[4] * 2 + t[5], lambda t, j: t[5], lambda t, j: 0]
        own = self.add(1, picks, "_e")
        self.quarters = [own] + [exchange(own, kind) for kind in ("first", "second", "across")]

    def result(self):
        late = [after(quarter, self.chain.sc) for quarter in self.quarters]
        return self.quarters + [exchange(quarter, "core") for quarter in late]


class Straight(Reduction):
    def near(self):
        pick = lambda t, j: (1 - t[4]) * 4 + j
        self.fly(self.add(4, [pick], "_b"), "near")

    def far(self):
        pick = lambda t, j: t[4] * 4 + (1 - t[5]) * 2 + j
        self.fly(self.add(2, [pick, lambda t, j: (1 - t[5]) * 2 + j], "_c"), "far")

    def second(self):
        pick = lambda t, j: t[4] * 4 + t[5] * 2 + j
        own = self.add(2, [pick, lambda t, j: t[5] * 2 + j, lambda t, j: j], "_d")
        self.stacks = [[[own, 0]]]
        self.fly(own, "second")

    def total(self):
        own = self.add(2, [lambda t, j: j], "_e")
        self.quarters = [own, exchange(own, "first")]


def join(first, second):
    both = Reduction(first.chain, None, None, first.name + second.name)
    first.land()
    second.land()
    both.stacks = first.stacks + second.stacks
    return both


def fast_step(
    tokens,
    lengths,
    owner,
    w_query,
    w_key,
    w_value,
    w_out,
    w_gate,
    w_up,
    w_down,
    gain_attn,
    gain_mlp,
    cotangent,
):
    place = lax.axis_index(AXES)
    slot = jnp.arange(8, dtype=jnp.int32)
    core = place & 1
    base = jnp.where(slot == 3, 3 + core, jnp.where(slot == 7, 4 - core, 0))
    base = jnp.where(slot == 4, 1, jnp.where(slot == 5, 2, base))
    row = (place >> base) & jnp.where(slot == 6, 7, 1)
    turned = jnp.abs(row - jnp.broadcast_to(owner[0, :1], (8,)))
    sc = jnp.where(slot == 1, turned, row)
    sc = jnp.where(slot == 2, jnp.broadcast_to(lengths, (8,)), sc)
    tables = position_tables(SEQ)
    cosine, sine = jnp.asarray(tables[0]), jnp.asarray(tables[1])
    gain_row = gain_attn.reshape(1, WIDTH)
    gain_mlp_row = gain_mlp.reshape(1, WIDTH)
    qkv_w = (w_query, w_key, w_value)
    ffn_w = (w_gate, w_up, w_down)
    chain = Chain(sc)

    qkv_send, n1, cs_v, ss_v, w_v = qkv_other_call(chain.sc, tokens, gain_attn, cosine, sine, *qkv_w)
    qkv_other = exchange(qkv_send, "core")
    qkv_own = qkv_own_call(chain.next(n1), n1, cs_v, ss_v, w_v)
    n1_other = exchange(n1, "core")
    dy_other = exchange(cotangent, "core")
    attn_t, lse, attn_own, attn_send, wo_v, *ffn_v = attend_call(
        chain.next(qkv_own), qkv_own, qkv_other, w_out, *ffn_w
    )
    attn_other = exchange(attn_send, "core")
    attn_rest = exchange(attn_own, "core")
    middle, n2 = proj_call(
        chain.next(lse, n1_other, dy_other), tokens, attn_own, attn_other, gain_mlp_row, wo_v
    )
    n2_other = exchange(n2, "core")
    rows = (n2, n2_other, cotangent, dy_other)
    send0, keep0, *acts0 = ffn_call(chain.next(n2, attn_rest), 0, *rows, *ffn_v)
    g0 = Straight(chain, send0, keep0, "g0")
    g0.start()
    send1, keep1, *acts1 = ffn_call(chain.next(acts0[0]), 1, *rows, *ffn_v)
    g1 = Reduction(chain, send1, keep1, "g1")
    g1.start()
    acc, acc_send, dn, dn_send = ffn_out_call(chain.next(acts1[0]), acts0, acts1, *ffn_v)
    dn_other = exchange(dn_send, "core")
    chain.next(dn_send)
    d_middle, db = middle_call(
        chain.next(dn_other, g0.flight), dn, dn_other, middle, cotangent, gain_mlp_row
    )
    chain.next(db)
    g0.near()
    db_other = exchange(db, "core")
    acc_other = exchange(after(acc_send, db_other), "core")
    d_own, d_send, qkv_v = attend_back_call(
        chain.sc,
        qkv_own,
        qkv_other,
        attn_t,
        lse,
        db,
        db_other,
        wo_v,
        cosine,
        sine,
        *qkv_w,
    )
    d_other = exchange(d_send, "core")
    chain.next(d_own, g0.flight, g1.flight)
    g1.second()
    g0.far()
    attn = (attn_own, attn_send, attn_other, attn_rest)
    send2, keep2, send3, keep3 = square_call(
        chain.sc, n1, n1_other, *attn, db, db_other, d_own, d_send
    )
    g2 = Reduction(chain, send2, keep2, "g2")
    g3 = Reduction(chain, send3, keep3, "g3")
    g2.start()
    g3.start()
    chain.next(send3)
    layer_out, input_grad = input_grad_call(
        chain.next(acc_other, d_other),
        tokens,
        gain_row,
        d_middle,
        middle,
        acc,
        acc_other,
        d_own,
        d_other,
        qkv_v,
    )
    chain.next(input_grad)
    g0.second()
    g1.near()
    g2.second()
    g1.far()
    g3.second()
    g2.near()
    g0.total()
    g3.near()
    g2.far()
    g3.far()
    g1.total()
    g23 = join(g2, g3)
    g23.total()
    first = g0.result()
    second = g1.result()
    third = g23.result()
    gate, up, down, gain_m = ffn_result_call(
        chain.sc, first, second, w_gate, w_up, gain_mlp.reshape(WIDTH, 1)
    )
    chain.next(gain_m)
    query, key, value, out, gain_a = square_result_call(
        chain.sc, third, *qkv_w, gain_attn.reshape(WIDTH, 1)
    )
    return (
        layer_out,
        input_grad,
        query,
        key,
        value,
        out,
        gate,
        up,
        down,
        gain_a,
        gain_m,
    )


def solution(mesh):
    in_specs = (
        P(("batch", "seq"), "seqb", None),
        P(("batch", "seq")),
        P(("batch", "seq"), None),
        P(),
        P(),
        P(),
        P(),
        P(),
        P(),
        P(),
        P(),
        P(),
        P(("batch", "seq"), "seqb", None),
    )
    out_specs = (
        P(("batch", "seq"), "seqb", None),
        P(("batch", "seq"), "seqb", None),
        P(("seq", "seqb"), None),
        P(("seq", "seqb"), None),
        P(("seq", "seqb"), None),
        P(("seq", "seqb"), None),
        P(("seq", "seqb"), None),
        P(("seq", "seqb"), None),
        P(("seq", "seqb"), None),
        P(("seq", "seqb")),
        P(("seq", "seqb")),
    )
    step = fast_step if fast_layout(mesh) else general_step
    return jax.shard_map(step, mesh=mesh, in_specs=in_specs, out_specs=out_specs, check_vma=False)
```

```python
import functools
import math

import jax
import jax.numpy as jnp
import numpy as np
from jax import lax
from jax.experimental import pallas as pl
from jax.experimental.pallas import tpu as pltpu
from jax.sharding import PartitionSpec as P

HEADS = 12
HEAD_DIM = 64


epsilon = 1e-05
rope_base = 10000.0
masked_score = -1e30


def rms_forward(rows, gain):
    factor = lax.rsqrt(jnp.mean(rows * rows, axis=-1, keepdims=True) + epsilon)
    return (rows * factor * gain, factor)


def rms_backward(rows, factor, gain, upstream):
    scaled = upstream * gain
    return factor * scaled - rows * (factor * factor * factor) * jnp.mean(
        rows * scaled, axis=-1, keepdims=True
    )


def rotation_tables(positions):
    half = HEAD_DIM // 2
    freq = rope_base ** (-(2.0 * jnp.arange(half, dtype=jnp.float32)) / HEAD_DIM)
    angles = positions.astype(jnp.float32)[..., None] * freq
    return (jnp.cos(angles), jnp.sin(angles))


def split_heads(rows):
    return rows.reshape(rows.shape[0], rows.shape[1], HEADS, HEAD_DIM)


def rotate(rows, cosine, sine, inverse):
    shaped = split_heads(rows)
    half = HEAD_DIM // 2
    first = shaped[..., :half]
    second = shaped[..., half:]
    cos_part = cosine[:, :, None, :]
    sin_part = sine[:, :, None, :]
    if inverse:
        turned = jnp.concatenate(
            [first * cos_part + second * sin_part, second * cos_part - first * sin_part], axis=-1
        )
    else:
        turned = jnp.concatenate(
            [first * cos_part - second * sin_part, second * cos_part + first * sin_part], axis=-1
        )
    return turned.reshape(rows.shape)


def range_positions(owner, count, span):
    offsets = jnp.arange(span, dtype=jnp.int32)
    return (owner[:, :, None] * span + offsets[None, None, :]).reshape(owner.shape[0], count)


def fold_keys(parts, combine, initial):
    return combine(
        initial,
        (
            lax.all_gather(parts[0], "seqb", axis=1, tiled=True),
            lax.all_gather(parts[1], "seqb", axis=1, tiled=True),
        ),
        jnp.int32(0),
    )


def general_step(
    tokens,
    lengths,
    owner,
    w_query,
    w_key,
    w_value,
    w_out,
    w_gate,
    w_up,
    w_down,
    gain_attn,
    gain_mlp,
    cotangent,
):
    seqs, span, width = tokens.shape
    scale = HEAD_DIM ** (-0.5)
    place = lax.axis_index("seqb")
    own_block = lax.dynamic_slice_in_dim(owner, place, 1, 1)
    local_pos = own_block * span + jnp.arange(span, dtype=jnp.int32)[None, :]
    local_live = local_pos < lengths[:, None]
    live_rows = local_live[:, :, None]
    inputs = jnp.where(live_rows, tokens.astype(jnp.float32), 0.0)
    normed, factor_attn = rms_forward(inputs, gain_attn)
    normed_low = normed.astype(jnp.bfloat16)
    cosine, sine = rotation_tables(local_pos)
    query_pre = jnp.einsum("scd,de->sce", normed_low, w_query, preferred_element_type=jnp.float32)
    key_pre = jnp.einsum("scd,de->sce", normed_low, w_key, preferred_element_type=jnp.float32)
    value_low = jnp.einsum(
        "scd,de->sce", normed_low, w_value, preferred_element_type=jnp.float32
    ).astype(jnp.bfloat16)
    query_rot = rotate(query_pre, cosine, sine, False).astype(jnp.bfloat16)
    key_rot = rotate(key_pre, cosine, sine, False).astype(jnp.bfloat16)
    query_heads = split_heads(query_rot)
    key_heads = split_heads(key_rot)
    value_heads = split_heads(value_low)

    def attend(state, piece, start):
        keys, values = piece
        count = keys.shape[1]
        key_pos = range_positions(owner, count, span)
        key_live = key_pos < lengths[:, None]
        stride = math.gcd(count, 512)

        def attend_one_block(index, inner):
            offset = index * stride
            key_block = split_heads(lax.dynamic_slice_in_dim(keys, offset, stride, 1))
            value_block = split_heads(lax.dynamic_slice_in_dim(values, offset, stride, 1))
            pos_block = lax.dynamic_slice_in_dim(key_pos, offset, stride, 1)
            live_block = lax.dynamic_slice_in_dim(key_live, offset, stride, 1)
            allowed = (
                (pos_block[:, None, :] <= local_pos[:, :, None])
                & live_block[:, None, :]
                & local_live[:, :, None]
            )

            def attend_update(carried):
                peak, total, summed = carried
                scores = (
                    jnp.einsum(
                        "sqhd,skhd->shqk",
                        query_heads,
                        key_block,
                        preferred_element_type=jnp.float32,
                    )
                    * scale
                )
                mask = allowed[:, None, :, :]
                new_peak = jnp.maximum(
                    peak, jnp.max(jnp.where(mask, scores, masked_score), axis=-1)
                )
                weights = jnp.where(mask, jnp.exp(scores - new_peak[..., None]), 0.0)
                factor = jnp.exp(peak - new_peak)
                total = total * factor + jnp.sum(weights, axis=-1)
                term = jnp.einsum(
                    "shqk,skhd->sqhd",
                    weights.astype(jnp.bfloat16),
                    value_block,
                    preferred_element_type=jnp.float32,
                )
                summed = (
                    split_heads(summed) * jnp.transpose(factor, (0, 2, 1))[..., None] + term
                ).reshape(summed.shape)
                return (new_peak, total, summed)

            return lax.cond(jnp.any(allowed), attend_update, lambda carried: carried, inner)

        return lax.fori_loop(0, count // stride, attend_one_block, state)

    start_state = (
        jnp.full((seqs, HEADS, span), masked_score, jnp.float32),
        jnp.zeros((seqs, HEADS, span), jnp.float32),
        jnp.zeros((seqs, span, width), jnp.float32),
    )
    peak, total, summed = fold_keys((key_rot, value_low), attend, start_state)
    safe_total = jnp.where(local_live[:, None, :], total, 1.0)
    attn = split_heads(summed) / jnp.transpose(safe_total, (0, 2, 1))[..., None]
    attn = jnp.where(local_live[:, :, None, None], attn, 0.0).reshape(seqs, span, width)
    log_total = jnp.where(local_live[:, None, :], peak + jnp.log(safe_total), 0.0)
    attn_low = attn.astype(jnp.bfloat16)
    middle = inputs + jnp.einsum("scd,de->sce", attn_low, w_out, preferred_element_type=jnp.float32)
    normed_mlp, factor_mlp = rms_forward(middle, gain_mlp)
    normed_mlp_low = normed_mlp.astype(jnp.bfloat16)
    gate = jnp.einsum("scd,df->scf", normed_mlp_low, w_gate, preferred_element_type=jnp.float32)
    up_proj = jnp.einsum("scd,df->scf", normed_mlp_low, w_up, preferred_element_type=jnp.float32)
    hidden = (jax.nn.silu(gate) * up_proj).astype(jnp.bfloat16)
    out = middle + jnp.einsum("scf,fd->scd", hidden, w_down, preferred_element_type=jnp.float32)
    layer_out = jnp.where(live_rows, out, 0.0).astype(jnp.bfloat16)
    upstream = jnp.where(live_rows, cotangent, jnp.zeros_like(cotangent))
    grad_down = jnp.einsum("scf,scd->fd", hidden, upstream, preferred_element_type=jnp.float32)
    d_hidden = jnp.einsum("scd,fd->scf", upstream, w_down, preferred_element_type=jnp.float32)
    sigmoid_gate = jax.nn.sigmoid(gate)
    d_gate = (d_hidden * up_proj * sigmoid_gate * (1.0 + gate * (1.0 - sigmoid_gate))).astype(
        jnp.bfloat16
    )
    d_up = (d_hidden * gate * sigmoid_gate).astype(jnp.bfloat16)
    grad_gate = jnp.einsum(
        "scd,scf->df", normed_mlp_low, d_gate, preferred_element_type=jnp.float32
    )
    grad_up = jnp.einsum("scd,scf->df", normed_mlp_low, d_up, preferred_element_type=jnp.float32)
    d_normed_mlp = jnp.einsum(
        "scf,df->scd", d_gate, w_gate, preferred_element_type=jnp.float32
    ) + jnp.einsum("scf,df->scd", d_up, w_up, preferred_element_type=jnp.float32)
    grad_gain_mlp = jnp.sum(d_normed_mlp * (middle * factor_mlp), axis=(0, 1))
    d_middle = upstream.astype(jnp.float32) + rms_backward(
        middle, factor_mlp, gain_mlp, d_normed_mlp
    )
    d_branch = d_middle.astype(jnp.bfloat16)
    grad_out = jnp.einsum("scd,sce->de", attn_low, d_branch, preferred_element_type=jnp.float32)
    d_attn = jnp.einsum("sce,de->scd", d_branch, w_out, preferred_element_type=jnp.float32).astype(
        jnp.bfloat16
    )
    first_done = (grad_out, grad_gate, grad_up, grad_down, grad_gain_mlp)
    delta = jnp.sum(split_heads(d_attn.astype(jnp.float32) * attn), axis=-1)
    delta_heads = jnp.transpose(delta, (0, 2, 1))
    grad_heads = split_heads(d_attn)

    def query_grads(state, piece, start):
        keys, values = piece
        count = keys.shape[1]
        key_pos = range_positions(owner, count, span)
        key_live = key_pos < lengths[:, None]
        stride = math.gcd(count, 512)

        def query_one_block(index, inner):
            offset = index * stride
            key_block = split_heads(lax.dynamic_slice_in_dim(keys, offset, stride, 1))
            value_block = split_heads(lax.dynamic_slice_in_dim(values, offset, stride, 1))
            pos_block = lax.dynamic_slice_in_dim(key_pos, offset, stride, 1)
            live_block = lax.dynamic_slice_in_dim(key_live, offset, stride, 1)
            allowed = (
                (pos_block[:, None, :] <= local_pos[:, :, None])
                & live_block[:, None, :]
                & local_live[:, :, None]
            )

            def query_update(carried):
                scores = (
                    jnp.einsum(
                        "sqhd,skhd->shqk",
                        query_heads,
                        key_block,
                        preferred_element_type=jnp.float32,
                    )
                    * scale
                )
                probs = jnp.where(
                    allowed[:, None, :, :], jnp.exp(scores - log_total[..., None]), 0.0
                )
                d_probs = jnp.einsum(
                    "sqhd,skhd->shqk", grad_heads, value_block, preferred_element_type=jnp.float32
                )
                d_scores = (probs * (d_probs - delta_heads[..., None])).astype(jnp.bfloat16)
                term = (
                    jnp.einsum(
                        "shqk,skhd->sqhd", d_scores, key_block, preferred_element_type=jnp.float32
                    )
                    * scale
                )
                return carried + term.reshape(carried.shape)

            return lax.cond(jnp.any(allowed), query_update, lambda carried: carried, inner)

        return lax.fori_loop(0, count // stride, query_one_block, state)

    zero_query = jnp.zeros((seqs, span, width), jnp.float32)
    d_query = fold_keys((key_rot, value_low), query_grads, zero_query)
    lse_all, delta_all = (
        lax.all_gather(jnp.transpose(log_total, (0, 2, 1)), "seqb", axis=1, tiled=True),
        lax.all_gather(delta, "seqb", axis=1, tiled=True),
    )
    zero_rows = jnp.zeros((seqs, span, width), jnp.float32)
    queries = lax.all_gather(query_rot, "seqb", axis=1, tiled=True)
    d_rows = lax.all_gather(d_attn, "seqb", axis=1, tiled=True)
    count = queries.shape[1]
    row_pos = range_positions(owner, count, span)
    row_live = row_pos < lengths[:, None]
    stride = math.gcd(count, 512)

    def key_one_block(index, inner):
        offset = index * stride
        query_block = split_heads(lax.dynamic_slice_in_dim(queries, offset, stride, 1))
        grad_block = split_heads(lax.dynamic_slice_in_dim(d_rows, offset, stride, 1))
        pos_block = lax.dynamic_slice_in_dim(row_pos, offset, stride, 1)
        live_block = lax.dynamic_slice_in_dim(row_live, offset, stride, 1)
        lse_block = jnp.transpose(lax.dynamic_slice_in_dim(lse_all, offset, stride, 1), (0, 2, 1))
        delta_block = jnp.transpose(
            lax.dynamic_slice_in_dim(delta_all, offset, stride, 1), (0, 2, 1)
        )
        allowed = (
            (local_pos[:, None, :] <= pos_block[:, :, None])
            & local_live[:, None, :]
            & live_block[:, :, None]
        )

        def key_update(carried):
            d_key, d_value = carried
            scores = (
                jnp.einsum(
                    "sqhd,skhd->shqk", query_block, key_heads, preferred_element_type=jnp.float32
                )
                * scale
            )
            probs = jnp.where(allowed[:, None, :, :], jnp.exp(scores - lse_block[..., None]), 0.0)
            value_term = jnp.einsum(
                "shqk,sqhd->skhd",
                probs.astype(jnp.bfloat16),
                grad_block,
                preferred_element_type=jnp.float32,
            )
            d_probs = jnp.einsum(
                "sqhd,skhd->shqk", grad_block, value_heads, preferred_element_type=jnp.float32
            )
            d_scores = (probs * (d_probs - delta_block[..., None])).astype(jnp.bfloat16)
            key_term = (
                jnp.einsum(
                    "shqk,sqhd->skhd", d_scores, query_block, preferred_element_type=jnp.float32
                )
                * scale
            )
            return (
                d_key + key_term.reshape(d_key.shape),
                d_value + value_term.reshape(d_value.shape),
            )

        return lax.cond(jnp.any(allowed), key_update, lambda carried: carried, inner)

    d_key, d_value = lax.fori_loop(0, count // stride, key_one_block, (zero_rows, zero_rows))
    d_query_pre = rotate(d_query, cosine, sine, True).astype(jnp.bfloat16)
    d_key_pre = rotate(d_key, cosine, sine, True).astype(jnp.bfloat16)
    d_value_low = d_value.astype(jnp.bfloat16)
    grad_query = jnp.einsum(
        "scd,sce->de", normed_low, d_query_pre, preferred_element_type=jnp.float32
    )
    grad_key = jnp.einsum("scd,sce->de", normed_low, d_key_pre, preferred_element_type=jnp.float32)
    grad_value = jnp.einsum(
        "scd,sce->de", normed_low, d_value_low, preferred_element_type=jnp.float32
    )
    d_normed = jnp.einsum("sce,de->scd", d_query_pre, w_query, preferred_element_type=jnp.float32)
    d_normed = d_normed + jnp.einsum(
        "sce,de->scd", d_key_pre, w_key, preferred_element_type=jnp.float32
    )
    d_normed = d_normed + jnp.einsum(
        "sce,de->scd", d_value_low, w_value, preferred_element_type=jnp.float32
    )
    grad_gain_attn = jnp.sum(d_normed * (inputs * factor_attn), axis=(0, 1))
    d_inputs = d_middle + rms_backward(inputs, factor_attn, gain_attn, d_normed)
    input_grad = jnp.where(live_rows, d_inputs, 0.0).astype(jnp.bfloat16)
    summed_parts = (
        lax.psum_scatter(grad_query, ("seq", "seqb"), scatter_dimension=0, tiled=True),
        lax.psum_scatter(grad_key, ("seq", "seqb"), scatter_dimension=0, tiled=True),
        lax.psum_scatter(grad_value, ("seq", "seqb"), scatter_dimension=0, tiled=True),
        lax.psum_scatter(grad_gain_attn, ("seq", "seqb"), scatter_dimension=0, tiled=True),
        lax.psum_scatter(first_done[0], ("seq", "seqb"), scatter_dimension=0, tiled=True),
        lax.psum_scatter(first_done[1], ("seq", "seqb"), scatter_dimension=0, tiled=True),
        lax.psum_scatter(first_done[2], ("seq", "seqb"), scatter_dimension=0, tiled=True),
        lax.psum_scatter(first_done[3], ("seq", "seqb"), scatter_dimension=0, tiled=True),
        lax.psum_scatter(first_done[4], ("seq", "seqb"), scatter_dimension=0, tiled=True),
    )
    all_done = (
        lax.psum(summed_parts[0].astype(jnp.bfloat16), "batch").astype(jnp.float32),
        lax.psum(summed_parts[1].astype(jnp.bfloat16), "batch").astype(jnp.float32),
        lax.psum(summed_parts[2].astype(jnp.bfloat16), "batch").astype(jnp.float32),
        lax.psum(summed_parts[3].astype(jnp.bfloat16), "batch").astype(jnp.float32),
        lax.psum(summed_parts[4].astype(jnp.bfloat16), "batch").astype(jnp.float32),
        lax.psum(summed_parts[5].astype(jnp.bfloat16), "batch").astype(jnp.float32),
        lax.psum(summed_parts[6].astype(jnp.bfloat16), "batch").astype(jnp.float32),
        lax.psum(summed_parts[7].astype(jnp.bfloat16), "batch").astype(jnp.float32),
        lax.psum(summed_parts[8].astype(jnp.bfloat16), "batch").astype(jnp.float32),
    )
    second_done = (all_done[0], all_done[1], all_done[2], all_done[3])
    first_done = (all_done[4], all_done[5], all_done[6], all_done[7], all_done[8])
    return (
        layer_out,
        input_grad,
        second_done[0],
        second_done[1],
        second_done[2],
        first_done[0],
        first_done[1],
        first_done[2],
        first_done[3],
        second_done[3],
        first_done[4],
    )


AXES = ("batch", "seq", "seqb")
BF = jnp.bfloat16
F32 = jnp.float32
MIB = 1 << 20
COST = 1e6
ADD_COST = 2e9
KERNEL_US = {
    "qkv_other": 4,
    "qkv_own": 4,
    "attend": 9,
    "proj": 3,
    "upstream": 2,
    "ffn_first": 8,
    "ffn_second": 8,
    "ffn_out": 9,
    "middle": 1.4,
    "attend_back": 14,
    "square": 5,
    "input_grad": 6.5,
    "ffn_result": 2,
    "square_result": 2,
}


def fast_layout(mesh):
    return mesh.shape["batch"] == 4 and mesh.shape["seq"] == 4 and mesh.shape["seqb"] == 2


def exchange(rows, kind):
    pairs = []
    for b in range(4):
        for s in range(4):
            for c in range(2):
                first = 1 if c == 0 else 2
                target = {
                    "core": (b, s, 1 - c),
                    "first": (b ^ first, s, c),
                    "second": (b ^ (3 - first), s, c),
                    "near": (b, s ^ 1, c),
                    "far": (b, s ^ 2, c),
                    "across": (b ^ 3, s, c),
                }[kind]
                pairs.append((b * 8 + s * 2 + c, target[0] * 8 + target[1] * 2 + target[2]))
    return lax.ppermute(rows, AXES, pairs)


def dot(a, b):
    return lax.dot_general(a, b, (((1,), (0,)), ((), ())), preferred_element_type=F32)


def dot_nt(a, b):
    return lax.dot_general(a, b, (((1,), (1,)), ((), ())), preferred_element_type=F32)


def position_tables(count):
    half = HEAD_DIM // 2
    freq = rope_base ** (-(2.0 * np.arange(half)) / HEAD_DIM)
    angles = np.arange(count)[:, None] * freq[None, :]
    cosine, sine = np.cos(angles), np.sin(angles)
    return (
        np.concatenate([cosine, cosine, cosine, cosine], 1).astype(np.float32),
        np.concatenate([-sine, sine, -sine, sine], 1).astype(np.float32),
    )


def swap_halves(u):
    lane = lax.broadcasted_iota(jnp.int32, u.shape, 1) % HEAD_DIM
    return jnp.where(lane < HEAD_DIM // 2, pltpu.roll(u, 96, 1), pltpu.roll(u, 32, 1))


def turn(rows, cosine, sine):
    parts = []
    for g in range(rows.shape[1] // 128):
        u = rows[:, g * 128 : (g + 1) * 128]
        parts.append(u * cosine + swap_halves(u) * sine)
    return parts[0] if len(parts) == 1 else jnp.concatenate(parts, axis=1)


def live_mask(sc, row0, count):
    span_pos = sc[1] * SPAN + row0 + lax.broadcasted_iota(jnp.int32, (count, 1), 0)
    return span_pos < sc[2]


SPAN = 512
SEQ = 1024
WIDTH = 768
GROUP = 384
HID = 2048


def hbm():
    return pl.BlockSpec(memory_space=pl.ANY)


def far_hbm():
    return pl.BlockSpec(memory_space=pltpu.HBM)


def after(sc, *deps):
    return lax.optimization_barrier((sc,) + deps)[0]


def dot_tn(a, b):
    return lax.dot_general(a, b, (((0,), (0,)), ((), ())), preferred_element_type=F32)


def whole(shape):
    return pl.BlockSpec(shape, lambda i, sc: (0,) * len(shape))


def call(body, name, sc, args, in_specs, out_shapes, out_specs, scratch, vmem, cost):
    flops, moved, trans = cost
    args = [
        pltpu.with_memory_space_constraint(a, pltpu.HBM) if spec.memory_space is pltpu.HBM else a
        for a, spec in zip(args, in_specs)
    ]
    return pl.pallas_call(
        body,
        name=name,
        out_shape=out_shapes,
        grid_spec=pltpu.PrefetchScalarGridSpec(
            num_scalar_prefetch=1,
            grid=(1,),
            in_specs=in_specs,
            out_specs=out_specs,
            scratch_shapes=scratch,
        ),
        compiler_params=pltpu.CompilerParams(vmem_limit_bytes=vmem * MIB),
        cost_estimate=pl.CostEstimate(
            flops=int(COST * KERNEL_US[name]), bytes_accessed=1000, transcendentals=0
        ),
    )(sc, *args)


def sds(shape, dtype=BF):
    return jax.ShapeDtypeStruct(shape, dtype)


def project(o_ref, n_ref, cs, ss, weight, t):
    for r in range(0, SPAN, 256):
        y = dot(n_ref[r : r + 256, :], weight)
        if t < 2:
            y = turn(y, cs[r : r + 256, :], ss[r : r + 256, :])
        if t == 0:
            y = y * (HEAD_DIM**-0.5)
        o_ref[t, r : r + 256, :] = y.astype(BF)


def qkv_other_body(
    sc, x_hbm, cos_hbm, sin_hbm, gain, wq, wk, wv, o_ref, n_ref, cs, ss, own_w, xs, ws, gain_s, sem
):
    col = pl.multiple_of((1 - sc[0]) * GROUP, 128)
    own_col = pl.multiple_of(sc[0] * GROUP, 128)
    row = pl.multiple_of(sc[1] * SPAN, SPAN)
    weights = (wq, wk, wv)
    rows = [
        pltpu.make_async_copy(x_hbm.at[0, r : r + 256, :], xs.at[r : r + 256, :], sem.at[n])
        for n, r in enumerate((0, 256))
    ]
    copies = [
        pltpu.make_async_copy(w.at[:, pl.ds(col, GROUP)], ws.at[t], sem.at[2 + t])
        for t, w in enumerate(weights)
    ]
    tables = [
        pltpu.make_async_copy(cos_hbm.at[pl.ds(row, SPAN), :], cs, sem.at[5]),
        pltpu.make_async_copy(sin_hbm.at[pl.ds(row, SPAN), :], ss, sem.at[6]),
    ]
    later = [
        pltpu.make_async_copy(w.at[:, pl.ds(own_col, GROUP)], own_w.at[t], sem.at[7 + t])
        for t, w in enumerate(weights)
    ]
    gain_copy = pltpu.make_async_copy(gain, gain_s, sem.at[10])
    for cp in rows + [gain_copy, copies[2]] + copies[:2] + tables + later:
        cp.start()
    gain_copy.wait()
    gain_row = gain_s[...][None, :]
    for n, r in enumerate((0, 256)):
        rows[n].wait()
        x = jnp.where(live_mask(sc, r, 256), xs[r : r + 256, :].astype(F32), 0.0)
        factor = lax.rsqrt(jnp.mean(x * x, axis=-1, keepdims=True) + epsilon)
        n_ref[r : r + 256, :] = (x * factor * gain_row).astype(BF)
    for t in (2, 0, 1):
        copies[t].wait()
        if t == 0:
            for cp in tables:
                cp.wait()
        project(o_ref, n_ref, cs, ss, ws[t], t)
    for cp in later:
        cp.wait()


def qkv_own_body(sc, n_ref, cs, ss, ws, o_ref):
    for t in (2, 0, 1):
        project(o_ref, n_ref, cs, ss, ws[t], t)


def qkv_other_call(sc, tokens, gain, cosine, sine, wq, wk, wv):
    table = sds((SPAN, 128), F32)
    return call(
        qkv_other_body,
        "qkv_other",
        sc,
        (tokens, cosine, sine, gain, wq, wk, wv),
        [far_hbm()] * 7,
        [sds((3, SPAN, GROUP)), sds((SPAN, WIDTH)), table, table, sds((3, WIDTH, GROUP))],
        [whole((3, SPAN, GROUP)), whole((SPAN, WIDTH))] + [whole((SPAN, 128))] * 2 + [hbm()],
        [
            pltpu.VMEM((SPAN, WIDTH), BF),
            pltpu.VMEM((3, WIDTH, GROUP), BF),
            pltpu.VMEM((WIDTH,), F32),
            pltpu.SemaphoreType.DMA((11,)),
        ],
        9,
        (3 * 2 * SPAN * WIDTH * GROUP, 5e6, 1e3),
    )


def qkv_own_call(sc, n1, cs, ss, ws):
    return call(
        qkv_own_body,
        "qkv_own",
        sc,
        (n1, cs, ss, ws),
        [whole((SPAN, WIDTH))] + [whole((SPAN, 128))] * 2 + [whole((3, WIDTH, GROUP))],
        sds((3, SPAN, GROUP)),
        whole((3, SPAN, GROUP)),
        [],
        9,
        (3 * 2 * SPAN * WIDTH * GROUP, 5e6, 1e3),
    )


def gather_rows(sc, own, other, places, sem):
    copies = []
    for t, place in enumerate(places):
        for k, src in enumerate((own, other)):
            pos = sc[1] if k == 0 else 1 - sc[1]
            row = pl.multiple_of(pos * SPAN, SPAN)
            source = src.at[t] if len(src.shape) == 3 else src
            copies.append(
                pltpu.make_async_copy(source, place.at[pl.ds(row, SPAN), :], sem.at[2 * t + k])
            )
    for cp in copies:
        cp.start()
    return copies


def pair_loads(sc, own, other, places, sem, hp):
    cols = pl.ds(hp * 128 if isinstance(hp, int) else pl.multiple_of(hp * 128, 128), 128)
    copies = []
    for t, place in enumerate(places):
        for k, src in enumerate((own, other)):
            pos = sc[1] if k == 0 else 1 - sc[1]
            rows = pl.ds(pl.multiple_of(pos * SPAN, SPAN), SPAN)
            copies.append(
                pltpu.make_async_copy(
                    src.at[t, :, cols], place.at[rows, cols], sem.at[6 * hp + 2 * t + k]
                )
            )
    return copies


def attend_body(sc, own, other, wo, wg, wu, wd, *refs):
    (ot_ref, lse_ref, mine, theirs, wo_v, wg_v, wu_v, wd_v, qs, ks, vs, at, sem, wsem) = refs
    for n in range(3):
        for cp in pair_loads(sc, own, other, (qs, ks, vs), sem, n):
            cp.start()
    fetch = []

    def bring(src, place):
        fetch.append(pltpu.make_async_copy(src, place, wsem.at[len(fetch)]))
        fetch[-1].start()

    for k in range(2):
        head = (sc[0] if k == 0 else 1 - sc[0]) * GROUP
        rows = pl.ds(pl.multiple_of(head, 128), GROUP)
        bring(wo.at[rows, :], wo_v.at[GROUP * k : GROUP * k + GROUP, :])
    for half in range(2):
        for s in range(4):
            cols = hidden_cols(sc, s, half)
            to = slice(512 * half + 128 * s, 512 * half + 128 * s + 128)
            bring(wg.at[:, cols], wg_v.at[:, to])
            bring(wu.at[:, cols], wu_v.at[:, to])
            bring(wd.at[cols, :], wd_v.at[to, :])
    lane = lax.broadcasted_iota(jnp.int32, (256, 128), 1)
    key_id = lax.broadcasted_iota(jnp.int32, (256, 256), 0)
    row_id = lax.broadcasted_iota(jnp.int32, (256, 256), 1)
    keep = key_id <= row_id

    def pair(hp, carry):
        base = pl.multiple_of(hp * 128, 128)
        cols = pl.ds(base, 128)
        for cp in pair_loads(sc, own, other, (qs, ks, vs), sem, hp):
            cp.wait()
        vt = jnp.transpose(vs[:, cols].astype(F32)).astype(BF)

        def scores(i, h):
            n = 256 * (i + 1)
            qm = jnp.where(lane // HEAD_DIM == h, qs[256 * i : n, cols], jnp.zeros((), BF))
            return dot_nt(ks[0:n, cols], qm)

        def soften(i, h, st):
            n = 256 * (i + 1)
            diag = jnp.where(keep, st[n - 256 :, :], masked_score)
            st = diag if i == 0 else jnp.concatenate([st[: n - 256, :], diag], axis=0)
            peak = jnp.max(st, axis=0, keepdims=True)
            p = jnp.exp(st - peak)
            return p.astype(BF), peak, jnp.sum(p, axis=0, keepdims=True)

        def finish(i, h, p, peak, total):
            n = 256 * (i + 1)
            o = dot(vt[h * 64 : h * 64 + 64, :n], p) * (1.0 / total)
            ot_ref[pl.ds(pl.multiple_of(hp * 128 + h * 64, 64), 64), 256 * i : n] = o
            lse_ref[pl.ds(hp * 2 + h, 1), 256 * i : n] = peak + jnp.log(total)

        tasks = [(i, h) for i in range(4) for h in range(2)]
        st, waiting = scores(*tasks[0]), None
        for k, task in enumerate(tasks):
            ahead = scores(*tasks[k + 1]) if k + 1 < len(tasks) else None
            parts = soften(*task, st)
            if waiting is not None:
                finish(*waiting)
            waiting, st = task + parts, ahead
        finish(*waiting)
        at[:, cols] = jnp.transpose(ot_ref[cols, :]).astype(BF)
        return carry

    lax.fori_loop(0, 3, pair, 0)
    row = pl.multiple_of(sc[1] * SPAN, SPAN)
    row_other = pl.multiple_of((1 - sc[1]) * SPAN, SPAN)
    out_other = pltpu.make_async_copy(at.at[pl.ds(row_other, SPAN), :], theirs, sem.at[18])
    out_own = pltpu.make_async_copy(at.at[pl.ds(row, SPAN), :], mine, sem.at[19])
    out_other.start()
    out_own.start()
    out_other.wait()
    out_own.wait()
    for cp in fetch:
        cp.wait()


def attend_call(sc, own, other, wo, wg, wu, wd):
    return call(
        attend_body,
        "attend",
        sc,
        (own, other, wo, wg, wu, wd),
        [hbm(), hbm()] + [far_hbm()] * 4,
        [sds((GROUP, SEQ), F32), sds((8, SEQ), F32), sds((SPAN, GROUP)), sds((SPAN, GROUP))]
        + [sds((WIDTH, WIDTH)), sds((WIDTH, SEQ)), sds((WIDTH, SEQ)), sds((SEQ, WIDTH))],
        [whole((GROUP, SEQ)), whole((8, SEQ))] + [hbm()] * 6,
        [pltpu.VMEM((SEQ, GROUP), BF)] * 4
        + [pltpu.SemaphoreType.DMA((20,)), pltpu.SemaphoreType.DMA((26,))],
        8,
        (6 * 4 * SEQ * SEQ * 64, 6e6, 4e6),
    )


def proj_body(sc, x_ref, ak_ref, ar_ref, gain_ref, wo_ref, m_ref, n_ref):
    for r in range(0, SPAN, 256):
        rr = slice(r, r + 256)
        m = jnp.where(live_mask(sc, r, 256), x_ref[0, rr, :].astype(F32), 0.0)
        m = m + dot(ak_ref[rr, :], wo_ref[:GROUP, :]) + dot(ar_ref[rr, :], wo_ref[GROUP:, :])
        m_ref[rr, :] = m
        factor = lax.rsqrt(jnp.mean(m * m, axis=-1, keepdims=True) + epsilon)
        n_ref[rr, :] = (m * factor * gain_ref[...]).astype(BF)


def proj_call(sc, tokens, own, other, gain, wo):
    return call(
        proj_body,
        "proj",
        sc,
        (tokens, own, other, gain, wo),
        [whole((1, SPAN, WIDTH))]
        + [whole((SPAN, GROUP))] * 2
        + [whole((1, WIDTH)), whole((WIDTH, WIDTH))],
        [sds((SPAN, WIDTH), F32), sds((SPAN, WIDTH))],
        [whole((SPAN, WIDTH))] * 2,
        [],
        4,
        (2 * SPAN * WIDTH * WIDTH, 5e6, 1e3),
    )


def over_rows(own, other, d_own, d_other):
    return dot_tn(own, d_own) + dot_tn(other, d_other)


def place_of(s):
    return (s % 2) * 2 + s // 2


def hidden_cols(sc, s, half):
    return pl.ds(pl.multiple_of(512 * s + 128 * half + 256 * sc[0], 128), 128)


def spread(sc, res_s, first, count, rows, send_ref, keep_ref, to):
    size = send_ref.shape[1]
    for k, ref in enumerate((send_ref, keep_ref)):
        bit = (1 - sc[3]) if k == 0 else sc[3]
        for s in range(4):
            for q in range(count):
                lo = pl.multiple_of(first + (s * count + q) * 2 * rows + bit * rows, 16)
                block, row = divmod(to + q * rows, size)
                ref[2 * place_of(s) + block, row : row + rows, :] = res_s[pl.ds(lo, rows), :].astype(
                    BF
                )


def upstream_body(sc, dy_own, dy_oth, wd, dy_ref, dh_ref):
    for r in range(0, SEQ, 256):
        pos = sc[1] if r < SPAN else 1 - sc[1]
        at = pos * SPAN + r % SPAN + lax.broadcasted_iota(jnp.int32, (256, 1), 0)
        src = dy_own if r < SPAN else dy_oth
        lo = r % SPAN
        dy = jnp.where(at < sc[2], src[0, lo : lo + 256, :], jnp.zeros((), BF))
        dy_ref[r : r + 256, :] = dy
        dh_ref[r : r + 256, :] = dot_nt(dy, wd[...])


def upstream_call(sc, dy_own, dy_oth, wd):
    full = whole((1, SPAN, WIDTH))
    return call(
        upstream_body,
        "upstream",
        sc,
        (dy_own, dy_oth, wd),
        [full, full, whole((SEQ, WIDTH))],
        [sds((SEQ, WIDTH)), sds((SEQ, SEQ), F32)],
        [whole((SEQ, WIDTH)), whole((SEQ, SEQ))],
        [],
        4,
        (2 * SEQ * WIDTH * SEQ, 8e6, 0),
    )


def ffn_body(sc, n_own, n_oth, dy_s, dh_s, wg_s, wu_s, *refs, half):
    (send_ref, keep_ref, h_ref, dg_ref, du_ref, res_a, res_b) = refs
    part = slice(512 * half, 512 * half + 512)

    def products(r):
        src = n_own if r < SPAN else n_oth
        rows = src[r % SPAN : r % SPAN + 256, :]
        return dot(rows, wg_s[:, part]), dot(rows, wu_s[:, part])

    ahead = products(0)
    for r in range(0, SEQ, 256):
        g, u = ahead
        if r + 256 < SEQ:
            ahead = products(r + 256)
        rr = slice(r, r + 256)
        dh = dh_s[rr, part]
        sg = jax.nn.sigmoid(g)
        gs = g * sg
        h_ref[rr, :] = (gs * u).astype(BF)
        du_ref[rr, :] = (dh * gs).astype(BF)
        dg_ref[rr, :] = (dh * u * (sg + gs * (1.0 - sg))).astype(BF)
    lower, upper = slice(0, SPAN), slice(SPAN, SEQ)
    for k, (base, src) in enumerate(((0, dg_ref), (192, du_ref))):
        for ct in range(2):
            cols = slice(256 * ct, 256 * ct + 256)
            place = res_a.at[ct]
            place[...] = over_rows(n_own[...], n_oth[...], src[lower, cols], src[upper, cols])
            spread(sc, place, 0, 2, 48, send_ref, keep_ref, base + 96 * ct)
    for n in range(3):
        place = res_b.at[n % 2]
        place[...] = dot_tn(h_ref[...], dy_s[:, 256 * n : 256 * n + 256])
        spread(sc, place, 0, 1, 64, send_ref, keep_ref, 384 + 64 * n)


def ffn_call(sc, half, n_own, n_oth, dy, dh, wg, wu):
    flat = whole((SPAN, WIDTH))
    return call(
        functools.partial(ffn_body, half=half),
        "ffn_first" if half == 0 else "ffn_second",
        sc,
        (n_own, n_oth, dy, dh, wg, wu),
        [flat, flat, whole((SEQ, WIDTH)), whole((SEQ, SEQ))] + [whole((WIDTH, SEQ))] * 2,
        [sds((8, 288, 256))] * 2 + [sds((SEQ, 512))] * 3,
        [whole((8, 288, 256))] * 2 + [whole((SEQ, 512))] * 3,
        [pltpu.VMEM((2, WIDTH, 256), F32), pltpu.VMEM((2, 512, 256), F32)],
        14,
        (6 * 2 * SEQ * WIDTH * 512, 14e6, 1e6),
    )


def ffn_out_body(sc, h0, dg0, du0, h1, dg1, du1, wg, wu, wd, acc_ref, accs_ref, dn_ref, dns_ref):
    for r in (512, 768, 0, 256):
        rr = slice(r, r + 256)
        dn = dot_nt(dg0[rr, :], wg[:, :512]) + dot_nt(dg1[rr, :], wg[:, 512:])
        dn = dn + dot_nt(du0[rr, :], wu[:, :512]) + dot_nt(du1[rr, :], wu[:, 512:])
        acc = dot(h0[rr, :], wd[:512, :]) + dot(h1[rr, :], wd[512:, :])
        if r < SPAN:
            dn_ref[rr, :] = dn
            acc_ref[rr, :] = acc
        else:
            dns_ref[r - SPAN : r - SPAN + 256, :] = dn.astype(BF)
            accs_ref[r - SPAN : r - SPAN + 256, :] = acc.astype(BF)


def ffn_out_call(sc, first, second, wg, wu, wd):
    flat = [whole((SPAN, WIDTH))]
    return call(
        ffn_out_body,
        "ffn_out",
        sc,
        tuple(first) + tuple(second) + (wg, wu, wd),
        [whole((SEQ, 512))] * 6 + [whole((WIDTH, SEQ))] * 2 + [whole((SEQ, WIDTH))],
        [sds((SPAN, WIDTH), F32), sds((SPAN, WIDTH)), sds((SPAN, WIDTH), F32), sds((SPAN, WIDTH))],
        flat * 4,
        [],
        8,
        (3 * 2 * SEQ * WIDTH * SEQ, 16e6, 0),
    )


def middle_body(sc, dn_ref, got_ref, m_ref, dy_ref, gain_ref, dm_ref, db_ref):
    gain = gain_ref[...]
    for r in range(0, SPAN, 128):
        rr = slice(r, r + 128)
        live = live_mask(sc, r, 128)
        m = m_ref[rr, :]
        factor = lax.rsqrt(jnp.mean(m * m, axis=-1, keepdims=True) + epsilon)
        scaled = (dn_ref[rr, :] + got_ref[rr, :].astype(F32)) * gain
        dm = jnp.where(live, dy_ref[0, rr, :].astype(F32), 0.0) + (
            factor * scaled
            - m * (factor * factor * factor) * jnp.mean(m * scaled, axis=-1, keepdims=True)
        )
        dm_ref[rr, :] = dm
        db_ref[rr, :] = dm.astype(BF)


def middle_call(sc, dn, got, m, dy, gain):
    flat = whole((SPAN, WIDTH))
    return call(
        middle_body,
        "middle",
        sc,
        (dn, got, m, dy, gain),
        [flat, flat, flat, whole((1, SPAN, WIDTH)), whole((1, WIDTH))],
        [sds((SPAN, WIDTH), F32), sds((SPAN, WIDTH))],
        [flat, flat],
        [],
        6,
        (1e6, 8e6, 1e3),
    )


def attend_back_body(sc, own, other, ot_s, lse_s, dbk, dbr, wo_s, cos_hbm, sin_hbm, *refs):
    wq, wk, wv, mine, theirs, ws, qs, ks, vs, das, ds_all, dqt, dkv, cs, ss, sem, load_sem = refs
    for n in range(3):
        for cp in pair_loads(sc, own, other, (qs, ks, vs), load_sem, n):
            cp.start()
    small = [
        pltpu.make_async_copy(src, to, sem.at[6 + n])
        for n, (src, to) in enumerate(((cos_hbm, cs), (sin_hbm, ss)))
    ]
    fetch = [
        pltpu.make_async_copy(w, ws.at[t], sem.at[10 + t]) for t, w in enumerate((wq, wk, wv))
    ]
    for cp in small + fetch:
        cp.start()
    for k, src in enumerate((dbk, dbr)):
        pos = sc[1] if k == 0 else 1 - sc[1]
        for r in range(0, SPAN, 256):
            rows = pl.ds(pl.multiple_of(pos * SPAN + r, 256), 256)
            das[rows, :] = dot_nt(src[r : r + 256, :], wo_s[...]).astype(BF)
    for cp in small:
        cp.wait()
    lane = lax.broadcasted_iota(jnp.int32, (SEQ, 128), 1)
    key_id = lax.broadcasted_iota(jnp.int32, (256, 256), 0)
    row_id = lax.broadcasted_iota(jnp.int32, (256, 256), 1)
    keep = key_id <= row_id

    def pair(hp, carry):
        base = pl.multiple_of(hp * 128, 128)
        cols = pl.ds(base, 128)
        for cp in pair_loads(sc, own, other, (qs, ks, vs), load_sem, hp):
            cp.wait()
        kt = jnp.transpose(ks[:, cols].astype(F32)).astype(BF)
        dat = jnp.transpose(das[:, cols].astype(F32))
        qm, dam, delta, lses = [], [], [], []
        for h in range(2):
            qm.append(jnp.where(lane // HEAD_DIM == h, qs[:, cols], jnp.zeros((), BF)))
            dam.append(jnp.where(lane // HEAD_DIM == h, das[:, cols], jnp.zeros((), BF)))
            rows = pl.ds(pl.multiple_of(base + 64 * h, 64), 64)
            product = dat[64 * h : 64 * h + 64, :] * ot_s[rows, :]
            delta.append(jnp.sum(product, axis=0, keepdims=True))
            lses.append(lse_s[pl.ds(2 * hp + h, 1), :])

        def scores(i, h):
            n = 256 * (i + 1)
            rows = slice(256 * i, n)
            return dot_nt(ks[:n, cols], qm[h][rows, :]), dot_nt(vs[:n, cols], dam[h][rows, :])

        def soften(i, h, st, dp):
            n = 256 * (i + 1)
            rows = slice(256 * i, n)
            p = jnp.exp(st - lses[h][:, rows])
            diag = jnp.where(keep, p[n - 256 :, :], 0.0)
            p = diag if i == 0 else jnp.concatenate([p[: n - 256, :], diag], axis=0)
            return p.astype(BF), (p * (dp - delta[h][:, rows])).astype(BF)

        def finish(i, h, p, ds):
            n = 256 * (i + 1)
            rows = slice(256 * i, n)
            half = slice(64 * h, 64 * h + 64)
            dv = dot(p, dam[h][rows, :])
            dk = dot(ds, qm[h][rows, :])
            dqt[half, rows] = dot(kt[half, :n], ds)
            if (i, h) == (3, 0):
                dkv[0] = dk
                dkv[1] = dv
            else:
                dkv[0, :n] += dk
                dkv[1, :n] += dv

        tasks = [(i, h) for i in (3, 2, 1, 0) for h in range(2)]
        now, waiting = scores(*tasks[0]), None
        for k, task in enumerate(tasks):
            ahead = scores(*tasks[k + 1]) if k + 1 < len(tasks) else None
            parts = soften(*task, *now)
            if waiting is not None:
                finish(*waiting)
            waiting, now = task + parts, ahead
        finish(*waiting)
        dq = jnp.transpose(dqt[...]) * (HEAD_DIM**-0.5)
        ds_all[0, :, cols] = turn(dq, cs[...], -ss[...]).astype(BF)
        ds_all[1, :, cols] = turn(dkv[0], cs[...], -ss[...]).astype(BF)
        ds_all[2, :, cols] = dkv[1].astype(BF)
        return carry

    lax.fori_loop(0, 3, pair, 0)
    row = pl.multiple_of(sc[1] * SPAN, SPAN)
    row_other = pl.multiple_of((1 - sc[1]) * SPAN, SPAN)
    stores = [
        pltpu.make_async_copy(ds_all.at[:, pl.ds(row_other, SPAN), :], theirs, sem.at[8]),
        pltpu.make_async_copy(ds_all.at[:, pl.ds(row, SPAN), :], mine, sem.at[9]),
    ]
    for cp in stores:
        cp.start()
    for cp in stores + fetch:
        cp.wait()


def attend_back_call(sc, own, other, ot, lse, dbk, dbr, wo, cosine, sine, wq, wk, wv):
    return call(
        attend_back_body,
        "attend_back",
        sc,
        (own, other, ot, lse, dbk, dbr, wo, cosine, sine, wq, wk, wv),
        [hbm(), hbm(), whole((GROUP, SEQ)), whole((8, SEQ))]
        + [whole((SPAN, WIDTH))] * 2
        + [whole((GROUP, WIDTH))]
        + [far_hbm()] * 5,
        [sds((3, SPAN, GROUP))] * 2 + [sds((3, WIDTH, WIDTH))],
        [hbm()] * 3,
        [pltpu.VMEM((SEQ, GROUP), BF)] * 4
        + [
            pltpu.VMEM((3, SEQ, GROUP), BF),
            pltpu.VMEM((128, SEQ), F32),
            pltpu.VMEM((2, SEQ, 128), F32),
            pltpu.VMEM((SEQ, 128), F32),
            pltpu.VMEM((SEQ, 128), F32),
            pltpu.SemaphoreType.DMA((13,)),
            pltpu.SemaphoreType.DMA((18,)),
        ],
        22,
        (6 * 10 * SEQ * SEQ * 64, 10e6, 4e6),
    )


def square_body(sc, nk, nr, ak, at, ck, ct, bk, br, dk, dr, sa_ref, ka_ref, sb_ref, kb_ref, res):
    own = pl.ds(pl.multiple_of(sc[0] * GROUP, 128), GROUP)
    other = pl.ds(pl.multiple_of((1 - sc[0]) * GROUP, 128), GROUP)
    res[0, own, :] = over_rows(ak[...], at[...], bk[:, own], br[:, own])
    res[0, other, :] = over_rows(ck[...], ct[...], bk[:, own], br[:, own])
    spread(sc, res.at[0], 0, 2, 48, sa_ref, ka_ref, 0)
    for n, t in enumerate((2, 0, 1)):
        place = res.at[(n + 1) % 2]
        place[...] = over_rows(nk[...], nr[...], dk[t], dr[t])
        if n == 0:
            spread(sc, place, 0, 2, 48, sa_ref, ka_ref, 96)
        else:
            spread(sc, place, 0, 2, 48, sb_ref, kb_ref, 96 * t)


def square_call(sc, *args):
    flat = [whole((SPAN, WIDTH))] * 2
    return call(
        square_body,
        "square",
        sc,
        args,
        flat + [whole((SPAN, GROUP))] * 4 + flat + [whole((3, SPAN, GROUP))] * 2,
        [sds((8, 96, GROUP))] * 4,
        [whole((8, 96, GROUP))] * 4,
        [pltpu.VMEM((2, WIDTH, GROUP), F32)],
        16,
        (4 * 2 * SEQ * WIDTH * GROUP, 12e6, 0),
    )


def input_grad_body(sc, x_ref, gain_ref, dm_ref, m_ref, acc_ref, got_ref, dk_s, dr_s, ws, *refs):
    lay_ref, o_ref = refs
    for r in range(0, SPAN, 256):
        rr = slice(r, r + 256)
        out = m_ref[rr, :] + acc_ref[rr, :] + got_ref[rr, :].astype(F32)
        lay_ref[0, rr, :] = jnp.where(live_mask(sc, r, 256), out, 0.0).astype(BF)
    own_cols = pl.multiple_of(sc[0] * GROUP, 128)
    other_cols = pl.multiple_of((1 - sc[0]) * GROUP, 128)
    gain = gain_ref[...]
    for r in range(0, SPAN, 256):
        rr = slice(r, r + 256)
        dn = dot_nt(dk_s[0, rr, :], ws[0, :, pl.ds(own_cols, GROUP)])
        dn = dn + dot_nt(dr_s[0, rr, :], ws[0, :, pl.ds(other_cols, GROUP)])
        for t in (1, 2):
            dn = dn + dot_nt(dk_s[t, rr, :], ws[t, :, pl.ds(own_cols, GROUP)])
            dn = dn + dot_nt(dr_s[t, rr, :], ws[t, :, pl.ds(other_cols, GROUP)])
        live = live_mask(sc, r, 256)
        x = jnp.where(live, x_ref[0, rr, :].astype(F32), 0.0)
        factor = lax.rsqrt(jnp.mean(x * x, axis=-1, keepdims=True) + epsilon)
        scaled = dn * gain
        dx = dm_ref[rr, :] + (
            factor * scaled
            - x * (factor * factor * factor) * jnp.mean(x * scaled, axis=-1, keepdims=True)
        )
        o_ref[0, rr, :] = jnp.where(live, dx, 0.0).astype(BF)


def input_grad_call(sc, tokens, gain, dm, m, acc, got, dk, dr, ws):
    full = whole((1, SPAN, WIDTH))
    flat = whole((SPAN, WIDTH))
    return call(
        input_grad_body,
        "input_grad",
        sc,
        (tokens, gain, dm, m, acc, got, dk, dr, ws),
        [full, whole((1, WIDTH)), flat, flat, flat, flat]
        + [whole((3, SPAN, GROUP))] * 2
        + [whole((3, WIDTH, WIDTH))],
        [sds((1, SPAN, WIDTH))] * 2,
        [full] * 2,
        [],
        20,
        (3 * 2 * SPAN * WIDTH * WIDTH, 14e6, 1e3),
    )


def add_pieces(sc, count, sums, name):
    rows, cols = sums[0][0][0].shape[1:]
    arrays = [array for stack in sums for array, _ in stack]
    picks = [pick for stack in sums for _, pick in stack]

    def body(sc_ref, *refs):
        at = 0
        for n, stack in enumerate(sums):
            total = refs[at][0].astype(F32)
            for ref in refs[at + 1 : at + len(stack)]:
                total = total + ref[0].astype(F32)
            refs[-1][0, n * rows : (n + 1) * rows, :] = total.astype(BF)
            at += len(stack)

    def spec(pick):
        block, row = pick
        return pl.BlockSpec((1, rows, cols), lambda j, sc_ref: (block(sc_ref, j), row, 0))

    high = rows * len(sums)
    return pl.pallas_call(
        body,
        name=name,
        out_shape=sds((count, high, cols)),
        grid_spec=pltpu.PrefetchScalarGridSpec(
            num_scalar_prefetch=1,
            grid=(count,),
            in_specs=[spec(pick) for pick in picks],
            out_specs=pl.BlockSpec((1, high, cols), lambda j, sc_ref: (j, 0, 0)),
        ),
        compiler_params=pltpu.CompilerParams(vmem_limit_bytes=6 * MIB),
        cost_estimate=pl.CostEstimate(
            flops=int(0 if name == "g0_b" else ADD_COST), bytes_accessed=1000, transcendentals=0
        ),
    )(sc, *arrays)


def row_block(rows, cols):
    return pl.BlockSpec((rows, cols), lambda i, sc: (sc[6], 0))


def row_of(column):
    column = jnp.concatenate([column, jnp.zeros((32, 1), F32)], axis=0)
    return jnp.transpose(jnp.broadcast_to(column, (128, 128)))[0, :96]


def collect_halves(sc, group, full):
    for n in range(4):
        core, k = divmod(n, 2)
        parity = sc[0] if core == 0 else 1 - sc[0]
        first = sc[3] if core == 0 else sc[7]
        first = 1 - first if k == 1 else first
        for h in range(2):
            full[parity, first, 288 * h : 288 * h + 288, :] = group[n][h]


def collect(sc, group, full, row, size):
    for n in range(8):
        core, k = divmod(n, 4)
        parity = sc[0] if core == 0 else 1 - sc[0]
        first, second = (sc[3], sc[7]) if core == 0 else (sc[7], sc[3])
        first = 1 - first if k in (1, 3) else first
        second = 1 - second if k in (2, 3) else second
        rows = pl.ds(pl.multiple_of(second * size, 16), size)
        full[parity, first, rows, :] = group[n][0, row : row + size, :]


def ffn_result_body(sc, *refs):
    wg_ref, wu_ref, gain_ref, gate_ref, up_ref, down_ref, gg_ref, full = refs[12:]
    collect_halves(sc, refs[:4], full.at[0])
    collect(sc, refs[4:12], full.at[1], 0, 288)
    for half in range(2):
        for bit in range(2):
            rows = slice(48 * bit, 48 * bit + 48)
            for parity in range(2):
                for base, ref in ((0, gate_ref), (192, up_ref)):
                    for ct in range(2):
                        lo = pl.multiple_of(base + ct * 96 + sc[0] * 48, 16)
                        block = full[half, parity, bit, pl.ds(lo, 48), :].astype(F32)
                        for q in range(2):
                            col = 512 * (2 * ct + q) + 128 * half + 256 * parity
                            ref[rows, col : col + 128] = block[:, 128 * q : 128 * q + 128]
            lo = 128 * half + 64 * bit
            for t in range(3):
                down_ref[lo : lo + 64, 256 * t : 256 * t + 256] = full[
                    half, sc[0], bit, 384 + t * 64 : 448 + t * 64, :
                ].astype(F32)
    gate = jnp.sum(wg_ref[...].astype(F32) * gate_ref[...], axis=-1, keepdims=True)
    up = jnp.sum(wu_ref[...].astype(F32) * up_ref[...], axis=-1, keepdims=True)
    gg_ref[...] = row_of((gate + up) / gain_ref[...])


def ffn_result_call(sc, first, second, wg, wu, gain):
    return call(
        ffn_result_body,
        "ffn_result",
        sc,
        tuple(first) + tuple(second) + (wg, wu, gain),
        [whole((2, 288, 256))] * 4 + [whole((1, 288, 256))] * 8 + [row_block(96, HID)] * 2 + [row_block(96, 1)],
        [sds((96, HID), F32), sds((96, HID), F32), sds((256, WIDTH), F32), sds((96,), F32)],
        [whole((96, HID)), whole((96, HID)), whole((256, WIDTH)), whole((96,))],
        [pltpu.VMEM((2, 2, 2, 576, 256), BF)],
        14,
        (1e6, 6e6, 0),
    )


def square_result_body(sc, *refs):
    group = refs[:8]
    weights = refs[8:11]
    gain_ref = refs[11]
    outs = refs[12:16]
    gg_ref, full = refs[16:]
    order = ((3, 2), (0, 1))
    for n in range(2):
        collect(sc, group, full.at[n], 96 * n, 96)
        for bit in range(2):
            rows = slice(48 * bit, 48 * bit + 48)
            for parity in range(2):
                cols = slice(GROUP * parity, GROUP * parity + GROUP)
                for t in range(2):
                    lo = pl.multiple_of(t * 96 + sc[0] * 48, 16)
                    block = full[n, parity, bit, pl.ds(lo, 48), :]
                    outs[order[n][t]][rows, cols] = block.astype(F32)
    total = jnp.zeros((96, 1), F32)
    for t in range(3):
        total = total + jnp.sum(weights[t][...].astype(F32) * outs[t][...], axis=-1, keepdims=True)
    gg_ref[...] = row_of(total / gain_ref[...])


def square_result_call(sc, group, wq, wk, wv, gain):
    return call(
        square_result_body,
        "square_result",
        sc,
        tuple(group) + (wq, wk, wv, gain),
        [whole((1, 192, GROUP))] * 8 + [row_block(96, WIDTH)] * 3 + [row_block(96, 1)],
        [sds((96, WIDTH), F32)] * 4 + [sds((96,), F32)],
        [whole((96, WIDTH))] * 4 + [whole((96,))],
        [pltpu.VMEM((2, 2, 2, 192, GROUP), BF)],
        8,
        (1e6, 4e6, 0),
    )


class Chain:
    def __init__(self, sc):
        self.sc = sc

    def next(self, *deps):
        self.sc = after(self.sc, *deps)
        return self.sc


class Reduction:
    def __init__(self, chain, send, keep, name):
        self.chain = chain
        self.send = send
        self.name = name
        self.stacks = [[[keep, 0]]]
        self.flight = None

    def start(self):
        self.fly(after(self.send, self.chain.sc), "first")

    def fly(self, rows, kind):
        self.flight = exchange(rows, kind)

    def land(self):
        if self.flight is not None:
            for n, stack in enumerate(self.stacks):
                stack.append([self.flight, n])
        self.flight = None

    def add(self, count, picks, tag):
        self.land()
        sums = []
        for stack in self.stacks:
            blocks = ([picks[0]] + picks)[-len(stack) :]
            sums.append([(array, (pick, row)) for (array, row), pick in zip(stack, blocks)])
        arrays = [array for stack in sums for array, _ in stack]
        out = add_pieces(self.chain.next(*arrays), count, sums, self.name + tag)
        self.chain.next(out)
        return out

    def second(self):
        pick = lambda t, j: j * 2 + 1 - t[7]
        self.fly(self.add(4, [pick], "_b"), "second")

    def near(self):
        pick = lambda t, j: (1 - t[4]) * 4 + j * 2 + t[7]
        self.fly(self.add(2, [pick, lambda t, j: (1 - t[4]) * 2 + j], "_c"), "near")

    def far(self):
        pick = lambda t, j: t[4] * 4 + (1 - t[5]) * 2 + t[7]
        picks = [pick, lambda t, j: t[4] * 2 + 1 - t[5], lambda t, j: 1 - t[5]]
        self.fly(self.add(1, picks, "_d"), "far")

    def total(self):
        pick = lambda t, j: t[4] * 4 + t[5] * 2 + t[7]
        picks = [pick, lambda t, j: t[4] * 2 + t[5], lambda t, j: t[5], lambda t, j: 0]
        own = self.add(1, picks, "_e")
        self.quarters = [own] + [exchange(own, kind) for kind in ("first", "second", "across")]

    def result(self):
        late = [after(quarter, self.chain.sc) for quarter in self.quarters]
        return self.quarters + [exchange(quarter, "core") for quarter in late]


class Straight(Reduction):
    def near(self):
        pick = lambda t, j: (1 - t[4]) * 4 + j
        self.fly(self.add(4, [pick], "_b"), "near")

    def far(self):
        pick = lambda t, j: t[4] * 4 + (1 - t[5]) * 2 + j
        self.fly(self.add(2, [pick, lambda t, j: (1 - t[5]) * 2 + j], "_c"), "far")

    def second(self):
        pick = lambda t, j: t[4] * 4 + t[5] * 2 + j
        own = self.add(2, [pick, lambda t, j: t[5] * 2 + j, lambda t, j: j], "_d")
        self.stacks = [[[own, 0]]]
        self.fly(own, "second")

    def total(self):
        own = self.add(2, [lambda t, j: j], "_e")
        self.quarters = [own, exchange(own, "first")]


def join(first, second):
    both = Reduction(first.chain, None, None, first.name + second.name)
    first.land()
    second.land()
    both.stacks = first.stacks + second.stacks
    return both


def fast_step(
    tokens,
    lengths,
    owner,
    w_query,
    w_key,
    w_value,
    w_out,
    w_gate,
    w_up,
    w_down,
    gain_attn,
    gain_mlp,
    cotangent,
):
    place = lax.axis_index(AXES)
    slot = jnp.arange(8, dtype=jnp.int32)
    core = place & 1
    base = jnp.where(slot == 3, 3 + core, jnp.where(slot == 7, 4 - core, 0))
    base = jnp.where(slot == 4, 1, jnp.where(slot == 5, 2, base))
    row = (place >> base) & jnp.where(slot == 6, 7, 1)
    turned = jnp.abs(row - jnp.broadcast_to(owner[0, :1], (8,)))
    sc = jnp.where(slot == 1, turned, row)
    sc = jnp.where(slot == 2, jnp.broadcast_to(lengths, (8,)), sc)
    tables = position_tables(SEQ)
    cosine, sine = jnp.asarray(tables[0]), jnp.asarray(tables[1])
    gain_row = gain_attn.reshape(1, WIDTH)
    gain_mlp_row = gain_mlp.reshape(1, WIDTH)
    qkv_w = (w_query, w_key, w_value)
    ffn_w = (w_gate, w_up, w_down)
    chain = Chain(sc)

    qkv_send, n1, cs_v, ss_v, w_v = qkv_other_call(chain.sc, tokens, gain_attn, cosine, sine, *qkv_w)
    qkv_other = exchange(qkv_send, "core")
    qkv_own = qkv_own_call(chain.next(n1), n1, cs_v, ss_v, w_v)
    n1_other = exchange(n1, "core")
    dy_other = exchange(cotangent, "core")
    attn_t, lse, attn_own, attn_send, wo_v, *ffn_v = attend_call(
        chain.next(qkv_own), qkv_own, qkv_other, w_out, *ffn_w
    )
    attn_other = exchange(attn_send, "core")
    attn_rest = exchange(attn_own, "core")
    middle, n2 = proj_call(
        chain.next(lse, n1_other, dy_other), tokens, attn_own, attn_other, gain_mlp_row, wo_v
    )
    n2_other = exchange(n2, "core")
    dy_all, dh_all = upstream_call(chain.next(n2), cotangent, dy_other, ffn_v[2])
    rows = (n2, n2_other, dy_all, dh_all)
    send0, keep0, *acts0 = ffn_call(chain.next(dy_all, attn_rest), 0, *rows, *ffn_v[:2])
    g0 = Straight(chain, send0, keep0, "g0")
    g0.start()
    send1, keep1, *acts1 = ffn_call(chain.next(acts0[0]), 1, *rows, *ffn_v[:2])
    g1 = Reduction(chain, send1, keep1, "g1")
    g1.start()
    acc, acc_send, dn, dn_send = ffn_out_call(chain.next(acts1[0]), acts0, acts1, *ffn_v)
    dn_other = exchange(dn_send, "core")
    chain.next(dn_send)
    d_middle, db = middle_call(
        chain.next(dn_other, g0.flight), dn, dn_other, middle, cotangent, gain_mlp_row
    )
    chain.next(db)
    g0.near()
    db_other = exchange(db, "core")
    acc_other = exchange(after(acc_send, db_other), "core")
    d_own, d_send, qkv_v = attend_back_call(
        chain.sc,
        qkv_own,
        qkv_other,
        attn_t,
        lse,
        db,
        db_other,
        wo_v,
        cosine,
        sine,
        *qkv_w,
    )
    d_other = exchange(d_send, "core")
    chain.next(d_own, g0.flight, g1.flight)
    g1.second()
    g0.far()
    attn = (attn_own, attn_send, attn_other, attn_rest)
    send2, keep2, send3, keep3 = square_call(
        chain.sc, n1, n1_other, *attn, db, db_other, d_own, d_send
    )
    g2 = Reduction(chain, send2, keep2, "g2")
    g3 = Reduction(chain, send3, keep3, "g3")
    g2.start()
    g3.start()
    chain.next(send3)
    layer_out, input_grad = input_grad_call(
        chain.next(acc_other, d_other),
        tokens,
        gain_row,
        d_middle,
        middle,
        acc,
        acc_other,
        d_own,
        d_other,
        qkv_v,
    )
    chain.next(input_grad)
    g0.second()
    g1.near()
    g2.second()
    g1.far()
    g3.second()
    g2.near()
    g0.total()
    g3.near()
    g2.far()
    g3.far()
    g1.total()
    g23 = join(g2, g3)
    g23.total()
    first = g0.result()
    second = g1.result()
    third = g23.result()
    gate, up, down, gain_m = ffn_result_call(
        chain.sc, first, second, w_gate, w_up, gain_mlp.reshape(WIDTH, 1)
    )
    chain.next(gain_m)
    query, key, value, out, gain_a = square_result_call(
        chain.sc, third, *qkv_w, gain_attn.reshape(WIDTH, 1)
    )
    return (
        layer_out,
        input_grad,
        query,
        key,
        value,
        out,
        gate,
        up,
        down,
        gain_a,
        gain_m,
    )


def solution(mesh):
    in_specs = (
        P(("batch", "seq"), "seqb", None),
        P(("batch", "seq")),
        P(("batch", "seq"), None),
        P(),
        P(),
        P(),
        P(),
        P(),
        P(),
        P(),
        P(),
        P(),
        P(("batch", "seq"), "seqb", None),
    )
    out_specs = (
        P(("batch", "seq"), "seqb", None),
        P(("batch", "seq"), "seqb", None),
        P(("seq", "seqb"), None),
        P(("seq", "seqb"), None),
        P(("seq", "seqb"), None),
        P(("seq", "seqb"), None),
        P(("seq", "seqb"), None),
        P(("seq", "seqb"), None),
        P(("seq", "seqb"), None),
        P(("seq", "seqb")),
        P(("seq", "seqb")),
    )
    step = fast_step if fast_layout(mesh) else general_step
    return jax.shard_map(step, mesh=mesh, in_specs=in_specs, out_specs=out_specs, check_vma=False)
```

```python
import functools
import math

import jax
import jax.numpy as jnp
import numpy as np
from jax import lax
from jax.experimental import pallas as pl
from jax.experimental.pallas import tpu as pltpu
from jax.sharding import PartitionSpec as P

HEADS = 12
HEAD_DIM = 64


epsilon = 1e-05
rope_base = 10000.0
masked_score = -1e30


def rms_forward(rows, gain):
    factor = lax.rsqrt(jnp.mean(rows * rows, axis=-1, keepdims=True) + epsilon)
    return (rows * factor * gain, factor)


def rms_backward(rows, factor, gain, upstream):
    scaled = upstream * gain
    return factor * scaled - rows * (factor * factor * factor) * jnp.mean(
        rows * scaled, axis=-1, keepdims=True
    )


def rotation_tables(positions):
    half = HEAD_DIM // 2
    freq = rope_base ** (-(2.0 * jnp.arange(half, dtype=jnp.float32)) / HEAD_DIM)
    angles = positions.astype(jnp.float32)[..., None] * freq
    return (jnp.cos(angles), jnp.sin(angles))


def split_heads(rows):
    return rows.reshape(rows.shape[0], rows.shape[1], HEADS, HEAD_DIM)


def rotate(rows, cosine, sine, inverse):
    shaped = split_heads(rows)
    half = HEAD_DIM // 2
    first = shaped[..., :half]
    second = shaped[..., half:]
    cos_part = cosine[:, :, None, :]
    sin_part = sine[:, :, None, :]
    if inverse:
        turned = jnp.concatenate(
            [first * cos_part + second * sin_part, second * cos_part - first * sin_part], axis=-1
        )
    else:
        turned = jnp.concatenate(
            [first * cos_part - second * sin_part, second * cos_part + first * sin_part], axis=-1
        )
    return turned.reshape(rows.shape)


def range_positions(owner, count, span):
    offsets = jnp.arange(span, dtype=jnp.int32)
    return (owner[:, :, None] * span + offsets[None, None, :]).reshape(owner.shape[0], count)


def fold_keys(parts, combine, initial):
    return combine(
        initial,
        (
            lax.all_gather(parts[0], "seqb", axis=1, tiled=True),
            lax.all_gather(parts[1], "seqb", axis=1, tiled=True),
        ),
        jnp.int32(0),
    )


def general_step(
    tokens,
    lengths,
    owner,
    w_query,
    w_key,
    w_value,
    w_out,
    w_gate,
    w_up,
    w_down,
    gain_attn,
    gain_mlp,
    cotangent,
):
    seqs, span, width = tokens.shape
    scale = HEAD_DIM ** (-0.5)
    place = lax.axis_index("seqb")
    own_block = lax.dynamic_slice_in_dim(owner, place, 1, 1)
    local_pos = own_block * span + jnp.arange(span, dtype=jnp.int32)[None, :]
    local_live = local_pos < lengths[:, None]
    live_rows = local_live[:, :, None]
    inputs = jnp.where(live_rows, tokens.astype(jnp.float32), 0.0)
    normed, factor_attn = rms_forward(inputs, gain_attn)
    normed_low = normed.astype(jnp.bfloat16)
    cosine, sine = rotation_tables(local_pos)
    query_pre = jnp.einsum("scd,de->sce", normed_low, w_query, preferred_element_type=jnp.float32)
    key_pre = jnp.einsum("scd,de->sce", normed_low, w_key, preferred_element_type=jnp.float32)
    value_low = jnp.einsum(
        "scd,de->sce", normed_low, w_value, preferred_element_type=jnp.float32
    ).astype(jnp.bfloat16)
    query_rot = rotate(query_pre, cosine, sine, False).astype(jnp.bfloat16)
    key_rot = rotate(key_pre, cosine, sine, False).astype(jnp.bfloat16)
    query_heads = split_heads(query_rot)
    key_heads = split_heads(key_rot)
    value_heads = split_heads(value_low)

    def attend(state, piece, start):
        keys, values = piece
        count = keys.shape[1]
        key_pos = range_positions(owner, count, span)
        key_live = key_pos < lengths[:, None]
        stride = math.gcd(count, 512)

        def attend_one_block(index, inner):
            offset = index * stride
            key_block = split_heads(lax.dynamic_slice_in_dim(keys, offset, stride, 1))
            value_block = split_heads(lax.dynamic_slice_in_dim(values, offset, stride, 1))
            pos_block = lax.dynamic_slice_in_dim(key_pos, offset, stride, 1)
            live_block = lax.dynamic_slice_in_dim(key_live, offset, stride, 1)
            allowed = (
                (pos_block[:, None, :] <= local_pos[:, :, None])
                & live_block[:, None, :]
                & local_live[:, :, None]
            )

            def attend_update(carried):
                peak, total, summed = carried
                scores = (
                    jnp.einsum(
                        "sqhd,skhd->shqk",
                        query_heads,
                        key_block,
                        preferred_element_type=jnp.float32,
                    )
                    * scale
                )
                mask = allowed[:, None, :, :]
                new_peak = jnp.maximum(
                    peak, jnp.max(jnp.where(mask, scores, masked_score), axis=-1)
                )
                weights = jnp.where(mask, jnp.exp(scores - new_peak[..., None]), 0.0)
                factor = jnp.exp(peak - new_peak)
                total = total * factor + jnp.sum(weights, axis=-1)
                term = jnp.einsum(
                    "shqk,skhd->sqhd",
                    weights.astype(jnp.bfloat16),
                    value_block,
                    preferred_element_type=jnp.float32,
                )
                summed = (
                    split_heads(summed) * jnp.transpose(factor, (0, 2, 1))[..., None] + term
                ).reshape(summed.shape)
                return (new_peak, total, summed)

            return lax.cond(jnp.any(allowed), attend_update, lambda carried: carried, inner)

        return lax.fori_loop(0, count // stride, attend_one_block, state)

    start_state = (
        jnp.full((seqs, HEADS, span), masked_score, jnp.float32),
        jnp.zeros((seqs, HEADS, span), jnp.float32),
        jnp.zeros((seqs, span, width), jnp.float32),
    )
    peak, total, summed = fold_keys((key_rot, value_low), attend, start_state)
    safe_total = jnp.where(local_live[:, None, :], total, 1.0)
    attn = split_heads(summed) / jnp.transpose(safe_total, (0, 2, 1))[..., None]
    attn = jnp.where(local_live[:, :, None, None], attn, 0.0).reshape(seqs, span, width)
    log_total = jnp.where(local_live[:, None, :], peak + jnp.log(safe_total), 0.0)
    attn_low = attn.astype(jnp.bfloat16)
    middle = inputs + jnp.einsum("scd,de->sce", attn_low, w_out, preferred_element_type=jnp.float32)
    normed_mlp, factor_mlp = rms_forward(middle, gain_mlp)
    normed_mlp_low = normed_mlp.astype(jnp.bfloat16)
    gate = jnp.einsum("scd,df->scf", normed_mlp_low, w_gate, preferred_element_type=jnp.float32)
    up_proj = jnp.einsum("scd,df->scf", normed_mlp_low, w_up, preferred_element_type=jnp.float32)
    hidden = (jax.nn.silu(gate) * up_proj).astype(jnp.bfloat16)
    out = middle + jnp.einsum("scf,fd->scd", hidden, w_down, preferred_element_type=jnp.float32)
    layer_out = jnp.where(live_rows, out, 0.0).astype(jnp.bfloat16)
    upstream = jnp.where(live_rows, cotangent, jnp.zeros_like(cotangent))
    grad_down = jnp.einsum("scf,scd->fd", hidden, upstream, preferred_element_type=jnp.float32)
    d_hidden = jnp.einsum("scd,fd->scf", upstream, w_down, preferred_element_type=jnp.float32)
    sigmoid_gate = jax.nn.sigmoid(gate)
    d_gate = (d_hidden * up_proj * sigmoid_gate * (1.0 + gate * (1.0 - sigmoid_gate))).astype(
        jnp.bfloat16
    )
    d_up = (d_hidden * gate * sigmoid_gate).astype(jnp.bfloat16)
    grad_gate = jnp.einsum(
        "scd,scf->df", normed_mlp_low, d_gate, preferred_element_type=jnp.float32
    )
    grad_up = jnp.einsum("scd,scf->df", normed_mlp_low, d_up, preferred_element_type=jnp.float32)
    d_normed_mlp = jnp.einsum(
        "scf,df->scd", d_gate, w_gate, preferred_element_type=jnp.float32
    ) + jnp.einsum("scf,df->scd", d_up, w_up, preferred_element_type=jnp.float32)
    grad_gain_mlp = jnp.sum(d_normed_mlp * (middle * factor_mlp), axis=(0, 1))
    d_middle = upstream.astype(jnp.float32) + rms_backward(
        middle, factor_mlp, gain_mlp, d_normed_mlp
    )
    d_branch = d_middle.astype(jnp.bfloat16)
    grad_out = jnp.einsum("scd,sce->de", attn_low, d_branch, preferred_element_type=jnp.float32)
    d_attn = jnp.einsum("sce,de->scd", d_branch, w_out, preferred_element_type=jnp.float32).astype(
        jnp.bfloat16
    )
    first_done = (grad_out, grad_gate, grad_up, grad_down, grad_gain_mlp)
    delta = jnp.sum(split_heads(d_attn.astype(jnp.float32) * attn), axis=-1)
    delta_heads = jnp.transpose(delta, (0, 2, 1))
    grad_heads = split_heads(d_attn)

    def query_grads(state, piece, start):
        keys, values = piece
        count = keys.shape[1]
        key_pos = range_positions(owner, count, span)
        key_live = key_pos < lengths[:, None]
        stride = math.gcd(count, 512)

        def query_one_block(index, inner):
            offset = index * stride
            key_block = split_heads(lax.dynamic_slice_in_dim(keys, offset, stride, 1))
            value_block = split_heads(lax.dynamic_slice_in_dim(values, offset, stride, 1))
            pos_block = lax.dynamic_slice_in_dim(key_pos, offset, stride, 1)
            live_block = lax.dynamic_slice_in_dim(key_live, offset, stride, 1)
            allowed = (
                (pos_block[:, None, :] <= local_pos[:, :, None])
                & live_block[:, None, :]
                & local_live[:, :, None]
            )

            def query_update(carried):
                scores = (
                    jnp.einsum(
                        "sqhd,skhd->shqk",
                        query_heads,
                        key_block,
                        preferred_element_type=jnp.float32,
                    )
                    * scale
                )
                probs = jnp.where(
                    allowed[:, None, :, :], jnp.exp(scores - log_total[..., None]), 0.0
                )
                d_probs = jnp.einsum(
                    "sqhd,skhd->shqk", grad_heads, value_block, preferred_element_type=jnp.float32
                )
                d_scores = (probs * (d_probs - delta_heads[..., None])).astype(jnp.bfloat16)
                term = (
                    jnp.einsum(
                        "shqk,skhd->sqhd", d_scores, key_block, preferred_element_type=jnp.float32
                    )
                    * scale
                )
                return carried + term.reshape(carried.shape)

            return lax.cond(jnp.any(allowed), query_update, lambda carried: carried, inner)

        return lax.fori_loop(0, count // stride, query_one_block, state)

    zero_query = jnp.zeros((seqs, span, width), jnp.float32)
    d_query = fold_keys((key_rot, value_low), query_grads, zero_query)
    lse_all, delta_all = (
        lax.all_gather(jnp.transpose(log_total, (0, 2, 1)), "seqb", axis=1, tiled=True),
        lax.all_gather(delta, "seqb", axis=1, tiled=True),
    )
    zero_rows = jnp.zeros((seqs, span, width), jnp.float32)
    queries = lax.all_gather(query_rot, "seqb", axis=1, tiled=True)
    d_rows = lax.all_gather(d_attn, "seqb", axis=1, tiled=True)
    count = queries.shape[1]
    row_pos = range_positions(owner, count, span)
    row_live = row_pos < lengths[:, None]
    stride = math.gcd(count, 512)

    def key_one_block(index, inner):
        offset = index * stride
        query_block = split_heads(lax.dynamic_slice_in_dim(queries, offset, stride, 1))
        grad_block = split_heads(lax.dynamic_slice_in_dim(d_rows, offset, stride, 1))
        pos_block = lax.dynamic_slice_in_dim(row_pos, offset, stride, 1)
        live_block = lax.dynamic_slice_in_dim(row_live, offset, stride, 1)
        lse_block = jnp.transpose(lax.dynamic_slice_in_dim(lse_all, offset, stride, 1), (0, 2, 1))
        delta_block = jnp.transpose(
            lax.dynamic_slice_in_dim(delta_all, offset, stride, 1), (0, 2, 1)
        )
        allowed = (
            (local_pos[:, None, :] <= pos_block[:, :, None])
            & local_live[:, None, :]
            & live_block[:, :, None]
        )

        def key_update(carried):
            d_key, d_value = carried
            scores = (
                jnp.einsum(
                    "sqhd,skhd->shqk", query_block, key_heads, preferred_element_type=jnp.float32
                )
                * scale
            )
            probs = jnp.where(allowed[:, None, :, :], jnp.exp(scores - lse_block[..., None]), 0.0)
            value_term = jnp.einsum(
                "shqk,sqhd->skhd",
                probs.astype(jnp.bfloat16),
                grad_block,
                preferred_element_type=jnp.float32,
            )
            d_probs = jnp.einsum(
                "sqhd,skhd->shqk", grad_block, value_heads, preferred_element_type=jnp.float32
            )
            d_scores = (probs * (d_probs - delta_block[..., None])).astype(jnp.bfloat16)
            key_term = (
                jnp.einsum(
                    "shqk,sqhd->skhd", d_scores, query_block, preferred_element_type=jnp.float32
                )
                * scale
            )
            return (
                d_key + key_term.reshape(d_key.shape),
                d_value + value_term.reshape(d_value.shape),
            )

        return lax.cond(jnp.any(allowed), key_update, lambda carried: carried, inner)

    d_key, d_value = lax.fori_loop(0, count // stride, key_one_block, (zero_rows, zero_rows))
    d_query_pre = rotate(d_query, cosine, sine, True).astype(jnp.bfloat16)
    d_key_pre = rotate(d_key, cosine, sine, True).astype(jnp.bfloat16)
    d_value_low = d_value.astype(jnp.bfloat16)
    grad_query = jnp.einsum(
        "scd,sce->de", normed_low, d_query_pre, preferred_element_type=jnp.float32
    )
    grad_key = jnp.einsum("scd,sce->de", normed_low, d_key_pre, preferred_element_type=jnp.float32)
    grad_value = jnp.einsum(
        "scd,sce->de", normed_low, d_value_low, preferred_element_type=jnp.float32
    )
    d_normed = jnp.einsum("sce,de->scd", d_query_pre, w_query, preferred_element_type=jnp.float32)
    d_normed = d_normed + jnp.einsum(
        "sce,de->scd", d_key_pre, w_key, preferred_element_type=jnp.float32
    )
    d_normed = d_normed + jnp.einsum(
        "sce,de->scd", d_value_low, w_value, preferred_element_type=jnp.float32
    )
    grad_gain_attn = jnp.sum(d_normed * (inputs * factor_attn), axis=(0, 1))
    d_inputs = d_middle + rms_backward(inputs, factor_attn, gain_attn, d_normed)
    input_grad = jnp.where(live_rows, d_inputs, 0.0).astype(jnp.bfloat16)
    summed_parts = (
        lax.psum_scatter(grad_query, ("seq", "seqb"), scatter_dimension=0, tiled=True),
        lax.psum_scatter(grad_key, ("seq", "seqb"), scatter_dimension=0, tiled=True),
        lax.psum_scatter(grad_value, ("seq", "seqb"), scatter_dimension=0, tiled=True),
        lax.psum_scatter(grad_gain_attn, ("seq", "seqb"), scatter_dimension=0, tiled=True),
        lax.psum_scatter(first_done[0], ("seq", "seqb"), scatter_dimension=0, tiled=True),
        lax.psum_scatter(first_done[1], ("seq", "seqb"), scatter_dimension=0, tiled=True),
        lax.psum_scatter(first_done[2], ("seq", "seqb"), scatter_dimension=0, tiled=True),
        lax.psum_scatter(first_done[3], ("seq", "seqb"), scatter_dimension=0, tiled=True),
        lax.psum_scatter(first_done[4], ("seq", "seqb"), scatter_dimension=0, tiled=True),
    )
    all_done = (
        lax.psum(summed_parts[0].astype(jnp.bfloat16), "batch").astype(jnp.float32),
        lax.psum(summed_parts[1].astype(jnp.bfloat16), "batch").astype(jnp.float32),
        lax.psum(summed_parts[2].astype(jnp.bfloat16), "batch").astype(jnp.float32),
        lax.psum(summed_parts[3].astype(jnp.bfloat16), "batch").astype(jnp.float32),
        lax.psum(summed_parts[4].astype(jnp.bfloat16), "batch").astype(jnp.float32),
        lax.psum(summed_parts[5].astype(jnp.bfloat16), "batch").astype(jnp.float32),
        lax.psum(summed_parts[6].astype(jnp.bfloat16), "batch").astype(jnp.float32),
        lax.psum(summed_parts[7].astype(jnp.bfloat16), "batch").astype(jnp.float32),
        lax.psum(summed_parts[8].astype(jnp.bfloat16), "batch").astype(jnp.float32),
    )
    second_done = (all_done[0], all_done[1], all_done[2], all_done[3])
    first_done = (all_done[4], all_done[5], all_done[6], all_done[7], all_done[8])
    return (
        layer_out,
        input_grad,
        second_done[0],
        second_done[1],
        second_done[2],
        first_done[0],
        first_done[1],
        first_done[2],
        first_done[3],
        second_done[3],
        first_done[4],
    )


AXES = ("batch", "seq", "seqb")
BF = jnp.bfloat16
F32 = jnp.float32
MIB = 1 << 20
COST = 1e6
ADD_COST = 2e9


def fast_layout(mesh):
    return mesh.shape["batch"] == 4 and mesh.shape["seq"] == 4 and mesh.shape["seqb"] == 2


def exchange(rows, kind):
    pairs = []
    for b in range(4):
        for s in range(4):
            for c in range(2):
                first = 1 if c == 0 else 2
                target = {
                    "core": (b, s, 1 - c),
                    "first": (b ^ first, s, c),
                    "second": (b ^ (3 - first), s, c),
                    "near": (b, s ^ 1, c),
                    "far": (b, s ^ 2, c),
                    "across": (b ^ 3, s, c),
                }[kind]
                pairs.append((b * 8 + s * 2 + c, target[0] * 8 + target[1] * 2 + target[2]))
    return lax.ppermute(rows, AXES, pairs)


def dot(a, b):
    return lax.dot_general(a, b, (((1,), (0,)), ((), ())), preferred_element_type=F32)


def dot_nt(a, b):
    return lax.dot_general(a, b, (((1,), (1,)), ((), ())), preferred_element_type=F32)


def position_tables(count):
    half = HEAD_DIM // 2
    freq = rope_base ** (-(2.0 * np.arange(half)) / HEAD_DIM)
    angles = np.arange(count)[:, None] * freq[None, :]
    cosine, sine = np.cos(angles), np.sin(angles)
    return (
        np.concatenate([cosine, cosine, cosine, cosine], 1).astype(np.float32),
        np.concatenate([-sine, sine, -sine, sine], 1).astype(np.float32),
    )


def swap_halves(u):
    lane = lax.broadcasted_iota(jnp.int32, u.shape, 1) % HEAD_DIM
    return jnp.where(lane < HEAD_DIM // 2, pltpu.roll(u, 96, 1), pltpu.roll(u, 32, 1))


def turn(rows, cosine, sine):
    parts = []
    for g in range(rows.shape[1] // 128):
        u = rows[:, g * 128 : (g + 1) * 128]
        parts.append(u * cosine + swap_halves(u) * sine)
    return parts[0] if len(parts) == 1 else jnp.concatenate(parts, axis=1)


def live_mask(sc, row0, count):
    span_pos = sc[1] * SPAN + row0 + lax.broadcasted_iota(jnp.int32, (count, 1), 0)
    return span_pos < sc[2]


SPAN = 512
SEQ = 1024
WIDTH = 768
GROUP = 384
HID = 2048


def hbm():
    return pl.BlockSpec(memory_space=pl.ANY)


def far_hbm():
    return pl.BlockSpec(memory_space=pltpu.HBM)


def after(sc, *deps):
    return lax.optimization_barrier((sc,) + deps)[0]


def dot_tn(a, b):
    return lax.dot_general(a, b, (((0,), (0,)), ((), ())), preferred_element_type=F32)


def whole(shape):
    return pl.BlockSpec(shape, lambda i, sc: (0,) * len(shape))


def call(body, name, sc, args, in_specs, out_shapes, out_specs, scratch, vmem, cost):
    flops, moved, trans = cost
    args = [
        pltpu.with_memory_space_constraint(a, pltpu.HBM) if spec.memory_space is pltpu.HBM else a
        for a, spec in zip(args, in_specs)
    ]
    return pl.pallas_call(
        body,
        name=name,
        out_shape=out_shapes,
        grid_spec=pltpu.PrefetchScalarGridSpec(
            num_scalar_prefetch=1,
            grid=(1,),
            in_specs=in_specs,
            out_specs=out_specs,
            scratch_shapes=scratch,
        ),
        compiler_params=pltpu.CompilerParams(vmem_limit_bytes=vmem * MIB),
        cost_estimate=pl.CostEstimate(
            flops=int(COST * 5), bytes_accessed=1000, transcendentals=0
        ),
    )(sc, *args)


def sds(shape, dtype=BF):
    return jax.ShapeDtypeStruct(shape, dtype)


def project(o_ref, n_ref, cs, ss, weight, t):
    for r in range(0, SPAN, 256):
        y = dot(n_ref[r : r + 256, :], weight)
        if t < 2:
            y = turn(y, cs[r : r + 256, :], ss[r : r + 256, :])
        if t == 0:
            y = y * (HEAD_DIM**-0.5)
        o_ref[t, r : r + 256, :] = y.astype(BF)


def qkv_other_body(
    sc, x_hbm, cos_hbm, sin_hbm, gain, wq, wk, wv, o_ref, n_ref, cs, ss, own_w, xs, ws, gain_s, sem
):
    col = pl.multiple_of((1 - sc[0]) * GROUP, 128)
    own_col = pl.multiple_of(sc[0] * GROUP, 128)
    row = pl.multiple_of(sc[1] * SPAN, SPAN)
    weights = (wq, wk, wv)
    rows = [
        pltpu.make_async_copy(x_hbm.at[0, r : r + 256, :], xs.at[r : r + 256, :], sem.at[n])
        for n, r in enumerate((0, 256))
    ]
    copies = [
        pltpu.make_async_copy(w.at[:, pl.ds(col, GROUP)], ws.at[t], sem.at[2 + t])
        for t, w in enumerate(weights)
    ]
    tables = [
        pltpu.make_async_copy(cos_hbm.at[pl.ds(row, SPAN), :], cs, sem.at[5]),
        pltpu.make_async_copy(sin_hbm.at[pl.ds(row, SPAN), :], ss, sem.at[6]),
    ]
    later = [
        pltpu.make_async_copy(w.at[:, pl.ds(own_col, GROUP)], own_w.at[t], sem.at[7 + t])
        for t, w in enumerate(weights)
    ]
    gain_copy = pltpu.make_async_copy(gain, gain_s, sem.at[10])
    for cp in rows + [gain_copy, copies[2]] + copies[:2] + tables + later:
        cp.start()
    gain_copy.wait()
    gain_row = gain_s[...][None, :]
    for n, r in enumerate((0, 256)):
        rows[n].wait()
        x = jnp.where(live_mask(sc, r, 256), xs[r : r + 256, :].astype(F32), 0.0)
        factor = lax.rsqrt(jnp.mean(x * x, axis=-1, keepdims=True) + epsilon)
        n_ref[r : r + 256, :] = (x * factor * gain_row).astype(BF)
    for t in (2, 0, 1):
        copies[t].wait()
        if t == 0:
            for cp in tables:
                cp.wait()
        project(o_ref, n_ref, cs, ss, ws[t], t)
    for cp in later:
        cp.wait()


def qkv_own_body(sc, n_ref, cs, ss, ws, o_ref):
    for t in (2, 0, 1):
        project(o_ref, n_ref, cs, ss, ws[t], t)


def qkv_other_call(sc, tokens, gain, cosine, sine, wq, wk, wv):
    table = sds((SPAN, 128), F32)
    return call(
        qkv_other_body,
        "qkv_other",
        sc,
        (tokens, cosine, sine, gain, wq, wk, wv),
        [far_hbm()] * 7,
        [sds((3, SPAN, GROUP)), sds((SPAN, WIDTH)), table, table, sds((3, WIDTH, GROUP))],
        [whole((3, SPAN, GROUP)), whole((SPAN, WIDTH))] + [whole((SPAN, 128))] * 2 + [hbm()],
        [
            pltpu.VMEM((SPAN, WIDTH), BF),
            pltpu.VMEM((3, WIDTH, GROUP), BF),
            pltpu.VMEM((WIDTH,), F32),
            pltpu.SemaphoreType.DMA((11,)),
        ],
        9,
        (3 * 2 * SPAN * WIDTH * GROUP, 5e6, 1e3),
    )


def qkv_own_call(sc, n1, cs, ss, ws):
    return call(
        qkv_own_body,
        "qkv_own",
        sc,
        (n1, cs, ss, ws),
        [whole((SPAN, WIDTH))] + [whole((SPAN, 128))] * 2 + [whole((3, WIDTH, GROUP))],
        sds((3, SPAN, GROUP)),
        whole((3, SPAN, GROUP)),
        [],
        9,
        (3 * 2 * SPAN * WIDTH * GROUP, 5e6, 1e3),
    )


def gather_rows(sc, own, other, places, sem):
    copies = []
    for t, place in enumerate(places):
        for k, src in enumerate((own, other)):
            pos = sc[1] if k == 0 else 1 - sc[1]
            row = pl.multiple_of(pos * SPAN, SPAN)
            source = src.at[t] if len(src.shape) == 3 else src
            copies.append(
                pltpu.make_async_copy(source, place.at[pl.ds(row, SPAN), :], sem.at[2 * t + k])
            )
    for cp in copies:
        cp.start()
    return copies


def pair_loads(sc, own, other, places, sem, hp):
    cols = pl.ds(hp * 128 if isinstance(hp, int) else pl.multiple_of(hp * 128, 128), 128)
    copies = []
    for t, place in enumerate(places):
        for k, src in enumerate((own, other)):
            pos = sc[1] if k == 0 else 1 - sc[1]
            rows = pl.ds(pl.multiple_of(pos * SPAN, SPAN), SPAN)
            copies.append(
                pltpu.make_async_copy(
                    src.at[t, :, cols], place.at[rows, cols], sem.at[6 * hp + 2 * t + k]
                )
            )
    return copies


def attend_body(sc, own, other, wo, wg, wu, wd, *refs):
    (ot_ref, lse_ref, mine, theirs, wo_v, wg_v, wu_v, wd_v, qs, ks, vs, at, sem, wsem) = refs
    for n in range(3):
        for cp in pair_loads(sc, own, other, (qs, ks, vs), sem, n):
            cp.start()
    fetch = []

    def bring(src, place):
        fetch.append(pltpu.make_async_copy(src, place, wsem.at[len(fetch)]))
        fetch[-1].start()

    for k in range(2):
        head = (sc[0] if k == 0 else 1 - sc[0]) * GROUP
        rows = pl.ds(pl.multiple_of(head, 128), GROUP)
        bring(wo.at[rows, :], wo_v.at[GROUP * k : GROUP * k + GROUP, :])
    for half in range(2):
        for s in range(4):
            cols = hidden_cols(sc, s, half)
            to = slice(512 * half + 128 * s, 512 * half + 128 * s + 128)
            bring(wg.at[:, cols], wg_v.at[:, to])
            bring(wu.at[:, cols], wu_v.at[:, to])
            bring(wd.at[cols, :], wd_v.at[to, :])
    lane = lax.broadcasted_iota(jnp.int32, (256, 128), 1)
    key_id = lax.broadcasted_iota(jnp.int32, (256, 256), 0)
    row_id = lax.broadcasted_iota(jnp.int32, (256, 256), 1)
    keep = key_id <= row_id

    def pair(hp, carry):
        base = pl.multiple_of(hp * 128, 128)
        cols = pl.ds(base, 128)
        for cp in pair_loads(sc, own, other, (qs, ks, vs), sem, hp):
            cp.wait()
        vt = jnp.transpose(vs[:, cols].astype(F32)).astype(BF)

        def scores(i, h):
            n = 256 * (i + 1)
            qm = jnp.where(lane // HEAD_DIM == h, qs[256 * i : n, cols], jnp.zeros((), BF))
            return dot_nt(ks[0:n, cols], qm)

        def soften(i, h, st):
            n = 256 * (i + 1)
            diag = jnp.where(keep, st[n - 256 :, :], masked_score)
            st = diag if i == 0 else jnp.concatenate([st[: n - 256, :], diag], axis=0)
            peak = jnp.max(st, axis=0, keepdims=True)
            p = jnp.exp(st - peak)
            return p.astype(BF), peak, jnp.sum(p, axis=0, keepdims=True)

        def finish(i, h, p, peak, total):
            n = 256 * (i + 1)
            o = dot(vt[h * 64 : h * 64 + 64, :n], p) * (1.0 / total)
            ot_ref[pl.ds(pl.multiple_of(hp * 128 + h * 64, 64), 64), 256 * i : n] = o
            lse_ref[pl.ds(hp * 2 + h, 1), 256 * i : n] = peak + jnp.log(total)

        tasks = [(i, h) for i in range(4) for h in range(2)]
        st, waiting = scores(*tasks[0]), None
        for k, task in enumerate(tasks):
            ahead = scores(*tasks[k + 1]) if k + 1 < len(tasks) else None
            parts = soften(*task, st)
            if waiting is not None:
                finish(*waiting)
            waiting, st = task + parts, ahead
        finish(*waiting)
        at[:, cols] = jnp.transpose(ot_ref[cols, :]).astype(BF)
        return carry

    lax.fori_loop(0, 3, pair, 0)
    row = pl.multiple_of(sc[1] * SPAN, SPAN)
    row_other = pl.multiple_of((1 - sc[1]) * SPAN, SPAN)
    out_other = pltpu.make_async_copy(at.at[pl.ds(row_other, SPAN), :], theirs, sem.at[18])
    out_own = pltpu.make_async_copy(at.at[pl.ds(row, SPAN), :], mine, sem.at[19])
    out_other.start()
    out_own.start()
    out_other.wait()
    out_own.wait()
    for cp in fetch:
        cp.wait()


def attend_call(sc, own, other, wo, wg, wu, wd):
    return call(
        attend_body,
        "attend",
        sc,
        (own, other, wo, wg, wu, wd),
        [hbm(), hbm()] + [far_hbm()] * 4,
        [sds((GROUP, SEQ), F32), sds((8, SEQ), F32), sds((SPAN, GROUP)), sds((SPAN, GROUP))]
        + [sds((WIDTH, WIDTH)), sds((WIDTH, SEQ)), sds((WIDTH, SEQ)), sds((SEQ, WIDTH))],
        [whole((GROUP, SEQ)), whole((8, SEQ))] + [hbm()] * 6,
        [pltpu.VMEM((SEQ, GROUP), BF)] * 4
        + [pltpu.SemaphoreType.DMA((20,)), pltpu.SemaphoreType.DMA((26,))],
        8,
        (6 * 4 * SEQ * SEQ * 64, 6e6, 4e6),
    )


def proj_body(sc, x_ref, ak_ref, ar_ref, gain_ref, wo_ref, m_ref, n_ref):
    for r in range(0, SPAN, 256):
        rr = slice(r, r + 256)
        m = jnp.where(live_mask(sc, r, 256), x_ref[0, rr, :].astype(F32), 0.0)
        m = m + dot(ak_ref[rr, :], wo_ref[:GROUP, :]) + dot(ar_ref[rr, :], wo_ref[GROUP:, :])
        m_ref[rr, :] = m
        factor = lax.rsqrt(jnp.mean(m * m, axis=-1, keepdims=True) + epsilon)
        n_ref[rr, :] = (m * factor * gain_ref[...]).astype(BF)


def proj_call(sc, tokens, own, other, gain, wo):
    return call(
        proj_body,
        "proj",
        sc,
        (tokens, own, other, gain, wo),
        [whole((1, SPAN, WIDTH))]
        + [whole((SPAN, GROUP))] * 2
        + [whole((1, WIDTH)), whole((WIDTH, WIDTH))],
        [sds((SPAN, WIDTH), F32), sds((SPAN, WIDTH))],
        [whole((SPAN, WIDTH))] * 2,
        [],
        4,
        (2 * SPAN * WIDTH * WIDTH, 5e6, 1e3),
    )


def over_rows(own, other, d_own, d_other):
    return dot_tn(own, d_own) + dot_tn(other, d_other)


def place_of(s):
    return (s % 2) * 2 + s // 2


def hidden_cols(sc, s, half):
    return pl.ds(pl.multiple_of(512 * s + 128 * half + 256 * sc[0], 128), 128)


def spread(sc, res_s, first, count, rows, send_ref, keep_ref, to):
    size = send_ref.shape[1]
    for k, ref in enumerate((send_ref, keep_ref)):
        bit = (1 - sc[3]) if k == 0 else sc[3]
        for s in range(4):
            for q in range(count):
                lo = pl.multiple_of(first + (s * count + q) * 2 * rows + bit * rows, 16)
                block, row = divmod(to + q * rows, size)
                ref[2 * place_of(s) + block, row : row + rows, :] = res_s[pl.ds(lo, rows), :].astype(
                    BF
                )


def upstream_body(sc, dy_own, dy_oth, wd, dy_ref, dh_ref):
    for r in range(0, SEQ, 256):
        pos = sc[1] if r < SPAN else 1 - sc[1]
        at = pos * SPAN + r % SPAN + lax.broadcasted_iota(jnp.int32, (256, 1), 0)
        src = dy_own if r < SPAN else dy_oth
        lo = r % SPAN
        dy = jnp.where(at < sc[2], src[0, lo : lo + 256, :], jnp.zeros((), BF))
        dy_ref[r : r + 256, :] = dy
        dh_ref[r : r + 256, :] = dot_nt(dy, wd[...])


def upstream_call(sc, dy_own, dy_oth, wd):
    full = whole((1, SPAN, WIDTH))
    return call(
        upstream_body,
        "upstream",
        sc,
        (dy_own, dy_oth, wd),
        [full, full, whole((SEQ, WIDTH))],
        [sds((SEQ, WIDTH)), sds((SEQ, SEQ), F32)],
        [whole((SEQ, WIDTH)), whole((SEQ, SEQ))],
        [],
        4,
        (2 * SEQ * WIDTH * SEQ, 8e6, 0),
    )


def ffn_body(sc, n_own, n_oth, dy_s, dh_s, wg_s, wu_s, *refs, half):
    (send_ref, keep_ref, h_ref, dg_ref, du_ref, res_a, res_b) = refs
    part = slice(512 * half, 512 * half + 512)

    def products(r):
        src = n_own if r < SPAN else n_oth
        rows = src[r % SPAN : r % SPAN + 256, :]
        return dot(rows, wg_s[:, part]), dot(rows, wu_s[:, part])

    ahead = products(0)
    for r in range(0, SEQ, 256):
        g, u = ahead
        if r + 256 < SEQ:
            ahead = products(r + 256)
        rr = slice(r, r + 256)
        dh = dh_s[rr, part]
        sg = jax.nn.sigmoid(g)
        gs = g * sg
        h_ref[rr, :] = (gs * u).astype(BF)
        du_ref[rr, :] = (dh * gs).astype(BF)
        dg_ref[rr, :] = (dh * u * (sg + gs * (1.0 - sg))).astype(BF)
    lower, upper = slice(0, SPAN), slice(SPAN, SEQ)
    for k, (base, src) in enumerate(((0, dg_ref), (192, du_ref))):
        for ct in range(2):
            cols = slice(256 * ct, 256 * ct + 256)
            place = res_a.at[ct]
            place[...] = over_rows(n_own[...], n_oth[...], src[lower, cols], src[upper, cols])
            spread(sc, place, 0, 2, 48, send_ref, keep_ref, base + 96 * ct)
    for n in range(3):
        place = res_b.at[n % 2]
        place[...] = dot_tn(h_ref[...], dy_s[:, 256 * n : 256 * n + 256])
        spread(sc, place, 0, 1, 64, send_ref, keep_ref, 384 + 64 * n)


def ffn_call(sc, half, n_own, n_oth, dy, dh, wg, wu):
    flat = whole((SPAN, WIDTH))
    return call(
        functools.partial(ffn_body, half=half),
        "ffn_first" if half == 0 else "ffn_second",
        sc,
        (n_own, n_oth, dy, dh, wg, wu),
        [flat, flat, whole((SEQ, WIDTH)), whole((SEQ, SEQ))] + [whole((WIDTH, SEQ))] * 2,
        [sds((8, 288, 256))] * 2 + [sds((SEQ, 512))] * 3,
        [whole((8, 288, 256))] * 2 + [whole((SEQ, 512))] * 3,
        [pltpu.VMEM((2, WIDTH, 256), F32), pltpu.VMEM((2, 512, 256), F32)],
        14,
        (6 * 2 * SEQ * WIDTH * 512, 14e6, 1e6),
    )


def ffn_out_body(sc, h0, dg0, du0, h1, dg1, du1, wg, wu, wd, acc_ref, accs_ref, dn_ref, dns_ref):
    for r in (512, 768, 0, 256):
        rr = slice(r, r + 256)
        dn = dot_nt(dg0[rr, :], wg[:, :512]) + dot_nt(dg1[rr, :], wg[:, 512:])
        dn = dn + dot_nt(du0[rr, :], wu[:, :512]) + dot_nt(du1[rr, :], wu[:, 512:])
        acc = dot(h0[rr, :], wd[:512, :]) + dot(h1[rr, :], wd[512:, :])
        if r < SPAN:
            dn_ref[rr, :] = dn
            acc_ref[rr, :] = acc
        else:
            dns_ref[r - SPAN : r - SPAN + 256, :] = dn.astype(BF)
            accs_ref[r - SPAN : r - SPAN + 256, :] = acc.astype(BF)


def ffn_out_call(sc, first, second, wg, wu, wd):
    flat = [whole((SPAN, WIDTH))]
    return call(
        ffn_out_body,
        "ffn_out",
        sc,
        tuple(first) + tuple(second) + (wg, wu, wd),
        [whole((SEQ, 512))] * 6 + [whole((WIDTH, SEQ))] * 2 + [whole((SEQ, WIDTH))],
        [sds((SPAN, WIDTH), F32), sds((SPAN, WIDTH)), sds((SPAN, WIDTH), F32), sds((SPAN, WIDTH))],
        flat * 4,
        [],
        8,
        (3 * 2 * SEQ * WIDTH * SEQ, 16e6, 0),
    )


def middle_body(sc, dn_ref, got_ref, m_ref, dy_ref, gain_ref, dm_ref, db_ref):
    gain = gain_ref[...]
    for r in range(0, SPAN, 128):
        rr = slice(r, r + 128)
        live = live_mask(sc, r, 128)
        m = m_ref[rr, :]
        factor = lax.rsqrt(jnp.mean(m * m, axis=-1, keepdims=True) + epsilon)
        scaled = (dn_ref[rr, :] + got_ref[rr, :].astype(F32)) * gain
        dm = jnp.where(live, dy_ref[0, rr, :].astype(F32), 0.0) + (
            factor * scaled
            - m * (factor * factor * factor) * jnp.mean(m * scaled, axis=-1, keepdims=True)
        )
        dm_ref[rr, :] = dm
        db_ref[rr, :] = dm.astype(BF)


def middle_call(sc, dn, got, m, dy, gain):
    flat = whole((SPAN, WIDTH))
    return call(
        middle_body,
        "middle",
        sc,
        (dn, got, m, dy, gain),
        [flat, flat, flat, whole((1, SPAN, WIDTH)), whole((1, WIDTH))],
        [sds((SPAN, WIDTH), F32), sds((SPAN, WIDTH))],
        [flat, flat],
        [],
        6,
        (1e6, 8e6, 1e3),
    )


def attend_back_body(sc, own, other, ot_s, lse_s, dbk, dbr, wo_s, cos_hbm, sin_hbm, *refs):
    wq, wk, wv, mine, theirs, ws, qs, ks, vs, das, ds_all, dqt, dkv, cs, ss, sem, load_sem = refs
    for n in range(3):
        for cp in pair_loads(sc, own, other, (qs, ks, vs), load_sem, n):
            cp.start()
    small = [
        pltpu.make_async_copy(src, to, sem.at[6 + n])
        for n, (src, to) in enumerate(((cos_hbm, cs), (sin_hbm, ss)))
    ]
    fetch = [
        pltpu.make_async_copy(w, ws.at[t], sem.at[10 + t]) for t, w in enumerate((wq, wk, wv))
    ]
    for cp in small + fetch:
        cp.start()
    for k, src in enumerate((dbk, dbr)):
        pos = sc[1] if k == 0 else 1 - sc[1]
        for r in range(0, SPAN, 256):
            rows = pl.ds(pl.multiple_of(pos * SPAN + r, 256), 256)
            das[rows, :] = dot_nt(src[r : r + 256, :], wo_s[...]).astype(BF)
    for cp in small:
        cp.wait()
    lane = lax.broadcasted_iota(jnp.int32, (SEQ, 128), 1)
    key_id = lax.broadcasted_iota(jnp.int32, (256, 256), 0)
    row_id = lax.broadcasted_iota(jnp.int32, (256, 256), 1)
    keep = key_id <= row_id

    def pair(hp, carry):
        base = pl.multiple_of(hp * 128, 128)
        cols = pl.ds(base, 128)
        for cp in pair_loads(sc, own, other, (qs, ks, vs), load_sem, hp):
            cp.wait()
        kt = jnp.transpose(ks[:, cols].astype(F32)).astype(BF)
        dat = jnp.transpose(das[:, cols].astype(F32))
        qm, dam, delta, lses = [], [], [], []
        for h in range(2):
            qm.append(jnp.where(lane // HEAD_DIM == h, qs[:, cols], jnp.zeros((), BF)))
            dam.append(jnp.where(lane // HEAD_DIM == h, das[:, cols], jnp.zeros((), BF)))
            rows = pl.ds(pl.multiple_of(base + 64 * h, 64), 64)
            product = dat[64 * h : 64 * h + 64, :] * ot_s[rows, :]
            delta.append(jnp.sum(product, axis=0, keepdims=True))
            lses.append(lse_s[pl.ds(2 * hp + h, 1), :])

        def scores(i, h):
            n = 256 * (i + 1)
            rows = slice(256 * i, n)
            return dot_nt(ks[:n, cols], qm[h][rows, :]), dot_nt(vs[:n, cols], dam[h][rows, :])

        def soften(i, h, st, dp):
            n = 256 * (i + 1)
            rows = slice(256 * i, n)
            p = jnp.exp(st - lses[h][:, rows])
            diag = jnp.where(keep, p[n - 256 :, :], 0.0)
            p = diag if i == 0 else jnp.concatenate([p[: n - 256, :], diag], axis=0)
            return p.astype(BF), (p * (dp - delta[h][:, rows])).astype(BF)

        def finish(i, h, p, ds):
            n = 256 * (i + 1)
            rows = slice(256 * i, n)
            half = slice(64 * h, 64 * h + 64)
            dv = dot(p, dam[h][rows, :])
            dk = dot(ds, qm[h][rows, :])
            dqt[half, rows] = dot(kt[half, :n], ds)
            if (i, h) == (3, 0):
                dkv[0] = dk
                dkv[1] = dv
            else:
                dkv[0, :n] += dk
                dkv[1, :n] += dv

        tasks = [(i, h) for i in (3, 2, 1, 0) for h in range(2)]
        now, waiting = scores(*tasks[0]), None
        for k, task in enumerate(tasks):
            ahead = scores(*tasks[k + 1]) if k + 1 < len(tasks) else None
            parts = soften(*task, *now)
            if waiting is not None:
                finish(*waiting)
            waiting, now = task + parts, ahead
        finish(*waiting)
        dq = jnp.transpose(dqt[...]) * (HEAD_DIM**-0.5)
        ds_all[0, :, cols] = turn(dq, cs[...], -ss[...]).astype(BF)
        ds_all[1, :, cols] = turn(dkv[0], cs[...], -ss[...]).astype(BF)
        ds_all[2, :, cols] = dkv[1].astype(BF)
        return carry

    lax.fori_loop(0, 3, pair, 0)
    row = pl.multiple_of(sc[1] * SPAN, SPAN)
    row_other = pl.multiple_of((1 - sc[1]) * SPAN, SPAN)
    stores = [
        pltpu.make_async_copy(ds_all.at[:, pl.ds(row_other, SPAN), :], theirs, sem.at[8]),
        pltpu.make_async_copy(ds_all.at[:, pl.ds(row, SPAN), :], mine, sem.at[9]),
    ]
    for cp in stores:
        cp.start()
    for cp in stores + fetch:
        cp.wait()


def attend_back_call(sc, own, other, ot, lse, dbk, dbr, wo, cosine, sine, wq, wk, wv):
    return call(
        attend_back_body,
        "attend_back",
        sc,
        (own, other, ot, lse, dbk, dbr, wo, cosine, sine, wq, wk, wv),
        [hbm(), hbm(), whole((GROUP, SEQ)), whole((8, SEQ))]
        + [whole((SPAN, WIDTH))] * 2
        + [whole((GROUP, WIDTH))]
        + [far_hbm()] * 5,
        [sds((3, SPAN, GROUP))] * 2 + [sds((3, WIDTH, WIDTH))],
        [hbm()] * 3,
        [pltpu.VMEM((SEQ, GROUP), BF)] * 4
        + [
            pltpu.VMEM((3, SEQ, GROUP), BF),
            pltpu.VMEM((128, SEQ), F32),
            pltpu.VMEM((2, SEQ, 128), F32),
            pltpu.VMEM((SEQ, 128), F32),
            pltpu.VMEM((SEQ, 128), F32),
            pltpu.SemaphoreType.DMA((13,)),
            pltpu.SemaphoreType.DMA((18,)),
        ],
        22,
        (6 * 10 * SEQ * SEQ * 64, 10e6, 4e6),
    )


def square_body(sc, nk, nr, ak, at, ck, ct, bk, br, dk, dr, sa_ref, ka_ref, sb_ref, kb_ref, res):
    own = pl.ds(pl.multiple_of(sc[0] * GROUP, 128), GROUP)
    other = pl.ds(pl.multiple_of((1 - sc[0]) * GROUP, 128), GROUP)
    res[0, own, :] = over_rows(ak[...], at[...], bk[:, own], br[:, own])
    res[0, other, :] = over_rows(ck[...], ct[...], bk[:, own], br[:, own])
    spread(sc, res.at[0], 0, 2, 48, sa_ref, ka_ref, 0)
    for n, t in enumerate((2, 0, 1)):
        place = res.at[(n + 1) % 2]
        place[...] = over_rows(nk[...], nr[...], dk[t], dr[t])
        if n == 0:
            spread(sc, place, 0, 2, 48, sa_ref, ka_ref, 96)
        else:
            spread(sc, place, 0, 2, 48, sb_ref, kb_ref, 96 * t)


def square_call(sc, *args):
    flat = [whole((SPAN, WIDTH))] * 2
    return call(
        square_body,
        "square",
        sc,
        args,
        flat + [whole((SPAN, GROUP))] * 4 + flat + [whole((3, SPAN, GROUP))] * 2,
        [sds((8, 96, GROUP))] * 4,
        [whole((8, 96, GROUP))] * 4,
        [pltpu.VMEM((2, WIDTH, GROUP), F32)],
        16,
        (4 * 2 * SEQ * WIDTH * GROUP, 12e6, 0),
    )


def input_grad_body(sc, x_ref, gain_ref, dm_ref, m_ref, acc_ref, got_ref, dk_s, dr_s, ws, *refs):
    lay_ref, o_ref = refs
    for r in range(0, SPAN, 256):
        rr = slice(r, r + 256)
        out = m_ref[rr, :] + acc_ref[rr, :] + got_ref[rr, :].astype(F32)
        lay_ref[0, rr, :] = jnp.where(live_mask(sc, r, 256), out, 0.0).astype(BF)
    own_cols = pl.multiple_of(sc[0] * GROUP, 128)
    other_cols = pl.multiple_of((1 - sc[0]) * GROUP, 128)
    gain = gain_ref[...]
    for r in range(0, SPAN, 256):
        rr = slice(r, r + 256)
        dn = dot_nt(dk_s[0, rr, :], ws[0, :, pl.ds(own_cols, GROUP)])
        dn = dn + dot_nt(dr_s[0, rr, :], ws[0, :, pl.ds(other_cols, GROUP)])
        for t in (1, 2):
            dn = dn + dot_nt(dk_s[t, rr, :], ws[t, :, pl.ds(own_cols, GROUP)])
            dn = dn + dot_nt(dr_s[t, rr, :], ws[t, :, pl.ds(other_cols, GROUP)])
        live = live_mask(sc, r, 256)
        x = jnp.where(live, x_ref[0, rr, :].astype(F32), 0.0)
        factor = lax.rsqrt(jnp.mean(x * x, axis=-1, keepdims=True) + epsilon)
        scaled = dn * gain
        dx = dm_ref[rr, :] + (
            factor * scaled
            - x * (factor * factor * factor) * jnp.mean(x * scaled, axis=-1, keepdims=True)
        )
        o_ref[0, rr, :] = jnp.where(live, dx, 0.0).astype(BF)


def input_grad_call(sc, tokens, gain, dm, m, acc, got, dk, dr, ws):
    full = whole((1, SPAN, WIDTH))
    flat = whole((SPAN, WIDTH))
    return call(
        input_grad_body,
        "input_grad",
        sc,
        (tokens, gain, dm, m, acc, got, dk, dr, ws),
        [full, whole((1, WIDTH)), flat, flat, flat, flat]
        + [whole((3, SPAN, GROUP))] * 2
        + [whole((3, WIDTH, WIDTH))],
        [sds((1, SPAN, WIDTH))] * 2,
        [full] * 2,
        [],
        20,
        (3 * 2 * SPAN * WIDTH * WIDTH, 14e6, 1e3),
    )


def add_pieces(sc, count, sums, name):
    rows, cols = sums[0][0][0].shape[1:]
    arrays = [array for stack in sums for array, _ in stack]
    picks = [pick for stack in sums for _, pick in stack]

    def body(sc_ref, *refs):
        at = 0
        for n, stack in enumerate(sums):
            total = refs[at][0].astype(F32)
            for ref in refs[at + 1 : at + len(stack)]:
                total = total + ref[0].astype(F32)
            refs[-1][0, n * rows : (n + 1) * rows, :] = total.astype(BF)
            at += len(stack)

    def spec(pick):
        block, row = pick
        return pl.BlockSpec((1, rows, cols), lambda j, sc_ref: (block(sc_ref, j), row, 0))

    high = rows * len(sums)
    return pl.pallas_call(
        body,
        name=name,
        out_shape=sds((count, high, cols)),
        grid_spec=pltpu.PrefetchScalarGridSpec(
            num_scalar_prefetch=1,
            grid=(count,),
            in_specs=[spec(pick) for pick in picks],
            out_specs=pl.BlockSpec((1, high, cols), lambda j, sc_ref: (j, 0, 0)),
        ),
        compiler_params=pltpu.CompilerParams(vmem_limit_bytes=6 * MIB),
        cost_estimate=pl.CostEstimate(
            flops=int(0 if name == "g0_b" else ADD_COST), bytes_accessed=1000, transcendentals=0
        ),
    )(sc, *arrays)


def row_block(rows, cols):
    return pl.BlockSpec((rows, cols), lambda i, sc: (sc[6], 0))


def row_of(column):
    column = jnp.concatenate([column, jnp.zeros((32, 1), F32)], axis=0)
    return jnp.transpose(jnp.broadcast_to(column, (128, 128)))[0, :96]


def collect_halves(sc, group, full):
    for n in range(4):
        core, k = divmod(n, 2)
        parity = sc[0] if core == 0 else 1 - sc[0]
        first = sc[3] if core == 0 else sc[7]
        first = 1 - first if k == 1 else first
        for h in range(2):
            full[parity, first, 288 * h : 288 * h + 288, :] = group[n][h]


def collect(sc, group, full, row, size):
    for n in range(8):
        core, k = divmod(n, 4)
        parity = sc[0] if core == 0 else 1 - sc[0]
        first, second = (sc[3], sc[7]) if core == 0 else (sc[7], sc[3])
        first = 1 - first if k in (1, 3) else first
        second = 1 - second if k in (2, 3) else second
        rows = pl.ds(pl.multiple_of(second * size, 16), size)
        full[parity, first, rows, :] = group[n][0, row : row + size, :]


def ffn_result_body(sc, *refs):
    wg_ref, wu_ref, gain_ref, gate_ref, up_ref, down_ref, gg_ref, full = refs[12:]
    collect_halves(sc, refs[:4], full.at[0])
    collect(sc, refs[4:12], full.at[1], 0, 288)
    for half in range(2):
        for bit in range(2):
            rows = slice(48 * bit, 48 * bit + 48)
            for parity in range(2):
                for base, ref in ((0, gate_ref), (192, up_ref)):
                    for ct in range(2):
                        lo = pl.multiple_of(base + ct * 96 + sc[0] * 48, 16)
                        block = full[half, parity, bit, pl.ds(lo, 48), :].astype(F32)
                        for q in range(2):
                            col = 512 * (2 * ct + q) + 128 * half + 256 * parity
                            ref[rows, col : col + 128] = block[:, 128 * q : 128 * q + 128]
            lo = 128 * half + 64 * bit
            for t in range(3):
                down_ref[lo : lo + 64, 256 * t : 256 * t + 256] = full[
                    half, sc[0], bit, 384 + t * 64 : 448 + t * 64, :
                ].astype(F32)
    gate = jnp.sum(wg_ref[...].astype(F32) * gate_ref[...], axis=-1, keepdims=True)
    up = jnp.sum(wu_ref[...].astype(F32) * up_ref[...], axis=-1, keepdims=True)
    gg_ref[...] = row_of((gate + up) / gain_ref[...])


def ffn_result_call(sc, first, second, wg, wu, gain):
    return call(
        ffn_result_body,
        "ffn_result",
        sc,
        tuple(first) + tuple(second) + (wg, wu, gain),
        [whole((2, 288, 256))] * 4 + [whole((1, 288, 256))] * 8 + [row_block(96, HID)] * 2 + [row_block(96, 1)],
        [sds((96, HID), F32), sds((96, HID), F32), sds((256, WIDTH), F32), sds((96,), F32)],
        [whole((96, HID)), whole((96, HID)), whole((256, WIDTH)), whole((96,))],
        [pltpu.VMEM((2, 2, 2, 576, 256), BF)],
        14,
        (1e6, 6e6, 0),
    )


def square_result_body(sc, *refs):
    group = refs[:8]
    weights = refs[8:11]
    gain_ref = refs[11]
    outs = refs[12:16]
    gg_ref, full = refs[16:]
    order = ((3, 2), (0, 1))
    for n in range(2):
        collect(sc, group, full.at[n], 96 * n, 96)
        for bit in range(2):
            rows = slice(48 * bit, 48 * bit + 48)
            for parity in range(2):
                cols = slice(GROUP * parity, GROUP * parity + GROUP)
                for t in range(2):
                    lo = pl.multiple_of(t * 96 + sc[0] * 48, 16)
                    block = full[n, parity, bit, pl.ds(lo, 48), :]
                    outs[order[n][t]][rows, cols] = block.astype(F32)
    total = jnp.zeros((96, 1), F32)
    for t in range(3):
        total = total + jnp.sum(weights[t][...].astype(F32) * outs[t][...], axis=-1, keepdims=True)
    gg_ref[...] = row_of(total / gain_ref[...])


def square_result_call(sc, group, wq, wk, wv, gain):
    return call(
        square_result_body,
        "square_result",
        sc,
        tuple(group) + (wq, wk, wv, gain),
        [whole((1, 192, GROUP))] * 8 + [row_block(96, WIDTH)] * 3 + [row_block(96, 1)],
        [sds((96, WIDTH), F32)] * 4 + [sds((96,), F32)],
        [whole((96, WIDTH))] * 4 + [whole((96,))],
        [pltpu.VMEM((2, 2, 2, 192, GROUP), BF)],
        8,
        (1e6, 4e6, 0),
    )


class Chain:
    def __init__(self, sc):
        self.sc = sc

    def next(self, *deps):
        self.sc = after(self.sc, *deps)
        return self.sc


class Reduction:
    def __init__(self, chain, send, keep, name):
        self.chain = chain
        self.send = send
        self.name = name
        self.stacks = [[[keep, 0]]]
        self.flight = None

    def start(self):
        self.fly(after(self.send, self.chain.sc), "first")

    def fly(self, rows, kind):
        self.flight = exchange(rows, kind)

    def land(self):
        if self.flight is not None:
            for n, stack in enumerate(self.stacks):
                stack.append([self.flight, n])
        self.flight = None

    def add(self, count, picks, tag):
        self.land()
        sums = []
        for stack in self.stacks:
            blocks = ([picks[0]] + picks)[-len(stack) :]
            sums.append([(array, (pick, row)) for (array, row), pick in zip(stack, blocks)])
        arrays = [array for stack in sums for array, _ in stack]
        out = add_pieces(self.chain.next(*arrays), count, sums, self.name + tag)
        self.chain.next(out)
        return out

    def second(self):
        pick = lambda t, j: j * 2 + 1 - t[7]
        self.fly(self.add(4, [pick], "_b"), "second")

    def near(self):
        pick = lambda t, j: (1 - t[4]) * 4 + j * 2 + t[7]
        self.fly(self.add(2, [pick, lambda t, j: (1 - t[4]) * 2 + j], "_c"), "near")

    def far(self):
        pick = lambda t, j: t[4] * 4 + (1 - t[5]) * 2 + t[7]
        picks = [pick, lambda t, j: t[4] * 2 + 1 - t[5], lambda t, j: 1 - t[5]]
        self.fly(self.add(1, picks, "_d"), "far")

    def total(self):
        pick = lambda t, j: t[4] * 4 + t[5] * 2 + t[7]
        picks = [pick, lambda t, j: t[4] * 2 + t[5], lambda t, j: t[5], lambda t, j: 0]
        own = self.add(1, picks, "_e")
        self.quarters = [own] + [exchange(own, kind) for kind in ("first", "second", "across")]

    def result(self):
        late = [after(quarter, self.chain.sc) for quarter in self.quarters]
        return self.quarters + [exchange(quarter, "core") for quarter in late]


class Straight(Reduction):
    def near(self):
        pick = lambda t, j: (1 - t[4]) * 4 + j
        self.fly(self.add(4, [pick], "_b"), "near")

    def far(self):
        pick = lambda t, j: t[4] * 4 + (1 - t[5]) * 2 + j
        self.fly(self.add(2, [pick, lambda t, j: (1 - t[5]) * 2 + j], "_c"), "far")

    def second(self):
        pick = lambda t, j: t[4] * 4 + t[5] * 2 + j
        own = self.add(2, [pick, lambda t, j: t[5] * 2 + j, lambda t, j: j], "_d")
        self.stacks = [[[own, 0]]]
        self.fly(own, "second")

    def total(self):
        own = self.add(2, [lambda t, j: j], "_e")
        self.quarters = [own, exchange(own, "first")]


def join(first, second):
    both = Reduction(first.chain, None, None, first.name + second.name)
    first.land()
    second.land()
    both.stacks = first.stacks + second.stacks
    return both


def fast_step(
    tokens,
    lengths,
    owner,
    w_query,
    w_key,
    w_value,
    w_out,
    w_gate,
    w_up,
    w_down,
    gain_attn,
    gain_mlp,
    cotangent,
):
    place = lax.axis_index(AXES)
    slot = jnp.arange(8, dtype=jnp.int32)
    core = place & 1
    base = jnp.where(slot == 3, 3 + core, jnp.where(slot == 7, 4 - core, 0))
    base = jnp.where(slot == 4, 1, jnp.where(slot == 5, 2, base))
    row = (place >> base) & jnp.where(slot == 6, 7, 1)
    turned = jnp.abs(row - jnp.broadcast_to(owner[0, :1], (8,)))
    sc = jnp.where(slot == 1, turned, row)
    sc = jnp.where(slot == 2, jnp.broadcast_to(lengths, (8,)), sc)
    tables = position_tables(SEQ)
    cosine, sine = jnp.asarray(tables[0]), jnp.asarray(tables[1])
    gain_row = gain_attn.reshape(1, WIDTH)
    gain_mlp_row = gain_mlp.reshape(1, WIDTH)
    qkv_w = (w_query, w_key, w_value)
    ffn_w = (w_gate, w_up, w_down)
    chain = Chain(sc)

    qkv_send, n1, cs_v, ss_v, w_v = qkv_other_call(chain.sc, tokens, gain_attn, cosine, sine, *qkv_w)
    qkv_other = exchange(qkv_send, "core")
    qkv_own = qkv_own_call(chain.next(n1), n1, cs_v, ss_v, w_v)
    n1_other = exchange(n1, "core")
    dy_other = exchange(cotangent, "core")
    attn_t, lse, attn_own, attn_send, wo_v, *ffn_v = attend_call(
        chain.next(qkv_own), qkv_own, qkv_other, w_out, *ffn_w
    )
    attn_other = exchange(attn_send, "core")
    attn_rest = exchange(attn_own, "core")
    middle, n2 = proj_call(
        chain.next(lse, n1_other, dy_other), tokens, attn_own, attn_other, gain_mlp_row, wo_v
    )
    n2_other = exchange(n2, "core")
    dy_all, dh_all = upstream_call(chain.next(n2), cotangent, dy_other, ffn_v[2])
    rows = (n2, n2_other, dy_all, dh_all)
    send0, keep0, *acts0 = ffn_call(chain.next(dy_all, attn_rest), 0, *rows, *ffn_v[:2])
    g0 = Straight(chain, send0, keep0, "g0")
    g0.start()
    send1, keep1, *acts1 = ffn_call(chain.next(acts0[0]), 1, *rows, *ffn_v[:2])
    g1 = Reduction(chain, send1, keep1, "g1")
    g1.start()
    acc, acc_send, dn, dn_send = ffn_out_call(chain.next(acts1[0]), acts0, acts1, *ffn_v)
    dn_other = exchange(dn_send, "core")
    chain.next(dn_send)
    d_middle, db = middle_call(
        chain.next(dn_other, g0.flight), dn, dn_other, middle, cotangent, gain_mlp_row
    )
    chain.next(db)
    g0.near()
    db_other = exchange(db, "core")
    acc_other = exchange(after(acc_send, db_other), "core")
    d_own, d_send, qkv_v = attend_back_call(
        chain.sc,
        qkv_own,
        qkv_other,
        attn_t,
        lse,
        db,
        db_other,
        wo_v,
        cosine,
        sine,
        *qkv_w,
    )
    d_other = exchange(d_send, "core")
    chain.next(d_own, g0.flight, g1.flight)
    g1.second()
    g0.far()
    attn = (attn_own, attn_send, attn_other, attn_rest)
    send2, keep2, send3, keep3 = square_call(
        chain.sc, n1, n1_other, *attn, db, db_other, d_own, d_send
    )
    g2 = Reduction(chain, send2, keep2, "g2")
    g3 = Reduction(chain, send3, keep3, "g3")
    g2.start()
    g3.start()
    chain.next(send3)
    layer_out, input_grad = input_grad_call(
        chain.next(acc_other, d_other),
        tokens,
        gain_row,
        d_middle,
        middle,
        acc,
        acc_other,
        d_own,
        d_other,
        qkv_v,
    )
    chain.next(input_grad)
    g0.second()
    g1.near()
    g2.second()
    g1.far()
    g3.second()
    g2.near()
    g0.total()
    g3.near()
    g2.far()
    g3.far()
    g1.total()
    g23 = join(g2, g3)
    g23.total()
    first = g0.result()
    second = g1.result()
    third = g23.result()
    gate, up, down, gain_m = ffn_result_call(
        chain.sc, first, second, w_gate, w_up, gain_mlp.reshape(WIDTH, 1)
    )
    chain.next(gain_m)
    query, key, value, out, gain_a = square_result_call(
        chain.sc, third, *qkv_w, gain_attn.reshape(WIDTH, 1)
    )
    return (
        layer_out,
        input_grad,
        query,
        key,
        value,
        out,
        gate,
        up,
        down,
        gain_a,
        gain_m,
    )


def solution(mesh):
    in_specs = (
        P(("batch", "seq"), "seqb", None),
        P(("batch", "seq")),
        P(("batch", "seq"), None),
        P(),
        P(),
        P(),
        P(),
        P(),
        P(),
        P(),
        P(),
        P(),
        P(("batch", "seq"), "seqb", None),
    )
    out_specs = (
        P(("batch", "seq"), "seqb", None),
        P(("batch", "seq"), "seqb", None),
        P(("seq", "seqb"), None),
        P(("seq", "seqb"), None),
        P(("seq", "seqb"), None),
        P(("seq", "seqb"), None),
        P(("seq", "seqb"), None),
        P(("seq", "seqb"), None),
        P(("seq", "seqb"), None),
        P(("seq", "seqb")),
        P(("seq", "seqb")),
    )
    step = fast_step if fast_layout(mesh) else general_step
    return jax.shard_map(step, mesh=mesh, in_specs=in_specs, out_specs=out_specs, check_vma=False)
```

```python
import functools
import math

import jax
import jax.numpy as jnp
import numpy as np
from jax import lax
from jax.experimental import pallas as pl
from jax.experimental.pallas import tpu as pltpu
from jax.sharding import PartitionSpec as P

HEADS = 12
HEAD_DIM = 64


epsilon = 1e-05
rope_base = 10000.0
masked_score = -1e30


def rms_forward(rows, gain):
    factor = lax.rsqrt(jnp.mean(rows * rows, axis=-1, keepdims=True) + epsilon)
    return (rows * factor * gain, factor)


def rms_backward(rows, factor, gain, upstream):
    scaled = upstream * gain
    return factor * scaled - rows * (factor * factor * factor) * jnp.mean(
        rows * scaled, axis=-1, keepdims=True
    )


def rotation_tables(positions):
    half = HEAD_DIM // 2
    freq = rope_base ** (-(2.0 * jnp.arange(half, dtype=jnp.float32)) / HEAD_DIM)
    angles = positions.astype(jnp.float32)[..., None] * freq
    return (jnp.cos(angles), jnp.sin(angles))


def split_heads(rows):
    return rows.reshape(rows.shape[0], rows.shape[1], HEADS, HEAD_DIM)


def rotate(rows, cosine, sine, inverse):
    shaped = split_heads(rows)
    half = HEAD_DIM // 2
    first = shaped[..., :half]
    second = shaped[..., half:]
    cos_part = cosine[:, :, None, :]
    sin_part = sine[:, :, None, :]
    if inverse:
        turned = jnp.concatenate(
            [first * cos_part + second * sin_part, second * cos_part - first * sin_part], axis=-1
        )
    else:
        turned = jnp.concatenate(
            [first * cos_part - second * sin_part, second * cos_part + first * sin_part], axis=-1
        )
    return turned.reshape(rows.shape)


def range_positions(owner, count, span):
    offsets = jnp.arange(span, dtype=jnp.int32)
    return (owner[:, :, None] * span + offsets[None, None, :]).reshape(owner.shape[0], count)


def fold_keys(parts, combine, initial):
    return combine(
        initial,
        (
            lax.all_gather(parts[0], "seqb", axis=1, tiled=True),
            lax.all_gather(parts[1], "seqb", axis=1, tiled=True),
        ),
        jnp.int32(0),
    )


def general_step(
    tokens,
    lengths,
    owner,
    w_query,
    w_key,
    w_value,
    w_out,
    w_gate,
    w_up,
    w_down,
    gain_attn,
    gain_mlp,
    cotangent,
):
    seqs, span, width = tokens.shape
    scale = HEAD_DIM ** (-0.5)
    place = lax.axis_index("seqb")
    own_block = lax.dynamic_slice_in_dim(owner, place, 1, 1)
    local_pos = own_block * span + jnp.arange(span, dtype=jnp.int32)[None, :]
    local_live = local_pos < lengths[:, None]
    live_rows = local_live[:, :, None]
    inputs = jnp.where(live_rows, tokens.astype(jnp.float32), 0.0)
    normed, factor_attn = rms_forward(inputs, gain_attn)
    normed_low = normed.astype(jnp.bfloat16)
    cosine, sine = rotation_tables(local_pos)
    query_pre = jnp.einsum("scd,de->sce", normed_low, w_query, preferred_element_type=jnp.float32)
    key_pre = jnp.einsum("scd,de->sce", normed_low, w_key, preferred_element_type=jnp.float32)
    value_low = jnp.einsum(
        "scd,de->sce", normed_low, w_value, preferred_element_type=jnp.float32
    ).astype(jnp.bfloat16)
    query_rot = rotate(query_pre, cosine, sine, False).astype(jnp.bfloat16)
    key_rot = rotate(key_pre, cosine, sine, False).astype(jnp.bfloat16)
    query_heads = split_heads(query_rot)
    key_heads = split_heads(key_rot)
    value_heads = split_heads(value_low)

    def attend(state, piece, start):
        keys, values = piece
        count = keys.shape[1]
        key_pos = range_positions(owner, count, span)
        key_live = key_pos < lengths[:, None]
        stride = math.gcd(count, 512)

        def attend_one_block(index, inner):
            offset = index * stride
            key_block = split_heads(lax.dynamic_slice_in_dim(keys, offset, stride, 1))
            value_block = split_heads(lax.dynamic_slice_in_dim(values, offset, stride, 1))
            pos_block = lax.dynamic_slice_in_dim(key_pos, offset, stride, 1)
            live_block = lax.dynamic_slice_in_dim(key_live, offset, stride, 1)
            allowed = (
                (pos_block[:, None, :] <= local_pos[:, :, None])
                & live_block[:, None, :]
                & local_live[:, :, None]
            )

            def attend_update(carried):
                peak, total, summed = carried
                scores = (
                    jnp.einsum(
                        "sqhd,skhd->shqk",
                        query_heads,
                        key_block,
                        preferred_element_type=jnp.float32,
                    )
                    * scale
                )
                mask = allowed[:, None, :, :]
                new_peak = jnp.maximum(
                    peak, jnp.max(jnp.where(mask, scores, masked_score), axis=-1)
                )
                weights = jnp.where(mask, jnp.exp(scores - new_peak[..., None]), 0.0)
                factor = jnp.exp(peak - new_peak)
                total = total * factor + jnp.sum(weights, axis=-1)
                term = jnp.einsum(
                    "shqk,skhd->sqhd",
                    weights.astype(jnp.bfloat16),
                    value_block,
                    preferred_element_type=jnp.float32,
                )
                summed = (
                    split_heads(summed) * jnp.transpose(factor, (0, 2, 1))[..., None] + term
                ).reshape(summed.shape)
                return (new_peak, total, summed)

            return lax.cond(jnp.any(allowed), attend_update, lambda carried: carried, inner)

        return lax.fori_loop(0, count // stride, attend_one_block, state)

    start_state = (
        jnp.full((seqs, HEADS, span), masked_score, jnp.float32),
        jnp.zeros((seqs, HEADS, span), jnp.float32),
        jnp.zeros((seqs, span, width), jnp.float32),
    )
    peak, total, summed = fold_keys((key_rot, value_low), attend, start_state)
    safe_total = jnp.where(local_live[:, None, :], total, 1.0)
    attn = split_heads(summed) / jnp.transpose(safe_total, (0, 2, 1))[..., None]
    attn = jnp.where(local_live[:, :, None, None], attn, 0.0).reshape(seqs, span, width)
    log_total = jnp.where(local_live[:, None, :], peak + jnp.log(safe_total), 0.0)
    attn_low = attn.astype(jnp.bfloat16)
    middle = inputs + jnp.einsum("scd,de->sce", attn_low, w_out, preferred_element_type=jnp.float32)
    normed_mlp, factor_mlp = rms_forward(middle, gain_mlp)
    normed_mlp_low = normed_mlp.astype(jnp.bfloat16)
    gate = jnp.einsum("scd,df->scf", normed_mlp_low, w_gate, preferred_element_type=jnp.float32)
    up_proj = jnp.einsum("scd,df->scf", normed_mlp_low, w_up, preferred_element_type=jnp.float32)
    hidden = (jax.nn.silu(gate) * up_proj).astype(jnp.bfloat16)
    out = middle + jnp.einsum("scf,fd->scd", hidden, w_down, preferred_element_type=jnp.float32)
    layer_out = jnp.where(live_rows, out, 0.0).astype(jnp.bfloat16)
    upstream = jnp.where(live_rows, cotangent, jnp.zeros_like(cotangent))
    grad_down = jnp.einsum("scf,scd->fd", hidden, upstream, preferred_element_type=jnp.float32)
    d_hidden = jnp.einsum("scd,fd->scf", upstream, w_down, preferred_element_type=jnp.float32)
    sigmoid_gate = jax.nn.sigmoid(gate)
    d_gate = (d_hidden * up_proj * sigmoid_gate * (1.0 + gate * (1.0 - sigmoid_gate))).astype(
        jnp.bfloat16
    )
    d_up = (d_hidden * gate * sigmoid_gate).astype(jnp.bfloat16)
    grad_gate = jnp.einsum(
        "scd,scf->df", normed_mlp_low, d_gate, preferred_element_type=jnp.float32
    )
    grad_up = jnp.einsum("scd,scf->df", normed_mlp_low, d_up, preferred_element_type=jnp.float32)
    d_normed_mlp = jnp.einsum(
        "scf,df->scd", d_gate, w_gate, preferred_element_type=jnp.float32
    ) + jnp.einsum("scf,df->scd", d_up, w_up, preferred_element_type=jnp.float32)
    grad_gain_mlp = jnp.sum(d_normed_mlp * (middle * factor_mlp), axis=(0, 1))
    d_middle = upstream.astype(jnp.float32) + rms_backward(
        middle, factor_mlp, gain_mlp, d_normed_mlp
    )
    d_branch = d_middle.astype(jnp.bfloat16)
    grad_out = jnp.einsum("scd,sce->de", attn_low, d_branch, preferred_element_type=jnp.float32)
    d_attn = jnp.einsum("sce,de->scd", d_branch, w_out, preferred_element_type=jnp.float32).astype(
        jnp.bfloat16
    )
    first_done = (grad_out, grad_gate, grad_up, grad_down, grad_gain_mlp)
    delta = jnp.sum(split_heads(d_attn.astype(jnp.float32) * attn), axis=-1)
    delta_heads = jnp.transpose(delta, (0, 2, 1))
    grad_heads = split_heads(d_attn)

    def query_grads(state, piece, start):
        keys, values = piece
        count = keys.shape[1]
        key_pos = range_positions(owner, count, span)
        key_live = key_pos < lengths[:, None]
        stride = math.gcd(count, 512)

        def query_one_block(index, inner):
            offset = index * stride
            key_block = split_heads(lax.dynamic_slice_in_dim(keys, offset, stride, 1))
            value_block = split_heads(lax.dynamic_slice_in_dim(values, offset, stride, 1))
            pos_block = lax.dynamic_slice_in_dim(key_pos, offset, stride, 1)
            live_block = lax.dynamic_slice_in_dim(key_live, offset, stride, 1)
            allowed = (
                (pos_block[:, None, :] <= local_pos[:, :, None])
                & live_block[:, None, :]
                & local_live[:, :, None]
            )

            def query_update(carried):
                scores = (
                    jnp.einsum(
                        "sqhd,skhd->shqk",
                        query_heads,
                        key_block,
                        preferred_element_type=jnp.float32,
                    )
                    * scale
                )
                probs = jnp.where(
                    allowed[:, None, :, :], jnp.exp(scores - log_total[..., None]), 0.0
                )
                d_probs = jnp.einsum(
                    "sqhd,skhd->shqk", grad_heads, value_block, preferred_element_type=jnp.float32
                )
                d_scores = (probs * (d_probs - delta_heads[..., None])).astype(jnp.bfloat16)
                term = (
                    jnp.einsum(
                        "shqk,skhd->sqhd", d_scores, key_block, preferred_element_type=jnp.float32
                    )
                    * scale
                )
                return carried + term.reshape(carried.shape)

            return lax.cond(jnp.any(allowed), query_update, lambda carried: carried, inner)

        return lax.fori_loop(0, count // stride, query_one_block, state)

    zero_query = jnp.zeros((seqs, span, width), jnp.float32)
    d_query = fold_keys((key_rot, value_low), query_grads, zero_query)
    lse_all, delta_all = (
        lax.all_gather(jnp.transpose(log_total, (0, 2, 1)), "seqb", axis=1, tiled=True),
        lax.all_gather(delta, "seqb", axis=1, tiled=True),
    )
    zero_rows = jnp.zeros((seqs, span, width), jnp.float32)
    queries = lax.all_gather(query_rot, "seqb", axis=1, tiled=True)
    d_rows = lax.all_gather(d_attn, "seqb", axis=1, tiled=True)
    count = queries.shape[1]
    row_pos = range_positions(owner, count, span)
    row_live = row_pos < lengths[:, None]
    stride = math.gcd(count, 512)

    def key_one_block(index, inner):
        offset = index * stride
        query_block = split_heads(lax.dynamic_slice_in_dim(queries, offset, stride, 1))
        grad_block = split_heads(lax.dynamic_slice_in_dim(d_rows, offset, stride, 1))
        pos_block = lax.dynamic_slice_in_dim(row_pos, offset, stride, 1)
        live_block = lax.dynamic_slice_in_dim(row_live, offset, stride, 1)
        lse_block = jnp.transpose(lax.dynamic_slice_in_dim(lse_all, offset, stride, 1), (0, 2, 1))
        delta_block = jnp.transpose(
            lax.dynamic_slice_in_dim(delta_all, offset, stride, 1), (0, 2, 1)
        )
        allowed = (
            (local_pos[:, None, :] <= pos_block[:, :, None])
            & local_live[:, None, :]
            & live_block[:, :, None]
        )

        def key_update(carried):
            d_key, d_value = carried
            scores = (
                jnp.einsum(
                    "sqhd,skhd->shqk", query_block, key_heads, preferred_element_type=jnp.float32
                )
                * scale
            )
            probs = jnp.where(allowed[:, None, :, :], jnp.exp(scores - lse_block[..., None]), 0.0)
            value_term = jnp.einsum(
                "shqk,sqhd->skhd",
                probs.astype(jnp.bfloat16),
                grad_block,
                preferred_element_type=jnp.float32,
            )
            d_probs = jnp.einsum(
                "sqhd,skhd->shqk", grad_block, value_heads, preferred_element_type=jnp.float32
            )
            d_scores = (probs * (d_probs - delta_block[..., None])).astype(jnp.bfloat16)
            key_term = (
                jnp.einsum(
                    "shqk,sqhd->skhd", d_scores, query_block, preferred_element_type=jnp.float32
                )
                * scale
            )
            return (
                d_key + key_term.reshape(d_key.shape),
                d_value + value_term.reshape(d_value.shape),
            )

        return lax.cond(jnp.any(allowed), key_update, lambda carried: carried, inner)

    d_key, d_value = lax.fori_loop(0, count // stride, key_one_block, (zero_rows, zero_rows))
    d_query_pre = rotate(d_query, cosine, sine, True).astype(jnp.bfloat16)
    d_key_pre = rotate(d_key, cosine, sine, True).astype(jnp.bfloat16)
    d_value_low = d_value.astype(jnp.bfloat16)
    grad_query = jnp.einsum(
        "scd,sce->de", normed_low, d_query_pre, preferred_element_type=jnp.float32
    )
    grad_key = jnp.einsum("scd,sce->de", normed_low, d_key_pre, preferred_element_type=jnp.float32)
    grad_value = jnp.einsum(
        "scd,sce->de", normed_low, d_value_low, preferred_element_type=jnp.float32
    )
    d_normed = jnp.einsum("sce,de->scd", d_query_pre, w_query, preferred_element_type=jnp.float32)
    d_normed = d_normed + jnp.einsum(
        "sce,de->scd", d_key_pre, w_key, preferred_element_type=jnp.float32
    )
    d_normed = d_normed + jnp.einsum(
        "sce,de->scd", d_value_low, w_value, preferred_element_type=jnp.float32
    )
    grad_gain_attn = jnp.sum(d_normed * (inputs * factor_attn), axis=(0, 1))
    d_inputs = d_middle + rms_backward(inputs, factor_attn, gain_attn, d_normed)
    input_grad = jnp.where(live_rows, d_inputs, 0.0).astype(jnp.bfloat16)
    summed_parts = (
        lax.psum_scatter(grad_query, ("seq", "seqb"), scatter_dimension=0, tiled=True),
        lax.psum_scatter(grad_key, ("seq", "seqb"), scatter_dimension=0, tiled=True),
        lax.psum_scatter(grad_value, ("seq", "seqb"), scatter_dimension=0, tiled=True),
        lax.psum_scatter(grad_gain_attn, ("seq", "seqb"), scatter_dimension=0, tiled=True),
        lax.psum_scatter(first_done[0], ("seq", "seqb"), scatter_dimension=0, tiled=True),
        lax.psum_scatter(first_done[1], ("seq", "seqb"), scatter_dimension=0, tiled=True),
        lax.psum_scatter(first_done[2], ("seq", "seqb"), scatter_dimension=0, tiled=True),
        lax.psum_scatter(first_done[3], ("seq", "seqb"), scatter_dimension=0, tiled=True),
        lax.psum_scatter(first_done[4], ("seq", "seqb"), scatter_dimension=0, tiled=True),
    )
    all_done = (
        lax.psum(summed_parts[0].astype(jnp.bfloat16), "batch").astype(jnp.float32),
        lax.psum(summed_parts[1].astype(jnp.bfloat16), "batch").astype(jnp.float32),
        lax.psum(summed_parts[2].astype(jnp.bfloat16), "batch").astype(jnp.float32),
        lax.psum(summed_parts[3].astype(jnp.bfloat16), "batch").astype(jnp.float32),
        lax.psum(summed_parts[4].astype(jnp.bfloat16), "batch").astype(jnp.float32),
        lax.psum(summed_parts[5].astype(jnp.bfloat16), "batch").astype(jnp.float32),
        lax.psum(summed_parts[6].astype(jnp.bfloat16), "batch").astype(jnp.float32),
        lax.psum(summed_parts[7].astype(jnp.bfloat16), "batch").astype(jnp.float32),
        lax.psum(summed_parts[8].astype(jnp.bfloat16), "batch").astype(jnp.float32),
    )
    second_done = (all_done[0], all_done[1], all_done[2], all_done[3])
    first_done = (all_done[4], all_done[5], all_done[6], all_done[7], all_done[8])
    return (
        layer_out,
        input_grad,
        second_done[0],
        second_done[1],
        second_done[2],
        first_done[0],
        first_done[1],
        first_done[2],
        first_done[3],
        second_done[3],
        first_done[4],
    )


AXES = ("batch", "seq", "seqb")
BF = jnp.bfloat16
F32 = jnp.float32
MIB = 1 << 20
COST = 1e6
ADD_COST = 2e9


def fast_layout(mesh):
    return mesh.shape["batch"] == 4 and mesh.shape["seq"] == 4 and mesh.shape["seqb"] == 2


def exchange(rows, kind):
    pairs = []
    for b in range(4):
        for s in range(4):
            for c in range(2):
                first = 1 if c == 0 else 2
                target = {
                    "core": (b, s, 1 - c),
                    "first": (b ^ first, s, c),
                    "second": (b ^ (3 - first), s, c),
                    "near": (b, s ^ 1, c),
                    "far": (b, s ^ 2, c),
                    "across": (b ^ 3, s, c),
                }[kind]
                pairs.append((b * 8 + s * 2 + c, target[0] * 8 + target[1] * 2 + target[2]))
    return lax.ppermute(rows, AXES, pairs)


def dot(a, b):
    return lax.dot_general(a, b, (((1,), (0,)), ((), ())), preferred_element_type=F32)


def dot_nt(a, b):
    return lax.dot_general(a, b, (((1,), (1,)), ((), ())), preferred_element_type=F32)


def position_tables(count):
    half = HEAD_DIM // 2
    freq = rope_base ** (-(2.0 * np.arange(half)) / HEAD_DIM)
    angles = np.arange(count)[:, None] * freq[None, :]
    cosine, sine = np.cos(angles), np.sin(angles)
    return (
        np.concatenate([cosine, cosine, cosine, cosine], 1).astype(np.float32),
        np.concatenate([-sine, sine, -sine, sine], 1).astype(np.float32),
    )


def swap_halves(u):
    lane = lax.broadcasted_iota(jnp.int32, u.shape, 1) % HEAD_DIM
    return jnp.where(lane < HEAD_DIM // 2, pltpu.roll(u, 96, 1), pltpu.roll(u, 32, 1))


def turn(rows, cosine, sine):
    parts = []
    for g in range(rows.shape[1] // 128):
        u = rows[:, g * 128 : (g + 1) * 128]
        parts.append(u * cosine + swap_halves(u) * sine)
    return parts[0] if len(parts) == 1 else jnp.concatenate(parts, axis=1)


def live_mask(sc, row0, count):
    span_pos = sc[1] * SPAN + row0 + lax.broadcasted_iota(jnp.int32, (count, 1), 0)
    return span_pos < sc[2]


SPAN = 512
SEQ = 1024
WIDTH = 768
GROUP = 384
HID = 2048


def hbm():
    return pl.BlockSpec(memory_space=pl.ANY)


def far_hbm():
    return pl.BlockSpec(memory_space=pltpu.HBM)


def after(sc, *deps):
    return lax.optimization_barrier((sc,) + deps)[0]


def dot_tn(a, b):
    return lax.dot_general(a, b, (((0,), (0,)), ((), ())), preferred_element_type=F32)


def whole(shape):
    return pl.BlockSpec(shape, lambda i, sc: (0,) * len(shape))


def call(body, name, sc, args, in_specs, out_shapes, out_specs, scratch, vmem, cost):
    flops, moved, trans = cost
    args = [
        pltpu.with_memory_space_constraint(a, pltpu.HBM) if spec.memory_space is pltpu.HBM else a
        for a, spec in zip(args, in_specs)
    ]
    return pl.pallas_call(
        body,
        name=name,
        out_shape=out_shapes,
        grid_spec=pltpu.PrefetchScalarGridSpec(
            num_scalar_prefetch=1,
            grid=(1,),
            in_specs=in_specs,
            out_specs=out_specs,
            scratch_shapes=scratch,
        ),
        compiler_params=pltpu.CompilerParams(vmem_limit_bytes=vmem * MIB),
        cost_estimate=pl.CostEstimate(
            flops=int(COST * 5), bytes_accessed=1000, transcendentals=0
        ),
    )(sc, *args)


def sds(shape, dtype=BF):
    return jax.ShapeDtypeStruct(shape, dtype)


def project(o_ref, n_ref, cs, ss, weight, t):
    for r in range(0, SPAN, 256):
        y = dot(n_ref[r : r + 256, :], weight)
        if t < 2:
            y = turn(y, cs[r : r + 256, :], ss[r : r + 256, :])
        if t == 0:
            y = y * (HEAD_DIM**-0.5)
        o_ref[t, r : r + 256, :] = y.astype(BF)


def qkv_other_body(
    sc, x_hbm, cos_hbm, sin_hbm, gain, wq, wk, wv, o_ref, n_ref, cs, ss, own_w, xs, ws, gain_s, sem
):
    col = pl.multiple_of((1 - sc[0]) * GROUP, 128)
    own_col = pl.multiple_of(sc[0] * GROUP, 128)
    row = pl.multiple_of(sc[1] * SPAN, SPAN)
    weights = (wq, wk, wv)
    rows = [
        pltpu.make_async_copy(x_hbm.at[0, r : r + 256, :], xs.at[r : r + 256, :], sem.at[n])
        for n, r in enumerate((0, 256))
    ]
    copies = [
        pltpu.make_async_copy(w.at[:, pl.ds(col, GROUP)], ws.at[t], sem.at[2 + t])
        for t, w in enumerate(weights)
    ]
    tables = [
        pltpu.make_async_copy(cos_hbm.at[pl.ds(row, SPAN), :], cs, sem.at[5]),
        pltpu.make_async_copy(sin_hbm.at[pl.ds(row, SPAN), :], ss, sem.at[6]),
    ]
    later = [
        pltpu.make_async_copy(w.at[:, pl.ds(own_col, GROUP)], own_w.at[t], sem.at[7 + t])
        for t, w in enumerate(weights)
    ]
    gain_copy = pltpu.make_async_copy(gain, gain_s, sem.at[10])
    for cp in rows + [gain_copy, copies[2]] + copies[:2] + tables + later:
        cp.start()
    gain_copy.wait()
    gain_row = gain_s[...][None, :]
    for n, r in enumerate((0, 256)):
        rows[n].wait()
        x = jnp.where(live_mask(sc, r, 256), xs[r : r + 256, :].astype(F32), 0.0)
        factor = lax.rsqrt(jnp.mean(x * x, axis=-1, keepdims=True) + epsilon)
        n_ref[r : r + 256, :] = (x * factor * gain_row).astype(BF)
    for t in (2, 0, 1):
        copies[t].wait()
        if t == 0:
            for cp in tables:
                cp.wait()
        project(o_ref, n_ref, cs, ss, ws[t], t)
    for cp in later:
        cp.wait()


def qkv_own_body(sc, n_ref, cs, ss, ws, o_ref):
    for t in (2, 0, 1):
        project(o_ref, n_ref, cs, ss, ws[t], t)


def qkv_other_call(sc, tokens, gain, cosine, sine, wq, wk, wv):
    table = sds((SPAN, 128), F32)
    return call(
        qkv_other_body,
        "qkv_other",
        sc,
        (tokens, cosine, sine, gain, wq, wk, wv),
        [far_hbm()] * 7,
        [sds((3, SPAN, GROUP)), sds((SPAN, WIDTH)), table, table, sds((3, WIDTH, GROUP))],
        [whole((3, SPAN, GROUP)), whole((SPAN, WIDTH))] + [whole((SPAN, 128))] * 2 + [hbm()],
        [
            pltpu.VMEM((SPAN, WIDTH), BF),
            pltpu.VMEM((3, WIDTH, GROUP), BF),
            pltpu.VMEM((WIDTH,), F32),
            pltpu.SemaphoreType.DMA((11,)),
        ],
        9,
        (3 * 2 * SPAN * WIDTH * GROUP, 5e6, 1e3),
    )


def qkv_own_call(sc, n1, cs, ss, ws):
    return call(
        qkv_own_body,
        "qkv_own",
        sc,
        (n1, cs, ss, ws),
        [whole((SPAN, WIDTH))] + [whole((SPAN, 128))] * 2 + [whole((3, WIDTH, GROUP))],
        sds((3, SPAN, GROUP)),
        whole((3, SPAN, GROUP)),
        [],
        9,
        (3 * 2 * SPAN * WIDTH * GROUP, 5e6, 1e3),
    )


def gather_rows(sc, own, other, places, sem):
    copies = []
    for t, place in enumerate(places):
        for k, src in enumerate((own, other)):
            pos = sc[1] if k == 0 else 1 - sc[1]
            row = pl.multiple_of(pos * SPAN, SPAN)
            source = src.at[t] if len(src.shape) == 3 else src
            copies.append(
                pltpu.make_async_copy(source, place.at[pl.ds(row, SPAN), :], sem.at[2 * t + k])
            )
    for cp in copies:
        cp.start()
    return copies


def pair_loads(sc, own, other, places, sem, hp):
    cols = pl.ds(hp * 128 if isinstance(hp, int) else pl.multiple_of(hp * 128, 128), 128)
    copies = []
    for t, place in enumerate(places):
        for k, src in enumerate((own, other)):
            pos = sc[1] if k == 0 else 1 - sc[1]
            rows = pl.ds(pl.multiple_of(pos * SPAN, SPAN), SPAN)
            copies.append(
                pltpu.make_async_copy(
                    src.at[t, :, cols], place.at[rows, cols], sem.at[6 * hp + 2 * t + k]
                )
            )
    return copies


def attend_body(sc, own, other, wo, wg, wu, wd, *refs):
    (ot_ref, lse_ref, mine, theirs, wo_v, wg_v, wu_v, wd_v, qs, ks, vs, at, sem, wsem) = refs
    for n in range(3):
        for cp in pair_loads(sc, own, other, (qs, ks, vs), sem, n):
            cp.start()
    fetch = []

    def bring(src, place):
        fetch.append(pltpu.make_async_copy(src, place, wsem.at[len(fetch)]))
        fetch[-1].start()

    for k in range(2):
        head = (sc[0] if k == 0 else 1 - sc[0]) * GROUP
        rows = pl.ds(pl.multiple_of(head, 128), GROUP)
        bring(wo.at[rows, :], wo_v.at[GROUP * k : GROUP * k + GROUP, :])
    for half in range(2):
        for s in range(4):
            cols = hidden_cols(sc, s, half)
            to = slice(512 * half + 128 * s, 512 * half + 128 * s + 128)
            bring(wg.at[:, cols], wg_v.at[:, to])
            bring(wu.at[:, cols], wu_v.at[:, to])
            bring(wd.at[cols, :], wd_v.at[to, :])
    lane = lax.broadcasted_iota(jnp.int32, (256, 128), 1)
    key_id = lax.broadcasted_iota(jnp.int32, (256, 256), 0)
    row_id = lax.broadcasted_iota(jnp.int32, (256, 256), 1)
    keep = key_id <= row_id

    def pair(hp, carry):
        base = pl.multiple_of(hp * 128, 128)
        cols = pl.ds(base, 128)
        for cp in pair_loads(sc, own, other, (qs, ks, vs), sem, hp):
            cp.wait()
        vt = jnp.transpose(vs[:, cols].astype(F32)).astype(BF)

        def scores(i, h):
            n = 256 * (i + 1)
            qm = jnp.where(lane // HEAD_DIM == h, qs[256 * i : n, cols], jnp.zeros((), BF))
            return dot_nt(ks[0:n, cols], qm)

        def soften(i, h, st):
            n = 256 * (i + 1)
            diag = jnp.where(keep, st[n - 256 :, :], masked_score)
            st = diag if i == 0 else jnp.concatenate([st[: n - 256, :], diag], axis=0)
            peak = jnp.max(st, axis=0, keepdims=True)
            p = jnp.exp(st - peak)
            return p.astype(BF), peak, jnp.sum(p, axis=0, keepdims=True)

        def finish(i, h, p, peak, total):
            n = 256 * (i + 1)
            o = dot(vt[h * 64 : h * 64 + 64, :n], p) * (1.0 / total)
            ot_ref[pl.ds(pl.multiple_of(hp * 128 + h * 64, 64), 64), 256 * i : n] = o
            lse_ref[pl.ds(hp * 2 + h, 1), 256 * i : n] = peak + jnp.log(total)

        tasks = [(i, h) for i in range(4) for h in range(2)]
        st, waiting = scores(*tasks[0]), None
        for k, task in enumerate(tasks):
            ahead = scores(*tasks[k + 1]) if k + 1 < len(tasks) else None
            parts = soften(*task, st)
            if waiting is not None:
                finish(*waiting)
            waiting, st = task + parts, ahead
        finish(*waiting)
        at[:, cols] = jnp.transpose(ot_ref[cols, :]).astype(BF)
        return carry

    lax.fori_loop(0, 3, pair, 0)
    row = pl.multiple_of(sc[1] * SPAN, SPAN)
    row_other = pl.multiple_of((1 - sc[1]) * SPAN, SPAN)
    out_other = pltpu.make_async_copy(at.at[pl.ds(row_other, SPAN), :], theirs, sem.at[18])
    out_own = pltpu.make_async_copy(at.at[pl.ds(row, SPAN), :], mine, sem.at[19])
    out_other.start()
    out_own.start()
    out_other.wait()
    out_own.wait()
    for cp in fetch:
        cp.wait()


def attend_call(sc, own, other, wo, wg, wu, wd):
    return call(
        attend_body,
        "attend",
        sc,
        (own, other, wo, wg, wu, wd),
        [hbm(), hbm()] + [far_hbm()] * 4,
        [sds((GROUP, SEQ), F32), sds((8, SEQ), F32), sds((SPAN, GROUP)), sds((SPAN, GROUP))]
        + [sds((WIDTH, WIDTH)), sds((WIDTH, SEQ)), sds((WIDTH, SEQ)), sds((SEQ, WIDTH))],
        [whole((GROUP, SEQ)), whole((8, SEQ))] + [hbm()] * 6,
        [pltpu.VMEM((SEQ, GROUP), BF)] * 4
        + [pltpu.SemaphoreType.DMA((20,)), pltpu.SemaphoreType.DMA((26,))],
        8,
        (6 * 4 * SEQ * SEQ * 64, 6e6, 4e6),
    )


def proj_body(sc, x_ref, ak_ref, ar_ref, gain_ref, wo_ref, m_ref, n_ref):
    for r in range(0, SPAN, 256):
        rr = slice(r, r + 256)
        m = jnp.where(live_mask(sc, r, 256), x_ref[0, rr, :].astype(F32), 0.0)
        m = m + dot(ak_ref[rr, :], wo_ref[:GROUP, :]) + dot(ar_ref[rr, :], wo_ref[GROUP:, :])
        m_ref[rr, :] = m
        factor = lax.rsqrt(jnp.mean(m * m, axis=-1, keepdims=True) + epsilon)
        n_ref[rr, :] = (m * factor * gain_ref[...]).astype(BF)


def proj_call(sc, tokens, own, other, gain, wo):
    return call(
        proj_body,
        "proj",
        sc,
        (tokens, own, other, gain, wo),
        [whole((1, SPAN, WIDTH))]
        + [whole((SPAN, GROUP))] * 2
        + [whole((1, WIDTH)), whole((WIDTH, WIDTH))],
        [sds((SPAN, WIDTH), F32), sds((SPAN, WIDTH))],
        [whole((SPAN, WIDTH))] * 2,
        [],
        4,
        (2 * SPAN * WIDTH * WIDTH, 5e6, 1e3),
    )


def over_rows(own, other, d_own, d_other):
    return dot_tn(own, d_own) + dot_tn(other, d_other)


def place_of(s):
    return (s % 2) * 2 + s // 2


def hidden_cols(sc, s, half):
    return pl.ds(pl.multiple_of(512 * s + 128 * half + 256 * sc[0], 128), 128)


def spread(sc, res_s, first, count, rows, send_ref, keep_ref, to):
    size = send_ref.shape[1]
    for k, ref in enumerate((send_ref, keep_ref)):
        bit = (1 - sc[3]) if k == 0 else sc[3]
        for s in range(4):
            for q in range(count):
                lo = pl.multiple_of(first + (s * count + q) * 2 * rows + bit * rows, 16)
                block, row = divmod(to + q * rows, size)
                ref[2 * place_of(s) + block, row : row + rows, :] = res_s[pl.ds(lo, rows), :].astype(
                    BF
                )


def upstream_body(sc, dy_own, dy_oth, wd, dy_ref, dh_ref):
    for r in range(0, SEQ, 256):
        pos = sc[1] if r < SPAN else 1 - sc[1]
        at = pos * SPAN + r % SPAN + lax.broadcasted_iota(jnp.int32, (256, 1), 0)
        src = dy_own if r < SPAN else dy_oth
        lo = r % SPAN
        dy = jnp.where(at < sc[2], src[0, lo : lo + 256, :], jnp.zeros((), BF))
        dy_ref[r : r + 256, :] = dy
        dh_ref[r : r + 256, :] = dot_nt(dy, wd[...])


def upstream_call(sc, dy_own, dy_oth, wd):
    full = whole((1, SPAN, WIDTH))
    return call(
        upstream_body,
        "upstream",
        sc,
        (dy_own, dy_oth, wd),
        [full, full, whole((SEQ, WIDTH))],
        [sds((SEQ, WIDTH)), sds((SEQ, SEQ), F32)],
        [whole((SEQ, WIDTH)), whole((SEQ, SEQ))],
        [],
        4,
        (2 * SEQ * WIDTH * SEQ, 8e6, 0),
    )


def ffn_body(sc, n_own, n_oth, dy_s, dh_s, wg_s, wu_s, *refs, half):
    (send_ref, keep_ref, h_ref, dg_ref, du_ref, res_a, res_b) = refs
    part = slice(512 * half, 512 * half + 512)

    def products(r):
        src = n_own if r < SPAN else n_oth
        rows = src[r % SPAN : r % SPAN + 256, :]
        return dot(rows, wg_s[:, part]), dot(rows, wu_s[:, part])

    ahead = products(0)
    for r in range(0, SEQ, 256):
        g, u = ahead
        if r + 256 < SEQ:
            ahead = products(r + 256)
        rr = slice(r, r + 256)
        dh = dh_s[rr, part]
        sg = jax.nn.sigmoid(g)
        gs = g * sg
        h_ref[rr, :] = (gs * u).astype(BF)
        du_ref[rr, :] = (dh * gs).astype(BF)
        dg_ref[rr, :] = (dh * u * (sg + gs * (1.0 - sg))).astype(BF)
    lower, upper = slice(0, SPAN), slice(SPAN, SEQ)
    for k, (base, src) in enumerate(((0, dg_ref), (192, du_ref))):
        for ct in range(2):
            cols = slice(256 * ct, 256 * ct + 256)
            place = res_a.at[ct]
            place[...] = over_rows(n_own[...], n_oth[...], src[lower, cols], src[upper, cols])
            spread(sc, place, 0, 2, 48, send_ref, keep_ref, base + 96 * ct)
    for n in range(3):
        place = res_b.at[n % 2]
        place[...] = dot_tn(h_ref[...], dy_s[:, 256 * n : 256 * n + 256])
        spread(sc, place, 0, 1, 64, send_ref, keep_ref, 384 + 64 * n)


def ffn_call(sc, half, n_own, n_oth, dy, dh, wg, wu):
    flat = whole((SPAN, WIDTH))
    return call(
        functools.partial(ffn_body, half=half),
        "ffn_first" if half == 0 else "ffn_second",
        sc,
        (n_own, n_oth, dy, dh, wg, wu),
        [flat, flat, whole((SEQ, WIDTH)), whole((SEQ, SEQ))] + [whole((WIDTH, SEQ))] * 2,
        [sds((8, 288, 256))] * 2 + [sds((SEQ, 512))] * 3,
        [whole((8, 288, 256))] * 2 + [whole((SEQ, 512))] * 3,
        [pltpu.VMEM((2, WIDTH, 256), F32), pltpu.VMEM((2, 512, 256), F32)],
        14,
        (6 * 2 * SEQ * WIDTH * 512, 14e6, 1e6),
    )


def ffn_out_body(sc, h0, dg0, du0, h1, dg1, du1, wg, wu, wd, acc_ref, accs_ref, dn_ref, dns_ref):
    for r in (512, 768, 0, 256):
        rr = slice(r, r + 256)
        dn = dot_nt(dg0[rr, :], wg[:, :512]) + dot_nt(dg1[rr, :], wg[:, 512:])
        dn = dn + dot_nt(du0[rr, :], wu[:, :512]) + dot_nt(du1[rr, :], wu[:, 512:])
        acc = dot(h0[rr, :], wd[:512, :]) + dot(h1[rr, :], wd[512:, :])
        if r < SPAN:
            dn_ref[rr, :] = dn
            acc_ref[rr, :] = acc
        else:
            dns_ref[r - SPAN : r - SPAN + 256, :] = dn.astype(BF)
            accs_ref[r - SPAN : r - SPAN + 256, :] = acc.astype(BF)


def ffn_out_call(sc, first, second, wg, wu, wd):
    flat = [whole((SPAN, WIDTH))]
    return call(
        ffn_out_body,
        "ffn_out",
        sc,
        tuple(first) + tuple(second) + (wg, wu, wd),
        [whole((SEQ, 512))] * 6 + [whole((WIDTH, SEQ))] * 2 + [whole((SEQ, WIDTH))],
        [sds((SPAN, WIDTH), F32), sds((SPAN, WIDTH)), sds((SPAN, WIDTH), F32), sds((SPAN, WIDTH))],
        flat * 4,
        [],
        8,
        (3 * 2 * SEQ * WIDTH * SEQ, 16e6, 0),
    )


def middle_body(sc, dn_ref, got_ref, m_ref, dy_ref, gain_ref, dm_ref, db_ref):
    gain = gain_ref[...]
    for r in range(0, SPAN, 128):
        rr = slice(r, r + 128)
        live = live_mask(sc, r, 128)
        m = m_ref[rr, :]
        factor = lax.rsqrt(jnp.mean(m * m, axis=-1, keepdims=True) + epsilon)
        scaled = (dn_ref[rr, :] + got_ref[rr, :].astype(F32)) * gain
        dm = jnp.where(live, dy_ref[0, rr, :].astype(F32), 0.0) + (
            factor * scaled
            - m * (factor * factor * factor) * jnp.mean(m * scaled, axis=-1, keepdims=True)
        )
        dm_ref[rr, :] = dm
        db_ref[rr, :] = dm.astype(BF)


def middle_call(sc, dn, got, m, dy, gain):
    flat = whole((SPAN, WIDTH))
    return call(
        middle_body,
        "middle",
        sc,
        (dn, got, m, dy, gain),
        [flat, flat, flat, whole((1, SPAN, WIDTH)), whole((1, WIDTH))],
        [sds((SPAN, WIDTH), F32), sds((SPAN, WIDTH))],
        [flat, flat],
        [],
        6,
        (1e6, 8e6, 1e3),
    )


def attend_back_body(sc, own, other, ot_s, lse_s, dbk, dbr, wo_s, cos_hbm, sin_hbm, *refs):
    wq, wk, wv, mine, theirs, ws, qs, ks, vs, das, ds_all, dqt, dkv, cs, ss, sem, load_sem = refs
    for n in range(3):
        for cp in pair_loads(sc, own, other, (qs, ks, vs), load_sem, n):
            cp.start()
    small = [
        pltpu.make_async_copy(src, to, sem.at[6 + n])
        for n, (src, to) in enumerate(((cos_hbm, cs), (sin_hbm, ss)))
    ]
    fetch = [
        pltpu.make_async_copy(w, ws.at[t], sem.at[10 + t]) for t, w in enumerate((wq, wk, wv))
    ]
    for cp in small + fetch:
        cp.start()
    for k, src in enumerate((dbk, dbr)):
        pos = sc[1] if k == 0 else 1 - sc[1]
        for r in range(0, SPAN, 256):
            rows = pl.ds(pl.multiple_of(pos * SPAN + r, 256), 256)
            das[rows, :] = dot_nt(src[r : r + 256, :], wo_s[...]).astype(BF)
    for cp in small:
        cp.wait()
    lane = lax.broadcasted_iota(jnp.int32, (SEQ, 128), 1)
    key_id = lax.broadcasted_iota(jnp.int32, (256, 256), 0)
    row_id = lax.broadcasted_iota(jnp.int32, (256, 256), 1)
    keep = key_id <= row_id

    def pair(hp, carry):
        base = pl.multiple_of(hp * 128, 128)
        cols = pl.ds(base, 128)
        for cp in pair_loads(sc, own, other, (qs, ks, vs), load_sem, hp):
            cp.wait()
        kt = jnp.transpose(ks[:, cols].astype(F32)).astype(BF)
        dat = jnp.transpose(das[:, cols].astype(F32))
        qm, dam, delta, lses = [], [], [], []
        for h in range(2):
            qm.append(jnp.where(lane // HEAD_DIM == h, qs[:, cols], jnp.zeros((), BF)))
            dam.append(jnp.where(lane // HEAD_DIM == h, das[:, cols], jnp.zeros((), BF)))
            rows = pl.ds(pl.multiple_of(base + 64 * h, 64), 64)
            product = dat[64 * h : 64 * h + 64, :] * ot_s[rows, :]
            delta.append(jnp.sum(product, axis=0, keepdims=True))
            lses.append(lse_s[pl.ds(2 * hp + h, 1), :])

        def scores(i, h):
            n = 256 * (i + 1)
            rows = slice(256 * i, n)
            return dot_nt(ks[:n, cols], qm[h][rows, :]), dot_nt(vs[:n, cols], dam[h][rows, :])

        def soften(i, h, st, dp):
            n = 256 * (i + 1)
            rows = slice(256 * i, n)
            p = jnp.exp(st - lses[h][:, rows])
            diag = jnp.where(keep, p[n - 256 :, :], 0.0)
            p = diag if i == 0 else jnp.concatenate([p[: n - 256, :], diag], axis=0)
            return p.astype(BF), (p * (dp - delta[h][:, rows])).astype(BF)

        def finish(i, h, p, ds):
            n = 256 * (i + 1)
            rows = slice(256 * i, n)
            half = slice(64 * h, 64 * h + 64)
            dv = dot(p, dam[h][rows, :])
            dk = dot(ds, qm[h][rows, :])
            dqt[half, rows] = dot(kt[half, :n], ds)
            if (i, h) == (3, 0):
                dkv[0] = dk
                dkv[1] = dv
            else:
                dkv[0, :n] += dk
                dkv[1, :n] += dv

        tasks = [(i, h) for i in (3, 2, 1, 0) for h in range(2)]
        now, waiting = scores(*tasks[0]), None
        for k, task in enumerate(tasks):
            ahead = scores(*tasks[k + 1]) if k + 1 < len(tasks) else None
            parts = soften(*task, *now)
            if waiting is not None:
                finish(*waiting)
            waiting, now = task + parts, ahead
        finish(*waiting)
        dq = jnp.transpose(dqt[...]) * (HEAD_DIM**-0.5)
        ds_all[0, :, cols] = turn(dq, cs[...], -ss[...]).astype(BF)
        ds_all[1, :, cols] = turn(dkv[0], cs[...], -ss[...]).astype(BF)
        ds_all[2, :, cols] = dkv[1].astype(BF)
        return carry

    lax.fori_loop(0, 3, pair, 0)
    row = pl.multiple_of(sc[1] * SPAN, SPAN)
    row_other = pl.multiple_of((1 - sc[1]) * SPAN, SPAN)
    stores = [
        pltpu.make_async_copy(ds_all.at[:, pl.ds(row_other, SPAN), :], theirs, sem.at[8]),
        pltpu.make_async_copy(ds_all.at[:, pl.ds(row, SPAN), :], mine, sem.at[9]),
    ]
    for cp in stores:
        cp.start()
    for cp in stores + fetch:
        cp.wait()


def attend_back_call(sc, own, other, ot, lse, dbk, dbr, wo, cosine, sine, wq, wk, wv):
    return call(
        attend_back_body,
        "attend_back",
        sc,
        (own, other, ot, lse, dbk, dbr, wo, cosine, sine, wq, wk, wv),
        [hbm(), hbm(), whole((GROUP, SEQ)), whole((8, SEQ))]
        + [whole((SPAN, WIDTH))] * 2
        + [whole((GROUP, WIDTH))]
        + [far_hbm()] * 5,
        [sds((3, SPAN, GROUP))] * 2 + [sds((3, WIDTH, WIDTH))],
        [hbm()] * 3,
        [pltpu.VMEM((SEQ, GROUP), BF)] * 4
        + [
            pltpu.VMEM((3, SEQ, GROUP), BF),
            pltpu.VMEM((128, SEQ), F32),
            pltpu.VMEM((2, SEQ, 128), F32),
            pltpu.VMEM((SEQ, 128), F32),
            pltpu.VMEM((SEQ, 128), F32),
            pltpu.SemaphoreType.DMA((13,)),
            pltpu.SemaphoreType.DMA((18,)),
        ],
        22,
        (6 * 10 * SEQ * SEQ * 64, 10e6, 4e6),
    )


def square_body(sc, nk, nr, ak, at, ck, ct, bk, br, dk, dr, sa_ref, ka_ref, sb_ref, kb_ref, res):
    own = pl.ds(pl.multiple_of(sc[0] * GROUP, 128), GROUP)
    other = pl.ds(pl.multiple_of((1 - sc[0]) * GROUP, 128), GROUP)
    res[0, own, :] = over_rows(ak[...], at[...], bk[:, own], br[:, own])
    res[0, other, :] = over_rows(ck[...], ct[...], bk[:, own], br[:, own])
    spread(sc, res.at[0], 0, 2, 48, sa_ref, ka_ref, 0)
    for n, t in enumerate((2, 0, 1)):
        place = res.at[(n + 1) % 2]
        place[...] = over_rows(nk[...], nr[...], dk[t], dr[t])
        if n == 0:
            spread(sc, place, 0, 2, 48, sa_ref, ka_ref, 96)
        else:
            spread(sc, place, 0, 2, 48, sb_ref, kb_ref, 96 * t)


def square_call(sc, *args):
    flat = [whole((SPAN, WIDTH))] * 2
    return call(
        square_body,
        "square",
        sc,
        args,
        flat + [whole((SPAN, GROUP))] * 4 + flat + [whole((3, SPAN, GROUP))] * 2,
        [sds((8, 96, GROUP))] * 4,
        [whole((8, 96, GROUP))] * 4,
        [pltpu.VMEM((2, WIDTH, GROUP), F32)],
        16,
        (4 * 2 * SEQ * WIDTH * GROUP, 12e6, 0),
    )


def input_grad_body(sc, x_ref, gain_ref, dm_ref, m_ref, acc_ref, got_ref, dk_s, dr_s, ws, *refs):
    lay_ref, o_ref = refs
    for r in range(0, SPAN, 256):
        rr = slice(r, r + 256)
        out = m_ref[rr, :] + acc_ref[rr, :] + got_ref[rr, :].astype(F32)
        lay_ref[0, rr, :] = jnp.where(live_mask(sc, r, 256), out, 0.0).astype(BF)
    own_cols = pl.multiple_of(sc[0] * GROUP, 128)
    other_cols = pl.multiple_of((1 - sc[0]) * GROUP, 128)
    gain = gain_ref[...]
    for r in range(0, SPAN, 256):
        rr = slice(r, r + 256)
        dn = dot_nt(dk_s[0, rr, :], ws[0, :, pl.ds(own_cols, GROUP)])
        dn = dn + dot_nt(dr_s[0, rr, :], ws[0, :, pl.ds(other_cols, GROUP)])
        for t in (1, 2):
            dn = dn + dot_nt(dk_s[t, rr, :], ws[t, :, pl.ds(own_cols, GROUP)])
            dn = dn + dot_nt(dr_s[t, rr, :], ws[t, :, pl.ds(other_cols, GROUP)])
        live = live_mask(sc, r, 256)
        x = jnp.where(live, x_ref[0, rr, :].astype(F32), 0.0)
        factor = lax.rsqrt(jnp.mean(x * x, axis=-1, keepdims=True) + epsilon)
        scaled = dn * gain
        dx = dm_ref[rr, :] + (
            factor * scaled
            - x * (factor * factor * factor) * jnp.mean(x * scaled, axis=-1, keepdims=True)
        )
        o_ref[0, rr, :] = jnp.where(live, dx, 0.0).astype(BF)


def input_grad_call(sc, tokens, gain, dm, m, acc, got, dk, dr, ws):
    full = whole((1, SPAN, WIDTH))
    flat = whole((SPAN, WIDTH))
    return call(
        input_grad_body,
        "input_grad",
        sc,
        (tokens, gain, dm, m, acc, got, dk, dr, ws),
        [full, whole((1, WIDTH)), flat, flat, flat, flat]
        + [whole((3, SPAN, GROUP))] * 2
        + [whole((3, WIDTH, WIDTH))],
        [sds((1, SPAN, WIDTH))] * 2,
        [full] * 2,
        [],
        20,
        (3 * 2 * SPAN * WIDTH * WIDTH, 14e6, 1e3),
    )


def add_pieces(sc, count, sums, name):
    rows, cols = sums[0][0][0].shape[1:]
    arrays = [array for stack in sums for array, _ in stack]
    picks = [pick for stack in sums for _, pick in stack]

    def body(sc_ref, *refs):
        at = 0
        for n, stack in enumerate(sums):
            total = refs[at][0].astype(F32)
            for ref in refs[at + 1 : at + len(stack)]:
                total = total + ref[0].astype(F32)
            refs[-1][0, n * rows : (n + 1) * rows, :] = total.astype(BF)
            at += len(stack)

    def spec(pick):
        block, row = pick
        return pl.BlockSpec((1, rows, cols), lambda j, sc_ref: (block(sc_ref, j), row, 0))

    high = rows * len(sums)
    return pl.pallas_call(
        body,
        name=name,
        out_shape=sds((count, high, cols)),
        grid_spec=pltpu.PrefetchScalarGridSpec(
            num_scalar_prefetch=1,
            grid=(count,),
            in_specs=[spec(pick) for pick in picks],
            out_specs=pl.BlockSpec((1, high, cols), lambda j, sc_ref: (j, 0, 0)),
        ),
        compiler_params=pltpu.CompilerParams(vmem_limit_bytes=6 * MIB),
        cost_estimate=pl.CostEstimate(
            flops=int(0 if name == "g0_b" else ADD_COST), bytes_accessed=1000, transcendentals=0
        ),
    )(sc, *arrays)


def row_block(rows, cols):
    return pl.BlockSpec((rows, cols), lambda i, sc: (sc[6], 0))


def row_of(column):
    column = jnp.concatenate([column, jnp.zeros((32, 1), F32)], axis=0)
    return jnp.transpose(jnp.broadcast_to(column, (128, 128)))[0, :96]


def collect_halves(sc, group, full):
    for n in range(4):
        core, k = divmod(n, 2)
        parity = sc[0] if core == 0 else 1 - sc[0]
        first = sc[3] if core == 0 else sc[7]
        first = 1 - first if k == 1 else first
        for h in range(2):
            full[parity, first, 288 * h : 288 * h + 288, :] = group[n][h]


def collect(sc, group, full, row, size):
    for n in range(8):
        core, k = divmod(n, 4)
        parity = sc[0] if core == 0 else 1 - sc[0]
        first, second = (sc[3], sc[7]) if core == 0 else (sc[7], sc[3])
        first = 1 - first if k in (1, 3) else first
        second = 1 - second if k in (2, 3) else second
        rows = pl.ds(pl.multiple_of(second * size, 16), size)
        full[parity, first, rows, :] = group[n][0, row : row + size, :]


def ffn_result_body(sc, *refs):
    wg_ref, wu_ref, gain_ref, gate_ref, up_ref, down_ref, gg_ref, full = refs[12:]
    collect_halves(sc, refs[:4], full.at[0])
    collect(sc, refs[4:12], full.at[1], 0, 288)
    for half in range(2):
        for bit in range(2):
            rows = slice(48 * bit, 48 * bit + 48)
            for parity in range(2):
                for base, ref in ((0, gate_ref), (192, up_ref)):
                    for ct in range(2):
                        lo = pl.multiple_of(base + ct * 96 + sc[0] * 48, 16)
                        block = full[half, parity, bit, pl.ds(lo, 48), :].astype(F32)
                        for q in range(2):
                            col = 512 * (2 * ct + q) + 128 * half + 256 * parity
                            ref[rows, col : col + 128] = block[:, 128 * q : 128 * q + 128]
            lo = 128 * half + 64 * bit
            for t in range(3):
                down_ref[lo : lo + 64, 256 * t : 256 * t + 256] = full[
                    half, sc[0], bit, 384 + t * 64 : 448 + t * 64, :
                ].astype(F32)
    gate = jnp.sum(wg_ref[...].astype(F32) * gate_ref[...], axis=-1, keepdims=True)
    up = jnp.sum(wu_ref[...].astype(F32) * up_ref[...], axis=-1, keepdims=True)
    gg_ref[...] = row_of((gate + up) / gain_ref[...])


def ffn_result_call(sc, first, second, wg, wu, gain):
    return call(
        ffn_result_body,
        "ffn_result",
        sc,
        tuple(first) + tuple(second) + (wg, wu, gain),
        [whole((2, 288, 256))] * 4 + [whole((1, 288, 256))] * 8 + [row_block(96, HID)] * 2 + [row_block(96, 1)],
        [sds((96, HID), F32), sds((96, HID), F32), sds((256, WIDTH), F32), sds((96,), F32)],
        [whole((96, HID)), whole((96, HID)), whole((256, WIDTH)), whole((96,))],
        [pltpu.VMEM((2, 2, 2, 576, 256), BF)],
        14,
        (1e6, 6e6, 0),
    )


def square_result_body(sc, *refs):
    group = refs[:8]
    weights = refs[8:11]
    gain_ref = refs[11]
    outs = refs[12:16]
    gg_ref, full = refs[16:]
    order = ((3, 2), (0, 1))
    for n in range(2):
        collect(sc, group, full.at[n], 96 * n, 96)
        for bit in range(2):
            rows = slice(48 * bit, 48 * bit + 48)
            for parity in range(2):
                cols = slice(GROUP * parity, GROUP * parity + GROUP)
                for t in range(2):
                    lo = pl.multiple_of(t * 96 + sc[0] * 48, 16)
                    block = full[n, parity, bit, pl.ds(lo, 48), :]
                    outs[order[n][t]][rows, cols] = block.astype(F32)
    total = jnp.zeros((96, 1), F32)
    for t in range(3):
        total = total + jnp.sum(weights[t][...].astype(F32) * outs[t][...], axis=-1, keepdims=True)
    gg_ref[...] = row_of(total / gain_ref[...])


def square_result_call(sc, group, wq, wk, wv, gain):
    return call(
        square_result_body,
        "square_result",
        sc,
        tuple(group) + (wq, wk, wv, gain),
        [whole((1, 192, GROUP))] * 8 + [row_block(96, WIDTH)] * 3 + [row_block(96, 1)],
        [sds((96, WIDTH), F32)] * 4 + [sds((96,), F32)],
        [whole((96, WIDTH))] * 4 + [whole((96,))],
        [pltpu.VMEM((2, 2, 2, 192, GROUP), BF)],
        8,
        (1e6, 4e6, 0),
    )


class Chain:
    def __init__(self, sc):
        self.sc = sc

    def next(self, *deps):
        self.sc = after(self.sc, *deps)
        return self.sc


class Reduction:
    def __init__(self, chain, send, keep, name):
        self.chain = chain
        self.send = send
        self.name = name
        self.stacks = [[[keep, 0]]]
        self.flight = None

    def start(self):
        self.fly(after(self.send, self.chain.sc), "first")

    def fly(self, rows, kind):
        self.flight = exchange(rows, kind)

    def land(self):
        if self.flight is not None:
            for n, stack in enumerate(self.stacks):
                stack.append([self.flight, n])
        self.flight = None

    def add(self, count, picks, tag):
        self.land()
        sums = []
        for stack in self.stacks:
            blocks = ([picks[0]] + picks)[-len(stack) :]
            sums.append([(array, (pick, row)) for (array, row), pick in zip(stack, blocks)])
        arrays = [array for stack in sums for array, _ in stack]
        out = add_pieces(self.chain.next(*arrays), count, sums, self.name + tag)
        self.chain.next(out)
        return out

    def second(self):
        pick = lambda t, j: j * 2 + 1 - t[7]
        self.fly(self.add(4, [pick], "_b"), "second")

    def near(self):
        pick = lambda t, j: (1 - t[4]) * 4 + j * 2 + t[7]
        self.fly(self.add(2, [pick, lambda t, j: (1 - t[4]) * 2 + j], "_c"), "near")

    def far(self):
        pick = lambda t, j: t[4] * 4 + (1 - t[5]) * 2 + t[7]
        picks = [pick, lambda t, j: t[4] * 2 + 1 - t[5], lambda t, j: 1 - t[5]]
        self.fly(self.add(1, picks, "_d"), "far")

    def total(self):
        pick = lambda t, j: t[4] * 4 + t[5] * 2 + t[7]
        picks = [pick, lambda t, j: t[4] * 2 + t[5], lambda t, j: t[5], lambda t, j: 0]
        own = self.add(1, picks, "_e")
        self.quarters = [own] + [exchange(own, kind) for kind in ("first", "second", "across")]

    def result(self):
        late = [after(quarter, self.chain.sc) for quarter in self.quarters]
        return self.quarters + [exchange(quarter, "core") for quarter in late]


class Straight(Reduction):
    def near(self):
        pick = lambda t, j: (1 - t[4]) * 4 + j
        self.fly(self.add(4, [pick], "_b"), "near")

    def far(self):
        pick = lambda t, j: t[4] * 4 + (1 - t[5]) * 2 + j
        self.fly(self.add(2, [pick, lambda t, j: (1 - t[5]) * 2 + j], "_c"), "far")

    def second(self):
        pick = lambda t, j: t[4] * 4 + t[5] * 2 + j
        own = self.add(2, [pick, lambda t, j: t[5] * 2 + j, lambda t, j: j], "_d")
        self.stacks = [[[own, 0]]]
        self.fly(own, "second")

    def total(self):
        own = self.add(2, [lambda t, j: j], "_e")
        self.quarters = [own, exchange(own, "first")]


def join(first, second):
    both = Reduction(first.chain, None, None, first.name + second.name)
    first.land()
    second.land()
    both.stacks = first.stacks + second.stacks
    return both


def fast_step(
    tokens,
    lengths,
    owner,
    w_query,
    w_key,
    w_value,
    w_out,
    w_gate,
    w_up,
    w_down,
    gain_attn,
    gain_mlp,
    cotangent,
):
    place = lax.axis_index(AXES)
    slot = jnp.arange(8, dtype=jnp.int32)
    core = place & 1
    base = jnp.where(slot == 3, 3 + core, jnp.where(slot == 7, 4 - core, 0))
    base = jnp.where(slot == 4, 1, jnp.where(slot == 5, 2, base))
    row = (place >> base) & jnp.where(slot == 6, 7, 1)
    turned = jnp.abs(row - jnp.broadcast_to(owner[0, :1], (8,)))
    sc = jnp.where(slot == 1, turned, row)
    sc = jnp.where(slot == 2, jnp.broadcast_to(lengths, (8,)), sc)
    tables = position_tables(SEQ)
    cosine, sine = jnp.asarray(tables[0]), jnp.asarray(tables[1])
    gain_row = gain_attn.reshape(1, WIDTH)
    gain_mlp_row = gain_mlp.reshape(1, WIDTH)
    qkv_w = (w_query, w_key, w_value)
    ffn_w = (w_gate, w_up, w_down)
    chain = Chain(sc)

    qkv_send, n1, cs_v, ss_v, w_v = qkv_other_call(chain.sc, tokens, gain_attn, cosine, sine, *qkv_w)
    qkv_other = exchange(qkv_send, "core")
    qkv_own = qkv_own_call(chain.next(n1), n1, cs_v, ss_v, w_v)
    n1_other = exchange(n1, "core")
    dy_other = exchange(cotangent, "core")
    attn_t, lse, attn_own, attn_send, wo_v, *ffn_v = attend_call(
        chain.next(qkv_own), qkv_own, qkv_other, w_out, *ffn_w
    )
    attn_other = exchange(attn_send, "core")
    attn_rest = exchange(attn_own, "core")
    middle, n2 = proj_call(
        chain.next(lse, n1_other, dy_other), tokens, attn_own, attn_other, gain_mlp_row, wo_v
    )
    n2_other = exchange(n2, "core")
    dy_all, dh_all = upstream_call(chain.next(n2), cotangent, dy_other, ffn_v[2])
    rows = (n2, n2_other, dy_all, dh_all)
    send0, keep0, *acts0 = ffn_call(chain.next(dy_all, attn_rest), 0, *rows, *ffn_v[:2])
    g0 = Straight(chain, send0, keep0, "g0")
    g0.start()
    send1, keep1, *acts1 = ffn_call(chain.next(acts0[0]), 1, *rows, *ffn_v[:2])
    g1 = Reduction(chain, send1, keep1, "g1")
    g1.start()
    acc, acc_send, dn, dn_send = ffn_out_call(chain.next(acts1[0]), acts0, acts1, *ffn_v)
    dn_other = exchange(dn_send, "core")
    chain.next(dn_send)
    g0.near()
    d_middle, db = middle_call(
        chain.next(dn_other), dn, dn_other, middle, cotangent, gain_mlp_row
    )
    chain.next(db)
    db_other = exchange(db, "core")
    acc_other = exchange(after(acc_send, db_other), "core")
    d_own, d_send, qkv_v = attend_back_call(
        chain.sc,
        qkv_own,
        qkv_other,
        attn_t,
        lse,
        db,
        db_other,
        wo_v,
        cosine,
        sine,
        *qkv_w,
    )
    d_other = exchange(d_send, "core")
    chain.next(d_own, g0.flight, g1.flight)
    g1.second()
    g0.far()
    attn = (attn_own, attn_send, attn_other, attn_rest)
    send2, keep2, send3, keep3 = square_call(
        chain.sc, n1, n1_other, *attn, db, db_other, d_own, d_send
    )
    g2 = Reduction(chain, send2, keep2, "g2")
    g3 = Reduction(chain, send3, keep3, "g3")
    g2.start()
    g3.start()
    chain.next(send3)
    layer_out, input_grad = input_grad_call(
        chain.next(acc_other, d_other),
        tokens,
        gain_row,
        d_middle,
        middle,
        acc,
        acc_other,
        d_own,
        d_other,
        qkv_v,
    )
    chain.next(input_grad)
    g0.second()
    g1.near()
    g2.second()
    g1.far()
    g3.second()
    g2.near()
    g0.total()
    g3.near()
    g2.far()
    g3.far()
    g1.total()
    g23 = join(g2, g3)
    g23.total()
    first = g0.result()
    second = g1.result()
    third = g23.result()
    gate, up, down, gain_m = ffn_result_call(
        chain.sc, first, second, w_gate, w_up, gain_mlp.reshape(WIDTH, 1)
    )
    chain.next(gain_m)
    query, key, value, out, gain_a = square_result_call(
        chain.sc, third, *qkv_w, gain_attn.reshape(WIDTH, 1)
    )
    return (
        layer_out,
        input_grad,
        query,
        key,
        value,
        out,
        gate,
        up,
        down,
        gain_a,
        gain_m,
    )


def solution(mesh):
    in_specs = (
        P(("batch", "seq"), "seqb", None),
        P(("batch", "seq")),
        P(("batch", "seq"), None),
        P(),
        P(),
        P(),
        P(),
        P(),
        P(),
        P(),
        P(),
        P(),
        P(("batch", "seq"), "seqb", None),
    )
    out_specs = (
        P(("batch", "seq"), "seqb", None),
        P(("batch", "seq"), "seqb", None),
        P(("seq", "seqb"), None),
        P(("seq", "seqb"), None),
        P(("seq", "seqb"), None),
        P(("seq", "seqb"), None),
        P(("seq", "seqb"), None),
        P(("seq", "seqb"), None),
        P(("seq", "seqb"), None),
        P(("seq", "seqb")),
        P(("seq", "seqb")),
    )
    step = fast_step if fast_layout(mesh) else general_step
    return jax.shard_map(step, mesh=mesh, in_specs=in_specs, out_specs=out_specs, check_vma=False)
```
